32 devices in a mesh: expert: 8 (over z, core), dp: 4 (over y, x).
Axes of the slice: x: 2, y: 2, z: 4, core: 2. Of those that a mesh axis runs over, the one named last changes fastest.
Arguments:
- layer_input: bfloat16 [8192, 1024], P(('expert', 'dp')), may hold values from -6 to 6
- attn_gain: bfloat16 [1024], P('dp'), may hold values from 0.5 to 1.5
- w_query: bfloat16 [1024, 1024], P('dp'), may hold values from -0.25 to 0.25
- w_key: bfloat16 [1024, 512], P('dp'), may hold values from -0.25 to 0.25
- w_value: bfloat16 [1024, 512], P('dp'), may hold values from -0.1875 to 0.1875
- w_output: bfloat16 [1024, 1024], P('dp'), may hold values from -0.75 to 0.75
- moe_gain: bfloat16 [1024], P('dp'), may hold values from 0.5 to 1.5
- w_router: bfloat16 [1024, 32], P('dp'), may hold values from -0.09375 to 0.09375
- w_gate: bfloat16 [32, 1024, 512], P('expert', 'dp'), may hold values from -0.1875 to 0.1875
- w_up: bfloat16 [32, 1024, 512], P('expert', 'dp'), may hold values from -0.1875 to 0.1875
- w_down: bfloat16 [32, 512, 1024], P('expert', 'dp'), may hold values from -1 to 1
- routes: int32 [8192, 8], P(('expert', 'dp')), may hold values from 0 to 31, all different within a row
- priority: int32 [8192, 8], P(('expert', 'dp')), may hold values from 0 to 2047, as said below
- prefix_len: int32 [8], P('expert'), may hold values from 102 to 512
- out_grad: bfloat16 [8192, 1024], P(('expert', 'dp')), may hold values from -6 to 6
Outputs:
- layer_output: bfloat16 [8192, 1024], P(('expert', 'dp'))
- input_grad: float32 [8192, 1024], P(('expert', 'dp'))
- attn_gain_grad: float32 [1024], P('dp')
- w_query_grad: float32 [1024, 1024], P('dp')
- w_key_grad: float32 [1024, 512], P('dp')
- w_value_grad: float32 [1024, 512], P('dp')
- w_output_grad: float32 [1024, 1024], P('dp')
- moe_gain_grad: float32 [1024], P('dp')
- w_router_grad: float32 [1024, 32], P('dp')
- w_gate_grad: float32 [32, 1024, 512], P('expert', 'dp')
- w_up_grad: float32 [32, 1024, 512], P('expert', 'dp')
- w_down_grad: float32 [32, 512, 1024], P('expert', 'dp')
The draws below stay inside these ranges and needn't reach their ends.
Inputs may be any that keep to these rules, and one draw needn't show every extreme that they name: `routes`: each row names 8 different experts. `priority`: within each aligned block of 256 rows the entries are a permutation of 0 to 2047.
All inputs are finite; a program needn't handle non-finite values.
Results may differ from the reference program's by a relative error of at most 0.017.
Values may be sent and summed in bfloat16 or wider, within the bound.
No kernel may reach another device: no remote copies, remote signals or barrier semaphores. Data moves between devices by JAX's collectives and lax.ppermute only.
A program may use at most 320 MiB of HBM per device.

```python
import math
import jax
import jax.numpy as jnp
from jax import lax

D = 1024
H = 16
KVH = 8
HD = 64
EXPERTS = 32
TOPK = 8
EFF = 512
TOK_DEV = 256
SEQ = 1024
NSEQ = 8
TOKENS = 8192
CAP = 80
N_DP = 4


def draw_priority(key, part):
    block_keys = jax.random.split(key, TOKENS // TOK_DEV)

    def one_block(block_key):
        return jax.random.permutation(block_key, TOK_DEV * TOPK)
    blocks = jax.vmap(one_block)(block_keys)
    return blocks.reshape(TOKENS, TOPK).astype(jnp.int32)


def set_ends(result, rng, least, top_value):
    longest = result.shape.index(max(result.shape))
    spots = []
    for shift in (0, 1):
        where = [jax.random.randint(jax.random.fold_in(rng, axis), (), 0, length) for axis, length in enumerate(result.shape)]
        where[longest] = (where[longest] + shift) % result.shape[longest]
        spots.append(tuple(where))
    return result.at[spots[0]].set(least).at[spots[1]].set(top_value)


def level_of(stream_key, shape, shards, low, top_value):
    factor_of, own = 1.0, jax.random.fold_in(stream_key, 6)
    for position, shards_of in shards:
        heights = jnp.exp(jax.random.uniform(jax.random.fold_in(own, position), (shards_of,), jnp.float32, low / len(shards), top_value / len(shards)))
        factor_of = factor_of * jnp.repeat(heights, shape[position] // shards_of).reshape([-1 if axis == position else 1 for axis in range(len(shape))])
    return factor_of


def picks_of(stream_key, rows, count, top, lift):
    sequence = jax.random.permutation(jax.random.fold_in(stream_key, 1), count)
    pull = sequence
    for power in range(3):
        pull = pull * pull // count
    pull = pull * lift // count
    tickets = jax.random.randint(jax.random.fold_in(stream_key, 2), (rows, count), 0, 4096) + pull
    holders = jax.random.permutation(jax.random.fold_in(stream_key, 3), rows)[jnp.arange(count) % rows]
    tickets = jnp.where(jnp.arange(rows)[:, None] == holders[None, :], 1 << 14, tickets)
    merit = tickets * count + jnp.arange(count)
    return lax.top_k(merit.astype(jnp.int32), top)[1].astype(jnp.int32)


def centred(key, extent, width, limit, cuts=(), kind=jnp.bfloat16):
    level = level_of(key, extent, cuts, -0.22, 0.18) if cuts else 1.0
    result = jax.random.normal(key, extent, jnp.float32) * width * level
    return jnp.minimum(jnp.maximum(result, -limit), limit).astype(kind)


def setup_inputs(seed: int = 0) -> dict:
    arg_keys = jax.random.split(jax.random.key(seed), 16)
    layer_input = centred(arg_keys[0], (TOKENS, D), 1.0, 6.0, ((0, 32),))
    attn_gain = jnp.clip(1.0 + 0.1 * jax.random.normal(arg_keys[1], (D,), jnp.float32), 0.5, 1.5).astype(jnp.bfloat16)
    w_query = centred(arg_keys[2], (D, H * HD), (D // 2) ** -0.5, 0.25, ((0, 4),))
    w_key = centred(arg_keys[3], (D, KVH * HD), (D // 2) ** -0.5, 0.25, ((0, 4),))
    w_value = centred(arg_keys[4], (D, KVH * HD), D ** -0.5, 0.1875, ((0, 4),))
    w_output = centred(arg_keys[5], (H * HD, D), (D // 16) ** -0.5, 0.75, ((0, 4),))
    moe_gain = jnp.clip(1.0 + 0.1 * jax.random.normal(arg_keys[6], (D,), jnp.float32), 0.5, 1.5).astype(jnp.bfloat16)
    w_router = centred(arg_keys[7], (D, EXPERTS), (4 * D) ** -0.5, 0.09375, ((0, 4),))
    w_gate = centred(arg_keys[8], (EXPERTS, D, EFF), D ** -0.5, 0.1875, ((0, 8), (1, 4)))
    w_up = centred(arg_keys[9], (EXPERTS, D, EFF), D ** -0.5, 0.1875, ((0, 8), (1, 4)))
    w_down = centred(arg_keys[10], (EXPERTS, EFF, D), (EFF // 16) ** -0.5, 1.0, ((0, 8), (1, 4)))
    routes = picks_of(arg_keys[11], TOKENS, EXPERTS, TOPK, 2048)
    priority = draw_priority(jax.random.fold_in(arg_keys[15], 71), 0)
    prefix_len = set_ends(jax.random.randint(arg_keys[13], (NSEQ,), SEQ // 10, SEQ // 2 + 1), jax.random.fold_in(arg_keys[13], 1), SEQ // 10, (SEQ // 2 + 1) - 1).astype(jnp.int32)
    out_grad = centred(arg_keys[14], (TOKENS, D), 1.0, 6.0, ((0, 32),))
    return dict(layer_input=layer_input, attn_gain=attn_gain, w_query=w_query, w_key=w_key, w_value=w_value, w_output=w_output, moe_gain=moe_gain, w_router=w_router, w_gate=w_gate, w_up=w_up, w_down=w_down, routes=routes, priority=priority, prefix_len=prefix_len, out_grad=out_grad)


EPSILON = 1e-06
ROPE_BASE = 10000.0
MASKED_SCORE = -1e+30
highest = lax.Precision.HIGHEST

@jax.custom_vjp
def low(v):
    return lax.optimization_barrier(v.astype(jnp.bfloat16)).astype(jnp.float32)

@jax.custom_vjp
def low_back(v):
    return v

def low_keep(v):
    return (low(v), None)

def low_pass(kept, grad):
    return (grad,)

def back_keep(v):
    return (v, None)

def back_low(kept, grad):
    return (low(grad),)
low.defvjp(low_keep, low_pass)
low_back.defvjp(back_keep, back_low)

def rms_norm(values, gain_vec):
    return values * lax.rsqrt(lax.optimization_barrier(jnp.mean(values * values, axis=-1, keepdims=True)) + EPSILON) * gain_vec

def rotate(vectors, places):
    half_dim = vectors.shape[-1] // 2
    frequency = jnp.exp(jnp.arange(half_dim, dtype=jnp.float32) * (-2.0 * math.log(ROPE_BASE) / vectors.shape[-1]))
    angles = places[:, None] * frequency[None, :]
    cosine = jnp.cos(angles)[:, None, :]
    sine_vals = jnp.sin(angles)[:, None, :]
    first_half = vectors[..., :half_dim]
    second = vectors[..., half_dim:]
    return jnp.concatenate([first_half * cosine - second * sine_vals, second * cosine + first_half * sine_vals], axis=-1)

def slot_table(route_blk, prio_blk):
    tok_rows = route_blk.shape[0]
    top_count = route_blk.shape[1]
    pair_count = tok_rows * top_count
    flat_route = route_blk.reshape(pair_count)
    flat_prio = prio_blk.reshape(pair_count)
    counter = jnp.arange(pair_count, dtype=jnp.int32)
    by_priority = jnp.zeros((pair_count,), jnp.int32).at[flat_prio].set(counter)
    ranked = flat_route[by_priority]
    onehot = (ranked[:, None] == jnp.arange(EXPERTS, dtype=jnp.int32)[None, :]).astype(jnp.int32)
    before = jnp.cumsum(onehot, axis=0) - onehot
    rank_sorted = lax.optimization_barrier(jnp.sum(before * onehot, axis=1))
    pair_rank = rank_sorted[flat_prio]
    slot_index = jnp.where(pair_rank < CAP, flat_route * CAP + pair_rank, EXPERTS * CAP).astype(jnp.int32)
    token_sources = jnp.full((EXPERTS * CAP + 1,), tok_rows, jnp.int32).at[slot_index].set(counter // top_count)
    return (slot_index.reshape(tok_rows, top_count), token_sources[:EXPERTS * CAP])

def pick_rows(source_rows, indices):
    return source_rows[indices]

def sequence_layer(weights, pieces):
    attn_gain, w_query, w_key, w_value, w_output, moe_gain, w_router, w_gate, w_up, w_down = weights
    seq_input, seq_routes, seq_prio, seq_prefix = pieces
    normed = low(rms_norm(seq_input, attn_gain))
    query_lin = low_back(jnp.dot(normed, w_query, precision=highest))
    key_lin = low_back(jnp.dot(normed, w_key, precision=highest))
    value_lin = low_back(low(jnp.dot(normed, w_value, precision=highest)))
    places = jnp.arange(SEQ, dtype=jnp.float32)
    query_rot = low(rotate(query_lin.reshape(SEQ, H, HD), places) * HD ** (-0.5))
    key_rot = low(rotate(key_lin.reshape(SEQ, KVH, HD), places))
    value_heads = value_lin.reshape(SEQ, KVH, HD)
    key_pos = jnp.arange(SEQ, dtype=jnp.int32)
    block_rows = min(512, SEQ)

    def attend(start):
        query_blk = lax.dynamic_slice_in_dim(query_rot, start, block_rows, 0).reshape(block_rows, KVH, H // KVH, HD)
        scores = low_back(jnp.einsum('qhgd,khd->hgqk', query_blk, key_rot, precision=highest))
        query_pos = start + jnp.arange(block_rows, dtype=jnp.int32)
        visible = (key_pos[None, :] <= query_pos[:, None]) | (key_pos[None, :] < seq_prefix)
        scores = jnp.where(visible, scores, MASKED_SCORE)
        row_max = lax.optimization_barrier(jnp.max(scores, axis=-1, keepdims=True))
        log_total = row_max + jnp.log(lax.optimization_barrier(jnp.sum(jnp.exp(scores - row_max), axis=-1, keepdims=True)))
        probs_low = low(jnp.exp(scores - log_total))
        mixed_vals = jnp.einsum('hgqk,khd->qhgd', probs_low, value_heads, precision=highest)
        return mixed_vals.reshape(block_rows, H * HD)
    starts = jnp.arange(SEQ // block_rows, dtype=jnp.int32) * block_rows
    attended = lax.map(jax.checkpoint(attend), starts).reshape(SEQ, H * HD)
    attended = low_back(low(attended))
    residual = seq_input + low_back(jnp.dot(attended, w_output, precision=highest))
    moe_in = low(rms_norm(residual, moe_gain))
    logits = low_back(jnp.dot(moe_in, w_router, precision=highest))
    gate_weights = jax.nn.softmax(jnp.take_along_axis(logits, seq_routes, axis=1), axis=-1)
    route_blocks = seq_routes.reshape(N_DP, TOK_DEV, TOPK)
    prio_blocks = seq_prio.reshape(N_DP, TOK_DEV, TOPK)
    slot_index, token_sources = jax.vmap(slot_table)(route_blocks, prio_blocks)
    padded_in = jnp.concatenate([moe_in.reshape(N_DP, TOK_DEV, D), jnp.zeros((N_DP, 1, D), jnp.float32)], axis=1)
    dispatched = jax.vmap(pick_rows)(padded_in, token_sources)
    expert_in = low_back(dispatched.reshape(N_DP, EXPERTS, CAP, D).transpose(1, 0, 2, 3).reshape(EXPERTS, N_DP * CAP, D))
    gate_proj = low_back(jnp.einsum('erd,edf->erf', expert_in, w_gate, precision=highest))
    up_proj = low_back(jnp.einsum('erd,edf->erf', expert_in, w_up, precision=highest))
    activated = low(jax.nn.silu(gate_proj) * up_proj)
    expert_out = low_back(low(jnp.einsum('erf,efd->erd', activated, w_down, precision=highest)))
    returned = expert_out.reshape(EXPERTS, N_DP, CAP, D).transpose(1, 0, 2, 3).reshape(N_DP, EXPERTS * CAP, D)
    returned = jnp.concatenate([returned, jnp.zeros((N_DP, 1, D), jnp.float32)], axis=1)
    per_pair = jax.vmap(pick_rows)(returned, slot_index).reshape(SEQ, TOPK, D)
    mixture = lax.optimization_barrier(jnp.sum(gate_weights[:, :, None] * per_pair, axis=1))
    return residual + mixture

def reference(layer_input, attn_gain, w_query, w_key, w_value, w_output, moe_gain, w_router, w_gate, w_up, w_down, routes, priority, prefix_len, out_grad):
    floats = tuple((tensor.astype(jnp.float32) for tensor in (layer_input, attn_gain, w_query, w_key, w_value, w_output, moe_gain, w_router, w_gate, w_up, w_down)))

    def forward(inputs, *weights):

        def per_sequence(unused, pieces):
            return (unused, sequence_layer(weights, pieces))
        unused_carry, outputs = lax.scan(per_sequence, jnp.zeros((), jnp.float32), (inputs.reshape(NSEQ, SEQ, D), routes.reshape(NSEQ, SEQ, TOPK), priority.reshape(NSEQ, SEQ, TOPK), prefix_len))
        return outputs.reshape(TOKENS, D)
    output, pullback = jax.vjp(forward, *floats)
    gradients = pullback(out_grad.astype(jnp.float32))
    return (output.astype(jnp.bfloat16), gradients[0], gradients[1], gradients[2], gradients[3], gradients[4], gradients[5], gradients[6], gradients[7], gradients[8], gradients[9], gradients[10])
```

```python
import math

import jax
import jax.numpy as jnp
from jax import lax
from jax.experimental import pallas as pl
from jax.experimental.pallas import tpu as pltpu
from jax.sharding import Mesh
from jax.sharding import PartitionSpec as P

H = 16
KVH = 8
HD = 64
EXPERTS = 32
EPSILON = 1e-06
ROPE_BASE = 10000.0
MASKED_SCORE = -1e30
F32 = jnp.float32
B16 = jnp.bfloat16
SWAP = [(0, 1), (1, 0)]
VMEM_LIMIT = 60 * 1024 * 1024


def rms_norm(values, gain_vec):
    return (
        values * lax.rsqrt(jnp.mean(values * values, axis=-1, keepdims=True) + EPSILON) * gain_vec
    )


def rotate(vectors, places):
    half_dim = vectors.shape[-1] // 2
    frequency = jnp.exp(
        jnp.arange(half_dim, dtype=F32) * (-2.0 * math.log(ROPE_BASE) / vectors.shape[-1])
    )
    angles = places[:, None] * frequency[None, :]
    cosine = jnp.cos(angles)[:, None, :]
    sine_vals = jnp.sin(angles)[:, None, :]
    first_half = vectors[..., :half_dim]
    second = vectors[..., half_dim:]
    return jnp.concatenate(
        [first_half * cosine - second * sine_vals, second * cosine + first_half * sine_vals],
        axis=-1,
    )


def swap_core(rows):
    return lax.ppermute(rows, "core", SWAP)


def cyclic(rows, size, shift):
    return lax.ppermute(rows, "z", [(i, (i + shift) % size) for i in range(size)])


def after(value, *others):
    return lax.optimization_barrier((value, *others))[0]


def grid_gather(shard):
    half = shard.shape[0] // 2
    from_x = lax.ppermute(shard, "x", SWAP)
    from_y = lax.ppermute(shard, "y", SWAP)
    diag_a = lax.ppermute(from_x[:half], "y", SWAP)
    diag_b = lax.ppermute(from_y[half:], "x", SWAP)
    return shard, from_x, from_y, diag_a, diag_b


def grid_scatter(first_a, rest_a, first_b, rest_b):
    got_a = lax.ppermute(first_a, "x", SWAP)
    got_b = lax.ppermute(first_b, "y", SWAP)
    onward_a = (rest_a[1].astype(F32) + got_a[1].astype(F32)).astype(B16)
    onward_b = (rest_b[1].astype(F32) + got_b[1].astype(F32)).astype(B16)
    last_a = lax.ppermute(onward_a, "y", SWAP)
    last_b = lax.ppermute(onward_b, "x", SWAP)
    return (
        rest_a[0].astype(F32) + got_a[0].astype(F32) + last_a.astype(F32),
        rest_b[0].astype(F32) + got_b[0].astype(F32) + last_b.astype(F32),
    )


def grid_scatter_rows(parts):
    own, to_x, to_y, diag = parts
    half = own.shape[0] // 2
    total = grid_scatter(
        jnp.stack([to_x[:half], diag[:half]]),
        (own[:half], to_y[:half]),
        jnp.stack([to_y[half:], diag[half:]]),
        (own[half:], to_x[half:]),
    )
    return jnp.concatenate(total, axis=0)


def column_gather(rows, size):
    mine = jnp.stack([rows] + [cyclic(rows, size, -k) for k in range(1, size)])
    return mine, swap_core(mine)


def column_scatter(mine, other, size):
    both = mine.astype(F32) + swap_core(other).astype(F32)
    low = both.astype(B16)
    total = both[0]
    for k in range(1, size):
        total = total + cyclic(low[k], size, k).astype(F32)
    return total


def assemble(places, parts, blocks):
    rows = blocks
    cols = parts[0].shape[1]

    def kernel(places_ref, *refs):
        out = refs[len(parts)]
        sems = refs[len(parts) + 1]
        copies = []
        for i, part in enumerate(parts):
            start = pl.multiple_of(places_ref[i] * rows, rows)
            copies.append(
                pltpu.make_async_copy(
                    refs[i], out.at[pl.ds(start, part.shape[0]), :], sems.at[i]
                )
            )
        for copy in copies:
            copy.start()
        for copy in copies:
            copy.wait()

    total = sum(part.shape[0] for part in parts)
    return pl.pallas_call(
        kernel,
        out_shape=jax.ShapeDtypeStruct((total, cols), parts[0].dtype),
        grid_spec=pltpu.PrefetchScalarGridSpec(
            num_scalar_prefetch=1,
            grid=(1,),
            in_specs=[pl.BlockSpec(memory_space=pl.ANY) for _ in parts],
            out_specs=pl.BlockSpec(memory_space=pl.ANY),
            scratch_shapes=[pltpu.SemaphoreType.DMA((len(parts),))],
        ),
        name="assemble",
    )(places, *parts)


def one_hot_slots(codes, capacity):
    slots = lax.broadcasted_iota(jnp.int32, (capacity, codes.shape[1]), 0).astype(F32)
    return [(slots == codes[e : e + 1, :]).astype(F32) for e in range(codes.shape[0])]


def row_of(table, index):
    at = lax.broadcasted_iota(jnp.int32, table.shape, 0)
    return jnp.sum(jnp.where(at == index, table, 0.0), axis=0, keepdims=True)


def dispatch_rows(ids, rows, code, router, local, capacity):
    pieces, tokens, width = rows.shape
    slots = local * capacity
    with_gates = router is not None

    def kernel(ids_ref, rows_ref, code_ref, *rest):
        table = code_ref[0]
        first = ids_ref[pieces]
        codes = jnp.concatenate([row_of(table, first + e) for e in range(local)], axis=0)
        picks = one_hot_slots(codes, capacity)
        select = jnp.concatenate([p.astype(B16) for p in picks], axis=0)
        out_ref = rest[1] if with_gates else rest[0]
        out_ref[0] = jnp.dot(select, rows_ref[0], preferred_element_type=F32).astype(B16)
        if with_gates:
            router_ref, gate_out = rest[0], rest[2]
            logits = lax.dot_general(
                router_ref[...], rows_ref[0], (((1,), (1,)), ((), ())), preferred_element_type=F32
            )
            routed = table >= 0.0
            peak = jnp.max(jnp.where(routed, logits, MASKED_SCORE), axis=0, keepdims=True)
            lifted = jnp.where(routed, jnp.exp(jnp.minimum(logits - peak, 0.0)), 0.0)
            gates = lifted / jnp.sum(lifted, axis=0, keepdims=True)
            for e in range(local):
                gate_row = row_of(gates, first + e)
                column = jnp.sum(picks[e] * gate_row, axis=1, keepdims=True)
                gate_out[0, e * capacity : (e + 1) * capacity, :] = jnp.broadcast_to(
                    column, (capacity, 128)
                )

    in_specs = [
        pl.BlockSpec((1, tokens, width), lambda p, ids: (p, 0, 0)),
        pl.BlockSpec((1, EXPERTS, tokens), lambda p, ids: (ids[p], 0, 0)),
    ]
    out_specs = [pl.BlockSpec((1, slots, width), lambda p, ids: (p, 0, 0))]
    out_shape = [jax.ShapeDtypeStruct((pieces, slots, width), B16)]
    args = [rows, code]
    if with_gates:
        in_specs.append(pl.BlockSpec((EXPERTS, width), lambda p, ids: (0, 0)))
        out_specs.append(pl.BlockSpec((1, slots, 128), lambda p, ids: (p, 0, 0)))
        out_shape.append(jax.ShapeDtypeStruct((pieces, slots, 128), F32))
        args.append(router)
    return pl.pallas_call(
        kernel,
        out_shape=out_shape,
        grid_spec=pltpu.PrefetchScalarGridSpec(
            num_scalar_prefetch=1, grid=(pieces,), in_specs=in_specs, out_specs=out_specs
        ),
        compiler_params=pltpu.CompilerParams(vmem_limit_bytes=VMEM_LIMIT),
        name="dispatch",
    )(ids, *args)


def combine_rows(ids, first, pieces, slot_rows, code, local, capacity):
    halves = len(slot_rows)
    slots, width = slot_rows[0].shape[1:]
    tokens = code.shape[-1]
    per = local // halves

    def kernel(ids_ref, code_ref, *rest):
        table = code_ref[0]
        lead = ids_ref[pieces]
        codes = jnp.concatenate([row_of(table, lead + e) for e in range(local)], axis=0)
        picks = one_hot_slots(codes, capacity)
        total = None
        for h in range(halves):
            select = jnp.concatenate(
                [p.astype(B16) for p in picks[h * per : (h + 1) * per]], axis=0
            )
            part = lax.dot_general(
                select, rest[h][0], (((0,), (0,)), ((), ())), preferred_element_type=F32
            )
            total = part if total is None else total + part
        rest[halves][0] = total.astype(B16)

    in_specs = [pl.BlockSpec((1, EXPERTS, tokens), lambda p, ids: (ids[p], 0, 0))]
    in_specs += [
        pl.BlockSpec((1, slots, width), lambda p, ids: (p + first, 0, 0)) for _ in range(halves)
    ]
    return pl.pallas_call(
        kernel,
        out_shape=jax.ShapeDtypeStruct((pieces, tokens, width), B16),
        grid_spec=pltpu.PrefetchScalarGridSpec(
            num_scalar_prefetch=1,
            grid=(pieces,),
            in_specs=in_specs,
            out_specs=pl.BlockSpec((1, tokens, width), lambda p, ids: (p, 0, 0)),
        ),
        compiler_params=pltpu.CompilerParams(vmem_limit_bytes=VMEM_LIMIT),
        name="combine",
    )(ids, code, *slot_rows)


def experts(order, start, count, skip, rows, grads, gates, weights, capacity, in_rows, mid_rows):
    half, _, width = rows[0].shape
    pieces = 2 * half
    n = len(weights)
    pack_rows, eff = weights[0].shape[1:]
    folds = width // eff
    total_rows = pieces * capacity
    split = n == 4
    first_half = count // 2
    large = total_rows > 1000

    def kernel(order_ref, *refs):
        rows_a, rows_b, grads_a, grads_b, gates_a, gates_b = refs[:6]
        pack = refs[6 : 6 + n]
        y_out, dx_out = refs[6 + n : 8 + n]
        outs = refs[8 + n : -6]
        full_g, full_u, full_d, grad_g, grad_u, grad_d = refs[-6:]

        def at_in(j):
            return pl.ds(pl.multiple_of(order_ref[j] * in_rows, in_rows), in_rows)

        def at_mid(j):
            return pl.ds(pl.multiple_of(order_ref[j] * mid_rows, mid_rows), mid_rows)

        for j in range(n):
            full_g[at_in(j), :] = pack[j][0, :in_rows]
            full_u[at_in(j), :] = pack[j][0, in_rows : 2 * in_rows]
            for f in range(folds):
                full_d[at_mid(j), f * eff : (f + 1) * eff] = pack[j][
                    0, 2 * in_rows + f * mid_rows : 2 * in_rows + (f + 1) * mid_rows
                ]

        def joined(a, b, w):
            return jnp.concatenate(
                [
                    a[...].reshape(half * capacity, w),
                    b[...].reshape(half * capacity, w),
                ],
                axis=0,
            )

        x = joined(rows_a, rows_b, width)
        g = joined(grads_a, grads_b, width)
        gate = joined(gates_a, gates_b, 128)[:, 0:1]
        nt = (((1,), (1,)), ((), ()))
        tn = (((0,), (0,)), ((), ()))
        gate_proj = jnp.dot(x, full_g[...], preferred_element_type=F32)
        up_proj = jnp.dot(x, full_u[...], preferred_element_type=F32)
        down_grad = lax.dot_general(g, full_d[...], nt, preferred_element_type=F32)
        sigmoid = 1.0 / (1.0 + jnp.exp(-gate_proj))
        silu = gate_proj * sigmoid
        activated = silu * up_proj
        slot_grad = jnp.sum(activated * down_grad, axis=1, keepdims=True)
        here = order_ref[n] + start + pl.program_id(0)
        lane = lax.broadcasted_iota(jnp.int32, (total_rows, 128), 1)
        high = slot_grad.astype(B16).astype(F32)
        tail = jnp.where(lane == here, high, jnp.where(lane == here + EXPERTS, slot_grad - high, 0.0))
        dx_out[:, :, width:] = tail.astype(B16).reshape(pieces, capacity, 128)
        scaled = (gate * activated).astype(B16)
        act_grad = gate * down_grad
        gate_grad = (act_grad * up_proj * (sigmoid * (1.0 + gate_proj * (1.0 - sigmoid)))).astype(
            B16
        )
        up_grad = (act_grad * silu).astype(B16)
        y = jnp.dot(scaled, full_d[...], preferred_element_type=F32)
        y_out[...] = y.astype(B16).reshape(pieces, capacity, width)
        dx = lax.dot_general(gate_grad, full_g[...], nt, preferred_element_type=F32)
        dx = dx + lax.dot_general(up_grad, full_u[...], nt, preferred_element_type=F32)
        dx_out[:, :, :width] = dx.astype(B16).reshape(pieces, capacity, width)
        grad_g[...] = lax.dot_general(x, gate_grad, tn, preferred_element_type=F32).astype(B16)
        grad_u[...] = lax.dot_general(x, up_grad, tn, preferred_element_type=F32).astype(B16)
        grad_d[...] = lax.dot_general(scaled, g, tn, preferred_element_type=F32).astype(B16)

        def give(ref, slot, j):
            ref[slot, 0, :in_rows] = grad_g[at_in(j), :]
            ref[slot, 0, in_rows : 2 * in_rows] = grad_u[at_in(j), :]
            for f in range(folds):
                ref[slot, 0, 2 * in_rows + f * mid_rows : 2 * in_rows + (f + 1) * mid_rows] = grad_d[
                    at_mid(j), f * eff : (f + 1) * eff
                ]

        if split:
            first_a, rest_a, first_b, rest_b = outs

            @pl.when(pl.program_id(0) < first_half)
            def _():
                give(first_a, 0, 1)
                give(first_a, 1, 3)
                give(rest_a, 0, 0)
                give(rest_a, 1, 2)

            @pl.when(pl.program_id(0) >= first_half)
            def _():
                give(first_b, 0, 2)
                give(first_b, 1, 3)
                give(rest_b, 0, 0)
                give(rest_b, 1, 1)
        else:
            for j in range(n):
                give(outs[0], j, j)

    def single():
        return dict(pipeline_mode=pl.Buffered(1)) if large else {}

    def rows_spec(w):
        return pl.BlockSpec((half, capacity, w), lambda e, o: (0, e + start, 0), **single())

    in_specs = [rows_spec(width)] * 4 + [rows_spec(128)] * 2
    for j in range(n):
        in_specs.append(
            pl.BlockSpec((1, pack_rows, eff), lambda e, o, lead=start - skip[j]: (e + lead, 0, 0))
        )
    slots = count * capacity
    out_specs = [
        pl.BlockSpec((pieces, capacity, w), lambda e, o: (0, e, 0), **single())
        for w in (width, width + 128)
    ]
    out_shape = [
        jax.ShapeDtypeStruct((pieces, slots, width), B16),
        jax.ShapeDtypeStruct((pieces, slots, width + 128), B16),
    ]
    if split:
        for at in (
            lambda e, o: (0, jnp.minimum(e, first_half - 1), 0, 0),
            lambda e, o: (0, jnp.maximum(e - first_half, 0), 0, 0),
        ):
            for _ in range(2):
                out_specs.append(pl.BlockSpec((2, 1, pack_rows, eff), at))
                out_shape.append(jax.ShapeDtypeStruct((2, first_half, pack_rows, eff), B16))
    else:
        out_specs.append(pl.BlockSpec((n, 1, pack_rows, eff), lambda e, o: (0, e, 0, 0)))
        out_shape.append(jax.ShapeDtypeStruct((n, count, pack_rows, eff), B16))
    results = pl.pallas_call(
        kernel,
        out_shape=out_shape,
        grid_spec=pltpu.PrefetchScalarGridSpec(
            num_scalar_prefetch=1,
            grid=(count,),
            in_specs=in_specs,
            out_specs=out_specs,
            scratch_shapes=[
                pltpu.VMEM((n * in_rows, eff), B16),
                pltpu.VMEM((n * in_rows, eff), B16),
                pltpu.VMEM((n * mid_rows, width), B16),
                pltpu.VMEM((n * in_rows, eff), B16),
                pltpu.VMEM((n * in_rows, eff), B16),
                pltpu.VMEM((n * mid_rows, width), B16),
            ],
        ),
        compiler_params=pltpu.CompilerParams(vmem_limit_bytes=VMEM_LIMIT),
        name="experts",
    )(order, *rows, *grads, *gates, *weights)
    return results[0], results[1], results[2:]


def make_body(z_size, small_grid):
    def dense_gather(shard, dp_index):
        if not small_grid:
            return lax.all_gather(shard, ("y", "x"), axis=0, tiled=True), shard
        rows = shard.shape[0]
        core = lax.axis_index("core")
        mine = lax.dynamic_slice_in_dim(shard, core * (rows // 2), rows // 2, 0)
        _, from_x, from_y, diag_a, diag_b = grid_gather(mine)
        moved = jnp.concatenate([from_x, from_y, diag_a, diag_b], axis=0)
        other = swap_core(moved)
        places = [2 * dp_index]
        parts = [shard]
        for source, which in ((moved, core), (other, 1 - core)):
            for j in range(3):
                places.append(2 * (dp_index ^ (j + 1)) + which)
                parts.append(source[j * (rows // 2) : (j + 1) * (rows // 2)])
        return assemble(jnp.stack(places), parts, rows // 2), moved

    def dense_sum(grads, dp_index):
        if not small_grid:
            return lax.psum_scatter(
                lax.psum(grads, ("z", "core")), ("y", "x"), scatter_dimension=0, tiled=True
            )
        rows, cols = grads.shape
        eighth = rows // 8
        core = lax.axis_index("core")
        split = grads.astype(B16).reshape(4, 2, eighth, cols)
        keep = lax.dynamic_index_in_dim(split, core, 1, keepdims=False)
        give = lax.dynamic_index_in_dim(split, 1 - core, 1, keepdims=False)
        both = (keep.astype(F32) + swap_core(give).astype(F32)).astype(B16)
        mine = grid_scatter_rows(
            [lax.dynamic_index_in_dim(both, dp_index ^ j, 0, keepdims=False) for j in range(4)]
        )
        step = 1
        while step < z_size:
            pairs = [(i, i ^ step) for i in range(z_size)]
            mine = mine + lax.ppermute(mine.astype(B16), "z", pairs).astype(F32)
            step *= 2
        low = mine.astype(B16)
        other = swap_core(low)
        first = jnp.where(core == 0, low, other)
        second = jnp.where(core == 0, other, low)
        return jnp.concatenate([first, second], axis=0).astype(F32)

    def body(
        layer_input,
        attn_gain,
        w_query,
        w_key,
        w_value,
        w_output,
        moe_gain,
        w_router,
        w_gate,
        w_up,
        w_down,
        routes,
        priority,
        prefix_len,
        out_grad,
    ):
        tok_rows, model_width = layer_input.shape
        dp_size = lax.axis_size("y") * lax.axis_size("x")
        dp_index = lax.axis_index("y") * lax.axis_size("x") + lax.axis_index("x")
        z = lax.axis_index("z")
        core = lax.axis_index("core")
        seq_len = tok_rows * dp_size
        top_count = routes.shape[1]
        local = w_gate.shape[0]
        capacity = 5 * tok_rows * top_count // (4 * EXPERTS)
        group_size = H // KVH
        score_scale = HD ** (-0.5)

        gains = jnp.stack([attn_gain, moe_gain], axis=1)
        rows = w_query.shape[0]
        head_pack = jnp.concatenate(
            [w_query, w_key, w_value, w_router, gains, jnp.zeros((rows, 94), B16)], axis=1
        )
        head_full, head_moved = dense_gather(head_pack, dp_index)
        full_output, tail_moved = dense_gather(after(w_output, head_moved), dp_index)
        wide = H * HD
        narrow = KVH * HD
        full_query = head_full[:, :wide]
        full_key = head_full[:, wide : wide + narrow]
        full_value = head_full[:, wide + narrow : wide + 2 * narrow]
        full_router = head_full[:, wide + 2 * narrow : wide + 2 * narrow + EXPERTS]
        full_attn_gain = head_full[:, wide + 2 * narrow + EXPERTS].astype(F32)
        full_moe_gain = head_full[:, wide + 2 * narrow + EXPERTS + 1].astype(F32)

        expert_ids = jnp.arange(EXPERTS, dtype=jnp.int32)
        hits = routes[:, :, None] == expert_ids[None, None, :]
        routed = jnp.any(hits, axis=1)
        place = jnp.where(
            routed, jnp.sum(jnp.where(hits, priority[:, :, None], 0), axis=1), jnp.int32(1 << 20)
        )
        ranks = jnp.sum((place[:, :, None] < place.T[None, :, :]).astype(F32), axis=0)
        code = lax.all_gather(jnp.where(routed.T, ranks, -1.0), ("z", "core"), axis=0, tiled=False)
        sources = (z + jnp.arange(z_size, dtype=jnp.int32)) % z_size
        lead = ((2 * z + core) * local).astype(jnp.int32)[None]
        ids_mine = jnp.concatenate([2 * sources + core, lead])
        ids_other = jnp.concatenate([2 * sources + 1 - core, lead])
        grads_mine, grads_other = column_gather(out_grad, z_size)
        (slot_grads_mine,) = dispatch_rows(ids_mine, grads_mine, code, None, local, capacity)
        (slot_grads_other,) = dispatch_rows(ids_other, grads_other, code, None, local, capacity)

        query_pos = dp_index * tok_rows + jnp.arange(tok_rows, dtype=jnp.int32)
        places = query_pos.astype(F32)
        in_float = layer_input.astype(F32)
        normed = rms_norm(in_float, full_attn_gain).astype(B16)
        query_lin = jnp.dot(normed, full_query, preferred_element_type=F32)
        key_lin = jnp.dot(normed, full_key, preferred_element_type=F32)
        value_low = jnp.dot(normed, full_value, preferred_element_type=F32).astype(B16)
        query_rot = (rotate(query_lin.reshape(tok_rows, H, HD), places) * score_scale).astype(B16)
        key_rot = rotate(key_lin.reshape(tok_rows, KVH, HD), places).astype(B16)
        key_rot = key_rot.reshape(tok_rows, narrow)
        both = jnp.concatenate([key_rot, value_low], axis=1)
        steps = jnp.arange(tok_rows, dtype=jnp.int32)
        eff = w_gate.shape[2]
        in_rows, mid_rows = w_gate.shape[1], w_down.shape[1]
        folds = [w_down[:, :, f * eff : (f + 1) * eff] for f in range(model_width // eff)]
        pack = jnp.concatenate([w_gate, w_up, *folds], axis=1)
        if small_grid:
            relative = dp_index ^ jnp.arange(4, dtype=jnp.int32)
            both_parts = grid_gather(both)
            both_all = jnp.concatenate(both_parts, axis=0)
            key_pos = (relative[:, None] * tok_rows + steps[None, :]).reshape(seq_len)
            halves, per = 2, local // 2
            expert_weights, skips = [], []
            for half in range(2):
                own = after(pack[half * per : (half + 1) * per], both_parts[1], both_parts[2])
                parts = grid_gather(own)
                diag = jnp.concatenate([parts[3], parts[4]], axis=0)
                expert_weights.append([own, parts[1], parts[2], diag])
                skips.append([half * per] * 4)
        else:
            relative = jnp.arange(dp_size, dtype=jnp.int32)
            both_all = lax.all_gather(both, ("y", "x"), axis=0, tiled=True)
            key_pos = jnp.arange(seq_len, dtype=jnp.int32)
            halves, per = 1, local
            every = lax.all_gather(pack, ("y", "x"), axis=0, tiled=False)
            expert_weights = [[every[j] for j in range(dp_size)]]
            skips = [[0] * dp_size]
        order = jnp.concatenate([relative, lead])
        key_all = both_all[:, :narrow]
        value_all = both_all[:, narrow:]
        visible = (key_pos[None, :] <= query_pos[:, None]) | (key_pos[None, :] < prefix_len[0])

        def head_scores(head_idx):
            query_head = query_rot[:, head_idx * group_size : (head_idx + 1) * group_size, :]
            key_head = key_all[:, head_idx * HD : (head_idx + 1) * HD]
            scores = jnp.einsum("qgd,kd->gqk", query_head, key_head, preferred_element_type=F32)
            return jnp.where(visible[None, :, :], scores, MASKED_SCORE)

        mixed_heads = []
        log_totals = []
        for head_idx in range(KVH):
            scores = head_scores(head_idx)
            row_max = jnp.max(scores, axis=-1, keepdims=True)
            log_total = row_max + jnp.log(
                jnp.sum(jnp.exp(scores - row_max), axis=-1, keepdims=True)
            )
            probs_low = jnp.exp(scores - log_total).astype(B16)
            value_head = value_all[:, head_idx * HD : (head_idx + 1) * HD]
            mixed_heads.append(
                jnp.einsum("gqk,kd->qgd", probs_low, value_head, preferred_element_type=F32)
            )
            log_totals.append(log_total)
        attended = jnp.concatenate(mixed_heads, axis=1).reshape(tok_rows, wide).astype(B16)
        residual = in_float + jnp.dot(attended, full_output, preferred_element_type=F32)
        moe_in = rms_norm(residual, full_moe_gain).astype(B16)

        rows_mine, rows_other = column_gather(moe_in, z_size)
        router_rows = full_router.T
        slot_rows_mine, slot_gates_mine = dispatch_rows(
            ids_mine, rows_mine, code, router_rows, local, capacity
        )
        slot_rows_other, slot_gates_other = dispatch_rows(
            ids_other, rows_other, code, router_rows, local, capacity
        )
        logits = jnp.dot(moe_in, full_router, preferred_element_type=F32)
        peak = jnp.max(jnp.where(routed, logits, MASKED_SCORE), axis=-1, keepdims=True)
        lifted = jnp.where(routed, jnp.exp(jnp.minimum(logits - peak, 0.0)), 0.0)
        gate_weights = lifted / jnp.sum(lifted, axis=-1, keepdims=True)
        ys, dxs, weight_grads = [], [], []
        for half in range(halves):
            y, dx, grads = experts(
                order,
                half * per,
                per,
                skips[half],
                (slot_rows_mine, slot_rows_other),
                (slot_grads_mine, slot_grads_other),
                (slot_gates_mine, slot_gates_other),
                expert_weights[half],
                capacity,
                in_rows,
                mid_rows,
            )
            ys.append(y)
            dxs.append(dx)
            weight_grads.append(grads)
        dx_other = combine_rows(ids_other, z_size, z_size, dxs, code, local, capacity)
        dx_mine = combine_rows(ids_mine, 0, z_size, dxs, code, local, capacity)
        moe_sum = column_scatter(dx_mine, dx_other, z_size)
        moe_in_grad = moe_sum[:, :model_width]
        gate_grad = (
            moe_sum[:, model_width : model_width + EXPERTS]
            + moe_sum[:, model_width + EXPERTS : model_width + 2 * EXPERTS]
        )
        y_other = combine_rows(ids_other, z_size, z_size, ys, code, local, capacity)
        y_mine = combine_rows(ids_mine, 0, z_size, ys, code, local, capacity)
        mixture = column_scatter(y_mine, y_other, z_size)
        layer_output = (residual + mixture).astype(B16)
        if small_grid:
            sums = []
            for grads in weight_grads:
                sums += list(grid_scatter(*grads))
            pack_grad = jnp.concatenate(sums, axis=0)
        else:
            pack_grad = lax.psum_scatter(
                weight_grads[0][0].astype(F32), ("y", "x"), scatter_dimension=0, tiled=False
            )
        down = 2 * in_rows
        expert_grads = [
            pack_grad[:, :in_rows],
            pack_grad[:, in_rows:down],
            jnp.concatenate(
                [
                    pack_grad[:, down + f * mid_rows : down + (f + 1) * mid_rows]
                    for f in range(model_width // eff)
                ],
                axis=2,
            ),
        ]

        grad_out = out_grad.astype(F32)
        centre = jnp.sum(gate_weights * gate_grad, axis=-1, keepdims=True)
        logit_low = (gate_weights * (gate_grad - centre)).astype(B16)
        router_grad = jnp.einsum("td,te->de", moe_in, logit_low, preferred_element_type=F32)
        moe_in_grad = moe_in_grad + jnp.einsum(
            "te,de->td", logit_low, full_router, preferred_element_type=F32
        )
        norm_value, second_pull = jax.vjp(rms_norm, residual, full_moe_gain)
        resid_norm_grad, moe_gain_grad = second_pull(moe_in_grad)
        residual_grad = grad_out + resid_norm_grad
        attn_out_grad = residual_grad.astype(B16)
        wout_grad = jnp.einsum("tc,td->cd", attended, attn_out_grad, preferred_element_type=F32)
        attended_grad = (
            jnp.einsum("td,cd->tc", attn_out_grad, full_output, preferred_element_type=F32)
            .astype(B16)
            .reshape(tok_rows, H, HD)
        )
        tail_grad = dense_sum(
            jnp.concatenate(
                [
                    wout_grad,
                    router_grad,
                    moe_gain_grad[:, None],
                    jnp.zeros((model_width, 95), F32),
                ],
                axis=1,
            ),
            dp_index,
        )
        query_grads = []
        key_parts = []
        value_parts = []
        for head_idx in range(KVH):
            scores = head_scores(head_idx)
            attention_probs = jnp.exp(scores - log_totals[head_idx])
            probs_low = attention_probs.astype(B16)
            grad_head = attended_grad[:, head_idx * group_size : (head_idx + 1) * group_size, :]
            query_head = query_rot[:, head_idx * group_size : (head_idx + 1) * group_size, :]
            key_head = key_all[:, head_idx * HD : (head_idx + 1) * HD]
            value_head = value_all[:, head_idx * HD : (head_idx + 1) * HD]
            probs_grad = jnp.einsum("qgd,kd->gqk", grad_head, value_head, preferred_element_type=F32)
            row_delta = jnp.sum(attention_probs * probs_grad, axis=-1, keepdims=True)
            score_grad = (attention_probs * (probs_grad - row_delta)).astype(B16)
            query_grads.append(
                jnp.einsum("gqk,kd->qgd", score_grad, key_head, preferred_element_type=F32)
            )
            key_parts.append(
                jnp.einsum("gqk,qgd->kd", score_grad, query_head, preferred_element_type=F32)
            )
            value_parts.append(
                jnp.einsum("gqk,qgd->kd", probs_low, grad_head, preferred_element_type=F32)
            )
        both_part = jnp.concatenate(key_parts + value_parts, axis=1)
        if small_grid:
            both_sum = grid_scatter_rows(both_part.astype(B16).reshape(4, tok_rows, 2 * narrow))
        else:
            both_sum = lax.psum_scatter(both_part, ("y", "x"), scatter_dimension=0, tiled=True)
        query_rot_grad = jnp.concatenate(query_grads, axis=1) * score_scale
        key_rot_grad = both_sum[:, :narrow].reshape(tok_rows, KVH, HD)
        value_grad = both_sum[:, narrow:].astype(B16)
        query_grad = rotate(query_rot_grad, -places).reshape(tok_rows, wide).astype(B16)
        key_grad = rotate(key_rot_grad, -places).reshape(tok_rows, narrow).astype(B16)
        wq_grad = jnp.einsum("td,tc->dc", normed, query_grad, preferred_element_type=F32)
        query_sum = dense_sum(wq_grad, dp_index)
        wk_grad = jnp.einsum("td,tc->dc", normed, key_grad, preferred_element_type=F32)
        wv_grad = jnp.einsum("td,tc->dc", normed, value_grad, preferred_element_type=F32)
        normed_grad = jnp.einsum("tc,dc->td", query_grad, full_query, preferred_element_type=F32)
        normed_grad = normed_grad + jnp.einsum(
            "tc,dc->td", key_grad, full_key, preferred_element_type=F32
        )
        normed_grad = normed_grad + jnp.einsum(
            "tc,dc->td", value_grad, full_value, preferred_element_type=F32
        )
        first_value, first_pull = jax.vjp(rms_norm, in_float, full_attn_gain)
        input_norm_grad, attn_gain_grad = first_pull(normed_grad)
        input_grad = residual_grad + input_norm_grad
        head_grad = dense_sum(
            jnp.concatenate(
                [
                    wk_grad,
                    wv_grad,
                    attn_gain_grad[:, None],
                    jnp.zeros((model_width, 127), F32),
                ],
                axis=1,
            ),
            dp_index,
        )
        return (
            layer_output,
            input_grad,
            head_grad[:, 2 * narrow],
            query_sum,
            head_grad[:, :narrow],
            head_grad[:, narrow : 2 * narrow],
            tail_grad[:, :wide],
            tail_grad[:, wide + EXPERTS],
            tail_grad[:, wide : wide + EXPERTS],
            expert_grads[0],
            expert_grads[1],
            expert_grads[2],
        )

    return body


def solution(mesh):
    groups = mesh.shape["expert"]
    members = mesh.shape["dp"]
    z_size = groups // 2
    side = math.isqrt(members)
    grid = Mesh(
        mesh.devices.reshape(z_size, 2, members // side, side), ("z", "core", "y", "x")
    )
    expert = ("z", "core")
    dp = ("y", "x")
    every = expert + dp
    placed = (
        P(every, None),
        P(dp),
        P(dp, None),
        P(dp, None),
        P(dp, None),
        P(dp, None),
        P(dp),
        P(dp, None),
        P(expert, dp, None),
        P(expert, dp, None),
        P(expert, dp, None),
        P(every, None),
        P(every, None),
        P(expert),
        P(every, None),
    )
    return jax.shard_map(
        make_body(z_size, members == 4 and side == 2),
        mesh=grid,
        in_specs=placed,
        out_specs=(
            P(every, None),
            P(every, None),
            P(dp),
            P(dp, None),
            P(dp, None),
            P(dp, None),
            P(dp, None),
            P(dp),
            P(dp, None),
            P(expert, dp, None),
            P(expert, dp, None),
            P(expert, dp, None),
        ),
        check_vma=False,
    )
```

```python
import math

import jax
import jax.numpy as jnp
from jax import lax
from jax.experimental import pallas as pl
from jax.experimental.pallas import tpu as pltpu
from jax.sharding import Mesh
from jax.sharding import PartitionSpec as P

H = 16
KVH = 8
HD = 64
EXPERTS = 32
EPSILON = 1e-06
ROPE_BASE = 10000.0
MASKED_SCORE = -1e30
F32 = jnp.float32
B16 = jnp.bfloat16
SWAP = [(0, 1), (1, 0)]
VMEM_LIMIT = 60 * 1024 * 1024


def rms_norm(values, gain_vec):
    return (
        values * lax.rsqrt(jnp.mean(values * values, axis=-1, keepdims=True) + EPSILON) * gain_vec
    )


def rotate(vectors, places):
    half_dim = vectors.shape[-1] // 2
    frequency = jnp.exp(
        jnp.arange(half_dim, dtype=F32) * (-2.0 * math.log(ROPE_BASE) / vectors.shape[-1])
    )
    angles = places[:, None] * frequency[None, :]
    cosine = jnp.cos(angles)[:, None, :]
    sine_vals = jnp.sin(angles)[:, None, :]
    first_half = vectors[..., :half_dim]
    second = vectors[..., half_dim:]
    return jnp.concatenate(
        [first_half * cosine - second * sine_vals, second * cosine + first_half * sine_vals],
        axis=-1,
    )


def swap_core(rows):
    return lax.ppermute(rows, "core", SWAP)


def cyclic(rows, size, shift):
    return lax.ppermute(rows, "z", [(i, (i + shift) % size) for i in range(size)])


def after(value, *others):
    return lax.optimization_barrier((value, *others))[0]


def grid_gather(shard):
    half = shard.shape[0] // 2
    from_x = lax.ppermute(shard, "x", SWAP)
    from_y = lax.ppermute(shard, "y", SWAP)
    diag_a = lax.ppermute(from_x[:half], "y", SWAP)
    diag_b = lax.ppermute(from_y[half:], "x", SWAP)
    return shard, from_x, from_y, diag_a, diag_b


def grid_scatter(first_a, rest_a, first_b, rest_b):
    got_a = lax.ppermute(first_a, "x", SWAP)
    got_b = lax.ppermute(first_b, "y", SWAP)
    onward_a = (rest_a[1].astype(F32) + got_a[1].astype(F32)).astype(B16)
    onward_b = (rest_b[1].astype(F32) + got_b[1].astype(F32)).astype(B16)
    last_a = lax.ppermute(onward_a, "y", SWAP)
    last_b = lax.ppermute(onward_b, "x", SWAP)
    return (
        rest_a[0].astype(F32) + got_a[0].astype(F32) + last_a.astype(F32),
        rest_b[0].astype(F32) + got_b[0].astype(F32) + last_b.astype(F32),
    )


def grid_scatter_rows(parts):
    own, to_x, to_y, diag = parts
    half = own.shape[0] // 2
    total = grid_scatter(
        jnp.stack([to_x[:half], diag[:half]]),
        (own[:half], to_y[:half]),
        jnp.stack([to_y[half:], diag[half:]]),
        (own[half:], to_x[half:]),
    )
    return jnp.concatenate(total, axis=0)


def column_gather(rows, size):
    mine = jnp.stack([rows] + [cyclic(rows, size, -k) for k in range(1, size)])
    return mine, swap_core(mine)


def column_scatter(mine, other, size):
    both = mine.astype(F32) + swap_core(other).astype(F32)
    low = both.astype(B16)
    total = both[0]
    for k in range(1, size):
        total = total + cyclic(low[k], size, k).astype(F32)
    return total


def assemble(places, shard, moved, other, rows):
    def kernel(places_ref, shard_ref, moved_ref, other_ref, out_ref):
        def put(i, value):
            start = pl.multiple_of(places_ref[i] * rows, rows)
            out_ref[pl.ds(start, value.shape[0]), :] = value

        put(0, shard_ref[...])
        for j in range(3):
            put(1 + j, moved_ref[j * rows : (j + 1) * rows, :])
            put(4 + j, other_ref[j * rows : (j + 1) * rows, :])

    def whole(array_shape):
        return pl.BlockSpec(array_shape, lambda i, places: (0, 0))

    out_rows, cols = 8 * rows, shard.shape[1]
    return pl.pallas_call(
        kernel,
        out_shape=jax.ShapeDtypeStruct((out_rows, cols), shard.dtype),
        grid_spec=pltpu.PrefetchScalarGridSpec(
            num_scalar_prefetch=1,
            grid=(1,),
            in_specs=[whole(a.shape) for a in (shard, moved, other)],
            out_specs=whole((out_rows, cols)),
        ),
        compiler_params=pltpu.CompilerParams(vmem_limit_bytes=VMEM_LIMIT),
        name="assemble",
    )(places, shard, moved, other)


def one_hot_slots(codes, capacity):
    slots = lax.broadcasted_iota(jnp.int32, (capacity, codes.shape[1]), 0).astype(F32)
    return [(slots == codes[e : e + 1, :]).astype(F32) for e in range(codes.shape[0])]


def row_of(table, index):
    at = lax.broadcasted_iota(jnp.int32, table.shape, 0)
    return jnp.sum(jnp.where(at == index, table, 0.0), axis=0, keepdims=True)


def pack_code(code):
    rows = code.shape[0] // 4
    wide = jnp.concatenate([code[c * rows : (c + 1) * rows] for c in range(4)], axis=1)
    return jnp.concatenate([wide, jnp.full((16 - rows, wide.shape[1]), -1.0, B16)], axis=0)


def unpack_code(block, tokens):
    rows = EXPERTS // 4
    wide = block.astype(F32)
    return jnp.concatenate(
        [wide[:rows, c * tokens : (c + 1) * tokens] for c in range(4)], axis=0
    )


def dispatch_rows(lead, packed, rows, router, local, capacity):
    pieces, packed_rows, width = packed.shape
    tokens = packed_rows - 16
    slots = local * capacity
    with_gates = router is not None

    def kernel(lead_ref, packed_ref, *rest):
        first = lead_ref[0]
        if with_gates:
            rows_ref, router_ref, out_ref, gate_out = rest
            table = unpack_code(packed_ref[0], tokens)
            source = rows_ref[0]
        else:
            (out_ref,) = rest
            table = unpack_code(packed_ref[0, tokens:, :], tokens)
            source = packed_ref[0, :tokens, :]
        codes = jnp.concatenate([row_of(table, first + e) for e in range(local)], axis=0)
        picks = one_hot_slots(codes, capacity)
        select = jnp.concatenate([p.astype(B16) for p in picks], axis=0)
        out_ref[0] = jnp.dot(select, source, preferred_element_type=F32).astype(B16)
        if with_gates:
            logits = lax.dot_general(
                router_ref[...], source, (((1,), (1,)), ((), ())), preferred_element_type=F32
            )
            routed = table >= 0.0
            peak = jnp.max(jnp.where(routed, logits, MASKED_SCORE), axis=0, keepdims=True)
            lifted = jnp.where(routed, jnp.exp(jnp.minimum(logits - peak, 0.0)), 0.0)
            gates = lifted / jnp.sum(lifted, axis=0, keepdims=True)
            for e in range(local):
                gate_row = row_of(gates, first + e)
                column = jnp.sum(picks[e] * gate_row, axis=1, keepdims=True)
                gate_out[0, e * capacity : (e + 1) * capacity, :] = jnp.broadcast_to(
                    column, (capacity, 128)
                )

    out_specs = [pl.BlockSpec((1, slots, width), lambda p, lead: (p, 0, 0))]
    out_shape = [jax.ShapeDtypeStruct((pieces, slots, width), B16)]
    args = [packed]
    if with_gates:
        in_specs = [
            pl.BlockSpec((1, 16, width), lambda p, lead: (p, tokens // 16, 0)),
            pl.BlockSpec((1, tokens, width), lambda p, lead: (p, 0, 0)),
            pl.BlockSpec((EXPERTS, width), lambda p, lead: (0, 0)),
        ]
        out_specs.append(pl.BlockSpec((1, slots, 128), lambda p, lead: (p, 0, 0)))
        out_shape.append(jax.ShapeDtypeStruct((pieces, slots, 128), F32))
        args += [rows, router]
    else:
        in_specs = [pl.BlockSpec((1, packed_rows, width), lambda p, lead: (p, 0, 0))]
    return pl.pallas_call(
        kernel,
        out_shape=out_shape,
        grid_spec=pltpu.PrefetchScalarGridSpec(
            num_scalar_prefetch=1, grid=(pieces,), in_specs=in_specs, out_specs=out_specs
        ),
        compiler_params=pltpu.CompilerParams(vmem_limit_bytes=VMEM_LIMIT),
        name="dispatch",
    )(lead, *args)


def combine_rows(lead, first, packed, slot_rows, local, capacity):
    pieces, packed_rows, code_width = packed.shape
    tokens = packed_rows - 16
    halves = len(slot_rows)
    slots, width = slot_rows[0].shape[1:]
    per = local // halves

    def kernel(lead_ref, code_ref, *rest):
        table = unpack_code(code_ref[0], tokens)
        here = lead_ref[0]
        codes = jnp.concatenate([row_of(table, here + e) for e in range(local)], axis=0)
        picks = one_hot_slots(codes, capacity)
        total = None
        for h in range(halves):
            select = jnp.concatenate(
                [p.astype(B16) for p in picks[h * per : (h + 1) * per]], axis=0
            )
            part = lax.dot_general(
                select, rest[h][0], (((0,), (0,)), ((), ())), preferred_element_type=F32
            )
            total = part if total is None else total + part
        rest[halves][0] = total.astype(B16)

    in_specs = [pl.BlockSpec((1, 16, code_width), lambda p, lead: (p, tokens // 16, 0))]
    in_specs += [
        pl.BlockSpec((1, slots, width), lambda p, lead: (p + first, 0, 0)) for _ in range(halves)
    ]
    return pl.pallas_call(
        kernel,
        out_shape=jax.ShapeDtypeStruct((pieces, tokens, width), B16),
        grid_spec=pltpu.PrefetchScalarGridSpec(
            num_scalar_prefetch=1,
            grid=(pieces,),
            in_specs=in_specs,
            out_specs=pl.BlockSpec((1, tokens, width), lambda p, lead: (p, 0, 0)),
        ),
        compiler_params=pltpu.CompilerParams(vmem_limit_bytes=VMEM_LIMIT),
        name="combine",
    )(lead, packed, *slot_rows)


def experts(order, start, count, skip, rows, grads, gates, weights, capacity, in_rows, mid_rows):
    half, _, width = rows[0].shape
    pieces = 2 * half
    n = len(weights)
    pack_rows, eff = weights[0].shape[1:]
    folds = width // eff
    total_rows = pieces * capacity
    split = n == 4
    first_half = count // 2
    large = total_rows > 1000

    def kernel(order_ref, *refs):
        rows_a, rows_b, grads_a, grads_b, gates_a, gates_b = refs[:6]
        pack = refs[6 : 6 + n]
        y_out, dx_out = refs[6 + n : 8 + n]
        outs = refs[8 + n : -6]
        full_g, full_u, full_d, grad_g, grad_u, grad_d = refs[-6:]

        def at_in(j):
            return pl.ds(pl.multiple_of(order_ref[j] * in_rows, in_rows), in_rows)

        def at_mid(j):
            return pl.ds(pl.multiple_of(order_ref[j] * mid_rows, mid_rows), mid_rows)

        for j in range(n):
            full_g[at_in(j), :] = pack[j][0, :in_rows]
            full_u[at_in(j), :] = pack[j][0, in_rows : 2 * in_rows]
            for f in range(folds):
                full_d[at_mid(j), f * eff : (f + 1) * eff] = pack[j][
                    0, 2 * in_rows + f * mid_rows : 2 * in_rows + (f + 1) * mid_rows
                ]

        def joined(a, b, w):
            return jnp.concatenate(
                [
                    a[...].reshape(half * capacity, w),
                    b[...].reshape(half * capacity, w),
                ],
                axis=0,
            )

        x = joined(rows_a, rows_b, width)
        g = joined(grads_a, grads_b, width)
        gate = joined(gates_a, gates_b, 128)[:, 0:1]
        nt = (((1,), (1,)), ((), ()))
        tn = (((0,), (0,)), ((), ()))
        gate_proj = jnp.dot(x, full_g[...], preferred_element_type=F32)
        up_proj = jnp.dot(x, full_u[...], preferred_element_type=F32)
        down_grad = lax.dot_general(g, full_d[...], nt, preferred_element_type=F32)
        sigmoid = 1.0 / (1.0 + jnp.exp(-gate_proj))
        silu = gate_proj * sigmoid
        activated = silu * up_proj
        slot_grad = jnp.sum(activated * down_grad, axis=1, keepdims=True)
        here = order_ref[n] + start + pl.program_id(0)
        lane = lax.broadcasted_iota(jnp.int32, (total_rows, 128), 1)
        high = slot_grad.astype(B16).astype(F32)
        tail = jnp.where(lane == here, high, jnp.where(lane == here + EXPERTS, slot_grad - high, 0.0))
        dx_out[:, :, width:] = tail.astype(B16).reshape(pieces, capacity, 128)
        scaled = (gate * activated).astype(B16)
        act_grad = gate * down_grad
        gate_grad = (act_grad * up_proj * (sigmoid * (1.0 + gate_proj * (1.0 - sigmoid)))).astype(
            B16
        )
        up_grad = (act_grad * silu).astype(B16)
        y = jnp.dot(scaled, full_d[...], preferred_element_type=F32)
        y_out[...] = y.astype(B16).reshape(pieces, capacity, width)
        dx = lax.dot_general(gate_grad, full_g[...], nt, preferred_element_type=F32)
        dx = dx + lax.dot_general(up_grad, full_u[...], nt, preferred_element_type=F32)
        dx_out[:, :, :width] = dx.astype(B16).reshape(pieces, capacity, width)
        grad_g[...] = lax.dot_general(x, gate_grad, tn, preferred_element_type=F32).astype(B16)
        grad_u[...] = lax.dot_general(x, up_grad, tn, preferred_element_type=F32).astype(B16)
        grad_d[...] = lax.dot_general(scaled, g, tn, preferred_element_type=F32).astype(B16)

        def give(ref, slot, j):
            ref[slot, 0, :in_rows] = grad_g[at_in(j), :]
            ref[slot, 0, in_rows : 2 * in_rows] = grad_u[at_in(j), :]
            for f in range(folds):
                ref[slot, 0, 2 * in_rows + f * mid_rows : 2 * in_rows + (f + 1) * mid_rows] = grad_d[
                    at_mid(j), f * eff : (f + 1) * eff
                ]

        if split:
            first_a, rest_a, first_b, rest_b = outs

            @pl.when(pl.program_id(0) < first_half)
            def _():
                give(first_a, 0, 1)
                give(first_a, 1, 3)
                give(rest_a, 0, 0)
                give(rest_a, 1, 2)

            @pl.when(pl.program_id(0) >= first_half)
            def _():
                give(first_b, 0, 2)
                give(first_b, 1, 3)
                give(rest_b, 0, 0)
                give(rest_b, 1, 1)
        else:
            for j in range(n):
                give(outs[0], j, j)

    def single():
        return dict(pipeline_mode=pl.Buffered(1)) if large else {}

    def rows_spec(w):
        return pl.BlockSpec((half, capacity, w), lambda e, o: (0, e + start, 0), **single())

    in_specs = [rows_spec(width)] * 4 + [rows_spec(128)] * 2
    for j in range(n):
        in_specs.append(
            pl.BlockSpec((1, pack_rows, eff), lambda e, o, lead=start - skip[j]: (e + lead, 0, 0))
        )
    slots = count * capacity
    out_specs = [
        pl.BlockSpec((pieces, capacity, w), lambda e, o: (0, e, 0), **single())
        for w in (width, width + 128)
    ]
    out_shape = [
        jax.ShapeDtypeStruct((pieces, slots, width), B16),
        jax.ShapeDtypeStruct((pieces, slots, width + 128), B16),
    ]
    if split:
        for at in (
            lambda e, o: (0, jnp.minimum(e, first_half - 1), 0, 0),
            lambda e, o: (0, jnp.maximum(e - first_half, 0), 0, 0),
        ):
            for _ in range(2):
                out_specs.append(pl.BlockSpec((2, 1, pack_rows, eff), at))
                out_shape.append(jax.ShapeDtypeStruct((2, first_half, pack_rows, eff), B16))
    else:
        out_specs.append(pl.BlockSpec((n, 1, pack_rows, eff), lambda e, o: (0, e, 0, 0)))
        out_shape.append(jax.ShapeDtypeStruct((n, count, pack_rows, eff), B16))
    results = pl.pallas_call(
        kernel,
        out_shape=out_shape,
        grid_spec=pltpu.PrefetchScalarGridSpec(
            num_scalar_prefetch=1,
            grid=(count,),
            in_specs=in_specs,
            out_specs=out_specs,
            scratch_shapes=[
                pltpu.VMEM((n * in_rows, eff), B16),
                pltpu.VMEM((n * in_rows, eff), B16),
                pltpu.VMEM((n * mid_rows, width), B16),
                pltpu.VMEM((n * in_rows, eff), B16),
                pltpu.VMEM((n * in_rows, eff), B16),
                pltpu.VMEM((n * mid_rows, width), B16),
            ],
        ),
        compiler_params=pltpu.CompilerParams(vmem_limit_bytes=VMEM_LIMIT),
        name="experts",
    )(order, *rows, *grads, *gates, *weights)
    return results[0], results[1], results[2:]


def make_body(z_size, small_grid):
    def dense_gather(shard, dp_index):
        if not small_grid:
            return lax.all_gather(shard, ("y", "x"), axis=0, tiled=True), shard
        rows = shard.shape[0]
        core = lax.axis_index("core")
        mine = lax.dynamic_slice_in_dim(shard, core * (rows // 2), rows // 2, 0)
        _, from_x, from_y, diag_a, diag_b = grid_gather(mine)
        moved = jnp.concatenate([from_x, from_y, diag_a, diag_b], axis=0)
        other = swap_core(moved)
        places = [2 * dp_index]
        for which in (core, 1 - core):
            places += [2 * (dp_index ^ (j + 1)) + which for j in range(3)]
        return assemble(jnp.stack(places), shard, moved, other, rows // 2), moved

    def dense_sum(grads, dp_index):
        if not small_grid:
            return lax.psum_scatter(
                lax.psum(grads, ("z", "core")), ("y", "x"), scatter_dimension=0, tiled=True
            )
        rows, cols = grads.shape
        eighth = rows // 8
        core = lax.axis_index("core")
        split = grads.astype(B16).reshape(4, 2, eighth, cols)
        keep = lax.dynamic_index_in_dim(split, core, 1, keepdims=False)
        give = lax.dynamic_index_in_dim(split, 1 - core, 1, keepdims=False)
        both = (keep.astype(F32) + swap_core(give).astype(F32)).astype(B16)
        mine = grid_scatter_rows(
            [lax.dynamic_index_in_dim(both, dp_index ^ j, 0, keepdims=False) for j in range(4)]
        )
        step = 1
        while step < z_size:
            pairs = [(i, i ^ step) for i in range(z_size)]
            mine = mine + lax.ppermute(mine.astype(B16), "z", pairs).astype(F32)
            step *= 2
        low = mine.astype(B16)
        other = swap_core(low)
        first = jnp.where(core == 0, low, other)
        second = jnp.where(core == 0, other, low)
        return jnp.concatenate([first, second], axis=0).astype(F32)

    def body(
        layer_input,
        attn_gain,
        w_query,
        w_key,
        w_value,
        w_output,
        moe_gain,
        w_router,
        w_gate,
        w_up,
        w_down,
        routes,
        priority,
        prefix_len,
        out_grad,
    ):
        tok_rows, model_width = layer_input.shape
        dp_size = lax.axis_size("y") * lax.axis_size("x")
        dp_index = lax.axis_index("y") * lax.axis_size("x") + lax.axis_index("x")
        z = lax.axis_index("z")
        core = lax.axis_index("core")
        seq_len = tok_rows * dp_size
        top_count = routes.shape[1]
        local = w_gate.shape[0]
        capacity = 5 * tok_rows * top_count // (4 * EXPERTS)
        group_size = H // KVH
        score_scale = HD ** (-0.5)

        gains = jnp.stack([attn_gain, moe_gain], axis=1)
        rows = w_query.shape[0]
        head_pack = jnp.concatenate(
            [w_query, w_key, w_value, w_router, gains, jnp.zeros((rows, 94), B16)], axis=1
        )
        head_full, head_moved = dense_gather(head_pack, dp_index)
        full_output, tail_moved = dense_gather(after(w_output, head_moved), dp_index)
        wide = H * HD
        narrow = KVH * HD
        full_query = head_full[:, :wide]
        full_key = head_full[:, wide : wide + narrow]
        full_value = head_full[:, wide + narrow : wide + 2 * narrow]
        full_router = head_full[:, wide + 2 * narrow : wide + 2 * narrow + EXPERTS]
        full_attn_gain = head_full[:, wide + 2 * narrow + EXPERTS].astype(F32)
        full_moe_gain = head_full[:, wide + 2 * narrow + EXPERTS + 1].astype(F32)

        expert_ids = jnp.arange(EXPERTS, dtype=jnp.int32)
        hits = routes[:, :, None] == expert_ids[None, None, :]
        routed = jnp.any(hits, axis=1)
        place = jnp.where(
            routed, jnp.sum(jnp.where(hits, priority[:, :, None], 0), axis=1), jnp.int32(1 << 20)
        )
        ranks = jnp.sum((place[:, :, None] < place.T[None, :, :]).astype(F32), axis=0)
        code = pack_code(jnp.where(routed.T, ranks, -1.0).astype(B16))
        lead = ((2 * z + core) * local).astype(jnp.int32)[None]
        grads_mine, grads_other = column_gather(
            jnp.concatenate([out_grad, code], axis=0), z_size
        )
        (slot_grads_mine,) = dispatch_rows(lead, grads_mine, None, None, local, capacity)
        (slot_grads_other,) = dispatch_rows(lead, grads_other, None, None, local, capacity)

        query_pos = dp_index * tok_rows + jnp.arange(tok_rows, dtype=jnp.int32)
        places = query_pos.astype(F32)
        in_float = layer_input.astype(F32)
        normed = rms_norm(in_float, full_attn_gain).astype(B16)
        query_lin = jnp.dot(normed, full_query, preferred_element_type=F32)
        key_lin = jnp.dot(normed, full_key, preferred_element_type=F32)
        value_low = jnp.dot(normed, full_value, preferred_element_type=F32).astype(B16)
        query_rot = (rotate(query_lin.reshape(tok_rows, H, HD), places) * score_scale).astype(B16)
        key_rot = rotate(key_lin.reshape(tok_rows, KVH, HD), places).astype(B16)
        key_rot = key_rot.reshape(tok_rows, narrow)
        both = jnp.concatenate([key_rot, value_low], axis=1)
        steps = jnp.arange(tok_rows, dtype=jnp.int32)
        eff = w_gate.shape[2]
        in_rows, mid_rows = w_gate.shape[1], w_down.shape[1]
        folds = [w_down[:, :, f * eff : (f + 1) * eff] for f in range(model_width // eff)]
        pack = jnp.concatenate([w_gate, w_up, *folds], axis=1)
        if small_grid:
            relative = dp_index ^ jnp.arange(4, dtype=jnp.int32)
            both_parts = grid_gather(both)
            both_all = jnp.concatenate(both_parts, axis=0)
            key_pos = (relative[:, None] * tok_rows + steps[None, :]).reshape(seq_len)
            halves, per = 2, local // 2
            expert_weights, skips = [], []
            for half in range(2):
                own = after(pack[half * per : (half + 1) * per], both_parts[1], both_parts[2])
                parts = grid_gather(own)
                diag = jnp.concatenate([parts[3], parts[4]], axis=0)
                expert_weights.append([own, parts[1], parts[2], diag])
                skips.append([half * per] * 4)
        else:
            relative = jnp.arange(dp_size, dtype=jnp.int32)
            both_all = lax.all_gather(both, ("y", "x"), axis=0, tiled=True)
            key_pos = jnp.arange(seq_len, dtype=jnp.int32)
            halves, per = 1, local
            every = lax.all_gather(pack, ("y", "x"), axis=0, tiled=False)
            expert_weights = [[every[j] for j in range(dp_size)]]
            skips = [[0] * dp_size]
        order = jnp.concatenate([relative, lead])
        key_all = both_all[:, :narrow]
        value_all = both_all[:, narrow:]
        visible = (key_pos[None, :] <= query_pos[:, None]) | (key_pos[None, :] < prefix_len[0])

        def head_scores(head_idx):
            query_head = query_rot[:, head_idx * group_size : (head_idx + 1) * group_size, :]
            key_head = key_all[:, head_idx * HD : (head_idx + 1) * HD]
            scores = jnp.einsum("qgd,kd->gqk", query_head, key_head, preferred_element_type=F32)
            return jnp.where(visible[None, :, :], scores, MASKED_SCORE)

        mixed_heads = []
        log_totals = []
        for head_idx in range(KVH):
            scores = head_scores(head_idx)
            row_max = jnp.max(scores, axis=-1, keepdims=True)
            log_total = row_max + jnp.log(
                jnp.sum(jnp.exp(scores - row_max), axis=-1, keepdims=True)
            )
            probs_low = jnp.exp(scores - log_total).astype(B16)
            value_head = value_all[:, head_idx * HD : (head_idx + 1) * HD]
            mixed_heads.append(
                jnp.einsum("gqk,kd->qgd", probs_low, value_head, preferred_element_type=F32)
            )
            log_totals.append(log_total)
        attended = jnp.concatenate(mixed_heads, axis=1).reshape(tok_rows, wide).astype(B16)
        residual = in_float + jnp.dot(attended, full_output, preferred_element_type=F32)
        moe_in = rms_norm(residual, full_moe_gain).astype(B16)

        rows_mine, rows_other = column_gather(moe_in, z_size)
        router_rows = full_router.T
        slot_rows_mine, slot_gates_mine = dispatch_rows(
            lead, grads_mine, rows_mine, router_rows, local, capacity
        )
        slot_rows_other, slot_gates_other = dispatch_rows(
            lead, grads_other, rows_other, router_rows, local, capacity
        )
        logits = jnp.dot(moe_in, full_router, preferred_element_type=F32)
        peak = jnp.max(jnp.where(routed, logits, MASKED_SCORE), axis=-1, keepdims=True)
        lifted = jnp.where(routed, jnp.exp(jnp.minimum(logits - peak, 0.0)), 0.0)
        gate_weights = lifted / jnp.sum(lifted, axis=-1, keepdims=True)
        ys, dxs, weight_grads = [], [], []
        for half in range(halves):
            y, dx, grads = experts(
                order,
                half * per,
                per,
                skips[half],
                (slot_rows_mine, slot_rows_other),
                (slot_grads_mine, slot_grads_other),
                (slot_gates_mine, slot_gates_other),
                expert_weights[half],
                capacity,
                in_rows,
                mid_rows,
            )
            ys.append(y)
            dxs.append(dx)
            weight_grads.append(grads)
        dx_other = combine_rows(lead, z_size, grads_other, dxs, local, capacity)
        dx_mine = combine_rows(lead, 0, grads_mine, dxs, local, capacity)
        moe_sum = column_scatter(dx_mine, dx_other, z_size)
        moe_in_grad = moe_sum[:, :model_width]
        gate_grad = (
            moe_sum[:, model_width : model_width + EXPERTS]
            + moe_sum[:, model_width + EXPERTS : model_width + 2 * EXPERTS]
        )
        y_other = combine_rows(lead, z_size, grads_other, ys, local, capacity)
        y_mine = combine_rows(lead, 0, grads_mine, ys, local, capacity)
        mixture = column_scatter(y_mine, y_other, z_size)
        layer_output = (residual + mixture).astype(B16)
        if small_grid:
            sums = []
            for grads in weight_grads:
                sums += list(grid_scatter(*grads))
            pack_grad = jnp.concatenate(sums, axis=0)
        else:
            pack_grad = lax.psum_scatter(
                weight_grads[0][0].astype(F32), ("y", "x"), scatter_dimension=0, tiled=False
            )
        down = 2 * in_rows
        expert_grads = [
            pack_grad[:, :in_rows],
            pack_grad[:, in_rows:down],
            jnp.concatenate(
                [
                    pack_grad[:, down + f * mid_rows : down + (f + 1) * mid_rows]
                    for f in range(model_width // eff)
                ],
                axis=2,
            ),
        ]

        grad_out = out_grad.astype(F32)
        centre = jnp.sum(gate_weights * gate_grad, axis=-1, keepdims=True)
        logit_low = (gate_weights * (gate_grad - centre)).astype(B16)
        router_grad = jnp.einsum("td,te->de", moe_in, logit_low, preferred_element_type=F32)
        moe_in_grad = moe_in_grad + jnp.einsum(
            "te,de->td", logit_low, full_router, preferred_element_type=F32
        )
        norm_value, second_pull = jax.vjp(rms_norm, residual, full_moe_gain)
        resid_norm_grad, moe_gain_grad = second_pull(moe_in_grad)
        residual_grad = grad_out + resid_norm_grad
        attn_out_grad = residual_grad.astype(B16)
        wout_grad = jnp.einsum("tc,td->cd", attended, attn_out_grad, preferred_element_type=F32)
        attended_grad = (
            jnp.einsum("td,cd->tc", attn_out_grad, full_output, preferred_element_type=F32)
            .astype(B16)
            .reshape(tok_rows, H, HD)
        )
        tail_grad = dense_sum(
            jnp.concatenate(
                [
                    wout_grad,
                    router_grad,
                    moe_gain_grad[:, None],
                    jnp.zeros((model_width, 95), F32),
                ],
                axis=1,
            ),
            dp_index,
        )
        query_grads = []
        key_parts = []
        value_parts = []
        for head_idx in range(KVH):
            scores = head_scores(head_idx)
            attention_probs = jnp.exp(scores - log_totals[head_idx])
            probs_low = attention_probs.astype(B16)
            grad_head = attended_grad[:, head_idx * group_size : (head_idx + 1) * group_size, :]
            query_head = query_rot[:, head_idx * group_size : (head_idx + 1) * group_size, :]
            key_head = key_all[:, head_idx * HD : (head_idx + 1) * HD]
            value_head = value_all[:, head_idx * HD : (head_idx + 1) * HD]
            probs_grad = jnp.einsum("qgd,kd->gqk", grad_head, value_head, preferred_element_type=F32)
            row_delta = jnp.sum(attention_probs * probs_grad, axis=-1, keepdims=True)
            score_grad = (attention_probs * (probs_grad - row_delta)).astype(B16)
            query_grads.append(
                jnp.einsum("gqk,kd->qgd", score_grad, key_head, preferred_element_type=F32)
            )
            key_parts.append(
                jnp.einsum("gqk,qgd->kd", score_grad, query_head, preferred_element_type=F32)
            )
            value_parts.append(
                jnp.einsum("gqk,qgd->kd", probs_low, grad_head, preferred_element_type=F32)
            )
        both_part = jnp.concatenate(key_parts + value_parts, axis=1)
        if small_grid:
            both_sum = grid_scatter_rows(both_part.astype(B16).reshape(4, tok_rows, 2 * narrow))
        else:
            both_sum = lax.psum_scatter(both_part, ("y", "x"), scatter_dimension=0, tiled=True)
        query_rot_grad = jnp.concatenate(query_grads, axis=1) * score_scale
        key_rot_grad = both_sum[:, :narrow].reshape(tok_rows, KVH, HD)
        value_grad = both_sum[:, narrow:].astype(B16)
        query_grad = rotate(query_rot_grad, -places).reshape(tok_rows, wide).astype(B16)
        key_grad = rotate(key_rot_grad, -places).reshape(tok_rows, narrow).astype(B16)
        wq_grad = jnp.einsum("td,tc->dc", normed, query_grad, preferred_element_type=F32)
        query_sum = dense_sum(wq_grad, dp_index)
        wk_grad = jnp.einsum("td,tc->dc", normed, key_grad, preferred_element_type=F32)
        wv_grad = jnp.einsum("td,tc->dc", normed, value_grad, preferred_element_type=F32)
        normed_grad = jnp.einsum("tc,dc->td", query_grad, full_query, preferred_element_type=F32)
        normed_grad = normed_grad + jnp.einsum(
            "tc,dc->td", key_grad, full_key, preferred_element_type=F32
        )
        normed_grad = normed_grad + jnp.einsum(
            "tc,dc->td", value_grad, full_value, preferred_element_type=F32
        )
        first_value, first_pull = jax.vjp(rms_norm, in_float, full_attn_gain)
        input_norm_grad, attn_gain_grad = first_pull(normed_grad)
        input_grad = residual_grad + input_norm_grad
        head_grad = dense_sum(
            jnp.concatenate(
                [
                    wk_grad,
                    wv_grad,
                    attn_gain_grad[:, None],
                    jnp.zeros((model_width, 127), F32),
                ],
                axis=1,
            ),
            dp_index,
        )
        return (
            layer_output,
            input_grad,
            head_grad[:, 2 * narrow],
            query_sum,
            head_grad[:, :narrow],
            head_grad[:, narrow : 2 * narrow],
            tail_grad[:, :wide],
            tail_grad[:, wide + EXPERTS],
            tail_grad[:, wide : wide + EXPERTS],
            expert_grads[0],
            expert_grads[1],
            expert_grads[2],
        )

    return body


def solution(mesh):
    groups = mesh.shape["expert"]
    members = mesh.shape["dp"]
    z_size = groups // 2
    side = math.isqrt(members)
    grid = Mesh(
        mesh.devices.reshape(z_size, 2, members // side, side), ("z", "core", "y", "x")
    )
    expert = ("z", "core")
    dp = ("y", "x")
    every = expert + dp
    placed = (
        P(every, None),
        P(dp),
        P(dp, None),
        P(dp, None),
        P(dp, None),
        P(dp, None),
        P(dp),
        P(dp, None),
        P(expert, dp, None),
        P(expert, dp, None),
        P(expert, dp, None),
        P(every, None),
        P(every, None),
        P(expert),
        P(every, None),
    )
    return jax.shard_map(
        make_body(z_size, members == 4 and side == 2),
        mesh=grid,
        in_specs=placed,
        out_specs=(
            P(every, None),
            P(every, None),
            P(dp),
            P(dp, None),
            P(dp, None),
            P(dp, None),
            P(dp, None),
            P(dp),
            P(dp, None),
            P(expert, dp, None),
            P(expert, dp, None),
            P(expert, dp, None),
        ),
        check_vma=False,
    )
```

```python
import math

import jax
import jax.numpy as jnp
from jax import lax
from jax.experimental import pallas as pl
from jax.experimental.pallas import tpu as pltpu
from jax.sharding import Mesh
from jax.sharding import PartitionSpec as P

H = 16
KVH = 8
HD = 64
EXPERTS = 32
EPSILON = 1e-06
ROPE_BASE = 10000.0
MASKED_SCORE = -1e30
F32 = jnp.float32
B16 = jnp.bfloat16
SWAP = [(0, 1), (1, 0)]
VMEM_LIMIT = 60 * 1024 * 1024


def rms_norm(values, gain_vec):
    return (
        values * lax.rsqrt(jnp.mean(values * values, axis=-1, keepdims=True) + EPSILON) * gain_vec
    )


def rotate(vectors, places):
    half_dim = vectors.shape[-1] // 2
    frequency = jnp.exp(
        jnp.arange(half_dim, dtype=F32) * (-2.0 * math.log(ROPE_BASE) / vectors.shape[-1])
    )
    angles = places[:, None] * frequency[None, :]
    cosine = jnp.cos(angles)[:, None, :]
    sine_vals = jnp.sin(angles)[:, None, :]
    first_half = vectors[..., :half_dim]
    second = vectors[..., half_dim:]
    return jnp.concatenate(
        [first_half * cosine - second * sine_vals, second * cosine + first_half * sine_vals],
        axis=-1,
    )


def swap_core(rows):
    return lax.ppermute(rows, "core", SWAP)


def cyclic(rows, size, shift):
    return lax.ppermute(rows, "z", [(i, (i + shift) % size) for i in range(size)])


def after(value, *others):
    return lax.optimization_barrier((value, *others))[0]


def grid_gather(shard):
    half = shard.shape[0] // 2
    from_x = lax.ppermute(shard, "x", SWAP)
    from_y = lax.ppermute(shard, "y", SWAP)
    diag_a = lax.ppermute(from_x[:half], "y", SWAP)
    diag_b = lax.ppermute(from_y[half:], "x", SWAP)
    return shard, from_x, from_y, diag_a, diag_b


def grid_scatter(first_a, rest_a, first_b, rest_b):
    got_a = lax.ppermute(first_a, "x", SWAP)
    got_b = lax.ppermute(first_b, "y", SWAP)
    onward_a = (rest_a[1].astype(F32) + got_a[1].astype(F32)).astype(B16)
    onward_b = (rest_b[1].astype(F32) + got_b[1].astype(F32)).astype(B16)
    last_a = lax.ppermute(onward_a, "y", SWAP)
    last_b = lax.ppermute(onward_b, "x", SWAP)
    return (
        rest_a[0].astype(F32) + got_a[0].astype(F32) + last_a.astype(F32),
        rest_b[0].astype(F32) + got_b[0].astype(F32) + last_b.astype(F32),
    )


def grid_scatter_rows(parts):
    own, to_x, to_y, diag = parts
    half = own.shape[0] // 2
    total = grid_scatter(
        jnp.stack([to_x[:half], diag[:half]]),
        (own[:half], to_y[:half]),
        jnp.stack([to_y[half:], diag[half:]]),
        (own[half:], to_x[half:]),
    )
    return jnp.concatenate(total, axis=0)


def column_gather(rows, size):
    mine = jnp.stack([rows] + [cyclic(rows, size, -k) for k in range(1, size)])
    return mine, swap_core(mine)


def column_scatter(mine, other, size):
    both = mine.astype(F32) + swap_core(other).astype(F32)
    low = both.astype(B16)
    total = both[0]
    for k in range(1, size):
        total = total + cyclic(low[k], size, k).astype(F32)
    return total


def assemble(places, shard, moved, other, rows):
    def kernel(places_ref, shard_ref, moved_ref, other_ref, out_ref):
        def put(i, value):
            start = pl.multiple_of(places_ref[i] * rows, rows)
            out_ref[pl.ds(start, value.shape[0]), :] = value

        put(0, shard_ref[...])
        for j in range(3):
            put(1 + j, moved_ref[j * rows : (j + 1) * rows, :])
            put(4 + j, other_ref[j * rows : (j + 1) * rows, :])

    def whole(array_shape):
        return pl.BlockSpec(array_shape, lambda i, places: (0, 0))

    out_rows, cols = 8 * rows, shard.shape[1]
    return pl.pallas_call(
        kernel,
        out_shape=jax.ShapeDtypeStruct((out_rows, cols), shard.dtype),
        grid_spec=pltpu.PrefetchScalarGridSpec(
            num_scalar_prefetch=1,
            grid=(1,),
            in_specs=[whole(a.shape) for a in (shard, moved, other)],
            out_specs=whole((out_rows, cols)),
        ),
        compiler_params=pltpu.CompilerParams(vmem_limit_bytes=VMEM_LIMIT),
        name="assemble",
    )(places, shard, moved, other)


def one_hot_slots(codes, capacity):
    slots = lax.broadcasted_iota(jnp.int32, (capacity, codes.shape[1]), 0).astype(F32)
    return [(slots == codes[e : e + 1, :]).astype(F32) for e in range(codes.shape[0])]


def row_of(table, index):
    at = lax.broadcasted_iota(jnp.int32, table.shape, 0)
    return jnp.sum(jnp.where(at == index, table, 0.0), axis=0, keepdims=True)


def pack_code(code):
    rows = code.shape[0] // 4
    wide = jnp.concatenate([code[c * rows : (c + 1) * rows] for c in range(4)], axis=1)
    return jnp.concatenate([wide, jnp.full((16 - rows, wide.shape[1]), -1.0, B16)], axis=0)


def unpack_code(block, tokens):
    rows = EXPERTS // 4
    wide = block.astype(F32)
    return jnp.concatenate(
        [wide[:rows, c * tokens : (c + 1) * tokens] for c in range(4)], axis=0
    )


def dispatch_rows(lead, packed, rows, router, local, capacity):
    pieces, packed_rows, width = packed.shape
    tokens = packed_rows - 16
    slots = local * capacity
    with_gates = router is not None

    def kernel(lead_ref, packed_ref, *rest):
        first = lead_ref[0]
        if with_gates:
            rows_ref, router_ref, out_ref, gate_out = rest
            table = unpack_code(packed_ref[0], tokens)
            source = rows_ref[0]
        else:
            (out_ref,) = rest
            table = unpack_code(packed_ref[0, tokens:, :], tokens)
            source = packed_ref[0, :tokens, :]
        codes = jnp.concatenate([row_of(table, first + e) for e in range(local)], axis=0)
        picks = one_hot_slots(codes, capacity)
        select = jnp.concatenate([p.astype(B16) for p in picks], axis=0)
        out_ref[0] = jnp.dot(select, source, preferred_element_type=F32).astype(B16)
        if with_gates:
            logits = lax.dot_general(
                router_ref[...], source, (((1,), (1,)), ((), ())), preferred_element_type=F32
            )
            routed = table >= 0.0
            peak = jnp.max(jnp.where(routed, logits, MASKED_SCORE), axis=0, keepdims=True)
            lifted = jnp.where(routed, jnp.exp(jnp.minimum(logits - peak, 0.0)), 0.0)
            gates = lifted / jnp.sum(lifted, axis=0, keepdims=True)
            for e in range(local):
                gate_row = row_of(gates, first + e)
                column = jnp.sum(picks[e] * gate_row, axis=1, keepdims=True)
                gate_out[0, e * capacity : (e + 1) * capacity, :] = jnp.broadcast_to(
                    column, (capacity, 128)
                )

    out_specs = [pl.BlockSpec((1, slots, width), lambda p, lead: (p, 0, 0))]
    out_shape = [jax.ShapeDtypeStruct((pieces, slots, width), B16)]
    args = [packed]
    if with_gates:
        in_specs = [
            pl.BlockSpec((1, 16, width), lambda p, lead: (p, tokens // 16, 0)),
            pl.BlockSpec((1, tokens, width), lambda p, lead: (p, 0, 0)),
            pl.BlockSpec((EXPERTS, width), lambda p, lead: (0, 0)),
        ]
        out_specs.append(pl.BlockSpec((1, slots, 128), lambda p, lead: (p, 0, 0)))
        out_shape.append(jax.ShapeDtypeStruct((pieces, slots, 128), F32))
        args += [rows, router]
    else:
        in_specs = [pl.BlockSpec((1, packed_rows, width), lambda p, lead: (p, 0, 0))]
    return pl.pallas_call(
        kernel,
        out_shape=out_shape,
        grid_spec=pltpu.PrefetchScalarGridSpec(
            num_scalar_prefetch=1, grid=(pieces,), in_specs=in_specs, out_specs=out_specs
        ),
        compiler_params=pltpu.CompilerParams(vmem_limit_bytes=VMEM_LIMIT),
        name="dispatch",
    )(lead, *args)


def combine_rows(lead, first, packed, slot_rows, local, capacity):
    pieces, packed_rows, code_width = packed.shape
    tokens = packed_rows - 16
    halves = len(slot_rows)
    slots, width = slot_rows[0].shape[1:]
    per = local // halves

    def kernel(lead_ref, code_ref, *rest):
        table = unpack_code(code_ref[0], tokens)
        here = lead_ref[0]
        codes = jnp.concatenate([row_of(table, here + e) for e in range(local)], axis=0)
        picks = one_hot_slots(codes, capacity)
        total = None
        for h in range(halves):
            select = jnp.concatenate(
                [p.astype(B16) for p in picks[h * per : (h + 1) * per]], axis=0
            )
            part = lax.dot_general(
                select, rest[h][0], (((0,), (0,)), ((), ())), preferred_element_type=F32
            )
            total = part if total is None else total + part
        rest[halves][0] = total.astype(B16)

    in_specs = [pl.BlockSpec((1, 16, code_width), lambda p, lead: (p, tokens // 16, 0))]
    in_specs += [
        pl.BlockSpec((1, slots, width), lambda p, lead: (p + first, 0, 0)) for _ in range(halves)
    ]
    return pl.pallas_call(
        kernel,
        out_shape=jax.ShapeDtypeStruct((pieces, tokens, width), B16),
        grid_spec=pltpu.PrefetchScalarGridSpec(
            num_scalar_prefetch=1,
            grid=(pieces,),
            in_specs=in_specs,
            out_specs=pl.BlockSpec((1, tokens, width), lambda p, lead: (p, 0, 0)),
        ),
        compiler_params=pltpu.CompilerParams(vmem_limit_bytes=VMEM_LIMIT),
        name="combine",
    )(lead, packed, *slot_rows)


def experts(order, start, count, skip, rows, grads, gates, weights, capacity, in_rows, mid_rows):
    half, _, width = rows[0].shape
    pieces = 2 * half
    n = len(weights)
    pack_rows, eff = weights[0].shape[1:]
    folds = width // eff
    total_rows = pieces * capacity
    split = n == 4
    first_half = count // 2
    large = total_rows > 1000

    def kernel(order_ref, *refs):
        rows_a, rows_b, grads_a, grads_b, gates_a, gates_b = refs[:6]
        pack = refs[6 : 6 + n]
        y_out, dx_out = refs[6 + n : 8 + n]
        outs = refs[8 + n : -6]
        full_g, full_u, full_d, grad_g, grad_u, grad_d = refs[-6:]

        def at_in(j):
            return pl.ds(pl.multiple_of(order_ref[j] * in_rows, in_rows), in_rows)

        def at_mid(j):
            return pl.ds(pl.multiple_of(order_ref[j] * mid_rows, mid_rows), mid_rows)

        for j in range(n):
            full_g[at_in(j), :] = pack[j][0, :in_rows]
            full_u[at_in(j), :] = pack[j][0, in_rows : 2 * in_rows]
            for f in range(folds):
                full_d[at_mid(j), f * eff : (f + 1) * eff] = pack[j][
                    0, 2 * in_rows + f * mid_rows : 2 * in_rows + (f + 1) * mid_rows
                ]

        def joined(a, b, w):
            return jnp.concatenate(
                [
                    a[...].reshape(half * capacity, w),
                    b[...].reshape(half * capacity, w),
                ],
                axis=0,
            )

        x = joined(rows_a, rows_b, width)
        g = joined(grads_a, grads_b, width)
        gate = joined(gates_a, gates_b, 128)[:, 0:1]
        nt = (((1,), (1,)), ((), ()))
        tn = (((0,), (0,)), ((), ()))
        gate_proj = jnp.dot(x, full_g[...], preferred_element_type=F32)
        up_proj = jnp.dot(x, full_u[...], preferred_element_type=F32)
        down_grad = lax.dot_general(g, full_d[...], nt, preferred_element_type=F32)
        sigmoid = 1.0 / (1.0 + jnp.exp(-gate_proj))
        silu = gate_proj * sigmoid
        activated = silu * up_proj
        slot_grad = jnp.sum(activated * down_grad, axis=1, keepdims=True)
        here = order_ref[n] + start + pl.program_id(0)
        lane = lax.broadcasted_iota(jnp.int32, (total_rows, 128), 1)
        high = slot_grad.astype(B16).astype(F32)
        tail = jnp.where(lane == here, high, jnp.where(lane == here + EXPERTS, slot_grad - high, 0.0))
        dx_out[:, :, width:] = tail.astype(B16).reshape(pieces, capacity, 128)
        scaled = (gate * activated).astype(B16)
        act_grad = gate * down_grad
        gate_grad = (act_grad * up_proj * (sigmoid * (1.0 + gate_proj * (1.0 - sigmoid)))).astype(
            B16
        )
        up_grad = (act_grad * silu).astype(B16)
        y = jnp.dot(scaled, full_d[...], preferred_element_type=F32)
        y_out[...] = y.astype(B16).reshape(pieces, capacity, width)
        dx = lax.dot_general(gate_grad, full_g[...], nt, preferred_element_type=F32)
        dx = dx + lax.dot_general(up_grad, full_u[...], nt, preferred_element_type=F32)
        dx_out[:, :, :width] = dx.astype(B16).reshape(pieces, capacity, width)
        grad_g[...] = lax.dot_general(x, gate_grad, tn, preferred_element_type=F32).astype(B16)
        grad_u[...] = lax.dot_general(x, up_grad, tn, preferred_element_type=F32).astype(B16)
        grad_d[...] = lax.dot_general(scaled, g, tn, preferred_element_type=F32).astype(B16)

        def give(ref, slot, j):
            ref[slot, 0, :in_rows] = grad_g[at_in(j), :]
            ref[slot, 0, in_rows : 2 * in_rows] = grad_u[at_in(j), :]
            for f in range(folds):
                ref[slot, 0, 2 * in_rows + f * mid_rows : 2 * in_rows + (f + 1) * mid_rows] = grad_d[
                    at_mid(j), f * eff : (f + 1) * eff
                ]

        if split:
            first_a, rest_a, first_b, rest_b = outs

            @pl.when(pl.program_id(0) < first_half)
            def _():
                give(first_a, 0, 1)
                give(first_a, 1, 3)
                give(rest_a, 0, 0)
                give(rest_a, 1, 2)

            @pl.when(pl.program_id(0) >= first_half)
            def _():
                give(first_b, 0, 2)
                give(first_b, 1, 3)
                give(rest_b, 0, 0)
                give(rest_b, 1, 1)
        else:
            for j in range(n):
                give(outs[0], j, j)

    def single():
        return dict(pipeline_mode=pl.Buffered(1)) if large else {}

    def rows_spec(w):
        return pl.BlockSpec((half, capacity, w), lambda e, o: (0, e + start, 0), **single())

    in_specs = [rows_spec(width)] * 4 + [rows_spec(128)] * 2
    for j in range(n):
        in_specs.append(
            pl.BlockSpec((1, pack_rows, eff), lambda e, o, lead=start - skip[j]: (e + lead, 0, 0))
        )
    slots = count * capacity
    out_specs = [
        pl.BlockSpec((pieces, capacity, w), lambda e, o: (0, e, 0), **single())
        for w in (width, width + 128)
    ]
    out_shape = [
        jax.ShapeDtypeStruct((pieces, slots, width), B16),
        jax.ShapeDtypeStruct((pieces, slots, width + 128), B16),
    ]
    if split:
        for at in (
            lambda e, o: (0, jnp.minimum(e, first_half - 1), 0, 0),
            lambda e, o: (0, jnp.maximum(e - first_half, 0), 0, 0),
        ):
            for _ in range(2):
                out_specs.append(pl.BlockSpec((2, 1, pack_rows, eff), at))
                out_shape.append(jax.ShapeDtypeStruct((2, first_half, pack_rows, eff), B16))
    else:
        out_specs.append(pl.BlockSpec((n, 1, pack_rows, eff), lambda e, o: (0, e, 0, 0)))
        out_shape.append(jax.ShapeDtypeStruct((n, count, pack_rows, eff), B16))
    results = pl.pallas_call(
        kernel,
        out_shape=out_shape,
        grid_spec=pltpu.PrefetchScalarGridSpec(
            num_scalar_prefetch=1,
            grid=(count,),
            in_specs=in_specs,
            out_specs=out_specs,
            scratch_shapes=[
                pltpu.VMEM((n * in_rows, eff), B16),
                pltpu.VMEM((n * in_rows, eff), B16),
                pltpu.VMEM((n * mid_rows, width), B16),
                pltpu.VMEM((n * in_rows, eff), B16),
                pltpu.VMEM((n * in_rows, eff), B16),
                pltpu.VMEM((n * mid_rows, width), B16),
            ],
        ),
        compiler_params=pltpu.CompilerParams(vmem_limit_bytes=VMEM_LIMIT),
        name="experts",
    )(order, *rows, *grads, *gates, *weights)
    return results[0], results[1], results[2:]


NT = (((1,), (1,)), ((), ()))
TN = (((0,), (0,)), ((), ()))
GROUPS = KVH // 2
EXTRA = 128


def turn(vectors, cosine, sine):
    lane = lax.broadcasted_iota(jnp.int32, vectors.shape, 1)
    ahead = pltpu.roll(vectors, 2 * HD - HD // 2, 1)
    behind = pltpu.roll(vectors, HD // 2, 1)
    return vectors * cosine + jnp.where(lane % HD < HD // 2, ahead, behind) * sine


def turn_tables(places):
    lane = jnp.arange(2 * HD, dtype=jnp.int32)
    frequency = jnp.exp(
        (lane % (HD // 2)).astype(F32) * (-2.0 * math.log(ROPE_BASE) / HD)
    )
    angles = places[:, None] * frequency[None, :]
    sign = jnp.where(lane % HD < HD // 2, -1.0, 1.0)
    return jnp.cos(angles), jnp.sin(angles) * sign[None, :]


def attention_forward(x_all, head_full, bias, cosine, sine, tok_rows):
    seq_len, width = x_all.shape
    scale = HD ** (-0.5)
    wide, narrow = H * HD, KVH * HD

    def kernel(
        x_ref, tail_ref, wq_ref, wk_ref, wv_ref, bias_ref, cos_ref, sin_ref,
        normed_ref, q_out, k_out, v_out, att_out, total_out, misc_out,
    ):
        @pl.when(pl.program_id(0) == 0)
        def _():
            rows = jnp.transpose(tail_ref[...].astype(F32))
            misc_out[...] = rows
            x = x_ref[...].astype(F32)
            scaled = x * lax.rsqrt(jnp.mean(x * x, axis=1, keepdims=True) + EPSILON)
            normed_ref[...] = (scaled * rows[EXPERTS : EXPERTS + 1, :]).astype(B16)

        normed = normed_ref[...]
        cos, sin = cos_ref[...], sin_ref[...]
        key = turn(jnp.dot(normed, wk_ref[...], preferred_element_type=F32), cos, sin).astype(B16)
        value = jnp.dot(normed, wv_ref[...], preferred_element_type=F32).astype(B16)
        query = jnp.dot(normed[:tok_rows], wq_ref[...], preferred_element_type=F32)
        cos, sin = cos[:tok_rows], sin[:tok_rows]
        query = jnp.concatenate(
            [turn(query[:, 128 * j : 128 * (j + 1)], cos, sin) for j in range(2)], axis=1
        )
        query = (query * scale).astype(B16)
        k_out[...] = key
        v_out[...] = value
        q_out[...] = query
        mixed, totals = [], []
        for j in range(4):
            lanes = slice(HD * (j // 2), HD * (j // 2 + 1))
            scores = lax.dot_general(
                key[:, lanes], query[:, HD * j : HD * (j + 1)], NT, preferred_element_type=F32
            )
            scores = scores + bias_ref[...]
            peak = jnp.max(scores, axis=0, keepdims=True)
            probs = jnp.exp(scores - peak)
            total = jnp.sum(probs, axis=0, keepdims=True)
            out = lax.dot_general(
                value[:, lanes], probs.astype(B16), TN, preferred_element_type=F32
            )
            mixed.append(out / total)
            totals.append(peak + jnp.log(total))
        att_out[...] = jnp.transpose(jnp.concatenate(mixed, axis=0)).astype(B16)
        total_out[0] = jnp.concatenate(totals + totals, axis=0)

    def fixed(*block):
        return pl.BlockSpec(block, lambda i: (0,) * len(block))

    def columns(rows, cols, lead=0):
        return pl.BlockSpec((rows, cols), lambda i: (0, lead + i))

    return pl.pallas_call(
        kernel,
        grid=(GROUPS,),
        in_specs=[
            fixed(seq_len, width),
            pl.BlockSpec((width, 128), lambda i: (0, (wide + 2 * narrow) // 128)),
            columns(width, 256),
            columns(width, 128, wide // 128),
            columns(width, 128, (wide + narrow) // 128),
            fixed(seq_len, tok_rows),
            fixed(seq_len, 128),
            fixed(seq_len, 128),
        ],
        out_specs=[
            fixed(seq_len, width),
            columns(tok_rows, 256),
            columns(seq_len, 128),
            columns(seq_len, 128),
            columns(tok_rows, 256),
            pl.BlockSpec((1, 8, tok_rows), lambda i: (i, 0, 0)),
            fixed(128, width),
        ],
        out_shape=[
            jax.ShapeDtypeStruct((seq_len, width), B16),
            jax.ShapeDtypeStruct((tok_rows, wide), B16),
            jax.ShapeDtypeStruct((seq_len, narrow), B16),
            jax.ShapeDtypeStruct((seq_len, narrow), B16),
            jax.ShapeDtypeStruct((tok_rows, wide), B16),
            jax.ShapeDtypeStruct((GROUPS, 8, tok_rows), F32),
            jax.ShapeDtypeStruct((128, width), F32),
        ],
        compiler_params=pltpu.CompilerParams(vmem_limit_bytes=VMEM_LIMIT),
        name="attention",
    )(x_all, head_full, head_full, head_full, head_full, bias, cosine, sine)


def attention_backward(
    where_here, out_grad_low, full_output, attended, moe_in, logit_low, moe_gain_row, saved,
    x_all, head_full, bias, cosine, sine,
):
    normed_all, query_rot, key_rot, value_all, totals = saved
    seq_len, width = x_all.shape
    tok_rows = query_rot.shape[0]
    scale = HD ** (-0.5)
    wide, narrow = H * HD, KVH * HD
    block = width // 8
    half = width // 2

    def kernel(
        here_ref, og_ref, wo_ref, att_ref, moe_ref, logit_ref, gain_ref,
        normed_ref, q_ref, k_ref, v_ref, total_ref,
        x_ref, wq_ref, wk_ref, wv_ref, bias_ref, cos_ref, sin_ref,
        first_out, second_out, normed_out, normed_t, grad_sum,
    ):
        step = pl.program_id(0)
        dp, core = here_ref[0], here_ref[1]

        @pl.when(step == 0)
        def _():
            normed_t[...] = jnp.transpose(normed_ref[...])
            grad_sum[...] = jnp.zeros((seq_len, width), F32)

        og = og_ref[...]
        att_grad = lax.dot_general(og, wo_ref[...], NT, preferred_element_type=F32).astype(B16)
        query, key, value = q_ref[...], k_ref[...], v_ref[...]
        query_grads, key_grads, value_grads = [], [], []
        for j in range(4):
            lanes = slice(HD * (j // 2), HD * (j // 2 + 1))
            mine = slice(HD * j, HD * (j + 1))
            scores = lax.dot_general(
                key[:, lanes], query[:, mine], NT, preferred_element_type=F32
            )
            probs = jnp.exp(scores + bias_ref[...] - total_ref[0, j : j + 1, :])
            probs_grad = lax.dot_general(
                value[:, lanes], att_grad[:, mine], NT, preferred_element_type=F32
            )
            delta = jnp.sum(probs * probs_grad, axis=0, keepdims=True)
            score_grad = (probs * (probs_grad - delta)).astype(B16)
            query_grads.append(
                lax.dot_general(key[:, lanes], score_grad, TN, preferred_element_type=F32)
            )
            key_part = jnp.dot(score_grad, query[:, mine], preferred_element_type=F32)
            value_part = jnp.dot(probs.astype(B16), att_grad[:, mine], preferred_element_type=F32)
            if j % 2 == 0:
                key_grads.append(key_part)
                value_grads.append(value_part)
            else:
                key_grads[-1] = key_grads[-1] + key_part
                value_grads[-1] = value_grads[-1] + value_part
        cos, sin = cos_ref[...], -sin_ref[...]
        kv_grad = jnp.concatenate(
            [turn(jnp.concatenate(key_grads, axis=1), cos, sin)] + value_grads, axis=1
        ).astype(B16)
        cos, sin = cos[:tok_rows], sin[:tok_rows]
        query_grad = jnp.transpose(jnp.concatenate(query_grads, axis=0)) * scale
        query_grad = jnp.concatenate(
            [turn(query_grad[:, 128 * j : 128 * (j + 1)], cos, sin) for j in range(2)], axis=1
        ).astype(B16)

        def give(out_ref, grad, lanes):
            for m in range(4):
                for c in range(2):
                    out_ref[core ^ c, dp ^ m, :, lanes] = grad[
                        (2 * m + c) * block : (2 * m + c + 1) * block
                    ].astype(B16)

        lanes = pl.ds(pl.multiple_of(step * 256, 256), 256)
        give(
            first_out,
            jnp.dot(normed_t[:, :tok_rows], query_grad, preferred_element_type=F32),
            lanes,
        )
        give(second_out, jnp.dot(normed_t[...], kv_grad, preferred_element_type=F32), lanes)
        out_part = lax.dot_general(att_ref[...], og, TN, preferred_element_type=F32).astype(B16)
        for c in range(2):
            rows = slice(c * block, (c + 1) * block)
            first_out[core ^ c, dp ^ step, :, wide : wide + half] = out_part[rows, :half]
            second_out[core ^ c, dp ^ step, :, wide : wide + half] = out_part[rows, half:]
        kv_weights = jnp.concatenate([wk_ref[...], wv_ref[...]], axis=1)
        grad_sum[...] += lax.dot_general(kv_grad, kv_weights, NT, preferred_element_type=F32)
        grad_sum[:tok_rows, :] += lax.dot_general(
            query_grad, wq_ref[...], NT, preferred_element_type=F32
        )

        @pl.when(step == GROUPS - 1)
        def _():
            total = grad_sum[...]
            normed_out[...] = total.astype(B16)
            x = x_ref[...].astype(F32)
            lifted = x * lax.rsqrt(jnp.mean(x * x, axis=1, keepdims=True) + EPSILON)
            gain = jnp.sum(total * lifted, axis=0, keepdims=True)
            row = lax.broadcasted_iota(jnp.int32, (EXTRA, width), 0)
            gains = jnp.where(
                row == EXPERTS, gain, jnp.where(row == EXPERTS + 1, gain_ref[...], 0.0)
            )
            extra = lax.dot_general(
                moe_ref[...], logit_ref[...], TN, preferred_element_type=F32
            ) + jnp.transpose(gains)
            give(first_out, extra, slice(wide + half, wide + half + EXTRA))

    def fixed(*shape):
        return pl.BlockSpec(shape, lambda i, here: (0,) * len(shape))

    def columns(rows, cols, lead=0):
        return pl.BlockSpec((rows, cols), lambda i, here: (0, lead + i))

    shapes = [
        jax.ShapeDtypeStruct((2, 4, block, wide + half + EXTRA), B16),
        jax.ShapeDtypeStruct((2, 4, block, 2 * narrow + half), B16),
        jax.ShapeDtypeStruct((seq_len, width), B16),
    ]
    return pl.pallas_call(
        kernel,
        out_shape=shapes,
        grid_spec=pltpu.PrefetchScalarGridSpec(
            num_scalar_prefetch=1,
            grid=(GROUPS,),
            in_specs=[
                fixed(tok_rows, width),
                pl.BlockSpec((256, width), lambda i, here: (i, 0)),
                columns(tok_rows, 256),
                fixed(tok_rows, width),
                fixed(tok_rows, EXTRA),
                fixed(1, width),
                fixed(seq_len, width),
                columns(tok_rows, 256),
                columns(seq_len, 128),
                columns(seq_len, 128),
                pl.BlockSpec((1, 8, tok_rows), lambda i, here: (i, 0, 0)),
                fixed(seq_len, width),
                columns(width, 256),
                columns(width, 128, wide // 128),
                columns(width, 128, (wide + narrow) // 128),
                fixed(seq_len, tok_rows),
                fixed(seq_len, 128),
                fixed(seq_len, 128),
            ],
            out_specs=[fixed(*shape.shape) for shape in shapes],
            scratch_shapes=[
                pltpu.VMEM((width, seq_len), B16),
                pltpu.VMEM((seq_len, width), F32),
            ],
        ),
        compiler_params=pltpu.CompilerParams(vmem_limit_bytes=VMEM_LIMIT),
        name="attention_grad",
    )(
        where_here, out_grad_low, full_output, attended, moe_in, logit_low, moe_gain_row,
        normed_all, query_rot, key_rot, value_all, totals,
        x_all, head_full, head_full, head_full, bias, cosine, sine,
    )


def make_body(z_size, small_grid):
    def dense_gather(shard, dp_index):
        if not small_grid:
            return lax.all_gather(shard, ("y", "x"), axis=0, tiled=True), shard
        rows = shard.shape[0]
        core = lax.axis_index("core")
        mine = lax.dynamic_slice_in_dim(shard, core * (rows // 2), rows // 2, 0)
        _, from_x, from_y, diag_a, diag_b = grid_gather(mine)
        moved = jnp.concatenate([from_x, from_y, diag_a, diag_b], axis=0)
        other = swap_core(moved)
        places = [2 * dp_index]
        for which in (core, 1 - core):
            places += [2 * (dp_index ^ (j + 1)) + which for j in range(3)]
        return assemble(jnp.stack(places), shard, moved, other, rows // 2), moved

    def across_z(mine, z):
        if z_size != 4:
            return lax.psum(mine.astype(F32), "z")
        rows = mine.shape[0] // z_size
        low = mine.astype(B16)
        total = lax.dynamic_slice_in_dim(mine, z * rows, rows, 0)
        for k in range(1, z_size):
            theirs = lax.dynamic_slice_in_dim(low, (z + k) % z_size * rows, rows, 0)
            total = total + cyclic(theirs, z_size, k).astype(F32)
        total = total.astype(B16)
        quarters = [total] + [cyclic(total, z_size, -k) for k in range(1, z_size)]
        places = (jnp.arange(z_size, dtype=jnp.int32) - z) % z_size
        return jnp.take(jnp.stack(quarters), places, axis=0).reshape(mine.shape).astype(F32)

    def dense_blocks_sum(blocks, z, core):
        both = (blocks[0].astype(F32) + swap_core(blocks[1]).astype(F32)).astype(B16)
        low = across_z(grid_scatter_rows(both), z).astype(B16)
        other = swap_core(low)
        first = jnp.where(core == 0, low, other)
        second = jnp.where(core == 0, other, low)
        return jnp.concatenate([first, second], axis=0).astype(F32)

    def dense_sum(grads):
        return lax.psum_scatter(
            lax.psum(grads, ("z", "core")), ("y", "x"), scatter_dimension=0, tiled=True
        )

    def body(
        layer_input,
        attn_gain,
        w_query,
        w_key,
        w_value,
        w_output,
        moe_gain,
        w_router,
        w_gate,
        w_up,
        w_down,
        routes,
        priority,
        prefix_len,
        out_grad,
    ):
        tok_rows, model_width = layer_input.shape
        dp_size = lax.axis_size("y") * lax.axis_size("x")
        dp_index = lax.axis_index("y") * lax.axis_size("x") + lax.axis_index("x")
        z = lax.axis_index("z")
        core = lax.axis_index("core")
        seq_len = tok_rows * dp_size
        top_count = routes.shape[1]
        local = w_gate.shape[0]
        capacity = 5 * tok_rows * top_count // (4 * EXPERTS)
        group_size = H // KVH
        score_scale = HD ** (-0.5)

        gains = jnp.stack([attn_gain, moe_gain], axis=1)
        rows = w_query.shape[0]
        head_pack = jnp.concatenate(
            [w_query, w_key, w_value, w_router, gains, jnp.zeros((rows, 94), B16)], axis=1
        )
        x_parts = grid_gather(layer_input) if small_grid else None
        head_full, head_moved = dense_gather(head_pack, dp_index)
        full_output, tail_moved = dense_gather(after(w_output, head_moved), dp_index)
        wide = H * HD
        narrow = KVH * HD
        full_query = head_full[:, :wide]
        full_key = head_full[:, wide : wide + narrow]
        full_value = head_full[:, wide + narrow : wide + 2 * narrow]

        expert_ids = jnp.arange(EXPERTS, dtype=jnp.int32)
        hits = routes[:, :, None] == expert_ids[None, None, :]
        routed = jnp.any(hits, axis=1)
        place = jnp.where(
            routed, jnp.sum(jnp.where(hits, priority[:, :, None], 0), axis=1), jnp.int32(1 << 20)
        )
        ranks = jnp.sum((place[:, :, None] < place.T[None, :, :]).astype(F32), axis=0)
        code = pack_code(jnp.where(routed.T, ranks, -1.0).astype(B16))
        lead = ((2 * z + core) * local).astype(jnp.int32)[None]
        grads_mine, grads_other = column_gather(
            jnp.concatenate([out_grad, code], axis=0), z_size
        )
        (slot_grads_mine,) = dispatch_rows(lead, grads_mine, None, None, local, capacity)
        (slot_grads_other,) = dispatch_rows(lead, grads_other, None, None, local, capacity)

        query_pos = dp_index * tok_rows + jnp.arange(tok_rows, dtype=jnp.int32)
        in_float = layer_input.astype(F32)
        steps = jnp.arange(tok_rows, dtype=jnp.int32)
        eff = w_gate.shape[2]
        in_rows, mid_rows = w_gate.shape[1], w_down.shape[1]
        folds = [w_down[:, :, f * eff : (f + 1) * eff] for f in range(model_width // eff)]
        pack = jnp.concatenate([w_gate, w_up, *folds], axis=1)
        if small_grid:
            relative = dp_index ^ jnp.arange(4, dtype=jnp.int32)
            key_pos = (relative[:, None] * tok_rows + steps[None, :]).reshape(seq_len)
            halves, per = 2, local // 2
            expert_weights, skips = [], []
            first = head_moved
            for half in range(2):
                own = after(pack[half * per : (half + 1) * per], first)
                parts = grid_gather(own)
                diag = jnp.concatenate([parts[3], parts[4]], axis=0)
                expert_weights.append([own, parts[1], parts[2], diag])
                skips.append([half * per] * 4)
                first = parts[1]
        else:
            relative = jnp.arange(dp_size, dtype=jnp.int32)
            key_pos = jnp.arange(seq_len, dtype=jnp.int32)
            halves, per = 1, local
            every = lax.all_gather(pack, ("y", "x"), axis=0, tiled=False)
            expert_weights = [[every[j] for j in range(dp_size)]]
            skips = [[0] * dp_size]
        order = jnp.concatenate([relative, lead])
        visible = (key_pos[None, :] <= query_pos[:, None]) | (key_pos[None, :] < prefix_len[0])
        if small_grid:
            x_all = jnp.concatenate(x_parts, axis=0)
            bias = jnp.where(visible.T, 0.0, MASKED_SCORE)
            cosine, sine = turn_tables(key_pos.astype(F32))
            normed_all, query_rot, key_rot, value_all, attended, totals, misc = attention_forward(
                x_all, head_full, bias, cosine, sine, tok_rows
            )
            router_rows = misc[:EXPERTS].astype(B16)
            full_attn_gain = misc[EXPERTS]
            full_moe_gain = misc[EXPERTS + 1]
        else:
            places = query_pos.astype(F32)
            router_rows = head_full[:, wide + 2 * narrow : wide + 2 * narrow + EXPERTS].T
            full_attn_gain = head_full[:, wide + 2 * narrow + EXPERTS].astype(F32)
            full_moe_gain = head_full[:, wide + 2 * narrow + EXPERTS + 1].astype(F32)
            normed = rms_norm(in_float, full_attn_gain).astype(B16)
            query_lin = jnp.dot(normed, full_query, preferred_element_type=F32)
            key_lin = jnp.dot(normed, full_key, preferred_element_type=F32)
            value_low = jnp.dot(normed, full_value, preferred_element_type=F32).astype(B16)
            query_rot = (rotate(query_lin.reshape(tok_rows, H, HD), places) * score_scale).astype(B16)
            key_rot = rotate(key_lin.reshape(tok_rows, KVH, HD), places).astype(B16)
            key_rot = key_rot.reshape(tok_rows, narrow)
            both = jnp.concatenate([key_rot, value_low], axis=1)
            both_all = lax.all_gather(both, ("y", "x"), axis=0, tiled=True)
            key_all = both_all[:, :narrow]
            value_all = both_all[:, narrow:]

            def head_scores(head_idx):
                query_head = query_rot[:, head_idx * group_size : (head_idx + 1) * group_size, :]
                key_head = key_all[:, head_idx * HD : (head_idx + 1) * HD]
                scores = jnp.einsum("qgd,kd->gqk", query_head, key_head, preferred_element_type=F32)
                return jnp.where(visible[None, :, :], scores, MASKED_SCORE)

            mixed_heads = []
            log_totals = []
            for head_idx in range(KVH):
                scores = head_scores(head_idx)
                row_max = jnp.max(scores, axis=-1, keepdims=True)
                log_total = row_max + jnp.log(
                    jnp.sum(jnp.exp(scores - row_max), axis=-1, keepdims=True)
                )
                probs_low = jnp.exp(scores - log_total).astype(B16)
                value_head = value_all[:, head_idx * HD : (head_idx + 1) * HD]
                mixed_heads.append(
                    jnp.einsum("gqk,kd->qgd", probs_low, value_head, preferred_element_type=F32)
                )
                log_totals.append(log_total)
            attended = jnp.concatenate(mixed_heads, axis=1).reshape(tok_rows, wide).astype(B16)
        residual = in_float + jnp.dot(attended, full_output, preferred_element_type=F32)
        moe_in = rms_norm(residual, full_moe_gain).astype(B16)

        rows_mine, rows_other = column_gather(moe_in, z_size)
        slot_rows_mine, slot_gates_mine = dispatch_rows(
            lead, grads_mine, rows_mine, router_rows, local, capacity
        )
        slot_rows_other, slot_gates_other = dispatch_rows(
            lead, grads_other, rows_other, router_rows, local, capacity
        )
        logits = lax.dot_general(moe_in, router_rows, NT, preferred_element_type=F32)
        peak = jnp.max(jnp.where(routed, logits, MASKED_SCORE), axis=-1, keepdims=True)
        lifted = jnp.where(routed, jnp.exp(jnp.minimum(logits - peak, 0.0)), 0.0)
        gate_weights = lifted / jnp.sum(lifted, axis=-1, keepdims=True)
        ys, dxs, weight_grads = [], [], []
        for half in range(halves):
            y, dx, grads = experts(
                order,
                half * per,
                per,
                skips[half],
                (slot_rows_mine, slot_rows_other),
                (slot_grads_mine, slot_grads_other),
                (slot_gates_mine, slot_gates_other),
                expert_weights[half],
                capacity,
                in_rows,
                mid_rows,
            )
            ys.append(y)
            dxs.append(dx)
            weight_grads.append(grads)
        dx_other = combine_rows(lead, z_size, grads_other, dxs, local, capacity)
        dx_mine = combine_rows(lead, 0, grads_mine, dxs, local, capacity)
        moe_sum = column_scatter(dx_mine, dx_other, z_size)
        moe_in_grad = moe_sum[:, :model_width]
        gate_grad = (
            moe_sum[:, model_width : model_width + EXPERTS]
            + moe_sum[:, model_width + EXPERTS : model_width + 2 * EXPERTS]
        )
        y_other = combine_rows(lead, z_size, grads_other, ys, local, capacity)
        y_mine = combine_rows(lead, 0, grads_mine, ys, local, capacity)
        mixture = column_scatter(y_mine, y_other, z_size)
        layer_output = (residual + mixture).astype(B16)
        if small_grid:
            sums = []
            for grads in weight_grads:
                sums += list(grid_scatter(*grads))
            pack_grad = jnp.concatenate(sums, axis=0)
        else:
            pack_grad = lax.psum_scatter(
                weight_grads[0][0].astype(F32), ("y", "x"), scatter_dimension=0, tiled=False
            )
        down = 2 * in_rows
        expert_grads = [
            pack_grad[:, :in_rows],
            pack_grad[:, in_rows:down],
            jnp.concatenate(
                [
                    pack_grad[:, down + f * mid_rows : down + (f + 1) * mid_rows]
                    for f in range(model_width // eff)
                ],
                axis=2,
            ),
        ]

        grad_out = out_grad.astype(F32)
        centre = jnp.sum(gate_weights * gate_grad, axis=-1, keepdims=True)
        logit_low = (gate_weights * (gate_grad - centre)).astype(B16)
        moe_in_grad = moe_in_grad + jnp.dot(logit_low, router_rows, preferred_element_type=F32)
        norm_value, second_pull = jax.vjp(rms_norm, residual, full_moe_gain)
        resid_norm_grad, moe_gain_grad = second_pull(moe_in_grad)
        residual_grad = grad_out + resid_norm_grad
        attn_out_grad = residual_grad.astype(B16)
        if small_grid:
            logit_wide = jnp.pad(logit_low, ((0, 0), (0, EXTRA - EXPERTS)))
            first_blocks, second_blocks, normed_part = attention_backward(
                jnp.stack([dp_index, core]).astype(jnp.int32),
                attn_out_grad,
                full_output,
                attended,
                moe_in,
                logit_wide,
                moe_gain_grad[None, :],
                (normed_all, query_rot, key_rot, value_all, totals),
                x_all,
                head_full,
                bias,
                cosine,
                sine,
            )
            first_sum = dense_blocks_sum(first_blocks, z, core)
            second_sum = dense_blocks_sum(second_blocks, z, core)
            normed_grad = grid_scatter_rows(normed_part.reshape(4, tok_rows, model_width))
            first_value, first_pull = jax.vjp(lambda v: rms_norm(v, full_attn_gain), in_float)
            input_grad = residual_grad + first_pull(normed_grad)[0]
            at = wide + model_width // 2
            query_sum = first_sum[:, :wide]
            output_sum = jnp.concatenate(
                [first_sum[:, wide:at], second_sum[:, 2 * narrow :]], axis=1
            )
            router_sum = first_sum[:, at : at + EXPERTS]
            attn_gain_sum = first_sum[:, at + EXPERTS]
            moe_gain_sum = first_sum[:, at + EXPERTS + 1]
            key_sum, value_sum = [
                jnp.concatenate(
                    [
                        second_sum[:, 256 * i + lead_col : 256 * i + lead_col + 128]
                        for i in range(GROUPS)
                    ],
                    axis=1,
                )
                for lead_col in (0, 128)
            ]
        else:
            router_grad = jnp.einsum("td,te->de", moe_in, logit_low, preferred_element_type=F32)
            wout_grad = jnp.einsum("tc,td->cd", attended, attn_out_grad, preferred_element_type=F32)
            attended_grad = (
                jnp.einsum("td,cd->tc", attn_out_grad, full_output, preferred_element_type=F32)
                .astype(B16)
                .reshape(tok_rows, H, HD)
            )
            query_grads = []
            key_parts = []
            value_parts = []
            for head_idx in range(KVH):
                scores = head_scores(head_idx)
                attention_probs = jnp.exp(scores - log_totals[head_idx])
                probs_low = attention_probs.astype(B16)
                grad_head = attended_grad[:, head_idx * group_size : (head_idx + 1) * group_size, :]
                query_head = query_rot[:, head_idx * group_size : (head_idx + 1) * group_size, :]
                key_head = key_all[:, head_idx * HD : (head_idx + 1) * HD]
                value_head = value_all[:, head_idx * HD : (head_idx + 1) * HD]
                probs_grad = jnp.einsum("qgd,kd->gqk", grad_head, value_head, preferred_element_type=F32)
                row_delta = jnp.sum(attention_probs * probs_grad, axis=-1, keepdims=True)
                score_grad = (attention_probs * (probs_grad - row_delta)).astype(B16)
                query_grads.append(
                    jnp.einsum("gqk,kd->qgd", score_grad, key_head, preferred_element_type=F32)
                )
                key_parts.append(
                    jnp.einsum("gqk,qgd->kd", score_grad, query_head, preferred_element_type=F32)
                )
                value_parts.append(
                    jnp.einsum("gqk,qgd->kd", probs_low, grad_head, preferred_element_type=F32)
                )
            both_part = jnp.concatenate(key_parts + value_parts, axis=1)
            both_sum = lax.psum_scatter(both_part, ("y", "x"), scatter_dimension=0, tiled=True)
            query_rot_grad = jnp.concatenate(query_grads, axis=1) * score_scale
            key_rot_grad = both_sum[:, :narrow].reshape(tok_rows, KVH, HD)
            value_grad = both_sum[:, narrow:].astype(B16)
            query_grad = rotate(query_rot_grad, -places).reshape(tok_rows, wide).astype(B16)
            key_grad = rotate(key_rot_grad, -places).reshape(tok_rows, narrow).astype(B16)
            wq_grad = jnp.einsum("td,tc->dc", normed, query_grad, preferred_element_type=F32)
            wk_grad = jnp.einsum("td,tc->dc", normed, key_grad, preferred_element_type=F32)
            wv_grad = jnp.einsum("td,tc->dc", normed, value_grad, preferred_element_type=F32)
            normed_grad = jnp.einsum("tc,dc->td", query_grad, full_query, preferred_element_type=F32)
            normed_grad = normed_grad + jnp.einsum(
                "tc,dc->td", key_grad, full_key, preferred_element_type=F32
            )
            normed_grad = normed_grad + jnp.einsum(
                "tc,dc->td", value_grad, full_value, preferred_element_type=F32
            )
            first_value, first_pull = jax.vjp(rms_norm, in_float, full_attn_gain)
            input_norm_grad, attn_gain_grad = first_pull(normed_grad)
            input_grad = residual_grad + input_norm_grad
            query_sum = dense_sum(wq_grad)
            key_sum = dense_sum(wk_grad)
            value_sum = dense_sum(wv_grad)
            output_sum = dense_sum(wout_grad)
            extra_sum = dense_sum(
                jnp.concatenate(
                    [
                        router_grad,
                        attn_gain_grad[:, None],
                        moe_gain_grad[:, None],
                        jnp.zeros((model_width, EXTRA - EXPERTS - 2), F32),
                    ],
                    axis=1,
                )
            )
            router_sum = extra_sum[:, :EXPERTS]
            attn_gain_sum = extra_sum[:, EXPERTS]
            moe_gain_sum = extra_sum[:, EXPERTS + 1]
        return (
            layer_output,
            input_grad,
            attn_gain_sum,
            query_sum,
            key_sum,
            value_sum,
            output_sum,
            moe_gain_sum,
            router_sum,
            expert_grads[0],
            expert_grads[1],
            expert_grads[2],
        )

    return body


def solution(mesh):
    groups = mesh.shape["expert"]
    members = mesh.shape["dp"]
    z_size = groups // 2
    side = math.isqrt(members)
    grid = Mesh(
        mesh.devices.reshape(z_size, 2, members // side, side), ("z", "core", "y", "x")
    )
    expert = ("z", "core")
    dp = ("y", "x")
    every = expert + dp
    placed = (
        P(every, None),
        P(dp),
        P(dp, None),
        P(dp, None),
        P(dp, None),
        P(dp, None),
        P(dp),
        P(dp, None),
        P(expert, dp, None),
        P(expert, dp, None),
        P(expert, dp, None),
        P(every, None),
        P(every, None),
        P(expert),
        P(every, None),
    )
    return jax.shard_map(
        make_body(z_size, members == 4 and side == 2),
        mesh=grid,
        in_specs=placed,
        out_specs=(
            P(every, None),
            P(every, None),
            P(dp),
            P(dp, None),
            P(dp, None),
            P(dp, None),
            P(dp, None),
            P(dp),
            P(dp, None),
            P(expert, dp, None),
            P(expert, dp, None),
            P(expert, dp, None),
        ),
        check_vma=False,
    )
```

```python
import math

import jax
import jax.numpy as jnp
from jax import lax
from jax.experimental import pallas as pl
from jax.experimental.pallas import tpu as pltpu
from jax.sharding import Mesh
from jax.sharding import PartitionSpec as P

H = 16
KVH = 8
HD = 64
EXPERTS = 32
EPSILON = 1e-06
ROPE_BASE = 10000.0
MASKED_SCORE = -1e30
F32 = jnp.float32
B16 = jnp.bfloat16
SWAP = [(0, 1), (1, 0)]
VMEM_LIMIT = 60 * 1024 * 1024


def rms_norm(values, gain_vec):
    return (
        values * lax.rsqrt(jnp.mean(values * values, axis=-1, keepdims=True) + EPSILON) * gain_vec
    )


def rotate(vectors, places):
    half_dim = vectors.shape[-1] // 2
    frequency = jnp.exp(
        jnp.arange(half_dim, dtype=F32) * (-2.0 * math.log(ROPE_BASE) / vectors.shape[-1])
    )
    angles = places[:, None] * frequency[None, :]
    cosine = jnp.cos(angles)[:, None, :]
    sine_vals = jnp.sin(angles)[:, None, :]
    first_half = vectors[..., :half_dim]
    second = vectors[..., half_dim:]
    return jnp.concatenate(
        [first_half * cosine - second * sine_vals, second * cosine + first_half * sine_vals],
        axis=-1,
    )


def swap_core(rows):
    return lax.ppermute(rows, "core", SWAP)


def cyclic(rows, size, shift):
    return lax.ppermute(rows, "z", [(i, (i + shift) % size) for i in range(size)])


def after(value, *others):
    return lax.optimization_barrier((value, *others))[0]


def gather_near(shard):
    return [lax.ppermute(shard, "x", SWAP), lax.ppermute(shard, "y", SWAP)]


def gather_far(near):
    from_x, from_y = near
    half = from_x.shape[0] // 2
    return [lax.ppermute(from_x[:half], "y", SWAP), lax.ppermute(from_y[half:], "x", SWAP)]


def grid_gather(shard):
    near = gather_near(shard)
    return near + gather_far(near)


def cross(to_x, to_y):
    return lax.ppermute(to_x, "x", SWAP), lax.ppermute(to_y, "y", SWAP)


def far_and_next(near, shard):
    from_x, from_y = near
    half = shard.shape[0] // 2
    return cross(
        jnp.concatenate([from_y[-half:], shard], axis=0),
        jnp.concatenate([from_x[-2 * half : -half], shard], axis=0),
    )


def plus_low(a, b):
    return (a.astype(F32) + b.astype(F32)).astype(B16)


def grid_scatter_first(first_a, first_b):
    return lax.ppermute(first_a, "x", SWAP), lax.ppermute(first_b, "y", SWAP)


def grid_scatter_second(got, rest_a, rest_b, *hold):
    got_a, got_b = got
    onward_a = (rest_a[1].astype(F32) + got_a[1].astype(F32)).astype(B16)
    onward_b = (rest_b[1].astype(F32) + got_b[1].astype(F32)).astype(B16)
    last_a = lax.ppermute(onward_a, "y", SWAP)
    last_b = lax.ppermute(onward_b, "x", SWAP)
    last_a, last_b = after((last_a, last_b), *hold)
    return (
        rest_a[0].astype(F32) + got_a[0].astype(F32) + last_a.astype(F32),
        rest_b[0].astype(F32) + got_b[0].astype(F32) + last_b.astype(F32),
    )


def row_halves(parts):
    own, to_x, to_y, diag = [parts[j] for j in range(4)]
    half = own.shape[0] // 2
    first = (
        jnp.stack([to_x[:half], diag[:half]]),
        jnp.stack([to_y[half:], diag[half:]]),
    )
    return first, (own[:half], to_y[:half]), (own[half:], to_x[half:])


def column_pieces(rows, size):
    return [rows] + [cyclic(rows, size, -k) for k in range(1, size)]


def column_low(mine, other):
    both = mine.astype(F32) + swap_core(other).astype(F32)
    return both[0], both.astype(B16)


def column_send(low, size):
    return [cyclic(low[k], size, k) for k in range(1, size)]


def column_sum(own, pieces):
    return own + sum(piece.astype(F32) for piece in pieces)


def assemble(places, shard, moved, other, rows):
    def kernel(places_ref, shard_ref, moved_ref, other_ref, out_ref):
        def put(i, value):
            start = pl.multiple_of(places_ref[i] * rows, rows)
            out_ref[pl.ds(start, value.shape[0]), :] = value

        put(0, shard_ref[...])
        for j in range(3):
            put(1 + j, moved_ref[j * rows : (j + 1) * rows, :])
            put(4 + j, other_ref[j * rows : (j + 1) * rows, :])

    def whole(array_shape):
        return pl.BlockSpec(array_shape, lambda i, places: (0, 0))

    out_rows, cols = 8 * rows, shard.shape[1]
    return pl.pallas_call(
        kernel,
        out_shape=jax.ShapeDtypeStruct((out_rows, cols), shard.dtype),
        grid_spec=pltpu.PrefetchScalarGridSpec(
            num_scalar_prefetch=1,
            grid=(1,),
            in_specs=[whole(a.shape) for a in (shard, moved, other)],
            out_specs=whole((out_rows, cols)),
        ),
        compiler_params=pltpu.CompilerParams(vmem_limit_bytes=VMEM_LIMIT),
        name="assemble",
    )(places, shard, moved, other)


def one_hot_slots(codes, capacity):
    slots = lax.broadcasted_iota(jnp.int32, (capacity, codes.shape[1]), 0).astype(F32)
    return [(slots == codes[e : e + 1, :]).astype(F32) for e in range(codes.shape[0])]


def row_of(table, index):
    at = lax.broadcasted_iota(jnp.int32, table.shape, 0)
    return jnp.sum(jnp.where(at == index, table, 0.0), axis=0, keepdims=True)


def pack_code(code):
    rows = code.shape[0] // 4
    wide = jnp.concatenate([code[c * rows : (c + 1) * rows] for c in range(4)], axis=1)
    return jnp.concatenate([wide, jnp.full((16 - rows, wide.shape[1]), -1.0, B16)], axis=0)


def unpack_code(block, tokens):
    rows = EXPERTS // 4
    wide = block.astype(F32)
    return jnp.concatenate(
        [wide[:rows, c * tokens : (c + 1) * tokens] for c in range(4)], axis=0
    )


def dispatch_rows(lead, packed, rows, router, local, capacity):
    pieces, packed_rows, width = packed.shape
    tokens = packed_rows - 16
    slots = local * capacity
    with_gates = router is not None

    def kernel(lead_ref, packed_ref, *rest):
        first = lead_ref[0]
        if with_gates:
            rows_ref, router_ref, out_ref, gate_out = rest
            table = unpack_code(packed_ref[0], tokens)
            source = rows_ref[0]
        else:
            (out_ref,) = rest
            table = unpack_code(packed_ref[0, tokens:, :], tokens)
            source = packed_ref[0, :tokens, :]
        codes = jnp.concatenate([row_of(table, first + e) for e in range(local)], axis=0)
        picks = one_hot_slots(codes, capacity)
        select = jnp.concatenate([p.astype(B16) for p in picks], axis=0)
        out_ref[0] = jnp.dot(select, source, preferred_element_type=F32).astype(B16)
        if with_gates:
            logits = lax.dot_general(
                router_ref[...], source, (((1,), (1,)), ((), ())), preferred_element_type=F32
            )
            routed = table >= 0.0
            peak = jnp.max(jnp.where(routed, logits, MASKED_SCORE), axis=0, keepdims=True)
            lifted = jnp.where(routed, jnp.exp(jnp.minimum(logits - peak, 0.0)), 0.0)
            gates = lifted / jnp.sum(lifted, axis=0, keepdims=True)
            for e in range(local):
                gate_row = row_of(gates, first + e)
                column = jnp.sum(picks[e] * gate_row, axis=1, keepdims=True)
                gate_out[0, e * capacity : (e + 1) * capacity, :] = jnp.broadcast_to(
                    column, (capacity, 128)
                )

    out_specs = [pl.BlockSpec((1, slots, width), lambda p, lead: (p, 0, 0))]
    out_shape = [jax.ShapeDtypeStruct((pieces, slots, width), B16)]
    args = [packed]
    if with_gates:
        in_specs = [
            pl.BlockSpec((1, 16, width), lambda p, lead: (p, tokens // 16, 0)),
            pl.BlockSpec((1, tokens, width), lambda p, lead: (p, 0, 0)),
            pl.BlockSpec((EXPERTS, width), lambda p, lead: (0, 0)),
        ]
        out_specs.append(pl.BlockSpec((1, slots, 128), lambda p, lead: (p, 0, 0)))
        out_shape.append(jax.ShapeDtypeStruct((pieces, slots, 128), F32))
        args += [rows, router]
    else:
        in_specs = [pl.BlockSpec((1, packed_rows, width), lambda p, lead: (p, 0, 0))]
    return pl.pallas_call(
        kernel,
        out_shape=out_shape,
        grid_spec=pltpu.PrefetchScalarGridSpec(
            num_scalar_prefetch=1, grid=(pieces,), in_specs=in_specs, out_specs=out_specs
        ),
        compiler_params=pltpu.CompilerParams(vmem_limit_bytes=VMEM_LIMIT),
        name="dispatch",
    )(lead, *args)


def combine_rows(lead, first, packed, slot_rows, local, capacity):
    pieces, packed_rows, code_width = packed.shape
    tokens = packed_rows - 16
    halves = len(slot_rows)
    slots, width = slot_rows[0].shape[1:]
    per = local // halves

    def kernel(lead_ref, code_ref, *rest):
        table = unpack_code(code_ref[0], tokens)
        here = lead_ref[0]
        codes = jnp.concatenate([row_of(table, here + e) for e in range(local)], axis=0)
        picks = one_hot_slots(codes, capacity)
        total = None
        for h in range(halves):
            select = jnp.concatenate(
                [p.astype(B16) for p in picks[h * per : (h + 1) * per]], axis=0
            )
            part = lax.dot_general(
                select, rest[h][0], (((0,), (0,)), ((), ())), preferred_element_type=F32
            )
            total = part if total is None else total + part
        rest[halves][0] = total.astype(B16)

    in_specs = [pl.BlockSpec((1, 16, code_width), lambda p, lead: (p, tokens // 16, 0))]
    in_specs += [
        pl.BlockSpec((1, slots, width), lambda p, lead: (p + first, 0, 0)) for _ in range(halves)
    ]
    return pl.pallas_call(
        kernel,
        out_shape=jax.ShapeDtypeStruct((pieces, tokens, width), B16),
        grid_spec=pltpu.PrefetchScalarGridSpec(
            num_scalar_prefetch=1,
            grid=(pieces,),
            in_specs=in_specs,
            out_specs=pl.BlockSpec((1, tokens, width), lambda p, lead: (p, 0, 0)),
        ),
        compiler_params=pltpu.CompilerParams(vmem_limit_bytes=VMEM_LIMIT),
        name="combine",
    )(lead, packed, *slot_rows)


def experts(order, start, count, rows, grads, gates, weights, chunks, capacity, in_rows, mid_rows):
    half, _, width = rows[0].shape
    pieces = 2 * half
    split = bool(chunks)
    n = 4 if split else len(weights)
    extra = [array for chunk in chunks for array, _ in chunk]
    given = len(weights) + len(extra)
    pack_rows, eff = weights[0].shape[1:]
    folds = width // eff
    total_rows = pieces * capacity
    first_half = count // 2
    large = total_rows > 1000

    def kernel(order_ref, *refs):
        rows_a, rows_b, grads_a, grads_b, gates_a, gates_b = refs[:6]
        pack = refs[6 : 6 + given]
        y_out, dx_out = refs[6 + given : 8 + given]
        outs = refs[8 + given : -6]
        full_g, full_u, full_d, grad_g, grad_u, grad_d = refs[-6:]

        def at_in(j):
            return pl.ds(pl.multiple_of(order_ref[j] * in_rows, in_rows), in_rows)

        def at_mid(j):
            return pl.ds(pl.multiple_of(order_ref[j] * mid_rows, mid_rows), mid_rows)

        def load(j, take):
            full_g[at_in(j), :] = take(0, in_rows)
            full_u[at_in(j), :] = take(in_rows, 2 * in_rows)
            for f in range(folds):
                full_d[at_mid(j), f * eff : (f + 1) * eff] = take(
                    2 * in_rows + f * mid_rows, 2 * in_rows + (f + 1) * mid_rows
                )

        def rows_from(ref, offset):
            return lambda lo, hi: ref[offset + lo : offset + hi, :]

        def two_halves(a, b):
            middle = pack_rows // 2

            def take(lo, hi):
                if hi <= middle:
                    return a(lo, hi)
                if lo >= middle:
                    return b(lo - middle, hi - middle)
                return jnp.concatenate([a(lo, middle), b(0, hi - middle)], axis=0)

            return take

        for j in range(len(weights)):
            load(j, lambda lo, hi, ref=pack[j]: ref[0, lo:hi])
        for c in range(len(chunks)):
            from_x, from_y, diag_a, diag_b = [
                rows_from(pack[1 + 4 * c + i], chunks[c][i][1]) for i in range(4)
            ]

            @pl.when(pl.program_id(0) == c)
            def _():
                load(1, from_x)
                load(2, from_y)
                load(3, two_halves(diag_a, diag_b))

        def joined(a, b, w):
            return jnp.concatenate(
                [
                    a[...].reshape(half * capacity, w),
                    b[...].reshape(half * capacity, w),
                ],
                axis=0,
            )

        x = joined(rows_a, rows_b, width)
        g = joined(grads_a, grads_b, width)
        gate = joined(gates_a, gates_b, 128)[:, 0:1]
        nt = (((1,), (1,)), ((), ()))
        tn = (((0,), (0,)), ((), ()))
        gate_proj = jnp.dot(x, full_g[...], preferred_element_type=F32)
        up_proj = jnp.dot(x, full_u[...], preferred_element_type=F32)
        down_grad = lax.dot_general(g, full_d[...], nt, preferred_element_type=F32)
        sigmoid = 1.0 / (1.0 + jnp.exp(-gate_proj))
        silu = gate_proj * sigmoid
        activated = silu * up_proj
        slot_grad = jnp.sum(activated * down_grad, axis=1, keepdims=True)
        here = order_ref[n] + start + pl.program_id(0)
        lane = lax.broadcasted_iota(jnp.int32, (total_rows, 128), 1)
        high = slot_grad.astype(B16).astype(F32)
        tail = jnp.where(lane == here, high, jnp.where(lane == here + EXPERTS, slot_grad - high, 0.0))
        dx_out[:, :, width:] = tail.astype(B16).reshape(pieces, capacity, 128)
        scaled = (gate * activated).astype(B16)
        act_grad = gate * down_grad
        gate_grad = (act_grad * up_proj * (sigmoid * (1.0 + gate_proj * (1.0 - sigmoid)))).astype(
            B16
        )
        up_grad = (act_grad * silu).astype(B16)
        y = jnp.dot(scaled, full_d[...], preferred_element_type=F32)
        y_out[...] = y.astype(B16).reshape(pieces, capacity, width)
        dx = lax.dot_general(gate_grad, full_g[...], nt, preferred_element_type=F32)
        dx = dx + lax.dot_general(up_grad, full_u[...], nt, preferred_element_type=F32)
        dx_out[:, :, :width] = dx.astype(B16).reshape(pieces, capacity, width)
        grad_g[...] = lax.dot_general(x, gate_grad, tn, preferred_element_type=F32).astype(B16)
        grad_u[...] = lax.dot_general(x, up_grad, tn, preferred_element_type=F32).astype(B16)
        grad_d[...] = lax.dot_general(scaled, g, tn, preferred_element_type=F32).astype(B16)

        def give(ref, slot, j):
            ref[slot, 0, :in_rows] = grad_g[at_in(j), :]
            ref[slot, 0, in_rows : 2 * in_rows] = grad_u[at_in(j), :]
            for f in range(folds):
                ref[slot, 0, 2 * in_rows + f * mid_rows : 2 * in_rows + (f + 1) * mid_rows] = grad_d[
                    at_mid(j), f * eff : (f + 1) * eff
                ]

        if split:

            @pl.when(pl.program_id(0) < first_half)
            def _():
                for j in range(4):
                    give(outs[j], 0, j)

            @pl.when(pl.program_id(0) >= first_half)
            def _():
                for j in range(4):
                    give(outs[4 + j], 0, j)
        else:
            for j in range(n):
                give(outs[0], j, j)

    def single():
        return dict(pipeline_mode=pl.Buffered(1)) if large else {}

    def rows_spec(w):
        return pl.BlockSpec((half, capacity, w), lambda e, o: (0, e + start, 0), **single())

    in_specs = [rows_spec(width)] * 4 + [rows_spec(128)] * 2
    for _ in weights:
        in_specs.append(pl.BlockSpec((1, pack_rows, eff), lambda e, o: (e + start, 0, 0)))
    for part in extra:
        in_specs.append(pl.BlockSpec(part.shape, lambda e, o: (0, 0)))
    slots = count * capacity
    out_specs = [
        pl.BlockSpec((pieces, capacity, w), lambda e, o: (0, e, 0), **single())
        for w in (width, width + 128)
    ]
    out_shape = [
        jax.ShapeDtypeStruct((pieces, slots, width), B16),
        jax.ShapeDtypeStruct((pieces, slots, width + 128), B16),
    ]
    if split:
        for at in (
            lambda e, o: (0, jnp.minimum(e, first_half - 1), 0, 0),
            lambda e, o: (0, jnp.maximum(e - first_half, 0), 0, 0),
        ):
            for _ in range(4):
                out_specs.append(pl.BlockSpec((1, 1, pack_rows, eff), at))
                out_shape.append(jax.ShapeDtypeStruct((1, first_half, pack_rows, eff), B16))
    else:
        out_specs.append(pl.BlockSpec((n, 1, pack_rows, eff), lambda e, o: (0, e, 0, 0)))
        out_shape.append(jax.ShapeDtypeStruct((n, count, pack_rows, eff), B16))
    results = pl.pallas_call(
        kernel,
        out_shape=out_shape,
        grid_spec=pltpu.PrefetchScalarGridSpec(
            num_scalar_prefetch=1,
            grid=(count,),
            in_specs=in_specs,
            out_specs=out_specs,
            scratch_shapes=[
                pltpu.VMEM((n * in_rows, eff), B16),
                pltpu.VMEM((n * in_rows, eff), B16),
                pltpu.VMEM((n * mid_rows, width), B16),
                pltpu.VMEM((n * in_rows, eff), B16),
                pltpu.VMEM((n * in_rows, eff), B16),
                pltpu.VMEM((n * mid_rows, width), B16),
            ],
        ),
        compiler_params=pltpu.CompilerParams(vmem_limit_bytes=VMEM_LIMIT),
        name="experts",
    )(order, *rows, *grads, *gates, *weights, *extra)
    return results[0], results[1], results[2:]


NT = (((1,), (1,)), ((), ()))
TN = (((0,), (0,)), ((), ()))
GROUPS = KVH // 2
EXTRA = 128


def turn(vectors, cosine, sine):
    lane = lax.broadcasted_iota(jnp.int32, vectors.shape, 1)
    ahead = pltpu.roll(vectors, 2 * HD - HD // 2, 1)
    behind = pltpu.roll(vectors, HD // 2, 1)
    return vectors * cosine + jnp.where(lane % HD < HD // 2, ahead, behind) * sine


def turn_tables(places):
    lane = jnp.arange(2 * HD, dtype=jnp.int32)
    frequency = jnp.exp(
        (lane % (HD // 2)).astype(F32) * (-2.0 * math.log(ROPE_BASE) / HD)
    )
    angles = places[:, None] * frequency[None, :]
    sign = jnp.where(lane % HD < HD // 2, -1.0, 1.0)
    return jnp.cos(angles), jnp.sin(angles) * sign[None, :]


def attention_forward(x_all, dense_full, bias, cosine, sine, tok_rows):
    seq_len, width = x_all.shape
    scale = HD ** (-0.5)
    wide, narrow = H * HD, KVH * HD

    def kernel(
        x_ref, tail_ref, wo_ref, wq_ref, wk_ref, wv_ref, bias_ref, cos_ref, sin_ref,
        normed_ref, q_out, k_out, v_out, att_out, total_out, misc_out, residual_out, moe_out,
    ):
        step = pl.program_id(0)

        @pl.when(step == 0)
        def _():
            rows = jnp.transpose(tail_ref[...].astype(F32))
            misc_out[...] = rows
            x = x_ref[...].astype(F32)
            scaled = x * lax.rsqrt(jnp.mean(x * x, axis=1, keepdims=True) + EPSILON)
            normed_ref[...] = (scaled * rows[EXPERTS : EXPERTS + 1, :]).astype(B16)
            residual_out[...] = x[:tok_rows]

        normed = normed_ref[...]
        cos, sin = cos_ref[...], sin_ref[...]
        key = turn(jnp.dot(normed, wk_ref[...], preferred_element_type=F32), cos, sin).astype(B16)
        value = jnp.dot(normed, wv_ref[...], preferred_element_type=F32).astype(B16)
        query = jnp.dot(normed[:tok_rows], wq_ref[...], preferred_element_type=F32)
        cos, sin = cos[:tok_rows], sin[:tok_rows]
        query = jnp.concatenate(
            [turn(query[:, 128 * j : 128 * (j + 1)], cos, sin) for j in range(2)], axis=1
        )
        query = (query * scale).astype(B16)
        k_out[...] = key
        v_out[...] = value
        q_out[...] = query
        mixed, totals = [], []
        for j in range(4):
            lanes = slice(HD * (j // 2), HD * (j // 2 + 1))
            scores = lax.dot_general(
                key[:, lanes], query[:, HD * j : HD * (j + 1)], NT, preferred_element_type=F32
            )
            scores = scores + bias_ref[...]
            peak = jnp.max(scores, axis=0, keepdims=True)
            probs = jnp.exp(scores - peak)
            total = jnp.sum(probs, axis=0, keepdims=True)
            out = lax.dot_general(
                value[:, lanes], probs.astype(B16), TN, preferred_element_type=F32
            )
            mixed.append(out / total)
            totals.append(peak + jnp.log(total))
        attended = jnp.transpose(jnp.concatenate(mixed, axis=0)).astype(B16)
        att_out[...] = attended
        total_out[0] = jnp.concatenate(totals + totals, axis=0)
        residual_out[...] += jnp.dot(attended, wo_ref[...], preferred_element_type=F32)

        @pl.when(step == GROUPS - 1)
        def _():
            total = residual_out[...]
            scaled = total * lax.rsqrt(jnp.mean(total * total, axis=1, keepdims=True) + EPSILON)
            moe_out[...] = (scaled * misc_out[EXPERTS + 1 : EXPERTS + 2, :]).astype(B16)

    def fixed(*block):
        return pl.BlockSpec(block, lambda i: (0,) * len(block))

    def columns(rows, cols, lead=0):
        return pl.BlockSpec((rows, cols), lambda i: (0, lead + i))

    return pl.pallas_call(
        kernel,
        grid=(GROUPS,),
        in_specs=[
            fixed(seq_len, width),
            pl.BlockSpec((width, 128), lambda i: (0, (width + wide + 2 * narrow) // 128)),
            pl.BlockSpec((256, width), lambda i: (i, 0)),
            columns(width, 256, width // 256),
            columns(width, 128, (width + wide) // 128),
            columns(width, 128, (width + wide + narrow) // 128),
            fixed(seq_len, tok_rows),
            fixed(seq_len, 128),
            fixed(seq_len, 128),
        ],
        out_specs=[
            fixed(seq_len, width),
            columns(tok_rows, 256),
            columns(seq_len, 128),
            columns(seq_len, 128),
            columns(tok_rows, 256),
            pl.BlockSpec((1, 8, tok_rows), lambda i: (i, 0, 0)),
            fixed(128, width),
            fixed(tok_rows, width),
            fixed(tok_rows, width),
        ],
        out_shape=[
            jax.ShapeDtypeStruct((seq_len, width), B16),
            jax.ShapeDtypeStruct((tok_rows, wide), B16),
            jax.ShapeDtypeStruct((seq_len, narrow), B16),
            jax.ShapeDtypeStruct((seq_len, narrow), B16),
            jax.ShapeDtypeStruct((tok_rows, wide), B16),
            jax.ShapeDtypeStruct((GROUPS, 8, tok_rows), F32),
            jax.ShapeDtypeStruct((128, width), F32),
            jax.ShapeDtypeStruct((tok_rows, width), F32),
            jax.ShapeDtypeStruct((tok_rows, width), B16),
        ],
        compiler_params=pltpu.CompilerParams(vmem_limit_bytes=VMEM_LIMIT),
        name="attention",
    )(x_all, *[dense_full] * 5, bias, cosine, sine)


def attention_backward(
    where_here, out_grad_low, attended, moe_in, logit_low, moe_gain_row, saved,
    x_all, dense_full, bias, cosine, sine,
):
    normed_all, query_rot, key_rot, value_all, totals = saved
    seq_len, width = x_all.shape
    tok_rows = query_rot.shape[0]
    scale = HD ** (-0.5)
    wide, narrow = H * HD, KVH * HD
    block = width // 8
    half = width // 2

    def kernel(
        here_ref, og_ref, wo_ref, att_ref, moe_ref, logit_ref, gain_ref,
        normed_ref, q_ref, k_ref, v_ref, total_ref,
        x_ref, wq_ref, wk_ref, wv_ref, bias_ref, cos_ref, sin_ref,
        first_out, second_out, normed_out, normed_t, grad_sum,
    ):
        step = pl.program_id(0)
        dp, core = here_ref[0], here_ref[1]

        @pl.when(step == 0)
        def _():
            normed_t[...] = jnp.transpose(normed_ref[...])
            grad_sum[...] = jnp.zeros((seq_len, width), F32)

        og = og_ref[...]
        att_grad = lax.dot_general(og, wo_ref[...], NT, preferred_element_type=F32).astype(B16)
        query, key, value = q_ref[...], k_ref[...], v_ref[...]
        query_grads, key_grads, value_grads = [], [], []
        for j in range(4):
            lanes = slice(HD * (j // 2), HD * (j // 2 + 1))
            mine = slice(HD * j, HD * (j + 1))
            scores = lax.dot_general(
                key[:, lanes], query[:, mine], NT, preferred_element_type=F32
            )
            probs = jnp.exp(scores + bias_ref[...] - total_ref[0, j : j + 1, :])
            probs_grad = lax.dot_general(
                value[:, lanes], att_grad[:, mine], NT, preferred_element_type=F32
            )
            delta = jnp.sum(probs * probs_grad, axis=0, keepdims=True)
            score_grad = (probs * (probs_grad - delta)).astype(B16)
            query_grads.append(
                lax.dot_general(key[:, lanes], score_grad, TN, preferred_element_type=F32)
            )
            key_part = jnp.dot(score_grad, query[:, mine], preferred_element_type=F32)
            value_part = jnp.dot(probs.astype(B16), att_grad[:, mine], preferred_element_type=F32)
            if j % 2 == 0:
                key_grads.append(key_part)
                value_grads.append(value_part)
            else:
                key_grads[-1] = key_grads[-1] + key_part
                value_grads[-1] = value_grads[-1] + value_part
        cos, sin = cos_ref[...], -sin_ref[...]
        kv_grad = jnp.concatenate(
            [turn(jnp.concatenate(key_grads, axis=1), cos, sin)] + value_grads, axis=1
        ).astype(B16)
        cos, sin = cos[:tok_rows], sin[:tok_rows]
        query_grad = jnp.transpose(jnp.concatenate(query_grads, axis=0)) * scale
        query_grad = jnp.concatenate(
            [turn(query_grad[:, 128 * j : 128 * (j + 1)], cos, sin) for j in range(2)], axis=1
        ).astype(B16)

        def give(out_ref, grad, lanes):
            for m in range(4):
                for c in range(2):
                    out_ref[core ^ c, dp ^ m, :, lanes] = grad[
                        (2 * m + c) * block : (2 * m + c + 1) * block
                    ].astype(B16)

        lanes = pl.ds(pl.multiple_of(step * 256, 256), 256)
        give(
            first_out,
            jnp.dot(normed_t[:, :tok_rows], query_grad, preferred_element_type=F32),
            lanes,
        )
        give(second_out, jnp.dot(normed_t[...], kv_grad, preferred_element_type=F32), lanes)
        out_part = lax.dot_general(att_ref[...], og, TN, preferred_element_type=F32).astype(B16)
        for c in range(2):
            rows = slice(c * block, (c + 1) * block)
            first_out[core ^ c, dp ^ step, :, wide : wide + half] = out_part[rows, :half]
            second_out[core ^ c, dp ^ step, :, wide : wide + half] = out_part[rows, half:]
        kv_weights = jnp.concatenate([wk_ref[...], wv_ref[...]], axis=1)
        grad_sum[...] += lax.dot_general(kv_grad, kv_weights, NT, preferred_element_type=F32)
        grad_sum[:tok_rows, :] += lax.dot_general(
            query_grad, wq_ref[...], NT, preferred_element_type=F32
        )

        @pl.when(step == GROUPS - 1)
        def _():
            total = grad_sum[...]
            normed_out[...] = total.astype(B16)
            x = x_ref[...].astype(F32)
            lifted = x * lax.rsqrt(jnp.mean(x * x, axis=1, keepdims=True) + EPSILON)
            gain = jnp.sum(total * lifted, axis=0, keepdims=True)
            row = lax.broadcasted_iota(jnp.int32, (EXTRA, width), 0)
            gains = jnp.where(
                row == EXPERTS, gain, jnp.where(row == EXPERTS + 1, gain_ref[...], 0.0)
            )
            extra = lax.dot_general(
                moe_ref[...], logit_ref[...], TN, preferred_element_type=F32
            ) + jnp.transpose(gains)
            give(first_out, extra, slice(wide + half, wide + half + EXTRA))

    def fixed(*shape):
        return pl.BlockSpec(shape, lambda i, here: (0,) * len(shape))

    def columns(rows, cols, lead=0):
        return pl.BlockSpec((rows, cols), lambda i, here: (0, lead + i))

    shapes = [
        jax.ShapeDtypeStruct((2, 4, block, wide + half + EXTRA), B16),
        jax.ShapeDtypeStruct((2, 4, block, 2 * narrow + half), B16),
        jax.ShapeDtypeStruct((seq_len, width), B16),
    ]
    return pl.pallas_call(
        kernel,
        out_shape=shapes,
        grid_spec=pltpu.PrefetchScalarGridSpec(
            num_scalar_prefetch=1,
            grid=(GROUPS,),
            in_specs=[
                fixed(tok_rows, width),
                pl.BlockSpec((256, width), lambda i, here: (i, 0)),
                columns(tok_rows, 256),
                fixed(tok_rows, width),
                fixed(tok_rows, EXTRA),
                fixed(1, width),
                fixed(seq_len, width),
                columns(tok_rows, 256),
                columns(seq_len, 128),
                columns(seq_len, 128),
                pl.BlockSpec((1, 8, tok_rows), lambda i, here: (i, 0, 0)),
                fixed(seq_len, width),
                columns(width, 256, width // 256),
                columns(width, 128, (width + wide) // 128),
                columns(width, 128, (width + wide + narrow) // 128),
                fixed(seq_len, tok_rows),
                fixed(seq_len, 128),
                fixed(seq_len, 128),
            ],
            out_specs=[fixed(*shape.shape) for shape in shapes],
            scratch_shapes=[
                pltpu.VMEM((width, seq_len), B16),
                pltpu.VMEM((seq_len, width), F32),
            ],
        ),
        compiler_params=pltpu.CompilerParams(vmem_limit_bytes=VMEM_LIMIT),
        name="attention_grad",
    )(
        where_here, out_grad_low, dense_full, attended, moe_in, logit_low, moe_gain_row,
        normed_all, query_rot, key_rot, value_all, totals,
        x_all, dense_full, dense_full, dense_full, bias, cosine, sine,
    )


def make_body(z_size, small_grid):
    def core_half(shard, core):
        rows = shard.shape[0] // 2
        return lax.dynamic_slice_in_dim(shard, core * rows, rows, 0)

    def dense_assemble(shard, parts, dp_index, core, *hold):
        rows = shard.shape[0] // 2
        moved = after(jnp.concatenate(parts, axis=0), *hold)
        other = swap_core(moved)
        places = [2 * dp_index]
        for which in (core, 1 - core):
            places += [2 * (dp_index ^ (j + 1)) + which for j in range(3)]
        return assemble(jnp.stack(places), shard, moved, other, rows)

    def across_z(mine, z):
        if z_size != 4:
            return lax.psum(mine.astype(F32), "z")
        rows = mine.shape[0] // z_size
        low = mine.astype(B16)
        total = lax.dynamic_slice_in_dim(mine, z * rows, rows, 0)
        for k in range(1, z_size):
            theirs = lax.dynamic_slice_in_dim(low, (z + k) % z_size * rows, rows, 0)
            total = total + cyclic(theirs, z_size, k).astype(F32)
        total = total.astype(B16)
        quarters = [total] + [cyclic(total, z_size, -k) for k in range(1, z_size)]
        places = (jnp.arange(z_size, dtype=jnp.int32) - z) % z_size
        return jnp.take(jnp.stack(quarters), places, axis=0).reshape(mine.shape).astype(F32)

    def core_sum(blocks):
        return (blocks[0].astype(F32) + swap_core(blocks[1]).astype(F32)).astype(B16)

    def dense_finish(halves, z, core):
        low = across_z(jnp.concatenate(halves, axis=0), z).astype(B16)
        other = swap_core(low)
        first = jnp.where(core == 0, low, other)
        second = jnp.where(core == 0, other, low)
        return jnp.concatenate([first, second], axis=0).astype(F32)

    def dense_sum(grads):
        return lax.psum_scatter(
            lax.psum(grads, ("z", "core")), ("y", "x"), scatter_dimension=0, tiled=True
        )

    def body(
        layer_input,
        attn_gain,
        w_query,
        w_key,
        w_value,
        w_output,
        moe_gain,
        w_router,
        w_gate,
        w_up,
        w_down,
        routes,
        priority,
        prefix_len,
        out_grad,
    ):
        tok_rows, model_width = layer_input.shape
        dp_size = lax.axis_size("y") * lax.axis_size("x")
        dp_index = lax.axis_index("y") * lax.axis_size("x") + lax.axis_index("x")
        z = lax.axis_index("z")
        core = lax.axis_index("core")
        seq_len = tok_rows * dp_size
        top_count = routes.shape[1]
        local = w_gate.shape[0]
        capacity = 5 * tok_rows * top_count // (4 * EXPERTS)
        group_size = H // KVH
        score_scale = HD ** (-0.5)

        gains = jnp.stack([attn_gain, moe_gain], axis=1)
        rows = w_query.shape[0]
        dense_pack = jnp.concatenate(
            [w_output, w_query, w_key, w_value, w_router, gains, jnp.zeros((rows, 94), B16)], axis=1
        )
        wide = H * HD
        narrow = KVH * HD
        expert_ids = jnp.arange(EXPERTS, dtype=jnp.int32)
        hits = routes[:, :, None] == expert_ids[None, None, :]
        routed = jnp.any(hits, axis=1)
        place = jnp.where(
            routed, jnp.sum(jnp.where(hits, priority[:, :, None], 0), axis=1), jnp.int32(1 << 20)
        )
        ranks = jnp.sum((place[:, :, None] < place.T[None, :, :]).astype(F32), axis=0)
        code = pack_code(jnp.where(routed.T, ranks, -1.0).astype(B16))
        lead = ((2 * z + core) * local).astype(jnp.int32)[None]
        grad_pieces = column_pieces(jnp.concatenate([out_grad, code], axis=0), z_size)

        if small_grid:
            side = tok_rows // 2
            x_pack = jnp.concatenate([layer_input[:side], layer_input[side:]], axis=1)
            start_parts = grid_gather(jnp.concatenate([x_pack, core_half(dense_pack, core)], axis=1))
            dense_parts = [part[:, 2 * model_width :] for part in start_parts]
            from_x, from_y, diag_a, diag_b = [
                [part[:, :model_width], part[:, model_width : 2 * model_width]]
                for part in start_parts
            ]
            x_all = jnp.concatenate(
                [layer_input, *from_x, *from_y, diag_a[0], diag_b[0], diag_a[1], diag_b[1]], axis=0
            )
            dense_full = dense_assemble(dense_pack, dense_parts, dp_index, core, grad_pieces[1])
        else:
            dense_full = lax.all_gather(dense_pack, ("y", "x"), axis=0, tiled=True)
            full_output = dense_full[:, :model_width]
            head_full = dense_full[:, model_width:]
            full_query = head_full[:, :wide]
            full_key = head_full[:, wide : wide + narrow]
            full_value = head_full[:, wide + narrow : wide + 2 * narrow]

        query_pos = dp_index * tok_rows + jnp.arange(tok_rows, dtype=jnp.int32)
        in_float = layer_input.astype(F32)
        steps = jnp.arange(tok_rows, dtype=jnp.int32)
        eff = w_gate.shape[2]
        in_rows, mid_rows = w_gate.shape[1], w_down.shape[1]
        folds = [w_down[:, :, f * eff : (f + 1) * eff] for f in range(model_width // eff)]
        pack = jnp.concatenate([w_gate, w_up, *folds], axis=1)
        if small_grid:
            relative = dp_index ^ jnp.arange(4, dtype=jnp.int32)
            key_pos = (relative[:, None] * tok_rows + steps[None, :]).reshape(seq_len)
            halves, per = 2, local // 2
            weights = [pack]
            near_0 = gather_near(after(pack[0], *start_parts[2:]))
            far_0 = gather_far(after(near_0, dense_full))
            near_1 = gather_near(after(pack[1], *near_0, dense_full))
        else:
            relative = jnp.arange(dp_size, dtype=jnp.int32)
            key_pos = jnp.arange(seq_len, dtype=jnp.int32)
            halves, per = 1, local
            every = lax.all_gather(pack, ("y", "x"), axis=0, tiled=False)
            weights = [every[j] for j in range(dp_size)]
            near_0 = ()
        order = jnp.concatenate([relative, lead])
        grads_mine = jnp.stack(after(grad_pieces, *near_0))
        grads_other = swap_core(grads_mine)
        visible = (key_pos[None, :] <= query_pos[:, None]) | (key_pos[None, :] < prefix_len[0])
        chunks = []
        if small_grid:
            x_all = after(x_all, grads_mine, *near_0)
            bias = jnp.where(visible.T, 0.0, MASKED_SCORE)
            cosine, sine = turn_tables(key_pos.astype(F32))
            (
                normed_all, query_rot, key_rot, value_all, attended, totals, misc, residual, moe_in,
            ) = attention_forward(x_all, dense_full, bias, cosine, sine, tok_rows)
            moe_in = after(moe_in, grads_other, *near_1, *far_0)
            router_rows = misc[:EXPERTS].astype(B16)
            full_attn_gain = misc[EXPERTS]
            full_moe_gain = misc[EXPERTS + 1]
        else:
            places = query_pos.astype(F32)
            router_rows = head_full[:, wide + 2 * narrow : wide + 2 * narrow + EXPERTS].T
            full_attn_gain = head_full[:, wide + 2 * narrow + EXPERTS].astype(F32)
            full_moe_gain = head_full[:, wide + 2 * narrow + EXPERTS + 1].astype(F32)
            normed = rms_norm(in_float, full_attn_gain).astype(B16)
            query_lin = jnp.dot(normed, full_query, preferred_element_type=F32)
            key_lin = jnp.dot(normed, full_key, preferred_element_type=F32)
            value_low = jnp.dot(normed, full_value, preferred_element_type=F32).astype(B16)
            query_rot = (rotate(query_lin.reshape(tok_rows, H, HD), places) * score_scale).astype(B16)
            key_rot = rotate(key_lin.reshape(tok_rows, KVH, HD), places).astype(B16)
            key_rot = key_rot.reshape(tok_rows, narrow)
            both = jnp.concatenate([key_rot, value_low], axis=1)
            both_all = lax.all_gather(both, ("y", "x"), axis=0, tiled=True)
            key_all = both_all[:, :narrow]
            value_all = both_all[:, narrow:]

            def head_scores(head_idx):
                query_head = query_rot[:, head_idx * group_size : (head_idx + 1) * group_size, :]
                key_head = key_all[:, head_idx * HD : (head_idx + 1) * HD]
                scores = jnp.einsum("qgd,kd->gqk", query_head, key_head, preferred_element_type=F32)
                return jnp.where(visible[None, :, :], scores, MASKED_SCORE)

            mixed_heads = []
            log_totals = []
            for head_idx in range(KVH):
                scores = head_scores(head_idx)
                row_max = jnp.max(scores, axis=-1, keepdims=True)
                log_total = row_max + jnp.log(
                    jnp.sum(jnp.exp(scores - row_max), axis=-1, keepdims=True)
                )
                probs_low = jnp.exp(scores - log_total).astype(B16)
                value_head = value_all[:, head_idx * HD : (head_idx + 1) * HD]
                mixed_heads.append(
                    jnp.einsum("gqk,kd->qgd", probs_low, value_head, preferred_element_type=F32)
                )
                log_totals.append(log_total)
            attended = jnp.concatenate(mixed_heads, axis=1).reshape(tok_rows, wide).astype(B16)
            residual = in_float + jnp.dot(attended, full_output, preferred_element_type=F32)
            moe_in = rms_norm(residual, full_moe_gain).astype(B16)

        row_pieces = column_pieces(moe_in, z_size)
        stage_1 = stage_2 = last_far = ()
        if small_grid:
            middle = pack.shape[1] // 2
            stage_1 = far_and_next(after(near_1, moe_in), pack[2])
        (slot_grads_mine,) = dispatch_rows(lead, after(grads_mine, moe_in), None, None, local, capacity)
        (slot_grads_other,) = dispatch_rows(
            lead, after(grads_other, slot_grads_mine, *stage_1), None, None, local, capacity
        )
        if small_grid:
            stage_2 = far_and_next(after(stage_1, slot_grads_other), pack[3])
            last_far = gather_far([part[middle:] for part in stage_2])
            chunks = [
                [(part, 0) for part in [*near_0, *far_0]],
                [(part, 0) for part in [*near_1, *stage_1[::-1]]],
                [(part, middle) for part in stage_1] + [(part, 0) for part in stage_2[::-1]],
                [(part, middle) for part in stage_2] + [(part, 0) for part in last_far],
            ]
        rows_mine = jnp.stack(after(row_pieces, slot_grads_other, *stage_1))
        rows_other = swap_core(rows_mine)
        slot_rows_mine, slot_gates_mine = dispatch_rows(
            lead, grads_mine, after(rows_mine, *stage_2), router_rows, local, capacity
        )
        slot_rows_other, slot_gates_other = dispatch_rows(
            lead, grads_other, after(rows_other, slot_rows_mine), router_rows, local, capacity
        )
        slot_rows_other = after(slot_rows_other, *last_far)
        logits = lax.dot_general(moe_in, router_rows, NT, preferred_element_type=F32)
        peak = jnp.max(jnp.where(routed, logits, MASKED_SCORE), axis=-1, keepdims=True)
        lifted = jnp.where(routed, jnp.exp(jnp.minimum(logits - peak, 0.0)), 0.0)
        gate_weights = lifted / jnp.sum(lifted, axis=-1, keepdims=True)
        ys, dxs, weight_grads, sums = [], [], [], []
        for half in range(halves):
            y, dx, grads = experts(
                order,
                half * per,
                per,
                (slot_rows_mine, slot_rows_other),
                (slot_grads_mine, slot_grads_other),
                (slot_gates_mine, slot_gates_other),
                weights,
                chunks[half * per : (half + 1) * per],
                capacity,
                in_rows,
                mid_rows,
            )
            ys.append(y)
            dxs.append(dx)
            weight_grads.append(grads)

        def grid_sum(grads, got):
            totals = []
            for half in range(2):
                own = grads[4 * half][0]
                direct, last = got[half][0], got[1 - half][1]
                totals.append(own.astype(F32) + direct.astype(F32) + last.astype(F32))
            return totals

        def second_step(grads, via, *more):
            _, x_a, y_a, _, _, x_b, y_b, _ = grads
            to_x = [x_a, plus_low(x_b, via[1])]
            to_y = [y_b, plus_low(y_a, via[0])]
            if more:
                to_x.append(more[0])
                to_y.append(more[1])
            return cross(jnp.concatenate(to_x, axis=0), jnp.concatenate(to_y, axis=0))

        if small_grid:
            early, late = weight_grads
            via = cross(early[3], early[7])
            dxs = after(dxs, *via)
            early_got = second_step(early, via, late[3], late[7])
        dx_other = combine_rows(lead, z_size, grads_other, dxs, local, capacity)
        dx_mine = combine_rows(lead, 0, grads_mine, dxs, local, capacity)
        dx_own, dx_low = column_low(dx_mine, dx_other)
        dx_pieces = column_send(dx_low, z_size)
        ys = after(ys, dx_low)
        y_other = combine_rows(lead, z_size, grads_other, ys, local, capacity)
        y_mine = combine_rows(lead, 0, grads_mine, ys, local, capacity)
        moe_sum = column_sum(dx_own, after(dx_pieces, y_other, y_mine))
        y_own, y_low = column_low(y_mine, after(y_other, moe_sum))
        y_pieces = [cyclic(y_low[k], z_size, k) for k in range(1, z_size) if 2 * k != z_size]
        if small_grid:
            late_got = second_step(late, [got[2:3] for got in after(early_got, moe_sum)])
        moe_in_grad = moe_sum[:, :model_width]
        gate_grad = (
            moe_sum[:, model_width : model_width + EXPERTS]
            + moe_sum[:, model_width + EXPERTS : model_width + 2 * EXPERTS]
        )
        grad_out = out_grad.astype(F32)
        centre = jnp.sum(gate_weights * gate_grad, axis=-1, keepdims=True)
        logit_low = (gate_weights * (gate_grad - centre)).astype(B16)
        moe_in_grad = moe_in_grad + jnp.dot(logit_low, router_rows, preferred_element_type=F32)
        norm_value, second_pull = jax.vjp(rms_norm, residual, full_moe_gain)
        resid_norm_grad, moe_gain_grad = second_pull(moe_in_grad)
        residual_grad = grad_out + resid_norm_grad
        attn_out_grad = residual_grad.astype(B16)
        if small_grid:
            logit_wide = jnp.pad(logit_low, ((0, 0), (0, EXTRA - EXPERTS)))
            first_blocks, second_blocks, normed_part = attention_backward(
                jnp.stack([dp_index, core]).astype(jnp.int32),
                after(attn_out_grad, y_low),
                attended,
                moe_in,
                logit_wide,
                moe_gain_grad[None, :],
                (normed_all, query_rot, key_rot, value_all, totals),
                x_all,
                dense_full,
                bias,
                cosine,
                sine,
            )
            y_pieces, late_got = after((y_pieces, late_got), normed_part)
            y_pieces.append(cyclic(after(y_low[z_size // 2], *y_pieces), z_size, z_size // 2))
            normed_first, normed_a, normed_b = row_halves(
                normed_part.reshape(4, tok_rows, model_width)
            )
            second_first, second_a, second_b = row_halves(core_sum(second_blocks))
            first_first, first_a, first_b = row_halves(core_sum(first_blocks))
            normed_got = grid_scatter_first(*normed_first)
            second_got = grid_scatter_first(*after(second_first, *normed_got))
            first_got = grid_scatter_first(*after(first_first, *second_got))
            second_sum = dense_finish(grid_scatter_second(second_got, second_a, second_b, *first_got), z, core)
            first_sum = dense_finish(grid_scatter_second(first_got, first_a, first_b), z, core)
            normed_grad = jnp.concatenate(
                grid_scatter_second(normed_got, normed_a, normed_b, *first_got), axis=0
            )
            first_value, first_pull = jax.vjp(lambda v: rms_norm(v, full_attn_gain), in_float)
            input_grad = residual_grad + first_pull(normed_grad)[0]
            y_pieces = after(y_pieces, second_sum)
            at = wide + model_width // 2
            query_sum = first_sum[:, :wide]
            output_sum = jnp.concatenate(
                [first_sum[:, wide:at], second_sum[:, 2 * narrow :]], axis=1
            )
            router_sum = first_sum[:, at : at + EXPERTS]
            attn_gain_sum = first_sum[:, at + EXPERTS]
            moe_gain_sum = first_sum[:, at + EXPERTS + 1]
            key_sum, value_sum = [
                jnp.concatenate(
                    [
                        second_sum[:, 256 * i + lead_col : 256 * i + lead_col + 128]
                        for i in range(GROUPS)
                    ],
                    axis=1,
                )
                for lead_col in (0, 128)
            ]
        else:
            router_grad = jnp.einsum("td,te->de", moe_in, logit_low, preferred_element_type=F32)
            wout_grad = jnp.einsum("tc,td->cd", attended, attn_out_grad, preferred_element_type=F32)
            attended_grad = (
                jnp.einsum("td,cd->tc", attn_out_grad, full_output, preferred_element_type=F32)
                .astype(B16)
                .reshape(tok_rows, H, HD)
            )
            query_grads = []
            key_parts = []
            value_parts = []
            for head_idx in range(KVH):
                scores = head_scores(head_idx)
                attention_probs = jnp.exp(scores - log_totals[head_idx])
                probs_low = attention_probs.astype(B16)
                grad_head = attended_grad[:, head_idx * group_size : (head_idx + 1) * group_size, :]
                query_head = query_rot[:, head_idx * group_size : (head_idx + 1) * group_size, :]
                key_head = key_all[:, head_idx * HD : (head_idx + 1) * HD]
                value_head = value_all[:, head_idx * HD : (head_idx + 1) * HD]
                probs_grad = jnp.einsum("qgd,kd->gqk", grad_head, value_head, preferred_element_type=F32)
                row_delta = jnp.sum(attention_probs * probs_grad, axis=-1, keepdims=True)
                score_grad = (attention_probs * (probs_grad - row_delta)).astype(B16)
                query_grads.append(
                    jnp.einsum("gqk,kd->qgd", score_grad, key_head, preferred_element_type=F32)
                )
                key_parts.append(
                    jnp.einsum("gqk,qgd->kd", score_grad, query_head, preferred_element_type=F32)
                )
                value_parts.append(
                    jnp.einsum("gqk,qgd->kd", probs_low, grad_head, preferred_element_type=F32)
                )
            both_part = jnp.concatenate(key_parts + value_parts, axis=1)
            both_sum = lax.psum_scatter(both_part, ("y", "x"), scatter_dimension=0, tiled=True)
            query_rot_grad = jnp.concatenate(query_grads, axis=1) * score_scale
            key_rot_grad = both_sum[:, :narrow].reshape(tok_rows, KVH, HD)
            value_grad = both_sum[:, narrow:].astype(B16)
            query_grad = rotate(query_rot_grad, -places).reshape(tok_rows, wide).astype(B16)
            key_grad = rotate(key_rot_grad, -places).reshape(tok_rows, narrow).astype(B16)
            wq_grad = jnp.einsum("td,tc->dc", normed, query_grad, preferred_element_type=F32)
            wk_grad = jnp.einsum("td,tc->dc", normed, key_grad, preferred_element_type=F32)
            wv_grad = jnp.einsum("td,tc->dc", normed, value_grad, preferred_element_type=F32)
            normed_grad = jnp.einsum("tc,dc->td", query_grad, full_query, preferred_element_type=F32)
            normed_grad = normed_grad + jnp.einsum(
                "tc,dc->td", key_grad, full_key, preferred_element_type=F32
            )
            normed_grad = normed_grad + jnp.einsum(
                "tc,dc->td", value_grad, full_value, preferred_element_type=F32
            )
            first_value, first_pull = jax.vjp(rms_norm, in_float, full_attn_gain)
            input_norm_grad, attn_gain_grad = first_pull(normed_grad)
            input_grad = residual_grad + input_norm_grad
            y_pieces.append(cyclic(y_low[z_size // 2], z_size, z_size // 2))
            query_sum = dense_sum(wq_grad)
            key_sum = dense_sum(wk_grad)
            value_sum = dense_sum(wv_grad)
            output_sum = dense_sum(wout_grad)
            extra_sum = dense_sum(
                jnp.concatenate(
                    [
                        router_grad,
                        attn_gain_grad[:, None],
                        moe_gain_grad[:, None],
                        jnp.zeros((model_width, EXTRA - EXPERTS - 2), F32),
                    ],
                    axis=1,
                )
            )
            router_sum = extra_sum[:, :EXPERTS]
            attn_gain_sum = extra_sum[:, EXPERTS]
            moe_gain_sum = extra_sum[:, EXPERTS + 1]
        layer_output = (residual + column_sum(y_own, y_pieces)).astype(B16)
        if small_grid:
            parts = grid_sum(early, early_got) + grid_sum(late, late_got)
            pack_grad = jnp.concatenate(parts, axis=0)
        else:
            pack_grad = lax.psum_scatter(
                weight_grads[0][0].astype(F32), ("y", "x"), scatter_dimension=0, tiled=False
            )
        down = 2 * in_rows
        expert_grads = [
            pack_grad[:, :in_rows],
            pack_grad[:, in_rows:down],
            jnp.concatenate(
                [
                    pack_grad[:, down + f * mid_rows : down + (f + 1) * mid_rows]
                    for f in range(model_width // eff)
                ],
                axis=2,
            ),
        ]

        return (
            layer_output,
            input_grad,
            attn_gain_sum,
            query_sum,
            key_sum,
            value_sum,
            output_sum,
            moe_gain_sum,
            router_sum,
            expert_grads[0],
            expert_grads[1],
            expert_grads[2],
        )

    return body


def solution(mesh):
    groups = mesh.shape["expert"]
    members = mesh.shape["dp"]
    z_size = groups // 2
    side = math.isqrt(members)
    grid = Mesh(
        mesh.devices.reshape(z_size, 2, members // side, side), ("z", "core", "y", "x")
    )
    expert = ("z", "core")
    dp = ("y", "x")
    every = expert + dp
    placed = (
        P(every, None),
        P(dp),
        P(dp, None),
        P(dp, None),
        P(dp, None),
        P(dp, None),
        P(dp),
        P(dp, None),
        P(expert, dp, None),
        P(expert, dp, None),
        P(expert, dp, None),
        P(every, None),
        P(every, None),
        P(expert),
        P(every, None),
    )
    return jax.shard_map(
        make_body(z_size, members == 4 and side == 2 and EXPERTS == 4 * groups),
        mesh=grid,
        in_specs=placed,
        out_specs=(
            P(every, None),
            P(every, None),
            P(dp),
            P(dp, None),
            P(dp, None),
            P(dp, None),
            P(dp, None),
            P(dp),
            P(dp, None),
            P(expert, dp, None),
            P(expert, dp, None),
            P(expert, dp, None),
        ),
        check_vma=False,
    )
```

```python
import math

import jax
import jax.numpy as jnp
from jax import lax
from jax.experimental import pallas as pl
from jax.experimental.pallas import tpu as pltpu
from jax.sharding import Mesh
from jax.sharding import PartitionSpec as P

H = 16
KVH = 8
HD = 64
EXPERTS = 32
EPSILON = 1e-06
ROPE_BASE = 10000.0
MASKED_SCORE = -1e30
F32 = jnp.float32
B16 = jnp.bfloat16
SWAP = [(0, 1), (1, 0)]
VMEM_LIMIT = 60 * 1024 * 1024


def rms_norm(values, gain_vec):
    return (
        values * lax.rsqrt(jnp.mean(values * values, axis=-1, keepdims=True) + EPSILON) * gain_vec
    )


def rotate(vectors, places):
    half_dim = vectors.shape[-1] // 2
    frequency = jnp.exp(
        jnp.arange(half_dim, dtype=F32) * (-2.0 * math.log(ROPE_BASE) / vectors.shape[-1])
    )
    angles = places[:, None] * frequency[None, :]
    cosine = jnp.cos(angles)[:, None, :]
    sine_vals = jnp.sin(angles)[:, None, :]
    first_half = vectors[..., :half_dim]
    second = vectors[..., half_dim:]
    return jnp.concatenate(
        [first_half * cosine - second * sine_vals, second * cosine + first_half * sine_vals],
        axis=-1,
    )


def swap_core(rows):
    return lax.ppermute(rows, "core", SWAP)


def cyclic(rows, size, shift):
    return lax.ppermute(rows, "z", [(i, (i + shift) % size) for i in range(size)])


def after(value, *others):
    return lax.optimization_barrier((value, *others))[0]


def gather_near(shard):
    return [lax.ppermute(shard, "x", SWAP), lax.ppermute(shard, "y", SWAP)]


def gather_far(near):
    from_x, from_y = near
    half = from_x.shape[0] // 2
    return [lax.ppermute(from_x[:half], "y", SWAP), lax.ppermute(from_y[half:], "x", SWAP)]


def grid_gather(shard):
    near = gather_near(shard)
    return near + gather_far(near)


def cross(to_x, to_y):
    return lax.ppermute(to_x, "x", SWAP), lax.ppermute(to_y, "y", SWAP)


def far_and_next(near, shard):
    from_x, from_y = near
    half = shard.shape[0] // 2
    return cross(
        jnp.concatenate([from_y[-half:], shard], axis=0),
        jnp.concatenate([from_x[-2 * half : -half], shard], axis=0),
    )


def plus_low(a, b):
    return (a.astype(F32) + b.astype(F32)).astype(B16)


def grid_scatter_first(first_a, first_b):
    return lax.ppermute(first_a, "x", SWAP), lax.ppermute(first_b, "y", SWAP)


def grid_scatter_second(got, rest_a, rest_b, *hold):
    got_a, got_b = got
    onward_a = (rest_a[1].astype(F32) + got_a[1].astype(F32)).astype(B16)
    onward_b = (rest_b[1].astype(F32) + got_b[1].astype(F32)).astype(B16)
    last_a = lax.ppermute(onward_a, "y", SWAP)
    last_b = lax.ppermute(onward_b, "x", SWAP)
    last_a, last_b = after((last_a, last_b), *hold)
    return (
        rest_a[0].astype(F32) + got_a[0].astype(F32) + last_a.astype(F32),
        rest_b[0].astype(F32) + got_b[0].astype(F32) + last_b.astype(F32),
    )


def row_halves(parts):
    own, to_x, to_y, diag = [parts[j] for j in range(4)]
    half = own.shape[0] // 2
    first = (
        jnp.stack([to_x[:half], diag[:half]]),
        jnp.stack([to_y[half:], diag[half:]]),
    )
    return first, (own[:half], to_y[:half]), (own[half:], to_x[half:])


def column_pieces(rows, size):
    return [rows] + [cyclic(rows, size, -k) for k in range(1, size)]


def column_send_some(low, size):
    return [cyclic(low[k], size, k) for k in range(1, size) if 2 * k != size]


def column_send_last(low, size, *hold):
    return [cyclic(after(low[size // 2], *hold), size, size // 2)]


def column_sum(own, pieces):
    return own.astype(F32) + sum(piece.astype(F32) for piece in pieces)


def assemble(places, shard, moved, other, rows):
    def kernel(places_ref, shard_ref, moved_ref, other_ref, out_ref):
        def put(i, value):
            start = pl.multiple_of(places_ref[i] * rows, rows)
            out_ref[pl.ds(start, value.shape[0]), :] = value

        put(0, shard_ref[...])
        for j in range(3):
            put(1 + j, moved_ref[j * rows : (j + 1) * rows, :])
            put(4 + j, other_ref[j * rows : (j + 1) * rows, :])

    def whole(array_shape):
        return pl.BlockSpec(array_shape, lambda i, places: (0, 0))

    out_rows, cols = 8 * rows, shard.shape[1]
    return pl.pallas_call(
        kernel,
        out_shape=jax.ShapeDtypeStruct((out_rows, cols), shard.dtype),
        grid_spec=pltpu.PrefetchScalarGridSpec(
            num_scalar_prefetch=1,
            grid=(1,),
            in_specs=[whole(a.shape) for a in (shard, moved, other)],
            out_specs=whole((out_rows, cols)),
        ),
        compiler_params=pltpu.CompilerParams(vmem_limit_bytes=VMEM_LIMIT),
        name="assemble",
    )(places, shard, moved, other)


def one_hot_slots(codes, capacity):
    slots = lax.broadcasted_iota(jnp.int32, (capacity, codes.shape[1]), 0).astype(F32)
    return [(slots == codes[e : e + 1, :]).astype(F32) for e in range(codes.shape[0])]


def row_of(table, index):
    at = lax.broadcasted_iota(jnp.int32, table.shape, 0)
    return jnp.sum(jnp.where(at == index, table, 0.0), axis=0, keepdims=True)


def pack_code(code):
    rows = code.shape[0] // 4
    wide = jnp.concatenate([code[c * rows : (c + 1) * rows] for c in range(4)], axis=1)
    return jnp.concatenate([wide, jnp.full((16 - rows, wide.shape[1]), -1.0, B16)], axis=0)


def unpack_code(block, tokens):
    rows = EXPERTS // 4
    wide = block.astype(F32)
    return jnp.concatenate(
        [wide[:rows, c * tokens : (c + 1) * tokens] for c in range(4)], axis=0
    )


def dispatch_rows(lead, packed, rows, router, local, capacity):
    pieces, packed_rows, width = packed.shape
    tokens = packed_rows - 16
    slots = local * capacity
    with_gates = router is not None

    def kernel(lead_ref, packed_ref, *rest):
        first = lead_ref[0]
        if with_gates:
            rows_ref, router_ref, out_ref, gate_out = rest
            table = unpack_code(packed_ref[0], tokens)
            source = rows_ref[0]
        else:
            (out_ref,) = rest
            table = unpack_code(packed_ref[0, tokens:, :], tokens)
            source = packed_ref[0, :tokens, :]
        codes = jnp.concatenate([row_of(table, first + e) for e in range(local)], axis=0)
        picks = one_hot_slots(codes, capacity)
        select = jnp.concatenate([p.astype(B16) for p in picks], axis=0)
        out_ref[0] = jnp.dot(select, source, preferred_element_type=F32).astype(B16)
        if with_gates:
            logits = lax.dot_general(
                router_ref[...], source, (((1,), (1,)), ((), ())), preferred_element_type=F32
            )
            routed = table >= 0.0
            peak = jnp.max(jnp.where(routed, logits, MASKED_SCORE), axis=0, keepdims=True)
            lifted = jnp.where(routed, jnp.exp(jnp.minimum(logits - peak, 0.0)), 0.0)
            gates = lifted / jnp.sum(lifted, axis=0, keepdims=True)
            for e in range(local):
                gate_row = row_of(gates, first + e)
                column = jnp.sum(picks[e] * gate_row, axis=1, keepdims=True)
                gate_out[0, e * capacity : (e + 1) * capacity, :] = jnp.broadcast_to(
                    column, (capacity, 128)
                )

    out_specs = [pl.BlockSpec((1, slots, width), lambda p, lead: (p, 0, 0))]
    out_shape = [jax.ShapeDtypeStruct((pieces, slots, width), B16)]
    args = [packed]
    if with_gates:
        in_specs = [
            pl.BlockSpec((1, 16, width), lambda p, lead: (p, tokens // 16, 0)),
            pl.BlockSpec((1, tokens, width), lambda p, lead: (p, 0, 0)),
            pl.BlockSpec((EXPERTS, width), lambda p, lead: (0, 0)),
        ]
        out_specs.append(pl.BlockSpec((1, slots, 128), lambda p, lead: (p, 0, 0)))
        out_shape.append(jax.ShapeDtypeStruct((pieces, slots, 128), F32))
        args += [rows, router]
    else:
        in_specs = [pl.BlockSpec((1, packed_rows, width), lambda p, lead: (p, 0, 0))]
    return pl.pallas_call(
        kernel,
        out_shape=out_shape,
        grid_spec=pltpu.PrefetchScalarGridSpec(
            num_scalar_prefetch=1, grid=(pieces,), in_specs=in_specs, out_specs=out_specs
        ),
        compiler_params=pltpu.CompilerParams(vmem_limit_bytes=VMEM_LIMIT),
        name="dispatch",
    )(lead, *args)


def combine_rows(lead, first, packed, slot_rows, local, capacity, addend=None):
    pieces, packed_rows, code_width = packed.shape
    tokens = packed_rows - 16
    halves = len(slot_rows)
    slots, width = slot_rows[0].shape[1:]
    per = local // halves

    def kernel(lead_ref, code_ref, *rest):
        table = unpack_code(code_ref[0], tokens)
        here = lead_ref[0]
        codes = jnp.concatenate([row_of(table, here + e) for e in range(local)], axis=0)
        picks = one_hot_slots(codes, capacity)
        total = None
        for h in range(halves):
            select = jnp.concatenate(
                [p.astype(B16) for p in picks[h * per : (h + 1) * per]], axis=0
            )
            part = lax.dot_general(
                select, rest[h][0], (((0,), (0,)), ((), ())), preferred_element_type=F32
            )
            total = part if total is None else total + part
        if addend is not None:
            total = total + rest[halves][0].astype(F32)
        rest[-1][0] = total.astype(B16)

    in_specs = [pl.BlockSpec((1, 16, code_width), lambda p, lead: (p, tokens // 16, 0))]
    in_specs += [
        pl.BlockSpec((1, slots, width), lambda p, lead: (p + first, 0, 0)) for _ in range(halves)
    ]
    added = [] if addend is None else [addend]
    in_specs += [pl.BlockSpec((1, tokens, width), lambda p, lead: (p, 0, 0)) for _ in added]
    return pl.pallas_call(
        kernel,
        out_shape=jax.ShapeDtypeStruct((pieces, tokens, width), B16),
        grid_spec=pltpu.PrefetchScalarGridSpec(
            num_scalar_prefetch=1,
            grid=(pieces,),
            in_specs=in_specs,
            out_specs=pl.BlockSpec((1, tokens, width), lambda p, lead: (p, 0, 0)),
        ),
        compiler_params=pltpu.CompilerParams(vmem_limit_bytes=VMEM_LIMIT),
        name="combine",
    )(lead, packed, *slot_rows, *added)


def experts(order, start, count, rows, grads, gates, weights, chunks, capacity, in_rows, mid_rows):
    half, _, width = rows[0].shape
    pieces = 2 * half
    split = bool(chunks)
    n = 4 if split else len(weights)
    extra = [array for chunk in chunks for array, _ in chunk]
    given = len(weights) + len(extra)
    pack_rows, eff = weights[0].shape[1:]
    folds = width // eff
    total_rows = pieces * capacity
    first_half = count // 2
    large = total_rows > 1000

    def kernel(order_ref, *refs):
        rows_a, rows_b, grads_a, grads_b, gates_a, gates_b = refs[:6]
        pack = refs[6 : 6 + given]
        y_out, dx_out = refs[6 + given : 8 + given]
        outs = refs[8 + given : -6]
        full_g, full_u, full_d, grad_g, grad_u, grad_d = refs[-6:]

        def at_in(j):
            return pl.ds(pl.multiple_of(order_ref[j] * in_rows, in_rows), in_rows)

        def at_mid(j):
            return pl.ds(pl.multiple_of(order_ref[j] * mid_rows, mid_rows), mid_rows)

        def load(j, take):
            full_g[at_in(j), :] = take(0, in_rows)
            full_u[at_in(j), :] = take(in_rows, 2 * in_rows)
            for f in range(folds):
                full_d[at_mid(j), f * eff : (f + 1) * eff] = take(
                    2 * in_rows + f * mid_rows, 2 * in_rows + (f + 1) * mid_rows
                )

        def rows_from(ref, offset):
            return lambda lo, hi: ref[offset + lo : offset + hi, :]

        def two_halves(a, b):
            middle = pack_rows // 2

            def take(lo, hi):
                if hi <= middle:
                    return a(lo, hi)
                if lo >= middle:
                    return b(lo - middle, hi - middle)
                return jnp.concatenate([a(lo, middle), b(0, hi - middle)], axis=0)

            return take

        for j in range(len(weights)):
            load(j, lambda lo, hi, ref=pack[j]: ref[0, lo:hi])
        for c in range(len(chunks)):
            from_x, from_y, diag_a, diag_b = [
                rows_from(pack[1 + 4 * c + i], chunks[c][i][1]) for i in range(4)
            ]

            @pl.when(pl.program_id(0) == c)
            def _():
                load(1, from_x)
                load(2, from_y)
                load(3, two_halves(diag_a, diag_b))

        def joined(a, b, w):
            return jnp.concatenate(
                [
                    a[...].reshape(half * capacity, w),
                    b[...].reshape(half * capacity, w),
                ],
                axis=0,
            )

        x = joined(rows_a, rows_b, width)
        g = joined(grads_a, grads_b, width)
        gate = joined(gates_a, gates_b, 128)[:, 0:1]
        nt = (((1,), (1,)), ((), ()))
        tn = (((0,), (0,)), ((), ()))
        gate_proj = jnp.dot(x, full_g[...], preferred_element_type=F32)
        up_proj = jnp.dot(x, full_u[...], preferred_element_type=F32)
        down_grad = lax.dot_general(g, full_d[...], nt, preferred_element_type=F32)
        sigmoid = 1.0 / (1.0 + jnp.exp(-gate_proj))
        silu = gate_proj * sigmoid
        activated = silu * up_proj
        slot_grad = jnp.sum(activated * down_grad, axis=1, keepdims=True)
        here = order_ref[n] + start + pl.program_id(0)
        lane = lax.broadcasted_iota(jnp.int32, (total_rows, 128), 1)
        high = slot_grad.astype(B16).astype(F32)
        tail = jnp.where(lane == here, high, jnp.where(lane == here + EXPERTS, slot_grad - high, 0.0))
        dx_out[:, :, width:] = tail.astype(B16).reshape(pieces, capacity, 128)
        scaled = (gate * activated).astype(B16)
        act_grad = gate * down_grad
        gate_grad = (act_grad * up_proj * (sigmoid * (1.0 + gate_proj * (1.0 - sigmoid)))).astype(
            B16
        )
        up_grad = (act_grad * silu).astype(B16)
        y = jnp.dot(scaled, full_d[...], preferred_element_type=F32)
        y_out[...] = y.astype(B16).reshape(pieces, capacity, width)
        dx = lax.dot_general(gate_grad, full_g[...], nt, preferred_element_type=F32)
        dx = dx + lax.dot_general(up_grad, full_u[...], nt, preferred_element_type=F32)
        dx_out[:, :, :width] = dx.astype(B16).reshape(pieces, capacity, width)
        grad_g[...] = lax.dot_general(x, gate_grad, tn, preferred_element_type=F32).astype(B16)
        grad_u[...] = lax.dot_general(x, up_grad, tn, preferred_element_type=F32).astype(B16)
        grad_d[...] = lax.dot_general(scaled, g, tn, preferred_element_type=F32).astype(B16)

        def give(ref, slot, j):
            ref[slot, 0, :in_rows] = grad_g[at_in(j), :]
            ref[slot, 0, in_rows : 2 * in_rows] = grad_u[at_in(j), :]
            for f in range(folds):
                ref[slot, 0, 2 * in_rows + f * mid_rows : 2 * in_rows + (f + 1) * mid_rows] = grad_d[
                    at_mid(j), f * eff : (f + 1) * eff
                ]

        if split:

            @pl.when(pl.program_id(0) < first_half)
            def _():
                for j in range(4):
                    give(outs[j], 0, j)

            @pl.when(pl.program_id(0) >= first_half)
            def _():
                for j in range(4):
                    give(outs[4 + j], 0, j)
        else:
            for j in range(n):
                give(outs[0], j, j)

    def single():
        return dict(pipeline_mode=pl.Buffered(1)) if large else {}

    def rows_spec(w):
        return pl.BlockSpec((half, capacity, w), lambda e, o: (0, e + start, 0), **single())

    in_specs = [rows_spec(width)] * 4 + [rows_spec(128)] * 2
    for _ in weights:
        in_specs.append(pl.BlockSpec((1, pack_rows, eff), lambda e, o: (e + start, 0, 0)))
    for part in extra:
        in_specs.append(pl.BlockSpec(part.shape, lambda e, o: (0, 0)))
    slots = count * capacity
    out_specs = [
        pl.BlockSpec((pieces, capacity, w), lambda e, o: (0, e, 0), **single())
        for w in (width, width + 128)
    ]
    out_shape = [
        jax.ShapeDtypeStruct((pieces, slots, width), B16),
        jax.ShapeDtypeStruct((pieces, slots, width + 128), B16),
    ]
    if split:
        for at in (
            lambda e, o: (0, jnp.minimum(e, first_half - 1), 0, 0),
            lambda e, o: (0, jnp.maximum(e - first_half, 0), 0, 0),
        ):
            for _ in range(4):
                out_specs.append(pl.BlockSpec((1, 1, pack_rows, eff), at))
                out_shape.append(jax.ShapeDtypeStruct((1, first_half, pack_rows, eff), B16))
    else:
        out_specs.append(pl.BlockSpec((n, 1, pack_rows, eff), lambda e, o: (0, e, 0, 0)))
        out_shape.append(jax.ShapeDtypeStruct((n, count, pack_rows, eff), B16))
    results = pl.pallas_call(
        kernel,
        out_shape=out_shape,
        grid_spec=pltpu.PrefetchScalarGridSpec(
            num_scalar_prefetch=1,
            grid=(count,),
            in_specs=in_specs,
            out_specs=out_specs,
            scratch_shapes=[
                pltpu.VMEM((n * in_rows, eff), B16),
                pltpu.VMEM((n * in_rows, eff), B16),
                pltpu.VMEM((n * mid_rows, width), B16),
                pltpu.VMEM((n * in_rows, eff), B16),
                pltpu.VMEM((n * in_rows, eff), B16),
                pltpu.VMEM((n * mid_rows, width), B16),
            ],
        ),
        compiler_params=pltpu.CompilerParams(vmem_limit_bytes=VMEM_LIMIT),
        name="experts",
    )(order, *rows, *grads, *gates, *weights, *extra)
    return results[0], results[1], results[2:]


NT = (((1,), (1,)), ((), ()))
TN = (((0,), (0,)), ((), ()))
GROUPS = KVH // 2
EXTRA = 128


def turn(vectors, cosine, sine):
    lane = lax.broadcasted_iota(jnp.int32, vectors.shape, 1)
    ahead = pltpu.roll(vectors, 2 * HD - HD // 2, 1)
    behind = pltpu.roll(vectors, HD // 2, 1)
    return vectors * cosine + jnp.where(lane % HD < HD // 2, ahead, behind) * sine


def turn_tables(places):
    lane = jnp.arange(2 * HD, dtype=jnp.int32)
    frequency = jnp.exp(
        (lane % (HD // 2)).astype(F32) * (-2.0 * math.log(ROPE_BASE) / HD)
    )
    angles = places[:, None] * frequency[None, :]
    sign = jnp.where(lane % HD < HD // 2, -1.0, 1.0)
    return jnp.cos(angles), jnp.sin(angles) * sign[None, :]


def attention_forward(x_own, x_parts, dense_full, bias, cosine, sine, routed):
    tok_rows, width = x_own.shape
    seq_len = 4 * tok_rows
    scale = HD ** (-0.5)
    wide, narrow = H * HD, KVH * HD

    def kernel(
        own_ref, xa_ref, xb_ref, ya_ref, yb_ref, da_ref, db_ref, ea_ref, eb_ref,
        tail_ref, wo_ref, wq_ref, wk_ref, wv_ref, bias_ref, cos_ref, sin_ref, routed_ref,
        x_ref, normed_ref, q_out, k_out, v_out, att_out, total_out, misc_out, residual_out, moe_out,
        gates_out,
    ):
        step = pl.program_id(0)

        @pl.when(step == 0)
        def _():
            rows = jnp.transpose(tail_ref[...].astype(F32))
            misc_out[...] = rows
            at = 0
            for ref in (own_ref, xa_ref, xb_ref, ya_ref, yb_ref, da_ref, ea_ref, db_ref, eb_ref):
                x_ref[at : at + ref.shape[0], :] = ref[...]
                at += ref.shape[0]
            x = x_ref[...].astype(F32)
            scaled = x * lax.rsqrt(jnp.mean(x * x, axis=1, keepdims=True) + EPSILON)
            normed_ref[...] = (scaled * rows[EXPERTS : EXPERTS + 1, :]).astype(B16)
            residual_out[...] = x[:tok_rows]

        normed = normed_ref[...]
        cos, sin = cos_ref[...], sin_ref[...]
        key = turn(jnp.dot(normed, wk_ref[...], preferred_element_type=F32), cos, sin).astype(B16)
        value = jnp.dot(normed, wv_ref[...], preferred_element_type=F32).astype(B16)
        query = jnp.dot(normed[:tok_rows], wq_ref[...], preferred_element_type=F32)
        cos, sin = cos[:tok_rows], sin[:tok_rows]
        query = jnp.concatenate(
            [turn(query[:, 128 * j : 128 * (j + 1)], cos, sin) for j in range(2)], axis=1
        )
        query = (query * scale).astype(B16)
        k_out[...] = key
        v_out[...] = value
        q_out[...] = query
        mixed, totals = [], []
        for j in range(4):
            lanes = slice(HD * (j // 2), HD * (j // 2 + 1))
            scores = lax.dot_general(
                key[:, lanes], query[:, HD * j : HD * (j + 1)], NT, preferred_element_type=F32
            )
            scores = scores + bias_ref[...]
            peak = jnp.max(scores, axis=0, keepdims=True)
            probs = jnp.exp(scores - peak)
            total = jnp.sum(probs, axis=0, keepdims=True)
            out = lax.dot_general(
                value[:, lanes], probs.astype(B16), TN, preferred_element_type=F32
            )
            mixed.append(out / total)
            totals.append(peak + jnp.log(total))
        attended = jnp.transpose(jnp.concatenate(mixed, axis=0)).astype(B16)
        att_out[...] = attended
        total_out[0] = jnp.concatenate(totals + totals, axis=0)
        residual_out[...] += jnp.dot(attended, wo_ref[...], preferred_element_type=F32)

        @pl.when(step == GROUPS - 1)
        def _():
            total = residual_out[...]
            scaled = total * lax.rsqrt(jnp.mean(total * total, axis=1, keepdims=True) + EPSILON)
            moe_in = (scaled * misc_out[EXPERTS + 1 : EXPERTS + 2, :]).astype(B16)
            moe_out[...] = moe_in
            logits = jnp.dot(moe_in, tail_ref[...], preferred_element_type=F32)
            here = routed_ref[...] > 0.0
            peak = jnp.max(jnp.where(here, logits, MASKED_SCORE), axis=1, keepdims=True)
            lifted = jnp.where(here, jnp.exp(jnp.minimum(logits - peak, 0.0)), 0.0)
            gates_out[...] = lifted / jnp.sum(lifted, axis=1, keepdims=True)

    def fixed(*block):
        return pl.BlockSpec(block, lambda i: (0,) * len(block))

    def columns(rows, cols, lead=0):
        return pl.BlockSpec((rows, cols), lambda i: (0, lead + i))

    return pl.pallas_call(
        kernel,
        grid=(GROUPS,),
        in_specs=[
            fixed(tok_rows, width),
            *[
                pl.BlockSpec((part.shape[0], width), lambda i, c=c: (0, c))
                for part in x_parts
                for c in range(2)
            ],
            pl.BlockSpec((width, 128), lambda i: (0, (width + wide + 2 * narrow) // 128)),
            pl.BlockSpec((256, width), lambda i: (i, 0)),
            columns(width, 256, width // 256),
            columns(width, 128, (width + wide) // 128),
            columns(width, 128, (width + wide + narrow) // 128),
            fixed(seq_len, tok_rows),
            fixed(seq_len, 128),
            fixed(seq_len, 128),
            fixed(tok_rows, 128),
        ],
        out_specs=[
            fixed(seq_len, width),
            fixed(seq_len, width),
            columns(tok_rows, 256),
            columns(seq_len, 128),
            columns(seq_len, 128),
            columns(tok_rows, 256),
            pl.BlockSpec((1, 8, tok_rows), lambda i: (i, 0, 0)),
            fixed(128, width),
            fixed(tok_rows, width),
            fixed(tok_rows, width),
            fixed(tok_rows, 128),
        ],
        out_shape=[
            jax.ShapeDtypeStruct((seq_len, width), B16),
            jax.ShapeDtypeStruct((seq_len, width), B16),
            jax.ShapeDtypeStruct((tok_rows, wide), B16),
            jax.ShapeDtypeStruct((seq_len, narrow), B16),
            jax.ShapeDtypeStruct((seq_len, narrow), B16),
            jax.ShapeDtypeStruct((tok_rows, wide), B16),
            jax.ShapeDtypeStruct((GROUPS, 8, tok_rows), F32),
            jax.ShapeDtypeStruct((128, width), F32),
            jax.ShapeDtypeStruct((tok_rows, width), F32),
            jax.ShapeDtypeStruct((tok_rows, width), B16),
            jax.ShapeDtypeStruct((tok_rows, 128), F32),
        ],
        compiler_params=pltpu.CompilerParams(vmem_limit_bytes=VMEM_LIMIT),
        name="attention",
    )(
        x_own, *[part for part in x_parts for _ in range(2)], *[dense_full] * 5,
        bias, cosine, sine, routed,
    )


def attention_backward(
    where_here, moe_sums, out_grad, residual, gates, misc, attended, moe_in, saved,
    dense_full, bias, cosine, sine,
):
    x_all, normed_all, query_rot, key_rot, value_all, totals = saved
    terms = len(moe_sums)
    seq_len, width = x_all.shape
    tok_rows = query_rot.shape[0]
    scale = HD ** (-0.5)
    wide, narrow = H * HD, KVH * HD
    block = width // 8
    output_at = wide + 2 * narrow

    def kernel(here_ref, *refs):
        sums = refs[:terms]
        (
            grad_ref, residual_ref, gates_ref, misc_ref, tail_ref, wo_ref, att_ref, moe_ref,
            normed_ref, q_ref, k_ref, v_ref, total_ref,
            x_ref, wq_ref, wk_ref, wv_ref, bias_ref, cos_ref, sin_ref,
            dense_out, normed_out, residual_out,
            normed_t, grad_sum, og_ref, logit_ref, gain_ref,
        ) = refs[terms:]
        step = pl.program_id(0)
        dp, core = here_ref[0], here_ref[1]

        @pl.when(step == 0)
        def _():
            normed_t[...] = jnp.transpose(normed_ref[...])
            grad_sum[...] = jnp.zeros((seq_len, width), F32)
            total = sums[0][0].astype(F32)
            for ref in sums[1:]:
                total = total + ref[...].astype(F32)
            behind = total[:, width:]
            gate_grad = behind + pltpu.roll(behind, 128 - EXPERTS, 1)
            gate = gates_ref[...]
            centre = jnp.sum(gate * gate_grad, axis=1, keepdims=True)
            logit_low = (gate * (gate_grad - centre)).astype(B16)
            logit_ref[...] = logit_low
            moe_grad = total[:, :width] + lax.dot_general(
                logit_low, tail_ref[...], NT, preferred_element_type=F32
            )
            residual = residual_ref[...]
            rate = lax.rsqrt(jnp.mean(residual * residual, axis=1, keepdims=True) + EPSILON)
            gain_ref[...] = jnp.sum(moe_grad * residual * rate, axis=0, keepdims=True)
            lifted = moe_grad * misc_ref[EXPERTS + 1 : EXPERTS + 2, :]
            inner = jnp.mean(lifted * residual, axis=1, keepdims=True)
            residual_grad = (
                grad_ref[...].astype(F32) + rate * lifted - residual * (rate * rate * rate * inner)
            )
            residual_out[...] = residual_grad
            og_ref[...] = residual_grad.astype(B16)

        og = og_ref[...]
        att_grad = lax.dot_general(og, wo_ref[...], NT, preferred_element_type=F32).astype(B16)
        query, key, value = q_ref[...], k_ref[...], v_ref[...]
        query_grads, key_grads, value_grads = [], [], []
        for j in range(4):
            lanes = slice(HD * (j // 2), HD * (j // 2 + 1))
            mine = slice(HD * j, HD * (j + 1))
            scores = lax.dot_general(
                key[:, lanes], query[:, mine], NT, preferred_element_type=F32
            )
            probs = jnp.exp(scores + bias_ref[...] - total_ref[0, j : j + 1, :])
            probs_grad = lax.dot_general(
                value[:, lanes], att_grad[:, mine], NT, preferred_element_type=F32
            )
            delta = jnp.sum(probs * probs_grad, axis=0, keepdims=True)
            score_grad = (probs * (probs_grad - delta)).astype(B16)
            query_grads.append(
                lax.dot_general(key[:, lanes], score_grad, TN, preferred_element_type=F32)
            )
            key_part = jnp.dot(score_grad, query[:, mine], preferred_element_type=F32)
            value_part = jnp.dot(probs.astype(B16), att_grad[:, mine], preferred_element_type=F32)
            if j % 2 == 0:
                key_grads.append(key_part)
                value_grads.append(value_part)
            else:
                key_grads[-1] = key_grads[-1] + key_part
                value_grads[-1] = value_grads[-1] + value_part
        cos, sin = cos_ref[...], -sin_ref[...]
        kv_grad = jnp.concatenate(
            [turn(jnp.concatenate(key_grads, axis=1), cos, sin)] + value_grads, axis=1
        ).astype(B16)
        cos, sin = cos[:tok_rows], sin[:tok_rows]
        query_grad = jnp.transpose(jnp.concatenate(query_grads, axis=0)) * scale
        query_grad = jnp.concatenate(
            [turn(query_grad[:, 128 * j : 128 * (j + 1)], cos, sin) for j in range(2)], axis=1
        ).astype(B16)

        def give(grad, lanes):
            for m in range(4):
                for c in range(2):
                    dense_out[core ^ c, dp ^ m, :, lanes] = grad[
                        (2 * m + c) * block : (2 * m + c + 1) * block
                    ].astype(B16)

        give(
            jnp.dot(normed_t[:, :tok_rows], query_grad, preferred_element_type=F32),
            pl.ds(pl.multiple_of(step * 256, 256), 256),
        )
        give(
            jnp.dot(normed_t[...], kv_grad, preferred_element_type=F32),
            pl.ds(pl.multiple_of(wide + step * 256, 256), 256),
        )
        out_part = lax.dot_general(att_ref[...], og, TN, preferred_element_type=F32).astype(B16)
        for c in range(2):
            rows = slice(c * block, (c + 1) * block)
            dense_out[core ^ c, dp ^ step, :, output_at : output_at + width] = out_part[rows]
        kv_weights = jnp.concatenate([wk_ref[...], wv_ref[...]], axis=1)
        grad_sum[...] += lax.dot_general(kv_grad, kv_weights, NT, preferred_element_type=F32)
        grad_sum[:tok_rows, :] += lax.dot_general(
            query_grad, wq_ref[...], NT, preferred_element_type=F32
        )

        @pl.when(step == GROUPS - 1)
        def _():
            total = grad_sum[...]
            normed_out[...] = total.astype(B16)
            x = x_ref[...].astype(F32)
            lifted = x * lax.rsqrt(jnp.mean(x * x, axis=1, keepdims=True) + EPSILON)
            gain = jnp.sum(total * lifted, axis=0, keepdims=True)
            row = lax.broadcasted_iota(jnp.int32, (EXTRA, width), 0)
            gains = jnp.where(
                row == EXPERTS, gain, jnp.where(row == EXPERTS + 1, gain_ref[...], 0.0)
            )
            extra = lax.dot_general(
                moe_ref[...], logit_ref[...], TN, preferred_element_type=F32
            ) + jnp.transpose(gains)
            give(extra, slice(output_at + width, output_at + width + EXTRA))

    def fixed(*shape):
        return pl.BlockSpec(shape, lambda i, here: (0,) * len(shape))

    def columns(rows, cols, lead=0):
        return pl.BlockSpec((rows, cols), lambda i, here: (0, lead + i))

    shapes = [
        jax.ShapeDtypeStruct((2, 4, block, output_at + width + EXTRA), B16),
        jax.ShapeDtypeStruct((seq_len, width), B16),
        jax.ShapeDtypeStruct((tok_rows, width), F32),
    ]
    return pl.pallas_call(
        kernel,
        out_shape=shapes,
        grid_spec=pltpu.PrefetchScalarGridSpec(
            num_scalar_prefetch=1,
            grid=(GROUPS,),
            in_specs=[
                pl.BlockSpec((1, tok_rows, width + 128), lambda i, here: (0, 0, 0)),
                *[fixed(tok_rows, width + 128)] * (terms - 1),
                fixed(tok_rows, width),
                fixed(tok_rows, width),
                fixed(tok_rows, 128),
                fixed(128, width),
                pl.BlockSpec(
                    (width, 128), lambda i, here: (0, (width + wide + 2 * narrow) // 128)
                ),
                pl.BlockSpec((256, width), lambda i, here: (i, 0)),
                columns(tok_rows, 256),
                fixed(tok_rows, width),
                fixed(seq_len, width),
                columns(tok_rows, 256),
                columns(seq_len, 128),
                columns(seq_len, 128),
                pl.BlockSpec((1, 8, tok_rows), lambda i, here: (i, 0, 0)),
                fixed(seq_len, width),
                columns(width, 256, width // 256),
                columns(width, 128, (width + wide) // 128),
                columns(width, 128, (width + wide + narrow) // 128),
                fixed(seq_len, tok_rows),
                fixed(seq_len, 128),
                fixed(seq_len, 128),
            ],
            out_specs=[fixed(*shape.shape) for shape in shapes],
            scratch_shapes=[
                pltpu.VMEM((width, seq_len), B16),
                pltpu.VMEM((seq_len, width), F32),
                pltpu.VMEM((tok_rows, width), B16),
                pltpu.VMEM((tok_rows, EXTRA), B16),
                pltpu.VMEM((1, width), F32),
            ],
        ),
        compiler_params=pltpu.CompilerParams(vmem_limit_bytes=VMEM_LIMIT),
        name="attention_grad",
    )(
        where_here, *moe_sums, out_grad, residual, gates, misc, dense_full, dense_full, attended,
        moe_in, normed_all, query_rot, key_rot, value_all, totals,
        x_all, dense_full, dense_full, dense_full, bias, cosine, sine,
    )


def make_body(z_size, small_grid):
    def core_half(shard, core):
        rows = shard.shape[0] // 2
        return lax.dynamic_slice_in_dim(shard, core * rows, rows, 0)

    def dense_assemble(shard, parts, dp_index, core, *hold):
        rows = shard.shape[0] // 2
        moved = after(jnp.concatenate(parts, axis=0), *hold)
        other = swap_core(moved)
        places = [2 * dp_index]
        for which in (core, 1 - core):
            places += [2 * (dp_index ^ (j + 1)) + which for j in range(3)]
        return assemble(jnp.stack(places), shard, moved, other, rows)

    def across_z(mine, z):
        if z_size != 4:
            return lax.psum(mine.astype(F32), "z")
        rows = mine.shape[0] // z_size
        low = mine.astype(B16)
        total = lax.dynamic_slice_in_dim(mine, z * rows, rows, 0)
        for k in range(1, z_size):
            theirs = lax.dynamic_slice_in_dim(low, (z + k) % z_size * rows, rows, 0)
            total = total + cyclic(theirs, z_size, k).astype(F32)
        total = total.astype(B16)
        quarters = [total] + [cyclic(total, z_size, -k) for k in range(1, z_size)]
        places = (jnp.arange(z_size, dtype=jnp.int32) - z) % z_size
        return jnp.take(jnp.stack(quarters), places, axis=0).reshape(mine.shape).astype(F32)

    def core_sum(blocks):
        return (blocks[0].astype(F32) + swap_core(blocks[1]).astype(F32)).astype(B16)

    def dense_finish(halves, z, core):
        low = across_z(jnp.concatenate(halves, axis=0), z).astype(B16)
        other = swap_core(low)
        first = jnp.where(core == 0, low, other)
        second = jnp.where(core == 0, other, low)
        return jnp.concatenate([first, second], axis=0).astype(F32)

    def dense_sum(grads):
        return lax.psum_scatter(
            lax.psum(grads, ("z", "core")), ("y", "x"), scatter_dimension=0, tiled=True
        )

    def body(
        layer_input,
        attn_gain,
        w_query,
        w_key,
        w_value,
        w_output,
        moe_gain,
        w_router,
        w_gate,
        w_up,
        w_down,
        routes,
        priority,
        prefix_len,
        out_grad,
    ):
        tok_rows, model_width = layer_input.shape
        dp_size = lax.axis_size("y") * lax.axis_size("x")
        dp_index = lax.axis_index("y") * lax.axis_size("x") + lax.axis_index("x")
        z = lax.axis_index("z")
        core = lax.axis_index("core")
        seq_len = tok_rows * dp_size
        top_count = routes.shape[1]
        local = w_gate.shape[0]
        capacity = 5 * tok_rows * top_count // (4 * EXPERTS)
        group_size = H // KVH
        score_scale = HD ** (-0.5)

        gains = jnp.stack([attn_gain, moe_gain], axis=1)
        rows = w_query.shape[0]
        dense_pack = jnp.concatenate(
            [w_output, w_query, w_key, w_value, w_router, gains, jnp.zeros((rows, 94), B16)], axis=1
        )
        wide = H * HD
        narrow = KVH * HD
        expert_ids = jnp.arange(EXPERTS, dtype=jnp.int32)
        hits = routes[:, :, None] == expert_ids[None, None, :]
        routed = jnp.any(hits, axis=1)
        place = jnp.where(
            routed, jnp.sum(jnp.where(hits, priority[:, :, None], 0), axis=1), jnp.int32(1 << 20)
        )
        ranks = jnp.sum((place[:, :, None] < place.T[None, :, :]).astype(F32), axis=0)
        code = pack_code(jnp.where(routed.T, ranks, -1.0).astype(B16))
        lead = ((2 * z + core) * local).astype(jnp.int32)[None]
        grad_pieces = column_pieces(jnp.concatenate([out_grad, code], axis=0), z_size)

        if small_grid:
            side = tok_rows // 2
            x_pack = jnp.concatenate([layer_input[:side], layer_input[side:]], axis=1)
            start_parts = grid_gather(jnp.concatenate([x_pack, core_half(dense_pack, core)], axis=1))
            dense_parts = [part[:, 2 * model_width :] for part in start_parts]
            dense_full = dense_assemble(dense_pack, dense_parts, dp_index, core, grad_pieces[1])
        else:
            dense_full = lax.all_gather(dense_pack, ("y", "x"), axis=0, tiled=True)
            full_output = dense_full[:, :model_width]
            head_full = dense_full[:, model_width:]
            full_query = head_full[:, :wide]
            full_key = head_full[:, wide : wide + narrow]
            full_value = head_full[:, wide + narrow : wide + 2 * narrow]

        query_pos = dp_index * tok_rows + jnp.arange(tok_rows, dtype=jnp.int32)
        in_float = layer_input.astype(F32)
        steps = jnp.arange(tok_rows, dtype=jnp.int32)
        eff = w_gate.shape[2]
        in_rows, mid_rows = w_gate.shape[1], w_down.shape[1]
        folds = [w_down[:, :, f * eff : (f + 1) * eff] for f in range(model_width // eff)]
        pack = jnp.concatenate([w_gate, w_up, *folds], axis=1)
        if small_grid:
            relative = dp_index ^ jnp.arange(4, dtype=jnp.int32)
            key_pos = (relative[:, None] * tok_rows + steps[None, :]).reshape(seq_len)
            halves, per = 2, local // 2
            weights = [pack]
            near_0 = gather_near(after(pack[0], *start_parts[2:]))
            far_0 = gather_far(after(near_0, dense_full))
            near_1 = gather_near(after(pack[1], *near_0, dense_full))
        else:
            relative = jnp.arange(dp_size, dtype=jnp.int32)
            key_pos = jnp.arange(seq_len, dtype=jnp.int32)
            halves, per = 1, local
            every = lax.all_gather(pack, ("y", "x"), axis=0, tiled=False)
            weights = [every[j] for j in range(dp_size)]
            near_0 = ()
        order = jnp.concatenate([relative, lead])
        grads_mine = jnp.stack(after(grad_pieces, *near_0, dense_full))
        grads_other = swap_core(grads_mine)
        visible = (key_pos[None, :] <= query_pos[:, None]) | (key_pos[None, :] < prefix_len[0])
        chunks = []
        if small_grid:
            bias_hold = (grads_mine, *near_0)
            bias = after(jnp.where(visible.T, 0.0, MASKED_SCORE), *bias_hold)
            cosine, sine = turn_tables(key_pos.astype(F32))
            (
                x_all, normed_all, query_rot, key_rot, value_all, attended, totals, misc, residual,
                moe_in, gates,
            ) = attention_forward(
                layer_input,
                start_parts,
                dense_full,
                bias,
                cosine,
                sine,
                jnp.pad(routed.astype(F32), ((0, 0), (0, 128 - EXPERTS))),
            )
            moe_in = after(moe_in, grads_other, *near_1, *far_0)
            router_rows = misc[:EXPERTS].astype(B16)
            full_attn_gain = misc[EXPERTS]
            full_moe_gain = misc[EXPERTS + 1]
        else:
            places = query_pos.astype(F32)
            router_rows = head_full[:, wide + 2 * narrow : wide + 2 * narrow + EXPERTS].T
            full_attn_gain = head_full[:, wide + 2 * narrow + EXPERTS].astype(F32)
            full_moe_gain = head_full[:, wide + 2 * narrow + EXPERTS + 1].astype(F32)
            normed = rms_norm(in_float, full_attn_gain).astype(B16)
            query_lin = jnp.dot(normed, full_query, preferred_element_type=F32)
            key_lin = jnp.dot(normed, full_key, preferred_element_type=F32)
            value_low = jnp.dot(normed, full_value, preferred_element_type=F32).astype(B16)
            query_rot = (rotate(query_lin.reshape(tok_rows, H, HD), places) * score_scale).astype(B16)
            key_rot = rotate(key_lin.reshape(tok_rows, KVH, HD), places).astype(B16)
            key_rot = key_rot.reshape(tok_rows, narrow)
            both = jnp.concatenate([key_rot, value_low], axis=1)
            both_all = lax.all_gather(both, ("y", "x"), axis=0, tiled=True)
            key_all = both_all[:, :narrow]
            value_all = both_all[:, narrow:]

            def head_scores(head_idx):
                query_head = query_rot[:, head_idx * group_size : (head_idx + 1) * group_size, :]
                key_head = key_all[:, head_idx * HD : (head_idx + 1) * HD]
                scores = jnp.einsum("qgd,kd->gqk", query_head, key_head, preferred_element_type=F32)
                return jnp.where(visible[None, :, :], scores, MASKED_SCORE)

            mixed_heads = []
            log_totals = []
            for head_idx in range(KVH):
                scores = head_scores(head_idx)
                row_max = jnp.max(scores, axis=-1, keepdims=True)
                log_total = row_max + jnp.log(
                    jnp.sum(jnp.exp(scores - row_max), axis=-1, keepdims=True)
                )
                probs_low = jnp.exp(scores - log_total).astype(B16)
                value_head = value_all[:, head_idx * HD : (head_idx + 1) * HD]
                mixed_heads.append(
                    jnp.einsum("gqk,kd->qgd", probs_low, value_head, preferred_element_type=F32)
                )
                log_totals.append(log_total)
            attended = jnp.concatenate(mixed_heads, axis=1).reshape(tok_rows, wide).astype(B16)
            residual = in_float + jnp.dot(attended, full_output, preferred_element_type=F32)
            moe_in = rms_norm(residual, full_moe_gain).astype(B16)

        row_pieces = column_pieces(moe_in, z_size)
        stage_1 = stage_2 = last_far = ()
        if small_grid:
            middle = pack.shape[1] // 2
            stage_1 = far_and_next(after(near_1, moe_in), pack[2])
        (slot_grads_mine,) = dispatch_rows(lead, after(grads_mine, moe_in), None, None, local, capacity)
        (slot_grads_other,) = dispatch_rows(
            lead,
            after(grads_other, slot_grads_mine, *stage_1, row_pieces[1], row_pieces[-1]),
            None,
            None,
            local,
            capacity,
        )
        if small_grid:
            stage_2 = far_and_next(after(stage_1, slot_grads_other), pack[3])
            last_far = gather_far([part[middle:] for part in stage_2])
            chunks = [
                [(part, 0) for part in [*near_0, *far_0]],
                [(part, 0) for part in [*near_1, *stage_1[::-1]]],
                [(part, middle) for part in stage_1] + [(part, 0) for part in stage_2[::-1]],
                [(part, middle) for part in stage_2] + [(part, 0) for part in last_far],
            ]
        row_pieces = after(row_pieces, slot_grads_other)
        rows_mine = after(jnp.stack(row_pieces), *stage_2)
        rows_other = jnp.stack([swap_core(piece) for piece in row_pieces])
        slot_rows_mine, slot_gates_mine = dispatch_rows(
            lead, grads_mine, rows_mine, router_rows, local, capacity
        )
        slot_rows_other, slot_gates_other = dispatch_rows(
            lead, grads_other, after(rows_other, slot_rows_mine), router_rows, local, capacity
        )
        slot_rows_other = after(slot_rows_other, *last_far)
        ys, dxs, weight_grads, sums = [], [], [], []
        for half in range(halves):
            y, dx, grads = experts(
                order,
                half * per,
                per,
                (slot_rows_mine, slot_rows_other),
                (slot_grads_mine, slot_grads_other),
                (slot_gates_mine, slot_gates_other),
                weights,
                chunks[half * per : (half + 1) * per],
                capacity,
                in_rows,
                mid_rows,
            )
            ys.append(y)
            dxs.append(dx)
            weight_grads.append(grads)

        def grid_sum(grads, got):
            totals = []
            for half in range(2):
                own = grads[4 * half][0]
                direct, last = got[half][0], got[1 - half][1]
                totals.append(own.astype(F32) + direct.astype(F32) + last.astype(F32))
            return totals

        def second_step(grads, via, *more):
            _, x_a, y_a, _, _, x_b, y_b, _ = grads
            to_x = [x_a, plus_low(x_b, via[1])]
            to_y = [y_b, plus_low(y_a, via[0])]
            if more:
                to_x.append(more[0])
                to_y.append(more[1])
            return cross(jnp.concatenate(to_x, axis=0), jnp.concatenate(to_y, axis=0))

        if small_grid:
            early, late = weight_grads
            via = cross(early[3], early[7])
            dxs = after(dxs, *via)
            early_got = second_step(early, via, late[3], late[7])
        dx_other = swap_core(combine_rows(lead, z_size, grads_other, dxs, local, capacity))
        dx_low = combine_rows(lead, 0, grads_mine, dxs, local, capacity, dx_other)
        dx_pieces = column_send_some(dx_low, z_size)
        y_other = combine_rows(lead, z_size, grads_other, after(ys, dx_low), local, capacity)
        dx_pieces, y_other = after((dx_pieces, y_other), y_other, *dx_pieces)
        dx_pieces += column_send_last(dx_low, z_size, *dx_pieces)
        ys, y_other = after((ys, swap_core(y_other)), *dx_pieces)
        y_low = combine_rows(lead, 0, grads_mine, ys, local, capacity, y_other)
        dx_pieces = after(dx_pieces, y_low)
        y_pieces = column_send_some(y_low, z_size)
        if small_grid:
            early_got = after(early_got, y_low)
            late_got = second_step(late, [got[2:3] for got in early_got])
        if small_grid:
            dense_blocks, normed_part, residual_grad = attention_backward(
                jnp.stack([dp_index, core]).astype(jnp.int32),
                (dx_low, *dx_pieces),
                out_grad,
                residual,
                gates,
                misc,
                attended,
                moe_in,
                (x_all, normed_all, query_rot, key_rot, value_all, totals),
                dense_full,
                after(bias, *early_got),
                cosine,
                sine,
            )
            late_got, y_pieces = after((late_got, y_pieces), normed_part)
            normed_part, dense_blocks = after((normed_part, dense_blocks), *late_got, *y_pieces)
            y_pieces += column_send_last(y_low, z_size, *y_pieces)
            normed_first, normed_a, normed_b = row_halves(
                normed_part.reshape(4, tok_rows, model_width)
            )
            dense_first, dense_a, dense_b = row_halves(core_sum(dense_blocks))
            normed_got = grid_scatter_first(*normed_first)
            dense_got = grid_scatter_first(*after(dense_first, *normed_got))
            dense_halves = after(grid_scatter_second(dense_got, dense_a, dense_b), *y_pieces)
            dense_total = dense_finish(dense_halves, z, core)
            normed_grad = jnp.concatenate(
                grid_scatter_second(normed_got, normed_a, normed_b, *dense_got), axis=0
            )
            first_value, first_pull = jax.vjp(lambda v: rms_norm(v, full_attn_gain), in_float)
            input_grad = residual_grad + first_pull(normed_grad)[0]
            kv_at = wide + 2 * narrow
            query_sum = dense_total[:, :wide]
            key_sum, value_sum = [
                jnp.concatenate(
                    [
                        dense_total[:, wide + 256 * i + lead_col : wide + 256 * i + lead_col + 128]
                        for i in range(GROUPS)
                    ],
                    axis=1,
                )
                for lead_col in (0, 128)
            ]
            output_sum = dense_total[:, kv_at : kv_at + model_width]
            router_sum = dense_total[:, kv_at + model_width : kv_at + model_width + EXPERTS]
            attn_gain_sum = dense_total[:, kv_at + model_width + EXPERTS]
            moe_gain_sum = dense_total[:, kv_at + model_width + EXPERTS + 1]
        else:
            y_pieces += column_send_last(y_low, z_size)
            moe_sum = column_sum(dx_low[0], dx_pieces)
            moe_in_grad = moe_sum[:, :model_width]
            gate_grad = (
                moe_sum[:, model_width : model_width + EXPERTS]
                + moe_sum[:, model_width + EXPERTS : model_width + 2 * EXPERTS]
            )
            logits = lax.dot_general(moe_in, router_rows, NT, preferred_element_type=F32)
            peak = jnp.max(jnp.where(routed, logits, MASKED_SCORE), axis=-1, keepdims=True)
            lifted = jnp.where(routed, jnp.exp(jnp.minimum(logits - peak, 0.0)), 0.0)
            gate_weights = lifted / jnp.sum(lifted, axis=-1, keepdims=True)
            grad_out = out_grad.astype(F32)
            centre = jnp.sum(gate_weights * gate_grad, axis=-1, keepdims=True)
            logit_low = (gate_weights * (gate_grad - centre)).astype(B16)
            moe_in_grad = moe_in_grad + jnp.dot(logit_low, router_rows, preferred_element_type=F32)
            norm_value, second_pull = jax.vjp(rms_norm, residual, full_moe_gain)
            resid_norm_grad, moe_gain_grad = second_pull(moe_in_grad)
            residual_grad = grad_out + resid_norm_grad
            attn_out_grad = residual_grad.astype(B16)
            router_grad = jnp.einsum("td,te->de", moe_in, logit_low, preferred_element_type=F32)
            wout_grad = jnp.einsum("tc,td->cd", attended, attn_out_grad, preferred_element_type=F32)
            attended_grad = (
                jnp.einsum("td,cd->tc", attn_out_grad, full_output, preferred_element_type=F32)
                .astype(B16)
                .reshape(tok_rows, H, HD)
            )
            query_grads = []
            key_parts = []
            value_parts = []
            for head_idx in range(KVH):
                scores = head_scores(head_idx)
                attention_probs = jnp.exp(scores - log_totals[head_idx])
                probs_low = attention_probs.astype(B16)
                grad_head = attended_grad[:, head_idx * group_size : (head_idx + 1) * group_size, :]
                query_head = query_rot[:, head_idx * group_size : (head_idx + 1) * group_size, :]
                key_head = key_all[:, head_idx * HD : (head_idx + 1) * HD]
                value_head = value_all[:, head_idx * HD : (head_idx + 1) * HD]
                probs_grad = jnp.einsum("qgd,kd->gqk", grad_head, value_head, preferred_element_type=F32)
                row_delta = jnp.sum(attention_probs * probs_grad, axis=-1, keepdims=True)
                score_grad = (attention_probs * (probs_grad - row_delta)).astype(B16)
                query_grads.append(
                    jnp.einsum("gqk,kd->qgd", score_grad, key_head, preferred_element_type=F32)
                )
                key_parts.append(
                    jnp.einsum("gqk,qgd->kd", score_grad, query_head, preferred_element_type=F32)
                )
                value_parts.append(
                    jnp.einsum("gqk,qgd->kd", probs_low, grad_head, preferred_element_type=F32)
                )
            both_part = jnp.concatenate(key_parts + value_parts, axis=1)
            both_sum = lax.psum_scatter(both_part, ("y", "x"), scatter_dimension=0, tiled=True)
            query_rot_grad = jnp.concatenate(query_grads, axis=1) * score_scale
            key_rot_grad = both_sum[:, :narrow].reshape(tok_rows, KVH, HD)
            value_grad = both_sum[:, narrow:].astype(B16)
            query_grad = rotate(query_rot_grad, -places).reshape(tok_rows, wide).astype(B16)
            key_grad = rotate(key_rot_grad, -places).reshape(tok_rows, narrow).astype(B16)
            wq_grad = jnp.einsum("td,tc->dc", normed, query_grad, preferred_element_type=F32)
            wk_grad = jnp.einsum("td,tc->dc", normed, key_grad, preferred_element_type=F32)
            wv_grad = jnp.einsum("td,tc->dc", normed, value_grad, preferred_element_type=F32)
            normed_grad = jnp.einsum("tc,dc->td", query_grad, full_query, preferred_element_type=F32)
            normed_grad = normed_grad + jnp.einsum(
                "tc,dc->td", key_grad, full_key, preferred_element_type=F32
            )
            normed_grad = normed_grad + jnp.einsum(
                "tc,dc->td", value_grad, full_value, preferred_element_type=F32
            )
            first_value, first_pull = jax.vjp(rms_norm, in_float, full_attn_gain)
            input_norm_grad, attn_gain_grad = first_pull(normed_grad)
            input_grad = residual_grad + input_norm_grad
            query_sum = dense_sum(wq_grad)
            key_sum = dense_sum(wk_grad)
            value_sum = dense_sum(wv_grad)
            output_sum = dense_sum(wout_grad)
            extra_sum = dense_sum(
                jnp.concatenate(
                    [
                        router_grad,
                        attn_gain_grad[:, None],
                        moe_gain_grad[:, None],
                        jnp.zeros((model_width, EXTRA - EXPERTS - 2), F32),
                    ],
                    axis=1,
                )
            )
            router_sum = extra_sum[:, :EXPERTS]
            attn_gain_sum = extra_sum[:, EXPERTS]
            moe_gain_sum = extra_sum[:, EXPERTS + 1]
        layer_output = (residual + column_sum(y_low[0], y_pieces)).astype(B16)
        if small_grid:
            parts = grid_sum(early, early_got) + grid_sum(late, late_got)
            pack_grad = jnp.concatenate(parts, axis=0)
        else:
            pack_grad = lax.psum_scatter(
                weight_grads[0][0].astype(F32), ("y", "x"), scatter_dimension=0, tiled=False
            )
        down = 2 * in_rows
        expert_grads = [
            pack_grad[:, :in_rows],
            pack_grad[:, in_rows:down],
            jnp.concatenate(
                [
                    pack_grad[:, down + f * mid_rows : down + (f + 1) * mid_rows]
                    for f in range(model_width // eff)
                ],
                axis=2,
            ),
        ]

        return (
            layer_output,
            input_grad,
            attn_gain_sum,
            query_sum,
            key_sum,
            value_sum,
            output_sum,
            moe_gain_sum,
            router_sum,
            expert_grads[0],
            expert_grads[1],
            expert_grads[2],
        )

    return body


def solution(mesh):
    groups = mesh.shape["expert"]
    members = mesh.shape["dp"]
    z_size = groups // 2
    side = math.isqrt(members)
    grid = Mesh(
        mesh.devices.reshape(z_size, 2, members // side, side), ("z", "core", "y", "x")
    )
    expert = ("z", "core")
    dp = ("y", "x")
    every = expert + dp
    placed = (
        P(every, None),
        P(dp),
        P(dp, None),
        P(dp, None),
        P(dp, None),
        P(dp, None),
        P(dp),
        P(dp, None),
        P(expert, dp, None),
        P(expert, dp, None),
        P(expert, dp, None),
        P(every, None),
        P(every, None),
        P(expert),
        P(every, None),
    )
    return jax.shard_map(
        make_body(z_size, members == 4 and side == 2 and EXPERTS == 4 * groups),
        mesh=grid,
        in_specs=placed,
        out_specs=(
            P(every, None),
            P(every, None),
            P(dp),
            P(dp, None),
            P(dp, None),
            P(dp, None),
            P(dp, None),
            P(dp),
            P(dp, None),
            P(expert, dp, None),
            P(expert, dp, None),
            P(expert, dp, None),
        ),
        check_vma=False,
    )
```

```python
import math

import jax
import jax.numpy as jnp
from jax import lax
from jax.experimental import pallas as pl
from jax.experimental.pallas import tpu as pltpu
from jax.sharding import Mesh
from jax.sharding import PartitionSpec as P

H = 16
KVH = 8
HD = 64
EXPERTS = 32
EPSILON = 1e-06
ROPE_BASE = 10000.0
MASKED_SCORE = -1e30
F32 = jnp.float32
B16 = jnp.bfloat16
SWAP = [(0, 1), (1, 0)]
VMEM_LIMIT = 60 * 1024 * 1024


def rms_norm(values, gain_vec):
    return (
        values * lax.rsqrt(jnp.mean(values * values, axis=-1, keepdims=True) + EPSILON) * gain_vec
    )


def rotate(vectors, places):
    half_dim = vectors.shape[-1] // 2
    frequency = jnp.exp(
        jnp.arange(half_dim, dtype=F32) * (-2.0 * math.log(ROPE_BASE) / vectors.shape[-1])
    )
    angles = places[:, None] * frequency[None, :]
    cosine = jnp.cos(angles)[:, None, :]
    sine_vals = jnp.sin(angles)[:, None, :]
    first_half = vectors[..., :half_dim]
    second = vectors[..., half_dim:]
    return jnp.concatenate(
        [first_half * cosine - second * sine_vals, second * cosine + first_half * sine_vals],
        axis=-1,
    )


def swap_core(rows):
    return lax.ppermute(rows, "core", SWAP)


def cyclic(rows, size, shift):
    return lax.ppermute(rows, "z", [(i, (i + shift) % size) for i in range(size)])


def after(value, *others):
    return lax.optimization_barrier((value, *others))[0]


def gather_near(shard):
    return [lax.ppermute(shard, "x", SWAP), lax.ppermute(shard, "y", SWAP)]


def gather_far(near):
    from_x, from_y = near
    half = from_x.shape[0] // 2
    return [lax.ppermute(from_x[:half], "y", SWAP), lax.ppermute(from_y[half:], "x", SWAP)]


def grid_gather(shard):
    near = gather_near(shard)
    return near + gather_far(near)


def cross(to_x, to_y):
    return lax.ppermute(to_x, "x", SWAP), lax.ppermute(to_y, "y", SWAP)


def far_and_next(near, shard):
    from_x, from_y = near
    half = shard.shape[0] // 2
    return cross(
        jnp.concatenate([from_y[-half:], shard], axis=0),
        jnp.concatenate([from_x[-2 * half : -half], shard], axis=0),
    )


def plus_low(a, b):
    return (a.astype(F32) + b.astype(F32)).astype(B16)


def grid_scatter_first(first_a, first_b):
    return lax.ppermute(first_a, "x", SWAP), lax.ppermute(first_b, "y", SWAP)


def grid_scatter_second(got, rest_a, rest_b, *hold):
    got_a, got_b = got
    onward_a = (rest_a[1].astype(F32) + got_a[1].astype(F32)).astype(B16)
    onward_b = (rest_b[1].astype(F32) + got_b[1].astype(F32)).astype(B16)
    last_a = lax.ppermute(onward_a, "y", SWAP)
    last_b = lax.ppermute(onward_b, "x", SWAP)
    last_a, last_b = after((last_a, last_b), *hold)
    return (
        rest_a[0].astype(F32) + got_a[0].astype(F32) + last_a.astype(F32),
        rest_b[0].astype(F32) + got_b[0].astype(F32) + last_b.astype(F32),
    )


def row_halves(parts):
    own, to_x, to_y, diag = [parts[j] for j in range(4)]
    half = own.shape[0] // 2
    first = (
        jnp.stack([to_x[:half], diag[:half]]),
        jnp.stack([to_y[half:], diag[half:]]),
    )
    return first, (own[:half], to_y[:half]), (own[half:], to_x[half:])


def column_pieces(rows, size):
    return [rows] + [cyclic(rows, size, -k) for k in range(1, size)]


def column_send_some(low, size):
    return [cyclic(low[k], size, k) for k in range(1, size) if 2 * k != size]


def column_send_last(low, size, *hold):
    return [cyclic(after(low[size // 2], *hold), size, size // 2)]


def column_sum(own, pieces):
    return own.astype(F32) + sum(piece.astype(F32) for piece in pieces)


def assemble(places, shard, moved, other, rows):
    def kernel(places_ref, shard_ref, moved_ref, other_ref, out_ref):
        def put(i, value):
            start = pl.multiple_of(places_ref[i] * rows, rows)
            out_ref[pl.ds(start, value.shape[0]), :] = value

        put(0, shard_ref[...])
        for j in range(3):
            put(1 + j, moved_ref[j * rows : (j + 1) * rows, :])
            put(4 + j, other_ref[j * rows : (j + 1) * rows, :])

    def whole(array_shape):
        return pl.BlockSpec(array_shape, lambda i, places: (0, 0))

    out_rows, cols = 8 * rows, shard.shape[1]
    return pl.pallas_call(
        kernel,
        out_shape=jax.ShapeDtypeStruct((out_rows, cols), shard.dtype),
        grid_spec=pltpu.PrefetchScalarGridSpec(
            num_scalar_prefetch=1,
            grid=(1,),
            in_specs=[whole(a.shape) for a in (shard, moved, other)],
            out_specs=whole((out_rows, cols)),
        ),
        compiler_params=pltpu.CompilerParams(vmem_limit_bytes=VMEM_LIMIT),
        name="assemble",
    )(places, shard, moved, other)


def one_hot_slots(codes, capacity):
    slots = lax.broadcasted_iota(jnp.int32, (capacity, codes.shape[1]), 0).astype(F32)
    return [(slots == codes[e : e + 1, :]).astype(F32) for e in range(codes.shape[0])]


def row_of(table, index):
    at = lax.broadcasted_iota(jnp.int32, table.shape, 0)
    return jnp.sum(jnp.where(at == index, table, 0.0), axis=0, keepdims=True)


def pack_code(code):
    rows = code.shape[0] // 4
    wide = jnp.concatenate([code[c * rows : (c + 1) * rows] for c in range(4)], axis=1)
    return jnp.concatenate([wide, jnp.full((16 - rows, wide.shape[1]), -1.0, B16)], axis=0)


def unpack_code(block, tokens):
    rows = EXPERTS // 4
    wide = block.astype(F32)
    return jnp.concatenate(
        [wide[:rows, c * tokens : (c + 1) * tokens] for c in range(4)], axis=0
    )


def dispatch_rows(lead, packed, rows, router, local, capacity):
    pieces, packed_rows, width = packed.shape
    tokens = packed_rows - 16
    slots = local * capacity
    with_gates = router is not None

    def kernel(lead_ref, packed_ref, *rest):
        first = lead_ref[0]
        if with_gates:
            router_ref, out_ref, gate_out, rows_ref = rest[pieces:]
            for p in range(pieces):

                @pl.when(pl.program_id(0) == p)
                def _():
                    rows_ref[...] = rest[p][...]

            table = unpack_code(packed_ref[0], tokens)
            source = rows_ref[...]
        else:
            (out_ref,) = rest
            table = unpack_code(packed_ref[0, tokens:, :], tokens)
            source = packed_ref[0, :tokens, :]
        codes = jnp.concatenate([row_of(table, first + e) for e in range(local)], axis=0)
        picks = one_hot_slots(codes, capacity)
        select = jnp.concatenate([p.astype(B16) for p in picks], axis=0)
        out_ref[0] = jnp.dot(select, source, preferred_element_type=F32).astype(B16)
        if with_gates:
            logits = lax.dot_general(
                router_ref[...], source, (((1,), (1,)), ((), ())), preferred_element_type=F32
            )
            routed = table >= 0.0
            peak = jnp.max(jnp.where(routed, logits, MASKED_SCORE), axis=0, keepdims=True)
            lifted = jnp.where(routed, jnp.exp(jnp.minimum(logits - peak, 0.0)), 0.0)
            gates = lifted / jnp.sum(lifted, axis=0, keepdims=True)
            for e in range(local):
                gate_row = row_of(gates, first + e)
                column = jnp.sum(picks[e] * gate_row, axis=1, keepdims=True)
                gate_out[0, e * capacity : (e + 1) * capacity, :] = jnp.broadcast_to(
                    column, (capacity, 128)
                )

    out_specs = [pl.BlockSpec((1, slots, width), lambda p, lead: (p, 0, 0))]
    out_shape = [jax.ShapeDtypeStruct((pieces, slots, width), B16)]
    args = [packed]
    if with_gates:
        in_specs = [
            pl.BlockSpec((1, 16, width), lambda p, lead: (p, tokens // 16, 0)),
            *[pl.BlockSpec((tokens, width), lambda p, lead: (0, 0)) for _ in rows],
            pl.BlockSpec((EXPERTS, width), lambda p, lead: (0, 0)),
        ]
        out_specs.append(pl.BlockSpec((1, slots, 128), lambda p, lead: (p, 0, 0)))
        out_shape.append(jax.ShapeDtypeStruct((pieces, slots, 128), F32))
        args += [*rows, router]
    else:
        in_specs = [pl.BlockSpec((1, packed_rows, width), lambda p, lead: (p, 0, 0))]
    return pl.pallas_call(
        kernel,
        out_shape=out_shape,
        grid_spec=pltpu.PrefetchScalarGridSpec(
            num_scalar_prefetch=1,
            grid=(pieces,),
            in_specs=in_specs,
            out_specs=out_specs,
            scratch_shapes=[pltpu.VMEM((tokens, width), B16)] if with_gates else [],
        ),
        compiler_params=pltpu.CompilerParams(vmem_limit_bytes=VMEM_LIMIT),
        name="dispatch",
    )(lead, *args)


def combine_rows(lead, first, packed, slot_rows, local, capacity, addend=None):
    pieces, packed_rows, code_width = packed.shape
    tokens = packed_rows - 16
    halves = len(slot_rows)
    slots, width = slot_rows[0].shape[1:]
    per = local // halves

    def kernel(lead_ref, code_ref, *rest):
        table = unpack_code(code_ref[0], tokens)
        here = lead_ref[0]
        codes = jnp.concatenate([row_of(table, here + e) for e in range(local)], axis=0)
        picks = one_hot_slots(codes, capacity)
        total = None
        for h in range(halves):
            select = jnp.concatenate(
                [p.astype(B16) for p in picks[h * per : (h + 1) * per]], axis=0
            )
            part = lax.dot_general(
                select, rest[h][0], (((0,), (0,)), ((), ())), preferred_element_type=F32
            )
            total = part if total is None else total + part
        if addend is None:
            rest[halves][0] = total.astype(B16)
        else:
            low = (total + rest[halves][0].astype(F32)).astype(B16)
            for p in range(pieces):

                @pl.when(pl.program_id(0) == p)
                def _():
                    rest[halves + 1 + p][...] = low

    in_specs = [pl.BlockSpec((1, 16, code_width), lambda p, lead: (p, tokens // 16, 0))]
    in_specs += [
        pl.BlockSpec((1, slots, width), lambda p, lead: (p + first, 0, 0)) for _ in range(halves)
    ]
    added = [] if addend is None else [addend]
    in_specs += [pl.BlockSpec((1, tokens, width), lambda p, lead: (p, 0, 0)) for _ in added]
    if addend is None:
        out_shape = jax.ShapeDtypeStruct((pieces, tokens, width), B16)
        out_specs = pl.BlockSpec((1, tokens, width), lambda p, lead: (p, 0, 0))
    else:
        out_shape = [jax.ShapeDtypeStruct((tokens, width), B16)] * pieces
        out_specs = [pl.BlockSpec((tokens, width), lambda p, lead: (0, 0))] * pieces
    return pl.pallas_call(
        kernel,
        out_shape=out_shape,
        grid_spec=pltpu.PrefetchScalarGridSpec(
            num_scalar_prefetch=1,
            grid=(pieces,),
            in_specs=in_specs,
            out_specs=out_specs,
        ),
        compiler_params=pltpu.CompilerParams(vmem_limit_bytes=VMEM_LIMIT),
        name="combine",
    )(lead, packed, *slot_rows, *added)


def experts(order, start, count, rows, grads, gates, weights, chunks, capacity, in_rows, mid_rows):
    half, _, width = rows[0].shape
    pieces = 2 * half
    split = bool(chunks)
    n = 4 if split else len(weights)
    extra = [array for chunk in chunks for array, _ in chunk]
    given = len(weights) + len(extra)
    pack_rows, eff = weights[0].shape[1:]
    folds = width // eff
    total_rows = pieces * capacity
    first_half = count // 2
    large = total_rows > 1000

    def kernel(order_ref, *refs):
        rows_a, rows_b, grads_a, grads_b, gates_a, gates_b = refs[:6]
        pack = refs[6 : 6 + given]
        y_out, dx_out = refs[6 + given : 8 + given]
        outs = refs[8 + given : -6]
        full_g, full_u, full_d, grad_g, grad_u, grad_d = refs[-6:]

        def at_in(j):
            return pl.ds(pl.multiple_of(order_ref[j] * in_rows, in_rows), in_rows)

        def at_mid(j):
            return pl.ds(pl.multiple_of(order_ref[j] * mid_rows, mid_rows), mid_rows)

        def load(j, take):
            full_g[at_in(j), :] = take(0, in_rows)
            full_u[at_in(j), :] = take(in_rows, 2 * in_rows)
            for f in range(folds):
                full_d[at_mid(j), f * eff : (f + 1) * eff] = take(
                    2 * in_rows + f * mid_rows, 2 * in_rows + (f + 1) * mid_rows
                )

        def rows_from(ref, offset):
            return lambda lo, hi: ref[offset + lo : offset + hi, :]

        def two_halves(a, b):
            middle = pack_rows // 2

            def take(lo, hi):
                if hi <= middle:
                    return a(lo, hi)
                if lo >= middle:
                    return b(lo - middle, hi - middle)
                return jnp.concatenate([a(lo, middle), b(0, hi - middle)], axis=0)

            return take

        for j in range(len(weights)):
            load(j, lambda lo, hi, ref=pack[j]: ref[0, lo:hi])
        for c in range(len(chunks)):
            from_x, from_y, diag_a, diag_b = [
                rows_from(pack[1 + 4 * c + i], chunks[c][i][1]) for i in range(4)
            ]

            @pl.when(pl.program_id(0) == c)
            def _():
                load(1, from_x)
                load(2, from_y)
                load(3, two_halves(diag_a, diag_b))

        def joined(a, b, w):
            return jnp.concatenate(
                [
                    a[...].reshape(half * capacity, w),
                    b[...].reshape(half * capacity, w),
                ],
                axis=0,
            )

        x = joined(rows_a, rows_b, width)
        g = joined(grads_a, grads_b, width)
        gate = joined(gates_a, gates_b, 128)[:, 0:1]
        nt = (((1,), (1,)), ((), ()))
        tn = (((0,), (0,)), ((), ()))
        gate_proj = jnp.dot(x, full_g[...], preferred_element_type=F32)
        up_proj = jnp.dot(x, full_u[...], preferred_element_type=F32)
        down_grad = lax.dot_general(g, full_d[...], nt, preferred_element_type=F32)
        sigmoid = 1.0 / (1.0 + jnp.exp(-gate_proj))
        silu = gate_proj * sigmoid
        activated = silu * up_proj
        slot_grad = jnp.sum(activated * down_grad, axis=1, keepdims=True)
        here = order_ref[n] + start + pl.program_id(0)
        lane = lax.broadcasted_iota(jnp.int32, (total_rows, 128), 1)
        high = slot_grad.astype(B16).astype(F32)
        tail = jnp.where(lane == here, high, jnp.where(lane == here + EXPERTS, slot_grad - high, 0.0))
        dx_out[:, :, width:] = tail.astype(B16).reshape(pieces, capacity, 128)
        scaled = (gate * activated).astype(B16)
        act_grad = gate * down_grad
        gate_grad = (act_grad * up_proj * (sigmoid * (1.0 + gate_proj * (1.0 - sigmoid)))).astype(
            B16
        )
        up_grad = (act_grad * silu).astype(B16)
        y = jnp.dot(scaled, full_d[...], preferred_element_type=F32)
        y_out[...] = y.astype(B16).reshape(pieces, capacity, width)
        dx = lax.dot_general(gate_grad, full_g[...], nt, preferred_element_type=F32)
        dx = dx + lax.dot_general(up_grad, full_u[...], nt, preferred_element_type=F32)
        dx_out[:, :, :width] = dx.astype(B16).reshape(pieces, capacity, width)
        grad_g[...] = lax.dot_general(x, gate_grad, tn, preferred_element_type=F32).astype(B16)
        grad_u[...] = lax.dot_general(x, up_grad, tn, preferred_element_type=F32).astype(B16)
        grad_d[...] = lax.dot_general(scaled, g, tn, preferred_element_type=F32).astype(B16)

        def give(ref, slot, j):
            ref[slot, 0, :in_rows] = grad_g[at_in(j), :]
            ref[slot, 0, in_rows : 2 * in_rows] = grad_u[at_in(j), :]
            for f in range(folds):
                ref[slot, 0, 2 * in_rows + f * mid_rows : 2 * in_rows + (f + 1) * mid_rows] = grad_d[
                    at_mid(j), f * eff : (f + 1) * eff
                ]

        if split:

            @pl.when(pl.program_id(0) < first_half)
            def _():
                for j in range(4):
                    give(outs[j], 0, j)

            @pl.when(pl.program_id(0) >= first_half)
            def _():
                for j in range(4):
                    give(outs[4 + j], 0, j)
        else:
            for j in range(n):
                give(outs[0], j, j)

    def single():
        return dict(pipeline_mode=pl.Buffered(1)) if large else {}

    def rows_spec(w):
        return pl.BlockSpec((half, capacity, w), lambda e, o: (0, e + start, 0), **single())

    in_specs = [rows_spec(width)] * 4 + [rows_spec(128)] * 2
    for _ in weights:
        in_specs.append(pl.BlockSpec((1, pack_rows, eff), lambda e, o: (e + start, 0, 0)))
    for part in extra:
        in_specs.append(pl.BlockSpec(part.shape, lambda e, o: (0, 0)))
    slots = count * capacity
    out_specs = [
        pl.BlockSpec((pieces, capacity, w), lambda e, o: (0, e, 0), **single())
        for w in (width, width + 128)
    ]
    out_shape = [
        jax.ShapeDtypeStruct((pieces, slots, width), B16),
        jax.ShapeDtypeStruct((pieces, slots, width + 128), B16),
    ]
    if split:
        for at in (
            lambda e, o: (0, jnp.minimum(e, first_half - 1), 0, 0),
            lambda e, o: (0, jnp.maximum(e - first_half, 0), 0, 0),
        ):
            for _ in range(4):
                out_specs.append(pl.BlockSpec((1, 1, pack_rows, eff), at))
                out_shape.append(jax.ShapeDtypeStruct((1, first_half, pack_rows, eff), B16))
    else:
        out_specs.append(pl.BlockSpec((n, 1, pack_rows, eff), lambda e, o: (0, e, 0, 0)))
        out_shape.append(jax.ShapeDtypeStruct((n, count, pack_rows, eff), B16))
    results = pl.pallas_call(
        kernel,
        out_shape=out_shape,
        grid_spec=pltpu.PrefetchScalarGridSpec(
            num_scalar_prefetch=1,
            grid=(count,),
            in_specs=in_specs,
            out_specs=out_specs,
            scratch_shapes=[
                pltpu.VMEM((n * in_rows, eff), B16),
                pltpu.VMEM((n * in_rows, eff), B16),
                pltpu.VMEM((n * mid_rows, width), B16),
                pltpu.VMEM((n * in_rows, eff), B16),
                pltpu.VMEM((n * in_rows, eff), B16),
                pltpu.VMEM((n * mid_rows, width), B16),
            ],
        ),
        compiler_params=pltpu.CompilerParams(vmem_limit_bytes=VMEM_LIMIT),
        name="experts",
    )(order, *rows, *grads, *gates, *weights, *extra)
    return results[0], results[1], results[2:]


NT = (((1,), (1,)), ((), ()))
TN = (((0,), (0,)), ((), ()))
GROUPS = KVH // 2
EXTRA = 128


def turn(vectors, cosine, sine):
    lane = lax.broadcasted_iota(jnp.int32, vectors.shape, 1)
    ahead = pltpu.roll(vectors, 2 * HD - HD // 2, 1)
    behind = pltpu.roll(vectors, HD // 2, 1)
    return vectors * cosine + jnp.where(lane % HD < HD // 2, ahead, behind) * sine


def turn_tables(places):
    lane = jnp.arange(2 * HD, dtype=jnp.int32)
    frequency = jnp.exp(
        (lane % (HD // 2)).astype(F32) * (-2.0 * math.log(ROPE_BASE) / HD)
    )
    angles = places[:, None] * frequency[None, :]
    sign = jnp.where(lane % HD < HD // 2, -1.0, 1.0)
    return jnp.cos(angles), jnp.sin(angles) * sign[None, :]


def attention_forward(x_own, x_parts, dense_full, bias, cosine, sine, routed):
    tok_rows, width = x_own.shape
    seq_len = 4 * tok_rows
    scale = HD ** (-0.5)
    wide, narrow = H * HD, KVH * HD

    def kernel(
        own_ref, xa_ref, xb_ref, ya_ref, yb_ref, da_ref, db_ref, ea_ref, eb_ref,
        tail_ref, wo_ref, wq_ref, wk_ref, wv_ref, bias_ref, cos_ref, sin_ref, routed_ref,
        x_ref, normed_ref, q_out, k_out, v_out, att_out, total_out, misc_out, residual_out, moe_out,
        gates_out,
    ):
        step = pl.program_id(0)

        @pl.when(step == 0)
        def _():
            rows = jnp.transpose(tail_ref[...].astype(F32))
            misc_out[...] = rows
            at = 0
            for ref in (own_ref, xa_ref, xb_ref, ya_ref, yb_ref, da_ref, ea_ref, db_ref, eb_ref):
                x_ref[at : at + ref.shape[0], :] = ref[...]
                at += ref.shape[0]
            x = x_ref[...].astype(F32)
            scaled = x * lax.rsqrt(jnp.mean(x * x, axis=1, keepdims=True) + EPSILON)
            normed_ref[...] = (scaled * rows[EXPERTS : EXPERTS + 1, :]).astype(B16)
            residual_out[...] = x[:tok_rows]

        normed = normed_ref[...]
        cos, sin = cos_ref[...], sin_ref[...]
        key = turn(jnp.dot(normed, wk_ref[...], preferred_element_type=F32), cos, sin).astype(B16)
        value = jnp.dot(normed, wv_ref[...], preferred_element_type=F32).astype(B16)
        query = jnp.dot(normed[:tok_rows], wq_ref[...], preferred_element_type=F32)
        cos, sin = cos[:tok_rows], sin[:tok_rows]
        query = jnp.concatenate(
            [turn(query[:, 128 * j : 128 * (j + 1)], cos, sin) for j in range(2)], axis=1
        )
        query = (query * scale).astype(B16)
        k_out[...] = key
        v_out[...] = value
        q_out[...] = query
        mixed, totals = [], []
        for j in range(4):
            lanes = slice(HD * (j // 2), HD * (j // 2 + 1))
            scores = lax.dot_general(
                key[:, lanes], query[:, HD * j : HD * (j + 1)], NT, preferred_element_type=F32
            )
            scores = scores + bias_ref[...]
            peak = jnp.max(scores, axis=0, keepdims=True)
            probs = jnp.exp(scores - peak)
            total = jnp.sum(probs, axis=0, keepdims=True)
            out = lax.dot_general(
                value[:, lanes], probs.astype(B16), TN, preferred_element_type=F32
            )
            mixed.append(out / total)
            totals.append(peak + jnp.log(total))
        attended = jnp.transpose(jnp.concatenate(mixed, axis=0)).astype(B16)
        att_out[...] = attended
        total_out[0] = jnp.concatenate(totals + totals, axis=0)
        residual_out[...] += jnp.dot(attended, wo_ref[...], preferred_element_type=F32)

        @pl.when(step == GROUPS - 1)
        def _():
            total = residual_out[...]
            scaled = total * lax.rsqrt(jnp.mean(total * total, axis=1, keepdims=True) + EPSILON)
            moe_in = (scaled * misc_out[EXPERTS + 1 : EXPERTS + 2, :]).astype(B16)
            moe_out[...] = moe_in
            logits = jnp.dot(moe_in, tail_ref[...], preferred_element_type=F32)
            here = routed_ref[...] > 0.0
            peak = jnp.max(jnp.where(here, logits, MASKED_SCORE), axis=1, keepdims=True)
            lifted = jnp.where(here, jnp.exp(jnp.minimum(logits - peak, 0.0)), 0.0)
            gates_out[...] = lifted / jnp.sum(lifted, axis=1, keepdims=True)

    def fixed(*block):
        return pl.BlockSpec(block, lambda i: (0,) * len(block))

    def columns(rows, cols, lead=0):
        return pl.BlockSpec((rows, cols), lambda i: (0, lead + i))

    return pl.pallas_call(
        kernel,
        grid=(GROUPS,),
        in_specs=[
            fixed(tok_rows, width),
            *[
                pl.BlockSpec((part.shape[0], width), lambda i, c=c: (0, c))
                for part in x_parts
                for c in range(2)
            ],
            pl.BlockSpec((width, 128), lambda i: (0, (width + wide + 2 * narrow) // 128)),
            pl.BlockSpec((256, width), lambda i: (i, 0)),
            columns(width, 256, width // 256),
            columns(width, 128, (width + wide) // 128),
            columns(width, 128, (width + wide + narrow) // 128),
            fixed(seq_len, tok_rows),
            fixed(seq_len, 128),
            fixed(seq_len, 128),
            fixed(tok_rows, 128),
        ],
        out_specs=[
            fixed(seq_len, width),
            fixed(seq_len, width),
            columns(tok_rows, 256),
            columns(seq_len, 128),
            columns(seq_len, 128),
            columns(tok_rows, 256),
            pl.BlockSpec((1, 8, tok_rows), lambda i: (i, 0, 0)),
            fixed(128, width),
            fixed(tok_rows, width),
            fixed(tok_rows, width),
            fixed(tok_rows, 128),
        ],
        out_shape=[
            jax.ShapeDtypeStruct((seq_len, width), B16),
            jax.ShapeDtypeStruct((seq_len, width), B16),
            jax.ShapeDtypeStruct((tok_rows, wide), B16),
            jax.ShapeDtypeStruct((seq_len, narrow), B16),
            jax.ShapeDtypeStruct((seq_len, narrow), B16),
            jax.ShapeDtypeStruct((tok_rows, wide), B16),
            jax.ShapeDtypeStruct((GROUPS, 8, tok_rows), F32),
            jax.ShapeDtypeStruct((128, width), F32),
            jax.ShapeDtypeStruct((tok_rows, width), F32),
            jax.ShapeDtypeStruct((tok_rows, width), B16),
            jax.ShapeDtypeStruct((tok_rows, 128), F32),
        ],
        compiler_params=pltpu.CompilerParams(vmem_limit_bytes=VMEM_LIMIT),
        name="attention",
    )(
        x_own, *[part for part in x_parts for _ in range(2)], *[dense_full] * 5,
        bias, cosine, sine, routed,
    )


def attention_backward(
    where_here, moe_sums, out_grad, residual, gates, misc, attended, moe_in, saved,
    dense_full, bias, cosine, sine,
):
    x_all, normed_all, query_rot, key_rot, value_all, totals = saved
    terms = len(moe_sums)
    seq_len, width = x_all.shape
    tok_rows = query_rot.shape[0]
    scale = HD ** (-0.5)
    wide, narrow = H * HD, KVH * HD
    block = width // 8
    output_at = wide + 2 * narrow

    def kernel(here_ref, *refs):
        sums = refs[:terms]
        (
            grad_ref, residual_ref, gates_ref, misc_ref, tail_ref, wo_ref, att_ref, moe_ref,
            normed_ref, q_ref, k_ref, v_ref, total_ref,
            x_ref, wq_ref, wk_ref, wv_ref, bias_ref, cos_ref, sin_ref,
            keep_out, give_out, first_a_out, first_b_out, rest_a_out, rest_b_out, residual_out,
            normed_t, grad_sum, og_ref, logit_ref, gain_ref,
        ) = refs[terms:]
        step = pl.program_id(0)
        dp, core = here_ref[0], here_ref[1]

        @pl.when(step == 0)
        def _():
            normed_t[...] = jnp.transpose(normed_ref[...])
            grad_sum[...] = jnp.zeros((seq_len, width), F32)
            total = sums[0][...].astype(F32)
            for ref in sums[1:]:
                total = total + ref[...].astype(F32)
            behind = total[:, width:]
            gate_grad = behind + pltpu.roll(behind, 128 - EXPERTS, 1)
            gate = gates_ref[...]
            centre = jnp.sum(gate * gate_grad, axis=1, keepdims=True)
            logit_low = (gate * (gate_grad - centre)).astype(B16)
            logit_ref[...] = logit_low
            moe_grad = total[:, :width] + lax.dot_general(
                logit_low, tail_ref[...], NT, preferred_element_type=F32
            )
            residual = residual_ref[...]
            rate = lax.rsqrt(jnp.mean(residual * residual, axis=1, keepdims=True) + EPSILON)
            gain_ref[...] = jnp.sum(moe_grad * residual * rate, axis=0, keepdims=True)
            lifted = moe_grad * misc_ref[EXPERTS + 1 : EXPERTS + 2, :]
            inner = jnp.mean(lifted * residual, axis=1, keepdims=True)
            residual_grad = (
                grad_ref[...].astype(F32) + rate * lifted - residual * (rate * rate * rate * inner)
            )
            residual_out[...] = residual_grad
            og_ref[...] = residual_grad.astype(B16)

        og = og_ref[...]
        att_grad = lax.dot_general(og, wo_ref[...], NT, preferred_element_type=F32).astype(B16)
        query, key, value = q_ref[...], k_ref[...], v_ref[...]
        query_grads, key_grads, value_grads = [], [], []
        for j in range(4):
            lanes = slice(HD * (j // 2), HD * (j // 2 + 1))
            mine = slice(HD * j, HD * (j + 1))
            scores = lax.dot_general(
                key[:, lanes], query[:, mine], NT, preferred_element_type=F32
            )
            probs = jnp.exp(scores + bias_ref[...] - total_ref[0, j : j + 1, :])
            probs_grad = lax.dot_general(
                value[:, lanes], att_grad[:, mine], NT, preferred_element_type=F32
            )
            delta = jnp.sum(probs * probs_grad, axis=0, keepdims=True)
            score_grad = (probs * (probs_grad - delta)).astype(B16)
            query_grads.append(
                lax.dot_general(key[:, lanes], score_grad, TN, preferred_element_type=F32)
            )
            key_part = jnp.dot(score_grad, query[:, mine], preferred_element_type=F32)
            value_part = jnp.dot(probs.astype(B16), att_grad[:, mine], preferred_element_type=F32)
            if j % 2 == 0:
                key_grads.append(key_part)
                value_grads.append(value_part)
            else:
                key_grads[-1] = key_grads[-1] + key_part
                value_grads[-1] = value_grads[-1] + value_part
        cos, sin = cos_ref[...], -sin_ref[...]
        kv_grad = jnp.concatenate(
            [turn(jnp.concatenate(key_grads, axis=1), cos, sin)] + value_grads, axis=1
        ).astype(B16)
        cos, sin = cos[:tok_rows], sin[:tok_rows]
        query_grad = jnp.transpose(jnp.concatenate(query_grads, axis=0)) * scale
        query_grad = jnp.concatenate(
            [turn(query_grad[:, 128 * j : 128 * (j + 1)], cos, sin) for j in range(2)], axis=1
        ).astype(B16)

        def put(at, lanes, rows):
            for c in range(2):

                @pl.when(core == c)
                def _():
                    keep_out[at, :, lanes] = rows[c].astype(B16)
                    give_out[at, :, lanes] = rows[1 - c].astype(B16)

        def give(grad, lanes):
            for m in range(4):
                put(
                    dp ^ m,
                    lanes,
                    [grad[(2 * m + c) * block : (2 * m + c + 1) * block] for c in range(2)],
                )

        give(
            jnp.dot(normed_t[:, :tok_rows], query_grad, preferred_element_type=F32),
            pl.ds(pl.multiple_of(step * 256, 256), 256),
        )
        give(
            jnp.dot(normed_t[...], kv_grad, preferred_element_type=F32),
            pl.ds(pl.multiple_of(wide + step * 256, 256), 256),
        )
        out_part = lax.dot_general(att_ref[...], og, TN, preferred_element_type=F32).astype(B16)
        put(dp ^ step, slice(output_at, output_at + width), [out_part[:block], out_part[block:]])
        kv_weights = jnp.concatenate([wk_ref[...], wv_ref[...]], axis=1)
        grad_sum[...] += lax.dot_general(kv_grad, kv_weights, NT, preferred_element_type=F32)
        grad_sum[:tok_rows, :] += lax.dot_general(
            query_grad, wq_ref[...], NT, preferred_element_type=F32
        )

        @pl.when(step == GROUPS - 1)
        def _():
            total = grad_sum[...]
            low = total.astype(B16)
            half = tok_rows // 2
            first_a_out[0] = low[tok_rows : tok_rows + half]
            first_a_out[1] = low[3 * tok_rows : 3 * tok_rows + half]
            first_b_out[0] = low[2 * tok_rows + half : 3 * tok_rows]
            first_b_out[1] = low[3 * tok_rows + half :]
            rest_a_out[0] = low[:half]
            rest_a_out[1] = low[2 * tok_rows : 2 * tok_rows + half]
            rest_b_out[0] = low[half:tok_rows]
            rest_b_out[1] = low[tok_rows + half : 2 * tok_rows]
            x = x_ref[...].astype(F32)
            lifted = x * lax.rsqrt(jnp.mean(x * x, axis=1, keepdims=True) + EPSILON)
            gain = jnp.sum(total * lifted, axis=0, keepdims=True)
            row = lax.broadcasted_iota(jnp.int32, (EXTRA, width), 0)
            gains = jnp.where(
                row == EXPERTS, gain, jnp.where(row == EXPERTS + 1, gain_ref[...], 0.0)
            )
            extra = lax.dot_general(
                moe_ref[...], logit_ref[...], TN, preferred_element_type=F32
            ) + jnp.transpose(gains)
            give(extra, slice(output_at + width, output_at + width + EXTRA))

    def fixed(*shape):
        return pl.BlockSpec(shape, lambda i, here: (0,) * len(shape))

    def columns(rows, cols, lead=0):
        return pl.BlockSpec((rows, cols), lambda i, here: (0, lead + i))

    shapes = [
        *[jax.ShapeDtypeStruct((4, block, output_at + width + EXTRA), B16)] * 2,
        *[jax.ShapeDtypeStruct((2, tok_rows // 2, width), B16)] * 4,
        jax.ShapeDtypeStruct((tok_rows, width), F32),
    ]
    keep, give, *parts, residual_grad = pl.pallas_call(
        kernel,
        out_shape=shapes,
        grid_spec=pltpu.PrefetchScalarGridSpec(
            num_scalar_prefetch=1,
            grid=(GROUPS,),
            in_specs=[
                *[fixed(tok_rows, width + 128)] * terms,
                fixed(tok_rows, width),
                fixed(tok_rows, width),
                fixed(tok_rows, 128),
                fixed(128, width),
                pl.BlockSpec(
                    (width, 128), lambda i, here: (0, (width + wide + 2 * narrow) // 128)
                ),
                pl.BlockSpec((256, width), lambda i, here: (i, 0)),
                columns(tok_rows, 256),
                fixed(tok_rows, width),
                fixed(seq_len, width),
                columns(tok_rows, 256),
                columns(seq_len, 128),
                columns(seq_len, 128),
                pl.BlockSpec((1, 8, tok_rows), lambda i, here: (i, 0, 0)),
                fixed(seq_len, width),
                columns(width, 256, width // 256),
                columns(width, 128, (width + wide) // 128),
                columns(width, 128, (width + wide + narrow) // 128),
                fixed(seq_len, tok_rows),
                fixed(seq_len, 128),
                fixed(seq_len, 128),
            ],
            out_specs=[fixed(*shape.shape) for shape in shapes],
            scratch_shapes=[
                pltpu.VMEM((width, seq_len), B16),
                pltpu.VMEM((seq_len, width), F32),
                pltpu.VMEM((tok_rows, width), B16),
                pltpu.VMEM((tok_rows, EXTRA), B16),
                pltpu.VMEM((1, width), F32),
            ],
        ),
        compiler_params=pltpu.CompilerParams(vmem_limit_bytes=VMEM_LIMIT),
        name="attention_grad",
    )(
        where_here, *moe_sums, out_grad, residual, gates, misc, dense_full, dense_full, attended,
        moe_in, normed_all, query_rot, key_rot, value_all, totals,
        x_all, dense_full, dense_full, dense_full, bias, cosine, sine,
    )
    return keep, give, tuple(parts[:2]), parts[2], parts[3], residual_grad


def core_halves(keep, got, hold):
    _, rows, cols = keep.shape
    half = rows // 2
    keep = after(keep, hold)

    def kernel(keep_ref, got_ref, first_a, first_b, rest_a, rest_b):
        def total(j, lo):
            mine = keep_ref[j, lo : lo + half, :].astype(F32)
            return (mine + got_ref[j, lo : lo + half, :].astype(F32)).astype(B16)

        first_a[0], first_a[1] = total(1, 0), total(3, 0)
        first_b[0], first_b[1] = total(2, half), total(3, half)
        rest_a[0], rest_a[1] = total(0, 0), total(2, 0)
        rest_b[0], rest_b[1] = total(0, half), total(1, half)

    step = cols // 5
    first_a, first_b, rest_a, rest_b = pl.pallas_call(
        kernel,
        grid=(5,),
        in_specs=[pl.BlockSpec((4, rows, step), lambda i: (0, 0, i))] * 2,
        out_specs=[pl.BlockSpec((2, half, step), lambda i: (0, 0, i))] * 4,
        out_shape=[jax.ShapeDtypeStruct((2, half, cols), B16)] * 4,
        compiler_params=pltpu.CompilerParams(vmem_limit_bytes=VMEM_LIMIT),
        name="core_halves",
    )(keep, got)
    return (first_a, first_b), rest_a, rest_b


def dense_outputs(core, mine, other, wide, narrow):
    rows, cols = mine.shape
    at = wide + 2 * narrow
    shapes = [(2 * rows, wide), (2 * rows, narrow), (2 * rows, narrow), (2 * rows, cols - at - EXTRA)]
    shapes.append((2 * rows, EXTRA))

    def kernel(core_ref, mine_ref, other_ref, query, key, value, output, extra):
        for c in range(2):
            for ref, side in ((mine_ref, c), (other_ref, 1 - c)):

                @pl.when(core_ref[0] == c)
                def _():
                    lines = slice(side * rows, (side + 1) * rows)
                    query[lines, :] = ref[:, :wide].astype(F32)
                    for i in range(GROUPS):
                        lead = wide + 256 * i
                        lanes = slice(128 * i, 128 * (i + 1))
                        key[lines, lanes] = ref[:, lead : lead + 128].astype(F32)
                        value[lines, lanes] = ref[:, lead + 128 : lead + 256].astype(F32)
                    output[lines, :] = ref[:, at : cols - EXTRA].astype(F32)
                    extra[lines, :] = ref[:, cols - EXTRA :].astype(F32)

    def fixed(shape):
        return pl.BlockSpec(shape, lambda i, core: (0, 0))

    query, key, value, output, extra = pl.pallas_call(
        kernel,
        out_shape=[jax.ShapeDtypeStruct(shape, F32) for shape in shapes],
        grid_spec=pltpu.PrefetchScalarGridSpec(
            num_scalar_prefetch=1,
            grid=(1,),
            in_specs=[fixed(mine.shape)] * 2,
            out_specs=[fixed(shape) for shape in shapes],
        ),
        compiler_params=pltpu.CompilerParams(vmem_limit_bytes=VMEM_LIMIT),
        name="dense_outputs",
    )(core.astype(jnp.int32)[None], mine, other)
    return query, key, value, output, extra[:, :EXPERTS], extra[:, EXPERTS], extra[:, EXPERTS + 1]


def make_body(z_size, small_grid):
    def core_half(shard, core):
        rows = shard.shape[0] // 2
        return lax.dynamic_slice_in_dim(shard, core * rows, rows, 0)

    def dense_assemble(shard, parts, dp_index, core, *hold):
        rows = shard.shape[0] // 2
        moved = after(jnp.concatenate(parts, axis=0), *hold)
        other = swap_core(moved)
        places = [2 * dp_index]
        for which in (core, 1 - core):
            places += [2 * (dp_index ^ (j + 1)) + which for j in range(3)]
        return assemble(jnp.stack(places), shard, moved, other, rows)

    def across_z(mine, z):
        if z_size != 4:
            return lax.psum(mine.astype(F32), "z").astype(B16)
        rows = mine.shape[0] // z_size
        low = mine.astype(B16)
        total = lax.dynamic_slice_in_dim(mine, z * rows, rows, 0)
        for k in range(1, z_size):
            theirs = lax.dynamic_slice_in_dim(low, (z + k) % z_size * rows, rows, 0)
            total = total + cyclic(theirs, z_size, k).astype(F32)
        total = total.astype(B16)
        quarters = [total] + [cyclic(total, z_size, -k) for k in range(1, z_size)]
        places = (jnp.arange(z_size, dtype=jnp.int32) - z) % z_size
        return jnp.take(jnp.stack(quarters), places, axis=0).reshape(mine.shape)

    def dense_sum(grads):
        return lax.psum_scatter(
            lax.psum(grads, ("z", "core")), ("y", "x"), scatter_dimension=0, tiled=True
        )

    def body(
        layer_input,
        attn_gain,
        w_query,
        w_key,
        w_value,
        w_output,
        moe_gain,
        w_router,
        w_gate,
        w_up,
        w_down,
        routes,
        priority,
        prefix_len,
        out_grad,
    ):
        tok_rows, model_width = layer_input.shape
        dp_size = lax.axis_size("y") * lax.axis_size("x")
        dp_index = lax.axis_index("y") * lax.axis_size("x") + lax.axis_index("x")
        z = lax.axis_index("z")
        core = lax.axis_index("core")
        seq_len = tok_rows * dp_size
        top_count = routes.shape[1]
        local = w_gate.shape[0]
        capacity = 5 * tok_rows * top_count // (4 * EXPERTS)
        group_size = H // KVH
        score_scale = HD ** (-0.5)

        gains = jnp.stack([attn_gain, moe_gain], axis=1)
        rows = w_query.shape[0]
        dense_pack = jnp.concatenate(
            [w_output, w_query, w_key, w_value, w_router, gains, jnp.zeros((rows, 94), B16)], axis=1
        )
        wide = H * HD
        narrow = KVH * HD
        expert_ids = jnp.arange(EXPERTS, dtype=jnp.int32)
        hits = routes[:, :, None] == expert_ids[None, None, :]
        routed = jnp.any(hits, axis=1)
        place = jnp.where(
            routed, jnp.sum(jnp.where(hits, priority[:, :, None], 0), axis=1), jnp.int32(1 << 20)
        )
        ranks = jnp.sum((place[:, :, None] < place.T[None, :, :]).astype(F32), axis=0)
        code = pack_code(jnp.where(routed.T, ranks, -1.0).astype(B16))
        lead = ((2 * z + core) * local).astype(jnp.int32)[None]
        grad_pieces = column_pieces(jnp.concatenate([out_grad, code], axis=0), z_size)

        if small_grid:
            side = tok_rows // 2
            x_pack = jnp.concatenate([layer_input[:side], layer_input[side:]], axis=1)
            start_parts = gather_near(jnp.concatenate([x_pack, core_half(dense_pack, core)], axis=1))
            start_parts += gather_far(after(start_parts, *grad_pieces[1::2]))
            dense_parts = [part[:, 2 * model_width :] for part in start_parts]
            dense_full = dense_assemble(dense_pack, dense_parts, dp_index, core)
        else:
            dense_full = lax.all_gather(dense_pack, ("y", "x"), axis=0, tiled=True)
            full_output = dense_full[:, :model_width]
            head_full = dense_full[:, model_width:]
            full_query = head_full[:, :wide]
            full_key = head_full[:, wide : wide + narrow]
            full_value = head_full[:, wide + narrow : wide + 2 * narrow]

        query_pos = dp_index * tok_rows + jnp.arange(tok_rows, dtype=jnp.int32)
        in_float = layer_input.astype(F32)
        steps = jnp.arange(tok_rows, dtype=jnp.int32)
        eff = w_gate.shape[2]
        in_rows, mid_rows = w_gate.shape[1], w_down.shape[1]
        folds = [w_down[:, :, f * eff : (f + 1) * eff] for f in range(model_width // eff)]
        pack = jnp.concatenate([w_gate, w_up, *folds], axis=1)
        if small_grid:
            relative = dp_index ^ jnp.arange(4, dtype=jnp.int32)
            key_pos = (relative[:, None] * tok_rows + steps[None, :]).reshape(seq_len)
            halves, per = 2, local // 2
            weights = [pack]
            near_0 = gather_near(after(pack[0], *start_parts[2:]))
            far_0 = gather_far(after(near_0, dense_full))
            near_1 = gather_near(after(pack[1], *near_0, dense_full))
        else:
            relative = jnp.arange(dp_size, dtype=jnp.int32)
            key_pos = jnp.arange(seq_len, dtype=jnp.int32)
            halves, per = 1, local
            every = lax.all_gather(pack, ("y", "x"), axis=0, tiled=False)
            weights = [every[j] for j in range(dp_size)]
            near_0 = ()
        order = jnp.concatenate([relative, lead])
        visible = (key_pos[None, :] <= query_pos[:, None]) | (key_pos[None, :] < prefix_len[0])
        chunks = []
        if small_grid:
            bias = after(jnp.where(visible.T, 0.0, MASKED_SCORE), *near_0)
            cosine, sine = turn_tables(key_pos.astype(F32))
            (
                x_all, normed_all, query_rot, key_rot, value_all, attended, totals, misc, residual,
                moe_in, gates,
            ) = attention_forward(
                layer_input,
                start_parts,
                dense_full,
                bias,
                cosine,
                sine,
                jnp.pad(routed.astype(F32), ((0, 0), (0, 128 - EXPERTS))),
            )
            moe_in = after(moe_in, *near_1, *far_0)
            router_rows = misc[:EXPERTS].astype(B16)
            full_attn_gain = misc[EXPERTS]
            full_moe_gain = misc[EXPERTS + 1]
        else:
            places = query_pos.astype(F32)
            router_rows = head_full[:, wide + 2 * narrow : wide + 2 * narrow + EXPERTS].T
            full_attn_gain = head_full[:, wide + 2 * narrow + EXPERTS].astype(F32)
            full_moe_gain = head_full[:, wide + 2 * narrow + EXPERTS + 1].astype(F32)
            normed = rms_norm(in_float, full_attn_gain).astype(B16)
            query_lin = jnp.dot(normed, full_query, preferred_element_type=F32)
            key_lin = jnp.dot(normed, full_key, preferred_element_type=F32)
            value_low = jnp.dot(normed, full_value, preferred_element_type=F32).astype(B16)
            query_rot = (rotate(query_lin.reshape(tok_rows, H, HD), places) * score_scale).astype(B16)
            key_rot = rotate(key_lin.reshape(tok_rows, KVH, HD), places).astype(B16)
            key_rot = key_rot.reshape(tok_rows, narrow)
            both = jnp.concatenate([key_rot, value_low], axis=1)
            both_all = lax.all_gather(both, ("y", "x"), axis=0, tiled=True)
            key_all = both_all[:, :narrow]
            value_all = both_all[:, narrow:]

            def head_scores(head_idx):
                query_head = query_rot[:, head_idx * group_size : (head_idx + 1) * group_size, :]
                key_head = key_all[:, head_idx * HD : (head_idx + 1) * HD]
                scores = jnp.einsum("qgd,kd->gqk", query_head, key_head, preferred_element_type=F32)
                return jnp.where(visible[None, :, :], scores, MASKED_SCORE)

            mixed_heads = []
            log_totals = []
            for head_idx in range(KVH):
                scores = head_scores(head_idx)
                row_max = jnp.max(scores, axis=-1, keepdims=True)
                log_total = row_max + jnp.log(
                    jnp.sum(jnp.exp(scores - row_max), axis=-1, keepdims=True)
                )
                probs_low = jnp.exp(scores - log_total).astype(B16)
                value_head = value_all[:, head_idx * HD : (head_idx + 1) * HD]
                mixed_heads.append(
                    jnp.einsum("gqk,kd->qgd", probs_low, value_head, preferred_element_type=F32)
                )
                log_totals.append(log_total)
            attended = jnp.concatenate(mixed_heads, axis=1).reshape(tok_rows, wide).astype(B16)
            residual = in_float + jnp.dot(attended, full_output, preferred_element_type=F32)
            moe_in = rms_norm(residual, full_moe_gain).astype(B16)

        row_pieces = column_pieces(moe_in, z_size)
        grads_mine = jnp.stack(after(grad_pieces, moe_in))
        grads_other = swap_core(grads_mine)
        stage_1 = stage_2 = last_far = ()
        if small_grid:
            middle = pack.shape[1] // 2
            stage_1 = far_and_next(after(near_1, moe_in), pack[2])
        (slot_grads_mine,) = dispatch_rows(lead, grads_mine, None, None, local, capacity)
        (slot_grads_other,) = dispatch_rows(
            lead,
            after(grads_other, slot_grads_mine, *stage_1, row_pieces[1], row_pieces[-1]),
            None,
            None,
            local,
            capacity,
        )
        if small_grid:
            stage_2 = far_and_next(after(stage_1, slot_grads_other), pack[3])
            last_far = gather_far([part[middle:] for part in stage_2])
            chunks = [
                [(part, 0) for part in [*near_0, *far_0]],
                [(part, 0) for part in [*near_1, *stage_1[::-1]]],
                [(part, middle) for part in stage_1] + [(part, 0) for part in stage_2[::-1]],
                [(part, middle) for part in stage_2] + [(part, 0) for part in last_far],
            ]
        row_pieces = after(row_pieces, slot_grads_other)
        rows_mine = after(row_pieces, *stage_2)
        rows_other = [swap_core(piece) for piece in row_pieces]
        slot_rows_mine, slot_gates_mine = dispatch_rows(
            lead, grads_mine, rows_mine, router_rows, local, capacity
        )
        slot_rows_other, slot_gates_other = dispatch_rows(
            lead, grads_other, after(rows_other, slot_rows_mine), router_rows, local, capacity
        )
        slot_rows_other = after(slot_rows_other, *last_far)
        ys, dxs, weight_grads, sums = [], [], [], []
        for half in range(halves):
            y, dx, grads = experts(
                order,
                half * per,
                per,
                (slot_rows_mine, slot_rows_other),
                (slot_grads_mine, slot_grads_other),
                (slot_gates_mine, slot_gates_other),
                weights,
                chunks[half * per : (half + 1) * per],
                capacity,
                in_rows,
                mid_rows,
            )
            ys.append(y)
            dxs.append(dx)
            weight_grads.append(grads)

        def grid_sum(grads, got):
            totals = []
            for half in range(2):
                own = grads[4 * half][0]
                direct, last = got[half][0], got[1 - half][1]
                totals.append(own.astype(F32) + direct.astype(F32) + last.astype(F32))
            return totals

        def second_step(grads, via, *more):
            _, x_a, y_a, _, _, x_b, y_b, _ = grads
            to_x = [x_a, plus_low(x_b, via[1])]
            to_y = [y_b, plus_low(y_a, via[0])]
            if more:
                to_x.append(more[0])
                to_y.append(more[1])
            return cross(jnp.concatenate(to_x, axis=0), jnp.concatenate(to_y, axis=0))

        if small_grid:
            early, late = weight_grads
            via = cross(early[3], early[7])
            dxs = after(dxs, *via)
            early_got = second_step(early, via, late[3], late[7])
        dx_other = swap_core(combine_rows(lead, z_size, grads_other, dxs, local, capacity))
        dx_low = combine_rows(lead, 0, grads_mine, dxs, local, capacity, dx_other)
        dx_pieces = column_send_some(dx_low, z_size) + column_send_last(dx_low, z_size)
        y_other = combine_rows(lead, z_size, grads_other, after(ys, dx_low), local, capacity)
        dx_pieces, y_other = after((dx_pieces, y_other), y_other, *dx_pieces)
        y_other = swap_core(y_other)
        if small_grid:
            early_got = after(early_got, *dx_pieces)
            late_got = second_step(late, [got[2:3] for got in early_got])
        if small_grid:
            keep, give, normed_first, normed_a, normed_b, residual_grad = attention_backward(
                jnp.stack([dp_index, core]).astype(jnp.int32),
                (dx_low[0], *dx_pieces),
                out_grad,
                residual,
                gates,
                misc,
                attended,
                moe_in,
                (x_all, normed_all, query_rot, key_rot, value_all, totals),
                dense_full,
                after(bias, *early_got),
                cosine,
                sine,
            )
            late_got, y_other = after((late_got, y_other), residual_grad)
            normed_first, keep, give = after((normed_first, keep, give), *late_got, y_other)
            y_low = combine_rows(lead, 0, grads_mine, ys, local, capacity, y_other)
            y_pieces = column_send_some(y_low, z_size)
            y_pieces += column_send_last(y_low, z_size, *y_pieces)
            dense_first, dense_a, dense_b = core_halves(keep, swap_core(give), y_low[0])
            normed_got = grid_scatter_first(*normed_first)
            dense_got = grid_scatter_first(*after(dense_first, *normed_got))
            dense_low = across_z(
                jnp.concatenate(grid_scatter_second(dense_got, dense_a, dense_b), axis=0), z
            )
            (
                query_sum, key_sum, value_sum, output_sum, router_sum, attn_gain_sum, moe_gain_sum,
            ) = dense_outputs(core, dense_low, swap_core(dense_low), wide, narrow)
            y_pieces = after(y_pieces, query_sum)
            normed_grad = jnp.concatenate(
                grid_scatter_second(normed_got, normed_a, normed_b, *dense_got), axis=0
            )
            first_value, first_pull = jax.vjp(lambda v: rms_norm(v, full_attn_gain), in_float)
            input_grad = residual_grad + first_pull(normed_grad)[0]
        else:
            y_low = combine_rows(lead, 0, grads_mine, ys, local, capacity, y_other)
            y_pieces = column_send_some(y_low, z_size) + column_send_last(y_low, z_size)
            moe_sum = column_sum(dx_low[0], dx_pieces)
            moe_in_grad = moe_sum[:, :model_width]
            gate_grad = (
                moe_sum[:, model_width : model_width + EXPERTS]
                + moe_sum[:, model_width + EXPERTS : model_width + 2 * EXPERTS]
            )
            logits = lax.dot_general(moe_in, router_rows, NT, preferred_element_type=F32)
            peak = jnp.max(jnp.where(routed, logits, MASKED_SCORE), axis=-1, keepdims=True)
            lifted = jnp.where(routed, jnp.exp(jnp.minimum(logits - peak, 0.0)), 0.0)
            gate_weights = lifted / jnp.sum(lifted, axis=-1, keepdims=True)
            grad_out = out_grad.astype(F32)
            centre = jnp.sum(gate_weights * gate_grad, axis=-1, keepdims=True)
            logit_low = (gate_weights * (gate_grad - centre)).astype(B16)
            moe_in_grad = moe_in_grad + jnp.dot(logit_low, router_rows, preferred_element_type=F32)
            norm_value, second_pull = jax.vjp(rms_norm, residual, full_moe_gain)
            resid_norm_grad, moe_gain_grad = second_pull(moe_in_grad)
            residual_grad = grad_out + resid_norm_grad
            attn_out_grad = residual_grad.astype(B16)
            router_grad = jnp.einsum("td,te->de", moe_in, logit_low, preferred_element_type=F32)
            wout_grad = jnp.einsum("tc,td->cd", attended, attn_out_grad, preferred_element_type=F32)
            attended_grad = (
                jnp.einsum("td,cd->tc", attn_out_grad, full_output, preferred_element_type=F32)
                .astype(B16)
                .reshape(tok_rows, H, HD)
            )
            query_grads = []
            key_parts = []
            value_parts = []
            for head_idx in range(KVH):
                scores = head_scores(head_idx)
                attention_probs = jnp.exp(scores - log_totals[head_idx])
                probs_low = attention_probs.astype(B16)
                grad_head = attended_grad[:, head_idx * group_size : (head_idx + 1) * group_size, :]
                query_head = query_rot[:, head_idx * group_size : (head_idx + 1) * group_size, :]
                key_head = key_all[:, head_idx * HD : (head_idx + 1) * HD]
                value_head = value_all[:, head_idx * HD : (head_idx + 1) * HD]
                probs_grad = jnp.einsum("qgd,kd->gqk", grad_head, value_head, preferred_element_type=F32)
                row_delta = jnp.sum(attention_probs * probs_grad, axis=-1, keepdims=True)
                score_grad = (attention_probs * (probs_grad - row_delta)).astype(B16)
                query_grads.append(
                    jnp.einsum("gqk,kd->qgd", score_grad, key_head, preferred_element_type=F32)
                )
                key_parts.append(
                    jnp.einsum("gqk,qgd->kd", score_grad, query_head, preferred_element_type=F32)
                )
                value_parts.append(
                    jnp.einsum("gqk,qgd->kd", probs_low, grad_head, preferred_element_type=F32)
                )
            both_part = jnp.concatenate(key_parts + value_parts, axis=1)
            both_sum = lax.psum_scatter(both_part, ("y", "x"), scatter_dimension=0, tiled=True)
            query_rot_grad = jnp.concatenate(query_grads, axis=1) * score_scale
            key_rot_grad = both_sum[:, :narrow].reshape(tok_rows, KVH, HD)
            value_grad = both_sum[:, narrow:].astype(B16)
            query_grad = rotate(query_rot_grad, -places).reshape(tok_rows, wide).astype(B16)
            key_grad = rotate(key_rot_grad, -places).reshape(tok_rows, narrow).astype(B16)
            wq_grad = jnp.einsum("td,tc->dc", normed, query_grad, preferred_element_type=F32)
            wk_grad = jnp.einsum("td,tc->dc", normed, key_grad, preferred_element_type=F32)
            wv_grad = jnp.einsum("td,tc->dc", normed, value_grad, preferred_element_type=F32)
            normed_grad = jnp.einsum("tc,dc->td", query_grad, full_query, preferred_element_type=F32)
            normed_grad = normed_grad + jnp.einsum(
                "tc,dc->td", key_grad, full_key, preferred_element_type=F32
            )
            normed_grad = normed_grad + jnp.einsum(
                "tc,dc->td", value_grad, full_value, preferred_element_type=F32
            )
            first_value, first_pull = jax.vjp(rms_norm, in_float, full_attn_gain)
            input_norm_grad, attn_gain_grad = first_pull(normed_grad)
            input_grad = residual_grad + input_norm_grad
            query_sum = dense_sum(wq_grad)
            key_sum = dense_sum(wk_grad)
            value_sum = dense_sum(wv_grad)
            output_sum = dense_sum(wout_grad)
            extra_sum = dense_sum(
                jnp.concatenate(
                    [
                        router_grad,
                        attn_gain_grad[:, None],
                        moe_gain_grad[:, None],
                        jnp.zeros((model_width, EXTRA - EXPERTS - 2), F32),
                    ],
                    axis=1,
                )
            )
            router_sum = extra_sum[:, :EXPERTS]
            attn_gain_sum = extra_sum[:, EXPERTS]
            moe_gain_sum = extra_sum[:, EXPERTS + 1]
        layer_output = (residual + column_sum(y_low[0], y_pieces)).astype(B16)
        if small_grid:
            parts = grid_sum(early, early_got) + grid_sum(late, late_got)
            pack_grad = jnp.concatenate(parts, axis=0)
        else:
            pack_grad = lax.psum_scatter(
                weight_grads[0][0].astype(F32), ("y", "x"), scatter_dimension=0, tiled=False
            )
        down = 2 * in_rows
        expert_grads = [
            pack_grad[:, :in_rows],
            pack_grad[:, in_rows:down],
            jnp.concatenate(
                [
                    pack_grad[:, down + f * mid_rows : down + (f + 1) * mid_rows]
                    for f in range(model_width // eff)
                ],
                axis=2,
            ),
        ]

        return (
            layer_output,
            input_grad,
            attn_gain_sum,
            query_sum,
            key_sum,
            value_sum,
            output_sum,
            moe_gain_sum,
            router_sum,
            expert_grads[0],
            expert_grads[1],
            expert_grads[2],
        )

    return body


def solution(mesh):
    groups = mesh.shape["expert"]
    members = mesh.shape["dp"]
    z_size = groups // 2
    side = math.isqrt(members)
    grid = Mesh(
        mesh.devices.reshape(z_size, 2, members // side, side), ("z", "core", "y", "x")
    )
    expert = ("z", "core")
    dp = ("y", "x")
    every = expert + dp
    placed = (
        P(every, None),
        P(dp),
        P(dp, None),
        P(dp, None),
        P(dp, None),
        P(dp, None),
        P(dp),
        P(dp, None),
        P(expert, dp, None),
        P(expert, dp, None),
        P(expert, dp, None),
        P(every, None),
        P(every, None),
        P(expert),
        P(every, None),
    )
    return jax.shard_map(
        make_body(z_size, members == 4 and side == 2 and EXPERTS == 4 * groups),
        mesh=grid,
        in_specs=placed,
        out_specs=(
            P(every, None),
            P(every, None),
            P(dp),
            P(dp, None),
            P(dp, None),
            P(dp, None),
            P(dp, None),
            P(dp),
            P(dp, None),
            P(expert, dp, None),
            P(expert, dp, None),
            P(expert, dp, None),
        ),
        check_vma=False,
    )
```

```python
import math

import jax
import jax.numpy as jnp
from jax import lax
from jax.experimental import pallas as pl
from jax.experimental.pallas import tpu as pltpu
from jax.sharding import Mesh
from jax.sharding import PartitionSpec as P

H = 16
KVH = 8
HD = 64
EXPERTS = 32
EPSILON = 1e-06
ROPE_BASE = 10000.0
MASKED_SCORE = -1e30
F32 = jnp.float32
B16 = jnp.bfloat16
SWAP = [(0, 1), (1, 0)]
VMEM_LIMIT = 60 * 1024 * 1024


def rms_norm(values, gain_vec):
    return (
        values * lax.rsqrt(jnp.mean(values * values, axis=-1, keepdims=True) + EPSILON) * gain_vec
    )


def rotate(vectors, places):
    half_dim = vectors.shape[-1] // 2
    frequency = jnp.exp(
        jnp.arange(half_dim, dtype=F32) * (-2.0 * math.log(ROPE_BASE) / vectors.shape[-1])
    )
    angles = places[:, None] * frequency[None, :]
    cosine = jnp.cos(angles)[:, None, :]
    sine_vals = jnp.sin(angles)[:, None, :]
    first_half = vectors[..., :half_dim]
    second = vectors[..., half_dim:]
    return jnp.concatenate(
        [first_half * cosine - second * sine_vals, second * cosine + first_half * sine_vals],
        axis=-1,
    )


def swap_core(rows):
    return lax.ppermute(rows, "core", SWAP)


def cyclic(rows, size, shift):
    return lax.ppermute(rows, "z", [(i, (i + shift) % size) for i in range(size)])


def after(value, *others):
    return lax.optimization_barrier((value, *others))[0]


def gather_near(shard):
    return [lax.ppermute(shard, "x", SWAP), lax.ppermute(shard, "y", SWAP)]


def gather_far(near):
    from_x, from_y = near
    half = from_x.shape[0] // 2
    return [lax.ppermute(from_x[:half], "y", SWAP), lax.ppermute(from_y[half:], "x", SWAP)]


def grid_gather(shard):
    near = gather_near(shard)
    return near + gather_far(near)


def cross(to_x, to_y):
    return lax.ppermute(to_x, "x", SWAP), lax.ppermute(to_y, "y", SWAP)


def far_and_next(near, shard):
    from_x, from_y = near
    half = shard.shape[0] // 2
    return cross(
        jnp.concatenate([from_y[-half:], shard], axis=0),
        jnp.concatenate([from_x[-2 * half : -half], shard], axis=0),
    )


def plus_low(a, b):
    return (a.astype(F32) + b.astype(F32)).astype(B16)


def grid_scatter_first(first_a, first_b):
    return lax.ppermute(first_a, "x", SWAP), lax.ppermute(first_b, "y", SWAP)


def grid_scatter_second(got, rest_a, rest_b, *hold):
    got_a, got_b = got
    onward_a = (rest_a[1].astype(F32) + got_a[1].astype(F32)).astype(B16)
    onward_b = (rest_b[1].astype(F32) + got_b[1].astype(F32)).astype(B16)
    last_a = lax.ppermute(onward_a, "y", SWAP)
    last_b = lax.ppermute(onward_b, "x", SWAP)
    last_a, last_b = after((last_a, last_b), *hold)
    return (
        rest_a[0].astype(F32) + got_a[0].astype(F32) + last_a.astype(F32),
        rest_b[0].astype(F32) + got_b[0].astype(F32) + last_b.astype(F32),
    )


def row_halves(parts):
    own, to_x, to_y, diag = [parts[j] for j in range(4)]
    half = own.shape[0] // 2
    first = (
        jnp.stack([to_x[:half], diag[:half]]),
        jnp.stack([to_y[half:], diag[half:]]),
    )
    return first, (own[:half], to_y[:half]), (own[half:], to_x[half:])


def column_pieces(rows, size):
    return [rows] + [cyclic(rows, size, -k) for k in range(1, size)]


def column_send_some(low, size):
    return [cyclic(low[k], size, k) for k in range(1, size) if 2 * k != size]


def column_send_last(low, size, *hold):
    return [cyclic(after(low[size // 2], *hold), size, size // 2)]


def column_sum(own, pieces):
    return own.astype(F32) + sum(piece.astype(F32) for piece in pieces)


def assemble(places, shard, moved, other, rows):
    def kernel(places_ref, shard_ref, moved_ref, other_ref, out_ref):
        def put(i, value):
            start = pl.multiple_of(places_ref[i] * rows, rows)
            out_ref[pl.ds(start, value.shape[0]), :] = value

        put(0, shard_ref[...])
        for j in range(3):
            put(1 + j, moved_ref[j * rows : (j + 1) * rows, :])
            put(4 + j, other_ref[j * rows : (j + 1) * rows, :])

    def whole(array_shape):
        return pl.BlockSpec(array_shape, lambda i, places: (0, 0))

    out_rows, cols = 8 * rows, shard.shape[1]
    return pl.pallas_call(
        kernel,
        out_shape=jax.ShapeDtypeStruct((out_rows, cols), shard.dtype),
        grid_spec=pltpu.PrefetchScalarGridSpec(
            num_scalar_prefetch=1,
            grid=(1,),
            in_specs=[whole(a.shape) for a in (shard, moved, other)],
            out_specs=whole((out_rows, cols)),
        ),
        compiler_params=pltpu.CompilerParams(vmem_limit_bytes=VMEM_LIMIT),
        name="assemble",
    )(places, shard, moved, other)


def one_hot_slots(codes, capacity):
    slots = lax.broadcasted_iota(jnp.int32, (capacity, codes.shape[1]), 0).astype(F32)
    return [(slots == codes[e : e + 1, :]).astype(F32) for e in range(codes.shape[0])]


def row_of(table, index):
    at = lax.broadcasted_iota(jnp.int32, table.shape, 0)
    return jnp.sum(jnp.where(at == index, table, 0.0), axis=0, keepdims=True)


def pack_code(code):
    rows = code.shape[0] // 4
    wide = jnp.concatenate([code[c * rows : (c + 1) * rows] for c in range(4)], axis=1)
    return jnp.concatenate([wide, jnp.full((16 - rows, wide.shape[1]), -1.0, B16)], axis=0)


def unpack_code(block, tokens):
    rows = EXPERTS // 4
    wide = block.astype(F32)
    return jnp.concatenate(
        [wide[:rows, c * tokens : (c + 1) * tokens] for c in range(4)], axis=0
    )


def dispatch_rows(lead, packed, rows, router, local, capacity):
    pieces, packed_rows, width = packed.shape
    tokens = packed_rows - 16
    slots = local * capacity
    with_gates = router is not None

    def kernel(lead_ref, packed_ref, *rest):
        first = lead_ref[0]
        if with_gates:
            router_ref, out_ref, gate_out, rows_ref = rest[pieces:]
            for p in range(pieces):

                @pl.when(pl.program_id(0) == p)
                def _():
                    rows_ref[...] = rest[p][...]

            table = unpack_code(packed_ref[0], tokens)
            source = rows_ref[...]
        else:
            (out_ref,) = rest
            table = unpack_code(packed_ref[0, tokens:, :], tokens)
            source = packed_ref[0, :tokens, :]
        codes = jnp.concatenate([row_of(table, first + e) for e in range(local)], axis=0)
        picks = one_hot_slots(codes, capacity)
        select = jnp.concatenate([p.astype(B16) for p in picks], axis=0)
        out_ref[0] = jnp.dot(select, source, preferred_element_type=F32).astype(B16)
        if with_gates:
            logits = lax.dot_general(
                router_ref[...], source, (((1,), (1,)), ((), ())), preferred_element_type=F32
            )
            routed = table >= 0.0
            peak = jnp.max(jnp.where(routed, logits, MASKED_SCORE), axis=0, keepdims=True)
            lifted = jnp.where(routed, jnp.exp(jnp.minimum(logits - peak, 0.0)), 0.0)
            gates = lifted / jnp.sum(lifted, axis=0, keepdims=True)
            for e in range(local):
                gate_row = row_of(gates, first + e)
                column = jnp.sum(picks[e] * gate_row, axis=1, keepdims=True)
                gate_out[0, e * capacity : (e + 1) * capacity, :] = jnp.broadcast_to(
                    column, (capacity, 128)
                )

    out_specs = [pl.BlockSpec((1, slots, width), lambda p, lead: (p, 0, 0))]
    out_shape = [jax.ShapeDtypeStruct((pieces, slots, width), B16)]
    args = [packed]
    if with_gates:
        in_specs = [
            pl.BlockSpec((1, 16, width), lambda p, lead: (p, tokens // 16, 0)),
            *[pl.BlockSpec((tokens, width), lambda p, lead: (0, 0)) for _ in rows],
            pl.BlockSpec((EXPERTS, width), lambda p, lead: (0, 0)),
        ]
        out_specs.append(pl.BlockSpec((1, slots, 128), lambda p, lead: (p, 0, 0)))
        out_shape.append(jax.ShapeDtypeStruct((pieces, slots, 128), F32))
        args += [*rows, router]
    else:
        in_specs = [pl.BlockSpec((1, packed_rows, width), lambda p, lead: (p, 0, 0))]
    return pl.pallas_call(
        kernel,
        out_shape=out_shape,
        grid_spec=pltpu.PrefetchScalarGridSpec(
            num_scalar_prefetch=1,
            grid=(pieces,),
            in_specs=in_specs,
            out_specs=out_specs,
            scratch_shapes=[pltpu.VMEM((tokens, width), B16)] if with_gates else [],
        ),
        compiler_params=pltpu.CompilerParams(vmem_limit_bytes=VMEM_LIMIT),
        name="dispatch",
    )(lead, *args)


def combine_rows(lead, first, packed, slot_rows, local, capacity, addend=None):
    pieces, packed_rows, code_width = packed.shape
    tokens = packed_rows - 16
    halves = len(slot_rows)
    slots, width = slot_rows[0].shape[1:]
    per = local // halves

    def kernel(lead_ref, code_ref, *rest):
        table = unpack_code(code_ref[0], tokens)
        here = lead_ref[0]
        codes = jnp.concatenate([row_of(table, here + e) for e in range(local)], axis=0)
        picks = one_hot_slots(codes, capacity)
        total = None
        for h in range(halves):
            select = jnp.concatenate(
                [p.astype(B16) for p in picks[h * per : (h + 1) * per]], axis=0
            )
            part = lax.dot_general(
                select, rest[h][0], (((0,), (0,)), ((), ())), preferred_element_type=F32
            )
            total = part if total is None else total + part
        if addend is None:
            rest[halves][0] = total.astype(B16)
        else:
            low = (total + rest[halves][0].astype(F32)).astype(B16)
            for p in range(pieces):

                @pl.when(pl.program_id(0) == p)
                def _():
                    rest[halves + 1 + p][...] = low

    in_specs = [pl.BlockSpec((1, 16, code_width), lambda p, lead: (p, tokens // 16, 0))]
    in_specs += [
        pl.BlockSpec((1, slots, width), lambda p, lead: (p + first, 0, 0)) for _ in range(halves)
    ]
    added = [] if addend is None else [addend]
    in_specs += [pl.BlockSpec((1, tokens, width), lambda p, lead: (p, 0, 0)) for _ in added]
    if addend is None:
        out_shape = jax.ShapeDtypeStruct((pieces, tokens, width), B16)
        out_specs = pl.BlockSpec((1, tokens, width), lambda p, lead: (p, 0, 0))
    else:
        out_shape = [jax.ShapeDtypeStruct((tokens, width), B16)] * pieces
        out_specs = [pl.BlockSpec((tokens, width), lambda p, lead: (0, 0))] * pieces
    return pl.pallas_call(
        kernel,
        out_shape=out_shape,
        grid_spec=pltpu.PrefetchScalarGridSpec(
            num_scalar_prefetch=1,
            grid=(pieces,),
            in_specs=in_specs,
            out_specs=out_specs,
        ),
        compiler_params=pltpu.CompilerParams(vmem_limit_bytes=VMEM_LIMIT),
        name="combine",
    )(lead, packed, *slot_rows, *added)


def experts(order, start, count, rows, grads, gates, weights, chunks, capacity, in_rows, mid_rows):
    half, _, width = rows[0].shape
    pieces = 2 * half
    split = bool(chunks)
    n = 4 if split else len(weights)
    extra = [array for chunk in chunks for array, _ in chunk]
    given = len(weights) + len(extra)
    pack_rows, eff = chunks[0][0][0].shape if split else weights[0].shape[1:]
    folds = width // eff
    total_rows = pieces * capacity
    first_half = count // 2
    large = total_rows > 1000

    def kernel(order_ref, *refs):
        rows_a, rows_b, grads_a, grads_b, gates_a, gates_b = refs[:6]
        pack = refs[6 : 6 + given]
        y_out, dx_out = refs[6 + given : 8 + given]
        outs = refs[8 + given : -6]
        full_g, full_u, full_d, grad_g, grad_u, grad_d = refs[-6:]

        def at_in(j):
            return pl.ds(pl.multiple_of(order_ref[j] * in_rows, in_rows), in_rows)

        def at_mid(j):
            return pl.ds(pl.multiple_of(order_ref[j] * mid_rows, mid_rows), mid_rows)

        def load(j, take):
            full_g[at_in(j), :] = take(0, in_rows)
            full_u[at_in(j), :] = take(in_rows, 2 * in_rows)
            for f in range(folds):
                full_d[at_mid(j), f * eff : (f + 1) * eff] = take(
                    2 * in_rows + f * mid_rows, 2 * in_rows + (f + 1) * mid_rows
                )

        def rows_from(ref, offset):
            return lambda lo, hi: ref[offset + lo : offset + hi, :]

        def two_halves(a, b):
            middle = pack_rows // 2

            def take(lo, hi):
                if hi <= middle:
                    return a(lo, hi)
                if lo >= middle:
                    return b(lo - middle, hi - middle)
                return jnp.concatenate([a(lo, middle), b(0, hi - middle)], axis=0)

            return take

        for j in range(len(weights)):
            load(j, lambda lo, hi, ref=pack[j]: ref[0, lo:hi])
        for c in range(len(chunks)):
            own, from_x, from_y, diag_a, diag_b = [
                rows_from(pack[5 * c + i], chunks[c][i][1]) for i in range(5)
            ]

            @pl.when(pl.program_id(0) == c)
            def _():
                load(0, own)
                load(1, from_x)
                load(2, from_y)
                load(3, two_halves(diag_a, diag_b))

        def joined(a, b, w):
            return jnp.concatenate(
                [
                    a[...].reshape(half * capacity, w),
                    b[...].reshape(half * capacity, w),
                ],
                axis=0,
            )

        x = joined(rows_a, rows_b, width)
        g = joined(grads_a, grads_b, width)
        gate = joined(gates_a, gates_b, 128)[:, 0:1]
        nt = (((1,), (1,)), ((), ()))
        tn = (((0,), (0,)), ((), ()))
        gate_proj = jnp.dot(x, full_g[...], preferred_element_type=F32)
        up_proj = jnp.dot(x, full_u[...], preferred_element_type=F32)
        down_grad = lax.dot_general(g, full_d[...], nt, preferred_element_type=F32)
        sigmoid = 1.0 / (1.0 + jnp.exp(-gate_proj))
        silu = gate_proj * sigmoid
        activated = silu * up_proj
        slot_grad = jnp.sum(activated * down_grad, axis=1, keepdims=True)
        here = order_ref[n] + start + pl.program_id(0)
        lane = lax.broadcasted_iota(jnp.int32, (total_rows, 128), 1)
        high = slot_grad.astype(B16).astype(F32)
        tail = jnp.where(lane == here, high, jnp.where(lane == here + EXPERTS, slot_grad - high, 0.0))
        dx_out[:, :, width:] = tail.astype(B16).reshape(pieces, capacity, 128)
        scaled = (gate * activated).astype(B16)
        act_grad = gate * down_grad
        gate_grad = (act_grad * up_proj * (sigmoid * (1.0 + gate_proj * (1.0 - sigmoid)))).astype(
            B16
        )
        up_grad = (act_grad * silu).astype(B16)
        y = jnp.dot(scaled, full_d[...], preferred_element_type=F32)
        y_out[...] = y.astype(B16).reshape(pieces, capacity, width)
        dx = lax.dot_general(gate_grad, full_g[...], nt, preferred_element_type=F32)
        dx = dx + lax.dot_general(up_grad, full_u[...], nt, preferred_element_type=F32)
        dx_out[:, :, :width] = dx.astype(B16).reshape(pieces, capacity, width)
        grad_g[...] = lax.dot_general(x, gate_grad, tn, preferred_element_type=F32).astype(B16)
        grad_u[...] = lax.dot_general(x, up_grad, tn, preferred_element_type=F32).astype(B16)
        grad_d[...] = lax.dot_general(scaled, g, tn, preferred_element_type=F32).astype(B16)

        def give(ref, slot, j):
            ref[slot, 0, :in_rows] = grad_g[at_in(j), :]
            ref[slot, 0, in_rows : 2 * in_rows] = grad_u[at_in(j), :]
            for f in range(folds):
                ref[slot, 0, 2 * in_rows + f * mid_rows : 2 * in_rows + (f + 1) * mid_rows] = grad_d[
                    at_mid(j), f * eff : (f + 1) * eff
                ]

        if split:

            @pl.when(pl.program_id(0) < first_half)
            def _():
                for j in range(4):
                    give(outs[j], 0, j)

            @pl.when(pl.program_id(0) >= first_half)
            def _():
                for j in range(4):
                    give(outs[4 + j], 0, j)
        else:
            for j in range(n):
                give(outs[0], j, j)

    def single():
        return dict(pipeline_mode=pl.Buffered(1)) if large else {}

    def rows_spec(w):
        return pl.BlockSpec((half, capacity, w), lambda e, o: (0, e + start, 0), **single())

    in_specs = [rows_spec(width)] * 4 + [rows_spec(128)] * 2
    for _ in weights:
        in_specs.append(pl.BlockSpec((1, pack_rows, eff), lambda e, o: (e + start, 0, 0)))
    for part in extra:
        in_specs.append(pl.BlockSpec(part.shape, lambda e, o: (0, 0)))
    slots = count * capacity
    out_specs = [
        pl.BlockSpec((pieces, capacity, w), lambda e, o: (0, e, 0), **single())
        for w in (width, width + 128)
    ]
    out_shape = [
        jax.ShapeDtypeStruct((pieces, slots, width), B16),
        jax.ShapeDtypeStruct((pieces, slots, width + 128), B16),
    ]
    if split:
        for at in (
            lambda e, o: (0, jnp.minimum(e, first_half - 1), 0, 0),
            lambda e, o: (0, jnp.maximum(e - first_half, 0), 0, 0),
        ):
            for _ in range(4):
                out_specs.append(pl.BlockSpec((1, 1, pack_rows, eff), at))
                out_shape.append(jax.ShapeDtypeStruct((1, first_half, pack_rows, eff), B16))
    else:
        out_specs.append(pl.BlockSpec((n, 1, pack_rows, eff), lambda e, o: (0, e, 0, 0)))
        out_shape.append(jax.ShapeDtypeStruct((n, count, pack_rows, eff), B16))
    results = pl.pallas_call(
        kernel,
        out_shape=out_shape,
        grid_spec=pltpu.PrefetchScalarGridSpec(
            num_scalar_prefetch=1,
            grid=(count,),
            in_specs=in_specs,
            out_specs=out_specs,
            scratch_shapes=[
                pltpu.VMEM((n * in_rows, eff), B16),
                pltpu.VMEM((n * in_rows, eff), B16),
                pltpu.VMEM((n * mid_rows, width), B16),
                pltpu.VMEM((n * in_rows, eff), B16),
                pltpu.VMEM((n * in_rows, eff), B16),
                pltpu.VMEM((n * mid_rows, width), B16),
            ],
        ),
        compiler_params=pltpu.CompilerParams(vmem_limit_bytes=VMEM_LIMIT),
        name="experts",
    )(order, *rows, *grads, *gates, *weights, *extra)
    return results[0], results[1], results[2:]


NT = (((1,), (1,)), ((), ()))
TN = (((0,), (0,)), ((), ()))
GROUPS = KVH // 2
EXTRA = 128


def turn(vectors, cosine, sine):
    lane = lax.broadcasted_iota(jnp.int32, vectors.shape, 1)
    ahead = pltpu.roll(vectors, 2 * HD - HD // 2, 1)
    behind = pltpu.roll(vectors, HD // 2, 1)
    return vectors * cosine + jnp.where(lane % HD < HD // 2, ahead, behind) * sine


def turn_tables(places):
    lane = jnp.arange(2 * HD, dtype=jnp.int32)
    frequency = jnp.exp(
        (lane % (HD // 2)).astype(F32) * (-2.0 * math.log(ROPE_BASE) / HD)
    )
    angles = places[:, None] * frequency[None, :]
    sign = jnp.where(lane % HD < HD // 2, -1.0, 1.0)
    return jnp.cos(angles), jnp.sin(angles) * sign[None, :]


def attention_forward(x_own, x_parts, dense_full, bias, cosine, sine, routed):
    tok_rows, width = x_own.shape
    seq_len = 4 * tok_rows
    scale = HD ** (-0.5)
    wide, narrow = H * HD, KVH * HD

    def kernel(
        own_ref, xa_ref, xb_ref, ya_ref, yb_ref, da_ref, db_ref, ea_ref, eb_ref,
        tail_ref, wo_ref, wq_ref, wk_ref, wv_ref, bias_ref, cos_ref, sin_ref, routed_ref,
        x_ref, normed_ref, q_out, k_out, v_out, att_out, total_out, misc_out, residual_out, moe_out,
        gates_out,
    ):
        step = pl.program_id(0)

        @pl.when(step == 0)
        def _():
            rows = jnp.transpose(tail_ref[...].astype(F32))
            misc_out[...] = rows
            at = 0
            for ref in (own_ref, xa_ref, xb_ref, ya_ref, yb_ref, da_ref, ea_ref, db_ref, eb_ref):
                x_ref[at : at + ref.shape[0], :] = ref[...]
                at += ref.shape[0]
            x = x_ref[...].astype(F32)
            scaled = x * lax.rsqrt(jnp.mean(x * x, axis=1, keepdims=True) + EPSILON)
            normed_ref[...] = (scaled * rows[EXPERTS : EXPERTS + 1, :]).astype(B16)
            residual_out[...] = x[:tok_rows]

        normed = normed_ref[...]
        cos, sin = cos_ref[...], sin_ref[...]
        key = turn(jnp.dot(normed, wk_ref[...], preferred_element_type=F32), cos, sin).astype(B16)
        value = jnp.dot(normed, wv_ref[...], preferred_element_type=F32).astype(B16)
        query = jnp.dot(normed[:tok_rows], wq_ref[...], preferred_element_type=F32)
        cos, sin = cos[:tok_rows], sin[:tok_rows]
        query = jnp.concatenate(
            [turn(query[:, 128 * j : 128 * (j + 1)], cos, sin) for j in range(2)], axis=1
        )
        query = (query * scale).astype(B16)
        k_out[...] = key
        v_out[...] = value
        q_out[...] = query
        mixed, totals = [], []
        for j in range(4):
            lanes = slice(HD * (j // 2), HD * (j // 2 + 1))
            scores = lax.dot_general(
                key[:, lanes], query[:, HD * j : HD * (j + 1)], NT, preferred_element_type=F32
            )
            scores = scores + bias_ref[...]
            peak = jnp.max(scores, axis=0, keepdims=True)
            probs = jnp.exp(scores - peak)
            total = jnp.sum(probs, axis=0, keepdims=True)
            out = lax.dot_general(
                value[:, lanes], probs.astype(B16), TN, preferred_element_type=F32
            )
            mixed.append(out / total)
            totals.append(peak + jnp.log(total))
        attended = jnp.transpose(jnp.concatenate(mixed, axis=0)).astype(B16)
        att_out[...] = attended
        total_out[0] = jnp.concatenate(totals + totals, axis=0)
        residual_out[...] += jnp.dot(attended, wo_ref[...], preferred_element_type=F32)

        @pl.when(step == GROUPS - 1)
        def _():
            total = residual_out[...]
            scaled = total * lax.rsqrt(jnp.mean(total * total, axis=1, keepdims=True) + EPSILON)
            moe_in = (scaled * misc_out[EXPERTS + 1 : EXPERTS + 2, :]).astype(B16)
            moe_out[...] = moe_in
            logits = jnp.dot(moe_in, tail_ref[...], preferred_element_type=F32)
            here = routed_ref[...] > 0.0
            peak = jnp.max(jnp.where(here, logits, MASKED_SCORE), axis=1, keepdims=True)
            lifted = jnp.where(here, jnp.exp(jnp.minimum(logits - peak, 0.0)), 0.0)
            gates_out[...] = lifted / jnp.sum(lifted, axis=1, keepdims=True)

    def fixed(*block):
        return pl.BlockSpec(block, lambda i: (0,) * len(block))

    def columns(rows, cols, lead=0):
        return pl.BlockSpec((rows, cols), lambda i: (0, lead + i))

    return pl.pallas_call(
        kernel,
        grid=(GROUPS,),
        in_specs=[
            fixed(tok_rows, width),
            *[
                pl.BlockSpec((part.shape[0], width), lambda i, c=c: (0, c))
                for part in x_parts
                for c in range(2)
            ],
            pl.BlockSpec((width, 128), lambda i: (0, (width + wide + 2 * narrow) // 128)),
            pl.BlockSpec((256, width), lambda i: (i, 0)),
            columns(width, 256, width // 256),
            columns(width, 128, (width + wide) // 128),
            columns(width, 128, (width + wide + narrow) // 128),
            fixed(seq_len, tok_rows),
            fixed(seq_len, 128),
            fixed(seq_len, 128),
            fixed(tok_rows, 128),
        ],
        out_specs=[
            fixed(seq_len, width),
            fixed(seq_len, width),
            columns(tok_rows, 256),
            columns(seq_len, 128),
            columns(seq_len, 128),
            columns(tok_rows, 256),
            pl.BlockSpec((1, 8, tok_rows), lambda i: (i, 0, 0)),
            fixed(128, width),
            fixed(tok_rows, width),
            fixed(tok_rows, width),
            fixed(tok_rows, 128),
        ],
        out_shape=[
            jax.ShapeDtypeStruct((seq_len, width), B16),
            jax.ShapeDtypeStruct((seq_len, width), B16),
            jax.ShapeDtypeStruct((tok_rows, wide), B16),
            jax.ShapeDtypeStruct((seq_len, narrow), B16),
            jax.ShapeDtypeStruct((seq_len, narrow), B16),
            jax.ShapeDtypeStruct((tok_rows, wide), B16),
            jax.ShapeDtypeStruct((GROUPS, 8, tok_rows), F32),
            jax.ShapeDtypeStruct((128, width), F32),
            jax.ShapeDtypeStruct((tok_rows, width), F32),
            jax.ShapeDtypeStruct((tok_rows, width), B16),
            jax.ShapeDtypeStruct((tok_rows, 128), F32),
        ],
        compiler_params=pltpu.CompilerParams(vmem_limit_bytes=VMEM_LIMIT),
        name="attention",
    )(
        x_own, *[part for part in x_parts for _ in range(2)], *[dense_full] * 5,
        bias, cosine, sine, routed,
    )


def attention_backward(
    where_here, moe_sums, out_grad, residual, gates, misc, attended, moe_in, saved,
    dense_full, bias, cosine, sine,
):
    x_all, normed_all, query_rot, key_rot, value_all, totals = saved
    terms = len(moe_sums)
    seq_len, width = x_all.shape
    tok_rows = query_rot.shape[0]
    scale = HD ** (-0.5)
    wide, narrow = H * HD, KVH * HD
    block = width // 8
    output_at = wide + 2 * narrow

    def kernel(here_ref, *refs):
        sums = refs[:terms]
        (
            grad_ref, residual_ref, gates_ref, misc_ref, tail_ref, wo_ref, att_ref, moe_ref,
            normed_ref, q_ref, k_ref, v_ref, total_ref,
            x_ref, wq_ref, wk_ref, wv_ref, bias_ref, cos_ref, sin_ref,
            dense_out, first_a_out, first_b_out, rest_a_out, rest_b_out, residual_out,
            normed_t, grad_sum, og_ref, logit_ref, gain_ref,
        ) = refs[terms:]
        step = pl.program_id(0)
        dp, core = here_ref[0], here_ref[1]

        @pl.when(step == 0)
        def _():
            normed_t[...] = jnp.transpose(normed_ref[...])
            grad_sum[...] = jnp.zeros((seq_len, width), F32)
            total = sums[0][...].astype(F32)
            for ref in sums[1:]:
                total = total + ref[...].astype(F32)
            behind = total[:, width:]
            gate_grad = behind + pltpu.roll(behind, 128 - EXPERTS, 1)
            gate = gates_ref[...]
            centre = jnp.sum(gate * gate_grad, axis=1, keepdims=True)
            logit_low = (gate * (gate_grad - centre)).astype(B16)
            logit_ref[...] = logit_low
            moe_grad = total[:, :width] + lax.dot_general(
                logit_low, tail_ref[...], NT, preferred_element_type=F32
            )
            residual = residual_ref[...]
            rate = lax.rsqrt(jnp.mean(residual * residual, axis=1, keepdims=True) + EPSILON)
            gain_ref[...] = jnp.sum(moe_grad * residual * rate, axis=0, keepdims=True)
            lifted = moe_grad * misc_ref[EXPERTS + 1 : EXPERTS + 2, :]
            inner = jnp.mean(lifted * residual, axis=1, keepdims=True)
            residual_grad = (
                grad_ref[...].astype(F32) + rate * lifted - residual * (rate * rate * rate * inner)
            )
            residual_out[...] = residual_grad
            og_ref[...] = residual_grad.astype(B16)

        og = og_ref[...]
        att_grad = lax.dot_general(og, wo_ref[...], NT, preferred_element_type=F32).astype(B16)
        query, key, value = q_ref[...], k_ref[...], v_ref[...]
        query_grads, key_grads, value_grads = [], [], []
        for j in range(4):
            lanes = slice(HD * (j // 2), HD * (j // 2 + 1))
            mine = slice(HD * j, HD * (j + 1))
            scores = lax.dot_general(
                key[:, lanes], query[:, mine], NT, preferred_element_type=F32
            )
            probs = jnp.exp(scores + bias_ref[...] - total_ref[0, j : j + 1, :])
            probs_grad = lax.dot_general(
                value[:, lanes], att_grad[:, mine], NT, preferred_element_type=F32
            )
            delta = jnp.sum(probs * probs_grad, axis=0, keepdims=True)
            score_grad = (probs * (probs_grad - delta)).astype(B16)
            query_grads.append(
                lax.dot_general(key[:, lanes], score_grad, TN, preferred_element_type=F32)
            )
            key_part = jnp.dot(score_grad, query[:, mine], preferred_element_type=F32)
            value_part = jnp.dot(probs.astype(B16), att_grad[:, mine], preferred_element_type=F32)
            if j % 2 == 0:
                key_grads.append(key_part)
                value_grads.append(value_part)
            else:
                key_grads[-1] = key_grads[-1] + key_part
                value_grads[-1] = value_grads[-1] + value_part
        cos, sin = cos_ref[...], -sin_ref[...]
        kv_grad = jnp.concatenate(
            [turn(jnp.concatenate(key_grads, axis=1), cos, sin)] + value_grads, axis=1
        ).astype(B16)
        cos, sin = cos[:tok_rows], sin[:tok_rows]
        query_grad = jnp.transpose(jnp.concatenate(query_grads, axis=0)) * scale
        query_grad = jnp.concatenate(
            [turn(query_grad[:, 128 * j : 128 * (j + 1)], cos, sin) for j in range(2)], axis=1
        ).astype(B16)

        def put(at, lanes, rows):
            for c in range(2):
                dense_out[core ^ c, at, :, lanes] = rows[c].astype(B16)

        def give(grad, lanes):
            for m in range(4):
                put(
                    dp ^ m,
                    lanes,
                    [grad[(2 * m + c) * block : (2 * m + c + 1) * block] for c in range(2)],
                )

        give(
            jnp.dot(normed_t[:, :tok_rows], query_grad, preferred_element_type=F32),
            pl.ds(pl.multiple_of(step * 256, 256), 256),
        )
        give(
            jnp.dot(normed_t[...], kv_grad, preferred_element_type=F32),
            pl.ds(pl.multiple_of(wide + step * 256, 256), 256),
        )
        out_part = lax.dot_general(att_ref[...], og, TN, preferred_element_type=F32).astype(B16)
        put(dp ^ step, slice(output_at, output_at + width), [out_part[:block], out_part[block:]])
        kv_weights = jnp.concatenate([wk_ref[...], wv_ref[...]], axis=1)
        grad_sum[...] += lax.dot_general(kv_grad, kv_weights, NT, preferred_element_type=F32)
        grad_sum[:tok_rows, :] += lax.dot_general(
            query_grad, wq_ref[...], NT, preferred_element_type=F32
        )

        @pl.when(step == GROUPS - 1)
        def _():
            total = grad_sum[...]
            low = total.astype(B16)
            half = tok_rows // 2
            first_a_out[0] = low[tok_rows : tok_rows + half]
            first_a_out[1] = low[3 * tok_rows : 3 * tok_rows + half]
            first_b_out[0] = low[2 * tok_rows + half : 3 * tok_rows]
            first_b_out[1] = low[3 * tok_rows + half :]
            rest_a_out[0] = low[:half]
            rest_a_out[1] = low[2 * tok_rows : 2 * tok_rows + half]
            rest_b_out[0] = low[half:tok_rows]
            rest_b_out[1] = low[tok_rows + half : 2 * tok_rows]
            x = x_ref[...].astype(F32)
            lifted = x * lax.rsqrt(jnp.mean(x * x, axis=1, keepdims=True) + EPSILON)
            gain = jnp.sum(total * lifted, axis=0, keepdims=True)
            row = lax.broadcasted_iota(jnp.int32, (EXTRA, width), 0)
            gains = jnp.where(
                row == EXPERTS, gain, jnp.where(row == EXPERTS + 1, gain_ref[...], 0.0)
            )
            extra = lax.dot_general(
                moe_ref[...], logit_ref[...], TN, preferred_element_type=F32
            ) + jnp.transpose(gains)
            give(extra, slice(output_at + width, output_at + width + EXTRA))

    def fixed(*shape):
        return pl.BlockSpec(shape, lambda i, here: (0,) * len(shape))

    def columns(rows, cols, lead=0):
        return pl.BlockSpec((rows, cols), lambda i, here: (0, lead + i))

    shapes = [
        jax.ShapeDtypeStruct((2, 4, block, output_at + width + EXTRA), B16),
        *[jax.ShapeDtypeStruct((2, tok_rows // 2, width), B16)] * 4,
        jax.ShapeDtypeStruct((tok_rows, width), F32),
    ]
    dense, *parts, residual_grad = pl.pallas_call(
        kernel,
        out_shape=shapes,
        grid_spec=pltpu.PrefetchScalarGridSpec(
            num_scalar_prefetch=1,
            grid=(GROUPS,),
            in_specs=[
                *[fixed(tok_rows, width + 128)] * terms,
                fixed(tok_rows, width),
                fixed(tok_rows, width),
                fixed(tok_rows, 128),
                fixed(128, width),
                pl.BlockSpec(
                    (width, 128), lambda i, here: (0, (width + wide + 2 * narrow) // 128)
                ),
                pl.BlockSpec((256, width), lambda i, here: (i, 0)),
                columns(tok_rows, 256),
                fixed(tok_rows, width),
                fixed(seq_len, width),
                columns(tok_rows, 256),
                columns(seq_len, 128),
                columns(seq_len, 128),
                pl.BlockSpec((1, 8, tok_rows), lambda i, here: (i, 0, 0)),
                fixed(seq_len, width),
                columns(width, 256, width // 256),
                columns(width, 128, (width + wide) // 128),
                columns(width, 128, (width + wide + narrow) // 128),
                fixed(seq_len, tok_rows),
                fixed(seq_len, 128),
                fixed(seq_len, 128),
            ],
            out_specs=[fixed(*shape.shape) for shape in shapes],
            scratch_shapes=[
                pltpu.VMEM((width, seq_len), B16),
                pltpu.VMEM((seq_len, width), F32),
                pltpu.VMEM((tok_rows, width), B16),
                pltpu.VMEM((tok_rows, EXTRA), B16),
                pltpu.VMEM((1, width), F32),
            ],
        ),
        compiler_params=pltpu.CompilerParams(vmem_limit_bytes=VMEM_LIMIT),
        name="attention_grad",
    )(
        where_here, *moe_sums, out_grad, residual, gates, misc, dense_full, dense_full, attended,
        moe_in, normed_all, query_rot, key_rot, value_all, totals,
        x_all, dense_full, dense_full, dense_full, bias, cosine, sine,
    )
    return dense, tuple(parts[:2]), parts[2], parts[3], residual_grad


def core_halves(blocks, got):
    _, _, rows, cols = blocks.shape
    half = rows // 2

    def kernel(keep_ref, got_ref, first_a, first_b, rest_a, rest_b):
        def total(j, lo):
            mine = keep_ref[0, j, lo : lo + half, :].astype(F32)
            return (mine + got_ref[j, lo : lo + half, :].astype(F32)).astype(B16)

        first_a[0], first_a[1] = total(1, 0), total(3, 0)
        first_b[0], first_b[1] = total(2, half), total(3, half)
        rest_a[0], rest_a[1] = total(0, 0), total(2, 0)
        rest_b[0], rest_b[1] = total(0, half), total(1, half)

    step = cols // 5
    first_a, first_b, rest_a, rest_b = pl.pallas_call(
        kernel,
        grid=(5,),
        in_specs=[
            pl.BlockSpec((1, 4, rows, step), lambda i: (0, 0, 0, i)),
            pl.BlockSpec((4, rows, step), lambda i: (0, 0, i)),
        ],
        out_specs=[pl.BlockSpec((2, half, step), lambda i: (0, 0, i))] * 4,
        out_shape=[jax.ShapeDtypeStruct((2, half, cols), B16)] * 4,
        compiler_params=pltpu.CompilerParams(vmem_limit_bytes=VMEM_LIMIT),
        name="core_halves",
    )(blocks, got)
    return (first_a, first_b), rest_a, rest_b


def dense_outputs(core, mine, other, wide, narrow):
    rows, cols = mine.shape
    at = wide + 2 * narrow
    shapes = [(2 * rows, wide), (2 * rows, narrow), (2 * rows, narrow), (2 * rows, cols - at - EXTRA)]
    shapes.append((2 * rows, EXTRA))

    def kernel(core_ref, mine_ref, other_ref, query, key, value, output, extra):
        for c in range(2):
            for ref, side in ((mine_ref, c), (other_ref, 1 - c)):

                @pl.when(core_ref[0] == c)
                def _():
                    lines = slice(side * rows, (side + 1) * rows)
                    query[lines, :] = ref[:, :wide].astype(F32)
                    for i in range(GROUPS):
                        lead = wide + 256 * i
                        lanes = slice(128 * i, 128 * (i + 1))
                        key[lines, lanes] = ref[:, lead : lead + 128].astype(F32)
                        value[lines, lanes] = ref[:, lead + 128 : lead + 256].astype(F32)
                    output[lines, :] = ref[:, at : cols - EXTRA].astype(F32)
                    extra[lines, :] = ref[:, cols - EXTRA :].astype(F32)

    def fixed(shape):
        return pl.BlockSpec(shape, lambda i, core: (0, 0))

    query, key, value, output, extra = pl.pallas_call(
        kernel,
        out_shape=[jax.ShapeDtypeStruct(shape, F32) for shape in shapes],
        grid_spec=pltpu.PrefetchScalarGridSpec(
            num_scalar_prefetch=1,
            grid=(1,),
            in_specs=[fixed(mine.shape)] * 2,
            out_specs=[fixed(shape) for shape in shapes],
        ),
        compiler_params=pltpu.CompilerParams(vmem_limit_bytes=VMEM_LIMIT),
        name="dense_outputs",
    )(core.astype(jnp.int32)[None], mine, other)
    return query, key, value, output, extra[:, :EXPERTS], extra[:, EXPERTS], extra[:, EXPERTS + 1]


def make_body(z_size, small_grid):
    def core_half(shard, core):
        rows = shard.shape[0] // 2
        return lax.dynamic_slice_in_dim(shard, core * rows, rows, 0)

    def dense_assemble(shard, parts, dp_index, core, *hold):
        rows = shard.shape[0] // 2
        moved = after(jnp.concatenate(parts, axis=0), *hold)
        other = swap_core(moved)
        places = [2 * dp_index]
        for which in (core, 1 - core):
            places += [2 * (dp_index ^ (j + 1)) + which for j in range(3)]
        return assemble(jnp.stack(places), shard, moved, other, rows)

    def across_z(mine, z):
        if z_size != 4:
            return lax.psum(mine.astype(F32), "z").astype(B16)
        rows = mine.shape[0] // z_size
        low = mine.astype(B16)
        total = lax.dynamic_slice_in_dim(mine, z * rows, rows, 0)
        for k in range(1, z_size):
            theirs = lax.dynamic_slice_in_dim(low, (z + k) % z_size * rows, rows, 0)
            total = total + cyclic(theirs, z_size, k).astype(F32)
        total = total.astype(B16)
        quarters = [total] + [cyclic(total, z_size, -k) for k in range(1, z_size)]
        places = (jnp.arange(z_size, dtype=jnp.int32) - z) % z_size
        return jnp.take(jnp.stack(quarters), places, axis=0).reshape(mine.shape)

    def dense_sum(grads):
        return lax.psum_scatter(
            lax.psum(grads, ("z", "core")), ("y", "x"), scatter_dimension=0, tiled=True
        )

    def body(
        layer_input,
        attn_gain,
        w_query,
        w_key,
        w_value,
        w_output,
        moe_gain,
        w_router,
        w_gate,
        w_up,
        w_down,
        routes,
        priority,
        prefix_len,
        out_grad,
    ):
        tok_rows, model_width = layer_input.shape
        dp_size = lax.axis_size("y") * lax.axis_size("x")
        dp_index = lax.axis_index("y") * lax.axis_size("x") + lax.axis_index("x")
        z = lax.axis_index("z")
        core = lax.axis_index("core")
        seq_len = tok_rows * dp_size
        top_count = routes.shape[1]
        local = w_gate.shape[0]
        capacity = 5 * tok_rows * top_count // (4 * EXPERTS)
        group_size = H // KVH
        score_scale = HD ** (-0.5)

        gains = jnp.stack([attn_gain, moe_gain], axis=1)
        rows = w_query.shape[0]
        dense_pack = jnp.concatenate(
            [w_output, w_query, w_key, w_value, w_router, gains, jnp.zeros((rows, 94), B16)], axis=1
        )
        wide = H * HD
        narrow = KVH * HD
        expert_ids = jnp.arange(EXPERTS, dtype=jnp.int32)
        hits = routes[:, :, None] == expert_ids[None, None, :]
        routed = jnp.any(hits, axis=1)
        place = jnp.where(
            routed, jnp.sum(jnp.where(hits, priority[:, :, None], 0), axis=1), jnp.int32(1 << 20)
        )
        ranks = jnp.sum((place[:, :, None] < place.T[None, :, :]).astype(F32), axis=0)
        code = pack_code(jnp.where(routed.T, ranks, -1.0).astype(B16))
        lead = ((2 * z + core) * local).astype(jnp.int32)[None]
        grad_pieces = column_pieces(jnp.concatenate([out_grad, code], axis=0), z_size)

        query_pos = dp_index * tok_rows + jnp.arange(tok_rows, dtype=jnp.int32)
        in_float = layer_input.astype(F32)
        steps = jnp.arange(tok_rows, dtype=jnp.int32)
        eff = w_gate.shape[2]
        in_rows, mid_rows = w_gate.shape[1], w_down.shape[1]
        folds = [w_down[:, :, f * eff : (f + 1) * eff] for f in range(model_width // eff)]
        if small_grid:
            relative = dp_index ^ jnp.arange(4, dtype=jnp.int32)
            key_pos = (relative[:, None] * tok_rows + steps[None, :]).reshape(seq_len)
        else:
            relative = jnp.arange(dp_size, dtype=jnp.int32)
            key_pos = jnp.arange(seq_len, dtype=jnp.int32)
        order = jnp.concatenate([relative, lead])
        visible = (key_pos[None, :] <= query_pos[:, None]) | (key_pos[None, :] < prefix_len[0])
        if small_grid:
            side = tok_rows // 2
            x_pack = jnp.concatenate([layer_input[:side], layer_input[side:]], axis=1)
            start_parts = gather_near(jnp.concatenate([x_pack, core_half(dense_pack, core)], axis=1))
            tables = (
                *turn_tables(key_pos.astype(F32)),
                jnp.where(visible.T, 0.0, MASKED_SCORE),
                jnp.pad(routed.astype(F32), ((0, 0), (0, 128 - EXPERTS))),
                [
                    jnp.concatenate([part[e] for part in (w_gate, w_up, *folds)], axis=0)
                    for e in range(local)
                ],
            )
            tables, grad_near = lax.optimization_barrier((tables, grad_pieces[1::2]))
            cosine, sine, bias, routed_wide, packs = tables
            start_parts += gather_far(after(start_parts, tables, *grad_near))
            dense_parts = [part[:, 2 * model_width :] for part in start_parts]
            dense_full = dense_assemble(dense_pack, dense_parts, dp_index, core)
        else:
            dense_full = lax.all_gather(dense_pack, ("y", "x"), axis=0, tiled=True)
            full_output = dense_full[:, :model_width]
            head_full = dense_full[:, model_width:]
            full_query = head_full[:, :wide]
            full_key = head_full[:, wide : wide + narrow]
            full_value = head_full[:, wide + narrow : wide + 2 * narrow]

        if small_grid:
            halves, per = 2, local // 2
            weights = []
            near_0 = gather_near(after(packs[0], *start_parts[2:]))
            far_0 = gather_far(after(near_0, dense_full))
            near_1 = gather_near(after(packs[1], *near_0, dense_full))
        else:
            halves, per = 1, local
            pack = jnp.concatenate([w_gate, w_up, *folds], axis=1)
            every = lax.all_gather(pack, ("y", "x"), axis=0, tiled=False)
            weights = [every[j] for j in range(dp_size)]
        chunks = []
        if small_grid:
            bias = after(bias, *near_0)
            (
                x_all, normed_all, query_rot, key_rot, value_all, attended, totals, misc, residual,
                moe_in, gates,
            ) = attention_forward(
                layer_input,
                start_parts,
                dense_full,
                bias,
                cosine,
                sine,
                routed_wide,
            )
            moe_in = after(moe_in, *near_1, *far_0)
            router_rows = misc[:EXPERTS].astype(B16)
            full_attn_gain = misc[EXPERTS]
            full_moe_gain = misc[EXPERTS + 1]
        else:
            places = query_pos.astype(F32)
            router_rows = head_full[:, wide + 2 * narrow : wide + 2 * narrow + EXPERTS].T
            full_attn_gain = head_full[:, wide + 2 * narrow + EXPERTS].astype(F32)
            full_moe_gain = head_full[:, wide + 2 * narrow + EXPERTS + 1].astype(F32)
            normed = rms_norm(in_float, full_attn_gain).astype(B16)
            query_lin = jnp.dot(normed, full_query, preferred_element_type=F32)
            key_lin = jnp.dot(normed, full_key, preferred_element_type=F32)
            value_low = jnp.dot(normed, full_value, preferred_element_type=F32).astype(B16)
            query_rot = (rotate(query_lin.reshape(tok_rows, H, HD), places) * score_scale).astype(B16)
            key_rot = rotate(key_lin.reshape(tok_rows, KVH, HD), places).astype(B16)
            key_rot = key_rot.reshape(tok_rows, narrow)
            both = jnp.concatenate([key_rot, value_low], axis=1)
            both_all = lax.all_gather(both, ("y", "x"), axis=0, tiled=True)
            key_all = both_all[:, :narrow]
            value_all = both_all[:, narrow:]

            def head_scores(head_idx):
                query_head = query_rot[:, head_idx * group_size : (head_idx + 1) * group_size, :]
                key_head = key_all[:, head_idx * HD : (head_idx + 1) * HD]
                scores = jnp.einsum("qgd,kd->gqk", query_head, key_head, preferred_element_type=F32)
                return jnp.where(visible[None, :, :], scores, MASKED_SCORE)

            mixed_heads = []
            log_totals = []
            for head_idx in range(KVH):
                scores = head_scores(head_idx)
                row_max = jnp.max(scores, axis=-1, keepdims=True)
                log_total = row_max + jnp.log(
                    jnp.sum(jnp.exp(scores - row_max), axis=-1, keepdims=True)
                )
                probs_low = jnp.exp(scores - log_total).astype(B16)
                value_head = value_all[:, head_idx * HD : (head_idx + 1) * HD]
                mixed_heads.append(
                    jnp.einsum("gqk,kd->qgd", probs_low, value_head, preferred_element_type=F32)
                )
                log_totals.append(log_total)
            attended = jnp.concatenate(mixed_heads, axis=1).reshape(tok_rows, wide).astype(B16)
            residual = in_float + jnp.dot(attended, full_output, preferred_element_type=F32)
            moe_in = rms_norm(residual, full_moe_gain).astype(B16)

        row_pieces = column_pieces(moe_in, z_size)
        grads_mine = jnp.stack(after(grad_pieces, moe_in))
        grads_other = swap_core(grads_mine)
        stage_1 = stage_2 = last_far = ()
        if small_grid:
            middle = packs[0].shape[0] // 2
            stage_1 = far_and_next(after(near_1, moe_in), packs[2])
        (slot_grads_mine,) = dispatch_rows(lead, grads_mine, None, None, local, capacity)
        (slot_grads_other,) = dispatch_rows(
            lead,
            after(grads_other, slot_grads_mine, *stage_1, row_pieces[1], row_pieces[-1]),
            None,
            None,
            local,
            capacity,
        )
        if small_grid:
            stage_2 = far_and_next(after(stage_1, slot_grads_other), packs[3])
            last_far = gather_far([part[middle:] for part in stage_2])
            chunks = [
                [(part, 0) for part in [packs[0], *near_0, *far_0]],
                [(part, 0) for part in [packs[1], *near_1, *stage_1[::-1]]],
                [(packs[2], 0)]
                + [(part, middle) for part in stage_1]
                + [(part, 0) for part in stage_2[::-1]],
                [(packs[3], 0)]
                + [(part, middle) for part in stage_2]
                + [(part, 0) for part in last_far],
            ]
        row_pieces = after(row_pieces, slot_grads_other)
        rows_mine = after(row_pieces, *stage_2)
        rows_other = [swap_core(piece) for piece in row_pieces]
        slot_rows_mine, slot_gates_mine = dispatch_rows(
            lead, grads_mine, rows_mine, router_rows, local, capacity
        )
        slot_rows_other, slot_gates_other = dispatch_rows(
            lead, grads_other, after(rows_other, slot_rows_mine), router_rows, local, capacity
        )
        slot_rows_other = after(slot_rows_other, *last_far)
        ys, dxs, weight_grads, sums = [], [], [], []
        for half in range(halves):
            y, dx, grads = experts(
                order,
                half * per,
                per,
                (slot_rows_mine, slot_rows_other),
                (slot_grads_mine, slot_grads_other),
                (slot_gates_mine, slot_gates_other),
                weights,
                chunks[half * per : (half + 1) * per],
                capacity,
                in_rows,
                mid_rows,
            )
            ys.append(y)
            dxs.append(dx)
            weight_grads.append(grads)

        def grid_sum(grads, got):
            totals = []
            for half in range(2):
                own = grads[4 * half][0]
                direct, last = got[half][0], got[1 - half][1]
                totals.append(own.astype(F32) + direct.astype(F32) + last.astype(F32))
            return totals

        def second_step(grads, via, *more):
            _, x_a, y_a, _, _, x_b, y_b, _ = grads
            to_x = [x_a, plus_low(x_b, via[1])]
            to_y = [y_b, plus_low(y_a, via[0])]
            if more:
                to_x.append(more[0])
                to_y.append(more[1])
            return cross(jnp.concatenate(to_x, axis=0), jnp.concatenate(to_y, axis=0))

        if small_grid:
            early, late = weight_grads
            via = cross(early[3], early[7])
            dxs = after(dxs, *via)
            early_got = second_step(early, via, late[3], late[7])
        dx_other = combine_rows(lead, z_size, grads_other, dxs, local, capacity)
        y_other = combine_rows(lead, z_size, grads_other, after(ys, dx_other), local, capacity)
        dx_other = after(swap_core(dx_other), y_other)
        dx_low = combine_rows(lead, 0, grads_mine, dxs, local, capacity, dx_other)
        dx_low, y_other = after((dx_low, swap_core(y_other)), dx_low[0])
        dx_pieces = column_send_some(dx_low, z_size) + column_send_last(dx_low, z_size)
        y_low = combine_rows(lead, 0, grads_mine, ys, local, capacity, y_other)
        dx_pieces = after(dx_pieces, *y_low)
        y_pieces = column_send_some(after(y_low, *dx_pieces), z_size)
        if small_grid:
            early_got = after(early_got, *dx_pieces)
            late_got = second_step(late, [got[2:3] for got in early_got])
        if small_grid:
            dense_blocks, normed_first, normed_a, normed_b, residual_grad = attention_backward(
                jnp.stack([dp_index, core]).astype(jnp.int32),
                (dx_low[0], *dx_pieces),
                out_grad,
                residual,
                gates,
                misc,
                attended,
                moe_in,
                (x_all, normed_all, query_rot, key_rot, value_all, totals),
                dense_full,
                after(bias, *early_got),
                cosine,
                sine,
            )
            late_got, y_pieces = after((late_got, y_pieces), residual_grad)
            normed_first, dense_blocks = after((normed_first, dense_blocks), *late_got, *y_pieces)
            y_pieces += column_send_last(y_low, z_size, *y_pieces)
            dense_first, dense_a, dense_b = core_halves(
                dense_blocks, swap_core(dense_blocks[1])
            )
            normed_got = grid_scatter_first(*normed_first)
            dense_got = grid_scatter_first(*after(dense_first, *normed_got))
            dense_low = across_z(
                jnp.concatenate(grid_scatter_second(dense_got, dense_a, dense_b), axis=0), z
            )
            (
                query_sum, key_sum, value_sum, output_sum, router_sum, attn_gain_sum, moe_gain_sum,
            ) = dense_outputs(core, dense_low, swap_core(dense_low), wide, narrow)
            y_pieces = after(y_pieces, *dense_got)
            normed_grad = jnp.concatenate(
                grid_scatter_second(normed_got, normed_a, normed_b, *dense_got), axis=0
            )
            first_value, first_pull = jax.vjp(lambda v: rms_norm(v, full_attn_gain), in_float)
            input_grad = residual_grad + first_pull(normed_grad)[0]
        else:
            y_pieces += column_send_last(y_low, z_size)
            moe_sum = column_sum(dx_low[0], dx_pieces)
            moe_in_grad = moe_sum[:, :model_width]
            gate_grad = (
                moe_sum[:, model_width : model_width + EXPERTS]
                + moe_sum[:, model_width + EXPERTS : model_width + 2 * EXPERTS]
            )
            logits = lax.dot_general(moe_in, router_rows, NT, preferred_element_type=F32)
            peak = jnp.max(jnp.where(routed, logits, MASKED_SCORE), axis=-1, keepdims=True)
            lifted = jnp.where(routed, jnp.exp(jnp.minimum(logits - peak, 0.0)), 0.0)
            gate_weights = lifted / jnp.sum(lifted, axis=-1, keepdims=True)
            grad_out = out_grad.astype(F32)
            centre = jnp.sum(gate_weights * gate_grad, axis=-1, keepdims=True)
            logit_low = (gate_weights * (gate_grad - centre)).astype(B16)
            moe_in_grad = moe_in_grad + jnp.dot(logit_low, router_rows, preferred_element_type=F32)
            norm_value, second_pull = jax.vjp(rms_norm, residual, full_moe_gain)
            resid_norm_grad, moe_gain_grad = second_pull(moe_in_grad)
            residual_grad = grad_out + resid_norm_grad
            attn_out_grad = residual_grad.astype(B16)
            router_grad = jnp.einsum("td,te->de", moe_in, logit_low, preferred_element_type=F32)
            wout_grad = jnp.einsum("tc,td->cd", attended, attn_out_grad, preferred_element_type=F32)
            attended_grad = (
                jnp.einsum("td,cd->tc", attn_out_grad, full_output, preferred_element_type=F32)
                .astype(B16)
                .reshape(tok_rows, H, HD)
            )
            query_grads = []
            key_parts = []
            value_parts = []
            for head_idx in range(KVH):
                scores = head_scores(head_idx)
                attention_probs = jnp.exp(scores - log_totals[head_idx])
                probs_low = attention_probs.astype(B16)
                grad_head = attended_grad[:, head_idx * group_size : (head_idx + 1) * group_size, :]
                query_head = query_rot[:, head_idx * group_size : (head_idx + 1) * group_size, :]
                key_head = key_all[:, head_idx * HD : (head_idx + 1) * HD]
                value_head = value_all[:, head_idx * HD : (head_idx + 1) * HD]
                probs_grad = jnp.einsum("qgd,kd->gqk", grad_head, value_head, preferred_element_type=F32)
                row_delta = jnp.sum(attention_probs * probs_grad, axis=-1, keepdims=True)
                score_grad = (attention_probs * (probs_grad - row_delta)).astype(B16)
                query_grads.append(
                    jnp.einsum("gqk,kd->qgd", score_grad, key_head, preferred_element_type=F32)
                )
                key_parts.append(
                    jnp.einsum("gqk,qgd->kd", score_grad, query_head, preferred_element_type=F32)
                )
                value_parts.append(
                    jnp.einsum("gqk,qgd->kd", probs_low, grad_head, preferred_element_type=F32)
                )
            both_part = jnp.concatenate(key_parts + value_parts, axis=1)
            both_sum = lax.psum_scatter(both_part, ("y", "x"), scatter_dimension=0, tiled=True)
            query_rot_grad = jnp.concatenate(query_grads, axis=1) * score_scale
            key_rot_grad = both_sum[:, :narrow].reshape(tok_rows, KVH, HD)
            value_grad = both_sum[:, narrow:].astype(B16)
            query_grad = rotate(query_rot_grad, -places).reshape(tok_rows, wide).astype(B16)
            key_grad = rotate(key_rot_grad, -places).reshape(tok_rows, narrow).astype(B16)
            wq_grad = jnp.einsum("td,tc->dc", normed, query_grad, preferred_element_type=F32)
            wk_grad = jnp.einsum("td,tc->dc", normed, key_grad, preferred_element_type=F32)
            wv_grad = jnp.einsum("td,tc->dc", normed, value_grad, preferred_element_type=F32)
            normed_grad = jnp.einsum("tc,dc->td", query_grad, full_query, preferred_element_type=F32)
            normed_grad = normed_grad + jnp.einsum(
                "tc,dc->td", key_grad, full_key, preferred_element_type=F32
            )
            normed_grad = normed_grad + jnp.einsum(
                "tc,dc->td", value_grad, full_value, preferred_element_type=F32
            )
            first_value, first_pull = jax.vjp(rms_norm, in_float, full_attn_gain)
            input_norm_grad, attn_gain_grad = first_pull(normed_grad)
            input_grad = residual_grad + input_norm_grad
            query_sum = dense_sum(wq_grad)
            key_sum = dense_sum(wk_grad)
            value_sum = dense_sum(wv_grad)
            output_sum = dense_sum(wout_grad)
            extra_sum = dense_sum(
                jnp.concatenate(
                    [
                        router_grad,
                        attn_gain_grad[:, None],
                        moe_gain_grad[:, None],
                        jnp.zeros((model_width, EXTRA - EXPERTS - 2), F32),
                    ],
                    axis=1,
                )
            )
            router_sum = extra_sum[:, :EXPERTS]
            attn_gain_sum = extra_sum[:, EXPERTS]
            moe_gain_sum = extra_sum[:, EXPERTS + 1]
        layer_output = (residual + column_sum(y_low[0], y_pieces)).astype(B16)
        if small_grid:
            parts = grid_sum(early, early_got) + grid_sum(late, late_got)
            pack_grad = jnp.concatenate(parts, axis=0)
        else:
            pack_grad = lax.psum_scatter(
                weight_grads[0][0].astype(F32), ("y", "x"), scatter_dimension=0, tiled=False
            )
        down = 2 * in_rows
        expert_grads = [
            pack_grad[:, :in_rows],
            pack_grad[:, in_rows:down],
            jnp.concatenate(
                [
                    pack_grad[:, down + f * mid_rows : down + (f + 1) * mid_rows]
                    for f in range(model_width // eff)
                ],
                axis=2,
            ),
        ]

        return (
            layer_output,
            input_grad,
            attn_gain_sum,
            query_sum,
            key_sum,
            value_sum,
            output_sum,
            moe_gain_sum,
            router_sum,
            expert_grads[0],
            expert_grads[1],
            expert_grads[2],
        )

    return body


def solution(mesh):
    groups = mesh.shape["expert"]
    members = mesh.shape["dp"]
    z_size = groups // 2
    side = math.isqrt(members)
    grid = Mesh(
        mesh.devices.reshape(z_size, 2, members // side, side), ("z", "core", "y", "x")
    )
    expert = ("z", "core")
    dp = ("y", "x")
    every = expert + dp
    placed = (
        P(every, None),
        P(dp),
        P(dp, None),
        P(dp, None),
        P(dp, None),
        P(dp, None),
        P(dp),
        P(dp, None),
        P(expert, dp, None),
        P(expert, dp, None),
        P(expert, dp, None),
        P(every, None),
        P(every, None),
        P(expert),
        P(every, None),
    )
    return jax.shard_map(
        make_body(z_size, members == 4 and side == 2 and EXPERTS == 4 * groups),
        mesh=grid,
        in_specs=placed,
        out_specs=(
            P(every, None),
            P(every, None),
            P(dp),
            P(dp, None),
            P(dp, None),
            P(dp, None),
            P(dp, None),
            P(dp),
            P(dp, None),
            P(expert, dp, None),
            P(expert, dp, None),
            P(expert, dp, None),
        ),
        check_vma=False,
    )
```

```python
import math

import jax
import jax.numpy as jnp
from jax import lax
from jax.experimental import pallas as pl
from jax.experimental.pallas import tpu as pltpu
from jax.sharding import Mesh
from jax.sharding import PartitionSpec as P

H = 16
KVH = 8
HD = 64
EXPERTS = 32
EPSILON = 1e-06
ROPE_BASE = 10000.0
MASKED_SCORE = -1e30
F32 = jnp.float32
B16 = jnp.bfloat16
SWAP = [(0, 1), (1, 0)]
VMEM_LIMIT = 60 * 1024 * 1024


def rms_norm(values, gain_vec):
    return (
        values * lax.rsqrt(jnp.mean(values * values, axis=-1, keepdims=True) + EPSILON) * gain_vec
    )


def rotate(vectors, places):
    half_dim = vectors.shape[-1] // 2
    frequency = jnp.exp(
        jnp.arange(half_dim, dtype=F32) * (-2.0 * math.log(ROPE_BASE) / vectors.shape[-1])
    )
    angles = places[:, None] * frequency[None, :]
    cosine = jnp.cos(angles)[:, None, :]
    sine_vals = jnp.sin(angles)[:, None, :]
    first_half = vectors[..., :half_dim]
    second = vectors[..., half_dim:]
    return jnp.concatenate(
        [first_half * cosine - second * sine_vals, second * cosine + first_half * sine_vals],
        axis=-1,
    )


def swap_core(rows):
    return lax.ppermute(rows, "core", SWAP)


def cyclic(rows, size, shift):
    return lax.ppermute(rows, "z", [(i, (i + shift) % size) for i in range(size)])


def after(value, *others):
    return lax.optimization_barrier((value, *others))[0]


def gather_near(shard):
    return [lax.ppermute(shard, "x", SWAP), lax.ppermute(shard, "y", SWAP)]


def gather_far(near):
    from_x, from_y = near
    half = from_x.shape[0] // 2
    return [lax.ppermute(from_x[:half], "y", SWAP), lax.ppermute(from_y[half:], "x", SWAP)]


def grid_gather(shard):
    near = gather_near(shard)
    return near + gather_far(near)


def cross(to_x, to_y):
    return lax.ppermute(to_x, "x", SWAP), lax.ppermute(to_y, "y", SWAP)


def far_and_next(near, shard):
    from_x, from_y = near
    half = shard.shape[0] // 2
    return cross(
        jnp.concatenate([from_y[-half:], shard], axis=0),
        jnp.concatenate([from_x[-2 * half : -half], shard], axis=0),
    )


def plus_low(a, b):
    return (a.astype(F32) + b.astype(F32)).astype(B16)


def grid_scatter_first(first_a, first_b):
    return lax.ppermute(first_a, "x", SWAP), lax.ppermute(first_b, "y", SWAP)


def grid_scatter_second(got, rest_a, rest_b, *early):
    got_a, got_b = after(got, *early)
    onward_a = (rest_a[1].astype(F32) + got_a[1].astype(F32)).astype(B16)
    onward_b = (rest_b[1].astype(F32) + got_b[1].astype(F32)).astype(B16)
    last_a = lax.ppermute(onward_a, "y", SWAP)
    last_b = lax.ppermute(onward_b, "x", SWAP)
    return (
        rest_a[0].astype(F32) + got_a[0].astype(F32) + last_a.astype(F32),
        rest_b[0].astype(F32) + got_b[0].astype(F32) + last_b.astype(F32),
    )


def row_halves(parts):
    own, to_x, to_y, diag = [parts[j] for j in range(4)]
    half = own.shape[0] // 2
    first = (
        jnp.stack([to_x[:half], diag[:half]]),
        jnp.stack([to_y[half:], diag[half:]]),
    )
    return first, (own[:half], to_y[:half]), (own[half:], to_x[half:])


def column_pieces(rows, size):
    return [rows] + [cyclic(rows, size, -k) for k in range(1, size)]


def column_send_some(low, size):
    return [cyclic(low[k], size, k) for k in range(1, size) if 2 * k != size]


def column_send_last(low, size, *hold):
    return [cyclic(after(low[size // 2], *hold), size, size // 2)]


def column_sum(own, pieces):
    return own.astype(F32) + sum(piece.astype(F32) for piece in pieces)


def assemble(places, shard, moved, other, rows):
    def kernel(places_ref, shard_ref, moved_ref, other_ref, out_ref):
        def put(i, value):
            start = pl.multiple_of(places_ref[i] * rows, rows)
            out_ref[pl.ds(start, value.shape[0]), :] = value

        put(0, shard_ref[...])
        for j in range(3):
            put(1 + j, moved_ref[j * rows : (j + 1) * rows, :])
            put(4 + j, other_ref[j * rows : (j + 1) * rows, :])

    def whole(array_shape):
        return pl.BlockSpec(array_shape, lambda i, places: (0, 0))

    out_rows, cols = 8 * rows, shard.shape[1]
    return pl.pallas_call(
        kernel,
        out_shape=jax.ShapeDtypeStruct((out_rows, cols), shard.dtype),
        grid_spec=pltpu.PrefetchScalarGridSpec(
            num_scalar_prefetch=1,
            grid=(1,),
            in_specs=[whole(a.shape) for a in (shard, moved, other)],
            out_specs=whole((out_rows, cols)),
        ),
        compiler_params=pltpu.CompilerParams(vmem_limit_bytes=VMEM_LIMIT),
        name="assemble",
    )(places, shard, moved, other)


def one_hot_slots(codes, capacity):
    slots = lax.broadcasted_iota(jnp.int32, (capacity, codes.shape[1]), 0).astype(F32)
    return [(slots == codes[e : e + 1, :]).astype(F32) for e in range(codes.shape[0])]


def row_of(table, index):
    at = lax.broadcasted_iota(jnp.int32, table.shape, 0)
    return jnp.sum(jnp.where(at == index, table, 0.0), axis=0, keepdims=True)


def pack_code(code):
    rows = code.shape[0] // 4
    wide = jnp.concatenate([code[c * rows : (c + 1) * rows] for c in range(4)], axis=1)
    return jnp.concatenate([wide, jnp.full((16 - rows, wide.shape[1]), -1.0, B16)], axis=0)


def unpack_code(block, tokens):
    rows = EXPERTS // 4
    wide = block.astype(F32)
    return jnp.concatenate(
        [wide[:rows, c * tokens : (c + 1) * tokens] for c in range(4)], axis=0
    )


def dispatch_rows(lead, packed, rows, router, local, capacity):
    pieces, packed_rows, width = packed.shape
    tokens = packed_rows - 16
    slots = local * capacity
    with_gates = router is not None

    def kernel(lead_ref, packed_ref, *rest):
        first = lead_ref[0]
        if with_gates:
            router_ref, out_ref, gate_out, rows_ref = rest[pieces:]
            for p in range(pieces):

                @pl.when(pl.program_id(0) == p)
                def _():
                    rows_ref[...] = rest[p][...]

            table = unpack_code(packed_ref[0], tokens)
            source = rows_ref[...]
        else:
            (out_ref,) = rest
            table = unpack_code(packed_ref[0, tokens:, :], tokens)
            source = packed_ref[0, :tokens, :]
        codes = jnp.concatenate([row_of(table, first + e) for e in range(local)], axis=0)
        picks = one_hot_slots(codes, capacity)
        select = jnp.concatenate([p.astype(B16) for p in picks], axis=0)
        out_ref[0] = jnp.dot(select, source, preferred_element_type=F32).astype(B16)
        if with_gates:
            logits = lax.dot_general(
                router_ref[...], source, (((1,), (1,)), ((), ())), preferred_element_type=F32
            )
            routed = table >= 0.0
            peak = jnp.max(jnp.where(routed, logits, MASKED_SCORE), axis=0, keepdims=True)
            lifted = jnp.where(routed, jnp.exp(jnp.minimum(logits - peak, 0.0)), 0.0)
            gates = lifted / jnp.sum(lifted, axis=0, keepdims=True)
            for e in range(local):
                gate_row = row_of(gates, first + e)
                column = jnp.sum(picks[e] * gate_row, axis=1, keepdims=True)
                gate_out[0, e * capacity : (e + 1) * capacity, :] = jnp.broadcast_to(
                    column, (capacity, 128)
                )

    out_specs = [pl.BlockSpec((1, slots, width), lambda p, lead: (p, 0, 0))]
    out_shape = [jax.ShapeDtypeStruct((pieces, slots, width), B16)]
    args = [packed]
    if with_gates:
        in_specs = [
            pl.BlockSpec((1, 16, width), lambda p, lead: (p, tokens // 16, 0)),
            *[pl.BlockSpec((tokens, width), lambda p, lead: (0, 0)) for _ in rows],
            pl.BlockSpec((EXPERTS, width), lambda p, lead: (0, 0)),
        ]
        out_specs.append(pl.BlockSpec((1, slots, 128), lambda p, lead: (p, 0, 0)))
        out_shape.append(jax.ShapeDtypeStruct((pieces, slots, 128), F32))
        args += [*rows, router]
    else:
        in_specs = [pl.BlockSpec((1, packed_rows, width), lambda p, lead: (p, 0, 0))]
    return pl.pallas_call(
        kernel,
        out_shape=out_shape,
        grid_spec=pltpu.PrefetchScalarGridSpec(
            num_scalar_prefetch=1,
            grid=(pieces,),
            in_specs=in_specs,
            out_specs=out_specs,
            scratch_shapes=[pltpu.VMEM((tokens, width), B16)] if with_gates else [],
        ),
        compiler_params=pltpu.CompilerParams(vmem_limit_bytes=VMEM_LIMIT),
        name="dispatch",
    )(lead, *args)


def combine_rows(lead, first, packed, slot_rows, local, capacity, addend=None):
    pieces, packed_rows, code_width = packed.shape
    tokens = packed_rows - 16
    halves = len(slot_rows)
    slots, width = slot_rows[0].shape[1:]
    per = local // halves

    def kernel(lead_ref, code_ref, *rest):
        table = unpack_code(code_ref[0], tokens)
        here = lead_ref[0]
        codes = jnp.concatenate([row_of(table, here + e) for e in range(local)], axis=0)
        picks = one_hot_slots(codes, capacity)
        total = None
        for h in range(halves):
            select = jnp.concatenate(
                [p.astype(B16) for p in picks[h * per : (h + 1) * per]], axis=0
            )
            part = lax.dot_general(
                select, rest[h][0], (((0,), (0,)), ((), ())), preferred_element_type=F32
            )
            total = part if total is None else total + part
        if addend is None:
            rest[halves][0] = total.astype(B16)
        else:
            low = (total + rest[halves][0].astype(F32)).astype(B16)
            for p in range(pieces):

                @pl.when(pl.program_id(0) == p)
                def _():
                    rest[halves + 1 + p][...] = low

    in_specs = [pl.BlockSpec((1, 16, code_width), lambda p, lead: (p, tokens // 16, 0))]
    in_specs += [
        pl.BlockSpec((1, slots, width), lambda p, lead: (p + first, 0, 0)) for _ in range(halves)
    ]
    added = [] if addend is None else [addend]
    in_specs += [pl.BlockSpec((1, tokens, width), lambda p, lead: (p, 0, 0)) for _ in added]
    if addend is None:
        out_shape = jax.ShapeDtypeStruct((pieces, tokens, width), B16)
        out_specs = pl.BlockSpec((1, tokens, width), lambda p, lead: (p, 0, 0))
    else:
        out_shape = [jax.ShapeDtypeStruct((tokens, width), B16)] * pieces
        out_specs = [pl.BlockSpec((tokens, width), lambda p, lead: (0, 0))] * pieces
    return pl.pallas_call(
        kernel,
        out_shape=out_shape,
        grid_spec=pltpu.PrefetchScalarGridSpec(
            num_scalar_prefetch=1,
            grid=(pieces,),
            in_specs=in_specs,
            out_specs=out_specs,
        ),
        compiler_params=pltpu.CompilerParams(vmem_limit_bytes=VMEM_LIMIT),
        name="combine",
    )(lead, packed, *slot_rows, *added)


def experts(order, start, count, rows, grads, gates, weights, chunks, capacity, in_rows, mid_rows):
    half, _, width = rows[0].shape
    pieces = 2 * half
    split = bool(chunks)
    n = 4 if split else len(weights)
    extra = [array for chunk in chunks for array, _ in chunk]
    given = len(weights) + len(extra)
    pack_rows, eff = chunks[0][0][0].shape if split else weights[0].shape[1:]
    folds = width // eff
    total_rows = pieces * capacity
    first_half = count // 2
    large = total_rows > 1000

    def kernel(order_ref, *refs):
        rows_a, rows_b, grads_a, grads_b, gates_a, gates_b = refs[:6]
        pack = refs[6 : 6 + given]
        y_out, dx_out = refs[6 + given : 8 + given]
        outs = refs[8 + given : -6]
        full_g, full_u, full_d, grad_g, grad_u, grad_d = refs[-6:]

        def at_in(j):
            return pl.ds(pl.multiple_of(order_ref[j] * in_rows, in_rows), in_rows)

        def at_mid(j):
            return pl.ds(pl.multiple_of(order_ref[j] * mid_rows, mid_rows), mid_rows)

        def load(j, take):
            full_g[at_in(j), :] = take(0, in_rows)
            full_u[at_in(j), :] = take(in_rows, 2 * in_rows)
            for f in range(folds):
                full_d[at_mid(j), f * eff : (f + 1) * eff] = take(
                    2 * in_rows + f * mid_rows, 2 * in_rows + (f + 1) * mid_rows
                )

        def rows_from(ref, offset):
            return lambda lo, hi: ref[offset + lo : offset + hi, :]

        def two_halves(a, b):
            middle = pack_rows // 2

            def take(lo, hi):
                if hi <= middle:
                    return a(lo, hi)
                if lo >= middle:
                    return b(lo - middle, hi - middle)
                return jnp.concatenate([a(lo, middle), b(0, hi - middle)], axis=0)

            return take

        for j in range(len(weights)):
            load(j, lambda lo, hi, ref=pack[j]: ref[0, lo:hi])
        for c in range(len(chunks)):
            own, from_x, from_y, diag_a, diag_b = [
                rows_from(pack[5 * c + i], chunks[c][i][1]) for i in range(5)
            ]

            @pl.when(pl.program_id(0) == c)
            def _():
                load(0, own)
                load(1, from_x)
                load(2, from_y)
                load(3, two_halves(diag_a, diag_b))

        def joined(a, b, w):
            return jnp.concatenate(
                [
                    a[...].reshape(half * capacity, w),
                    b[...].reshape(half * capacity, w),
                ],
                axis=0,
            )

        x = joined(rows_a, rows_b, width)
        g = joined(grads_a, grads_b, width)
        gate = joined(gates_a, gates_b, 128)[:, 0:1]
        nt = (((1,), (1,)), ((), ()))
        tn = (((0,), (0,)), ((), ()))
        gate_proj = jnp.dot(x, full_g[...], preferred_element_type=F32)
        up_proj = jnp.dot(x, full_u[...], preferred_element_type=F32)
        down_grad = lax.dot_general(g, full_d[...], nt, preferred_element_type=F32)
        sigmoid = 1.0 / (1.0 + jnp.exp(-gate_proj))
        silu = gate_proj * sigmoid
        activated = silu * up_proj
        slot_grad = jnp.sum(activated * down_grad, axis=1, keepdims=True)
        here = order_ref[n] + start + pl.program_id(0)
        lane = lax.broadcasted_iota(jnp.int32, (total_rows, 128), 1)
        high = slot_grad.astype(B16).astype(F32)
        tail = jnp.where(lane == here, high, jnp.where(lane == here + EXPERTS, slot_grad - high, 0.0))
        dx_out[:, :, width:] = tail.astype(B16).reshape(pieces, capacity, 128)
        scaled = (gate * activated).astype(B16)
        act_grad = gate * down_grad
        gate_grad = (act_grad * up_proj * (sigmoid * (1.0 + gate_proj * (1.0 - sigmoid)))).astype(
            B16
        )
        up_grad = (act_grad * silu).astype(B16)
        y = jnp.dot(scaled, full_d[...], preferred_element_type=F32)
        y_out[...] = y.astype(B16).reshape(pieces, capacity, width)
        dx = lax.dot_general(gate_grad, full_g[...], nt, preferred_element_type=F32)
        dx = dx + lax.dot_general(up_grad, full_u[...], nt, preferred_element_type=F32)
        dx_out[:, :, :width] = dx.astype(B16).reshape(pieces, capacity, width)
        grad_g[...] = lax.dot_general(x, gate_grad, tn, preferred_element_type=F32).astype(B16)
        grad_u[...] = lax.dot_general(x, up_grad, tn, preferred_element_type=F32).astype(B16)
        grad_d[...] = lax.dot_general(scaled, g, tn, preferred_element_type=F32).astype(B16)

        def give(ref, slot, j):
            ref[slot, 0, :in_rows] = grad_g[at_in(j), :]
            ref[slot, 0, in_rows : 2 * in_rows] = grad_u[at_in(j), :]
            for f in range(folds):
                ref[slot, 0, 2 * in_rows + f * mid_rows : 2 * in_rows + (f + 1) * mid_rows] = grad_d[
                    at_mid(j), f * eff : (f + 1) * eff
                ]

        if split:

            @pl.when(pl.program_id(0) < first_half)
            def _():
                for j in range(4):
                    give(outs[j], 0, j)

            @pl.when(pl.program_id(0) >= first_half)
            def _():
                for j in range(4):
                    give(outs[4 + j], 0, j)
        else:
            for j in range(n):
                give(outs[0], j, j)

    def single():
        return dict(pipeline_mode=pl.Buffered(1)) if large else {}

    def rows_spec(w):
        return pl.BlockSpec((half, capacity, w), lambda e, o: (0, e + start, 0), **single())

    in_specs = [rows_spec(width)] * 4 + [rows_spec(128)] * 2
    for _ in weights:
        in_specs.append(pl.BlockSpec((1, pack_rows, eff), lambda e, o: (e + start, 0, 0)))
    for part in extra:
        in_specs.append(pl.BlockSpec(part.shape, lambda e, o: (0, 0)))
    slots = count * capacity
    out_specs = [
        pl.BlockSpec((pieces, capacity, w), lambda e, o: (0, e, 0), **single())
        for w in (width, width + 128)
    ]
    out_shape = [
        jax.ShapeDtypeStruct((pieces, slots, width), B16),
        jax.ShapeDtypeStruct((pieces, slots, width + 128), B16),
    ]
    if split:
        for at in (
            lambda e, o: (0, jnp.minimum(e, first_half - 1), 0, 0),
            lambda e, o: (0, jnp.maximum(e - first_half, 0), 0, 0),
        ):
            for _ in range(4):
                out_specs.append(pl.BlockSpec((1, 1, pack_rows, eff), at))
                out_shape.append(jax.ShapeDtypeStruct((1, first_half, pack_rows, eff), B16))
    else:
        out_specs.append(pl.BlockSpec((n, 1, pack_rows, eff), lambda e, o: (0, e, 0, 0)))
        out_shape.append(jax.ShapeDtypeStruct((n, count, pack_rows, eff), B16))
    results = pl.pallas_call(
        kernel,
        out_shape=out_shape,
        grid_spec=pltpu.PrefetchScalarGridSpec(
            num_scalar_prefetch=1,
            grid=(count,),
            in_specs=in_specs,
            out_specs=out_specs,
            scratch_shapes=[
                pltpu.VMEM((n * in_rows, eff), B16),
                pltpu.VMEM((n * in_rows, eff), B16),
                pltpu.VMEM((n * mid_rows, width), B16),
                pltpu.VMEM((n * in_rows, eff), B16),
                pltpu.VMEM((n * in_rows, eff), B16),
                pltpu.VMEM((n * mid_rows, width), B16),
            ],
        ),
        compiler_params=pltpu.CompilerParams(vmem_limit_bytes=VMEM_LIMIT),
        name="experts",
    )(order, *rows, *grads, *gates, *weights, *extra)
    return results[0], results[1], results[2:]


NT = (((1,), (1,)), ((), ()))
TN = (((0,), (0,)), ((), ()))
GROUPS = KVH // 2
EXTRA = 128


def turn(vectors, cosine, sine):
    lane = lax.broadcasted_iota(jnp.int32, vectors.shape, 1)
    ahead = pltpu.roll(vectors, 2 * HD - HD // 2, 1)
    behind = pltpu.roll(vectors, HD // 2, 1)
    return vectors * cosine + jnp.where(lane % HD < HD // 2, ahead, behind) * sine


def turn_tables(places):
    lane = jnp.arange(2 * HD, dtype=jnp.int32)
    frequency = jnp.exp(
        (lane % (HD // 2)).astype(F32) * (-2.0 * math.log(ROPE_BASE) / HD)
    )
    angles = places[:, None] * frequency[None, :]
    sign = jnp.where(lane % HD < HD // 2, -1.0, 1.0)
    return jnp.cos(angles), jnp.sin(angles) * sign[None, :]


def attention_forward(x_own, x_parts, dense_full, bias, cosine, sine, routed):
    tok_rows, width = x_own.shape
    seq_len = 4 * tok_rows
    scale = HD ** (-0.5)
    wide, narrow = H * HD, KVH * HD

    def kernel(
        own_ref, xa_ref, xb_ref, ya_ref, yb_ref, da_ref, db_ref, ea_ref, eb_ref,
        tail_ref, wo_ref, wq_ref, wk_ref, wv_ref, bias_ref, cos_ref, sin_ref, routed_ref,
        x_ref, normed_ref, q_out, k_out, v_out, att_out, total_out, misc_out, residual_out, moe_out,
        gates_out,
    ):
        step = pl.program_id(0)

        @pl.when(step == 0)
        def _():
            rows = jnp.transpose(tail_ref[...].astype(F32))
            misc_out[...] = rows
            at = 0
            for ref in (own_ref, xa_ref, xb_ref, ya_ref, yb_ref, da_ref, ea_ref, db_ref, eb_ref):
                x_ref[at : at + ref.shape[0], :] = ref[...]
                at += ref.shape[0]
            x = x_ref[...].astype(F32)
            scaled = x * lax.rsqrt(jnp.mean(x * x, axis=1, keepdims=True) + EPSILON)
            normed_ref[...] = (scaled * rows[EXPERTS : EXPERTS + 1, :]).astype(B16)
            residual_out[...] = x[:tok_rows]

        normed = normed_ref[...]
        cos, sin = cos_ref[...], sin_ref[...]
        key = turn(jnp.dot(normed, wk_ref[...], preferred_element_type=F32), cos, sin).astype(B16)
        value = jnp.dot(normed, wv_ref[...], preferred_element_type=F32).astype(B16)
        query = jnp.dot(normed[:tok_rows], wq_ref[...], preferred_element_type=F32)
        cos, sin = cos[:tok_rows], sin[:tok_rows]
        query = jnp.concatenate(
            [turn(query[:, 128 * j : 128 * (j + 1)], cos, sin) for j in range(2)], axis=1
        )
        query = (query * scale).astype(B16)
        k_out[...] = key
        v_out[...] = value
        q_out[...] = query
        mixed, totals = [], []
        for j in range(4):
            lanes = slice(HD * (j // 2), HD * (j // 2 + 1))
            scores = lax.dot_general(
                key[:, lanes], query[:, HD * j : HD * (j + 1)], NT, preferred_element_type=F32
            )
            scores = scores + bias_ref[...]
            peak = jnp.max(scores, axis=0, keepdims=True)
            probs = jnp.exp(scores - peak)
            total = jnp.sum(probs, axis=0, keepdims=True)
            out = lax.dot_general(
                value[:, lanes], probs.astype(B16), TN, preferred_element_type=F32
            )
            mixed.append(out / total)
            totals.append(peak + jnp.log(total))
        attended = jnp.transpose(jnp.concatenate(mixed, axis=0)).astype(B16)
        att_out[...] = attended
        total_out[0] = jnp.concatenate(totals + totals, axis=0)
        residual_out[...] += jnp.dot(attended, wo_ref[...], preferred_element_type=F32)

        @pl.when(step == GROUPS - 1)
        def _():
            total = residual_out[...]
            scaled = total * lax.rsqrt(jnp.mean(total * total, axis=1, keepdims=True) + EPSILON)
            moe_in = (scaled * misc_out[EXPERTS + 1 : EXPERTS + 2, :]).astype(B16)
            moe_out[...] = moe_in
            logits = jnp.dot(moe_in, tail_ref[...], preferred_element_type=F32)
            here = routed_ref[...] > 0.0
            peak = jnp.max(jnp.where(here, logits, MASKED_SCORE), axis=1, keepdims=True)
            lifted = jnp.where(here, jnp.exp(jnp.minimum(logits - peak, 0.0)), 0.0)
            gates_out[...] = lifted / jnp.sum(lifted, axis=1, keepdims=True)

    def fixed(*block):
        return pl.BlockSpec(block, lambda i: (0,) * len(block))

    def columns(rows, cols, lead=0):
        return pl.BlockSpec((rows, cols), lambda i: (0, lead + i))

    return pl.pallas_call(
        kernel,
        grid=(GROUPS,),
        in_specs=[
            fixed(tok_rows, width),
            *[
                pl.BlockSpec((part.shape[0], width), lambda i, c=c: (0, c))
                for part in x_parts
                for c in range(2)
            ],
            pl.BlockSpec((width, 128), lambda i: (0, (width + wide + 2 * narrow) // 128)),
            pl.BlockSpec((256, width), lambda i: (i, 0)),
            columns(width, 256, width // 256),
            columns(width, 128, (width + wide) // 128),
            columns(width, 128, (width + wide + narrow) // 128),
            fixed(seq_len, tok_rows),
            fixed(seq_len, 128),
            fixed(seq_len, 128),
            fixed(tok_rows, 128),
        ],
        out_specs=[
            fixed(seq_len, width),
            fixed(seq_len, width),
            columns(tok_rows, 256),
            columns(seq_len, 128),
            columns(seq_len, 128),
            columns(tok_rows, 256),
            pl.BlockSpec((1, 8, tok_rows), lambda i: (i, 0, 0)),
            fixed(128, width),
            fixed(tok_rows, width),
            fixed(tok_rows, width),
            fixed(tok_rows, 128),
        ],
        out_shape=[
            jax.ShapeDtypeStruct((seq_len, width), B16),
            jax.ShapeDtypeStruct((seq_len, width), B16),
            jax.ShapeDtypeStruct((tok_rows, wide), B16),
            jax.ShapeDtypeStruct((seq_len, narrow), B16),
            jax.ShapeDtypeStruct((seq_len, narrow), B16),
            jax.ShapeDtypeStruct((tok_rows, wide), B16),
            jax.ShapeDtypeStruct((GROUPS, 8, tok_rows), F32),
            jax.ShapeDtypeStruct((128, width), F32),
            jax.ShapeDtypeStruct((tok_rows, width), F32),
            jax.ShapeDtypeStruct((tok_rows, width), B16),
            jax.ShapeDtypeStruct((tok_rows, 128), F32),
        ],
        compiler_params=pltpu.CompilerParams(vmem_limit_bytes=VMEM_LIMIT),
        name="attention",
    )(
        x_own, *[part for part in x_parts for _ in range(2)], *[dense_full] * 5,
        bias, cosine, sine, routed,
    )


def attention_backward(
    where_here, moe_sums, out_grad, residual, gates, misc, attended, moe_in, saved,
    dense_full, bias, cosine, sine,
):
    x_all, normed_all, query_rot, key_rot, value_all, totals = saved
    terms = len(moe_sums)
    seq_len, width = x_all.shape
    tok_rows = query_rot.shape[0]
    scale = HD ** (-0.5)
    wide, narrow = H * HD, KVH * HD
    block = width // 8
    output_at = wide + 2 * narrow

    def kernel(here_ref, *refs):
        sums = refs[:terms]
        (
            grad_ref, residual_ref, gates_ref, misc_ref, tail_ref, wo_ref, att_ref, moe_ref,
            normed_ref, q_ref, k_ref, v_ref, total_ref,
            x_ref, wq_ref, wk_ref, wv_ref, bias_ref, cos_ref, sin_ref,
            keep_out, give_out, first_a_out, first_b_out, rest_a_out, rest_b_out, residual_out,
            normed_t, grad_sum, og_ref, logit_ref, gain_ref,
        ) = refs[terms:]
        step = pl.program_id(0)
        dp, core = here_ref[0], here_ref[1]

        @pl.when(step == 0)
        def _():
            normed_t[...] = jnp.transpose(normed_ref[...])
            grad_sum[...] = jnp.zeros((seq_len, width), F32)
            total = sums[0][...].astype(F32)
            for ref in sums[1:]:
                total = total + ref[...].astype(F32)
            behind = total[:, width:]
            gate_grad = behind + pltpu.roll(behind, 128 - EXPERTS, 1)
            gate = gates_ref[...]
            centre = jnp.sum(gate * gate_grad, axis=1, keepdims=True)
            logit_low = (gate * (gate_grad - centre)).astype(B16)
            logit_ref[...] = logit_low
            moe_grad = total[:, :width] + lax.dot_general(
                logit_low, tail_ref[...], NT, preferred_element_type=F32
            )
            residual = residual_ref[...]
            rate = lax.rsqrt(jnp.mean(residual * residual, axis=1, keepdims=True) + EPSILON)
            gain_ref[...] = jnp.sum(moe_grad * residual * rate, axis=0, keepdims=True)
            lifted = moe_grad * misc_ref[EXPERTS + 1 : EXPERTS + 2, :]
            inner = jnp.mean(lifted * residual, axis=1, keepdims=True)
            residual_grad = (
                grad_ref[...].astype(F32) + rate * lifted - residual * (rate * rate * rate * inner)
            )
            residual_out[...] = residual_grad
            og_ref[...] = residual_grad.astype(B16)

        og = og_ref[...]
        att_grad = lax.dot_general(og, wo_ref[...], NT, preferred_element_type=F32).astype(B16)
        query, key, value = q_ref[...], k_ref[...], v_ref[...]
        query_grads, key_grads, value_grads = [], [], []
        for j in range(4):
            lanes = slice(HD * (j // 2), HD * (j // 2 + 1))
            mine = slice(HD * j, HD * (j + 1))
            scores = lax.dot_general(
                key[:, lanes], query[:, mine], NT, preferred_element_type=F32
            )
            probs = jnp.exp(scores + bias_ref[...] - total_ref[0, j : j + 1, :])
            probs_grad = lax.dot_general(
                value[:, lanes], att_grad[:, mine], NT, preferred_element_type=F32
            )
            delta = jnp.sum(probs * probs_grad, axis=0, keepdims=True)
            score_grad = (probs * (probs_grad - delta)).astype(B16)
            query_grads.append(
                lax.dot_general(key[:, lanes], score_grad, TN, preferred_element_type=F32)
            )
            key_part = jnp.dot(score_grad, query[:, mine], preferred_element_type=F32)
            value_part = jnp.dot(probs.astype(B16), att_grad[:, mine], preferred_element_type=F32)
            if j % 2 == 0:
                key_grads.append(key_part)
                value_grads.append(value_part)
            else:
                key_grads[-1] = key_grads[-1] + key_part
                value_grads[-1] = value_grads[-1] + value_part
        cos, sin = cos_ref[...], -sin_ref[...]
        kv_grad = jnp.concatenate(
            [turn(jnp.concatenate(key_grads, axis=1), cos, sin)] + value_grads, axis=1
        ).astype(B16)
        cos, sin = cos[:tok_rows], sin[:tok_rows]
        query_grad = jnp.transpose(jnp.concatenate(query_grads, axis=0)) * scale
        query_grad = jnp.concatenate(
            [turn(query_grad[:, 128 * j : 128 * (j + 1)], cos, sin) for j in range(2)], axis=1
        ).astype(B16)

        def put(at, lanes, rows):
            keep_out[at, :, lanes] = jnp.where(core == 0, rows[0], rows[1]).astype(B16)
            give_out[at, :, lanes] = jnp.where(core == 0, rows[1], rows[0]).astype(B16)

        def give(grad, lanes):
            for m in range(4):
                put(
                    dp ^ m,
                    lanes,
                    [grad[(2 * m + c) * block : (2 * m + c + 1) * block] for c in range(2)],
                )

        give(
            jnp.dot(normed_t[:, :tok_rows], query_grad, preferred_element_type=F32),
            pl.ds(pl.multiple_of(step * 256, 256), 256),
        )
        give(
            jnp.dot(normed_t[...], kv_grad, preferred_element_type=F32),
            pl.ds(pl.multiple_of(wide + step * 256, 256), 256),
        )
        out_part = lax.dot_general(att_ref[...], og, TN, preferred_element_type=F32).astype(B16)
        put(dp ^ step, slice(output_at, output_at + width), [out_part[:block], out_part[block:]])
        kv_weights = jnp.concatenate([wk_ref[...], wv_ref[...]], axis=1)
        grad_sum[...] += lax.dot_general(kv_grad, kv_weights, NT, preferred_element_type=F32)
        grad_sum[:tok_rows, :] += lax.dot_general(
            query_grad, wq_ref[...], NT, preferred_element_type=F32
        )

        @pl.when(step == GROUPS - 1)
        def _():
            total = grad_sum[...]
            low = total.astype(B16)
            half = tok_rows // 2
            first_a_out[0] = low[tok_rows : tok_rows + half]
            first_a_out[1] = low[3 * tok_rows : 3 * tok_rows + half]
            first_b_out[0] = low[2 * tok_rows + half : 3 * tok_rows]
            first_b_out[1] = low[3 * tok_rows + half :]
            rest_a_out[0] = low[:half]
            rest_a_out[1] = low[2 * tok_rows : 2 * tok_rows + half]
            rest_b_out[0] = low[half:tok_rows]
            rest_b_out[1] = low[tok_rows + half : 2 * tok_rows]
            x = x_ref[...].astype(F32)
            lifted = x * lax.rsqrt(jnp.mean(x * x, axis=1, keepdims=True) + EPSILON)
            gain = jnp.sum(total * lifted, axis=0, keepdims=True)
            row = lax.broadcasted_iota(jnp.int32, (EXTRA, width), 0)
            gains = jnp.where(
                row == EXPERTS, gain, jnp.where(row == EXPERTS + 1, gain_ref[...], 0.0)
            )
            extra = lax.dot_general(
                moe_ref[...], logit_ref[...], TN, preferred_element_type=F32
            ) + jnp.transpose(gains)
            give(extra, slice(output_at + width, output_at + width + EXTRA))

    def fixed(*shape):
        return pl.BlockSpec(shape, lambda i, here: (0,) * len(shape))

    def columns(rows, cols, lead=0):
        return pl.BlockSpec((rows, cols), lambda i, here: (0, lead + i))

    shapes = [
        *[jax.ShapeDtypeStruct((4, block, output_at + width + EXTRA), B16)] * 2,
        *[jax.ShapeDtypeStruct((2, tok_rows // 2, width), B16)] * 4,
        jax.ShapeDtypeStruct((tok_rows, width), F32),
    ]
    keep, give, *parts, residual_grad = pl.pallas_call(
        kernel,
        out_shape=shapes,
        grid_spec=pltpu.PrefetchScalarGridSpec(
            num_scalar_prefetch=1,
            grid=(GROUPS,),
            in_specs=[
                *[fixed(tok_rows, width + 128)] * terms,
                fixed(tok_rows, width),
                fixed(tok_rows, width),
                fixed(tok_rows, 128),
                fixed(128, width),
                pl.BlockSpec(
                    (width, 128), lambda i, here: (0, (width + wide + 2 * narrow) // 128)
                ),
                pl.BlockSpec((256, width), lambda i, here: (i, 0)),
                columns(tok_rows, 256),
                fixed(tok_rows, width),
                fixed(seq_len, width),
                columns(tok_rows, 256),
                columns(seq_len, 128),
                columns(seq_len, 128),
                pl.BlockSpec((1, 8, tok_rows), lambda i, here: (i, 0, 0)),
                fixed(seq_len, width),
                columns(width, 256, width // 256),
                columns(width, 128, (width + wide) // 128),
                columns(width, 128, (width + wide + narrow) // 128),
                fixed(seq_len, tok_rows),
                fixed(seq_len, 128),
                fixed(seq_len, 128),
            ],
            out_specs=[fixed(*shape.shape) for shape in shapes],
            scratch_shapes=[
                pltpu.VMEM((width, seq_len), B16),
                pltpu.VMEM((seq_len, width), F32),
                pltpu.VMEM((tok_rows, width), B16),
                pltpu.VMEM((tok_rows, EXTRA), B16),
                pltpu.VMEM((1, width), F32),
            ],
        ),
        compiler_params=pltpu.CompilerParams(vmem_limit_bytes=VMEM_LIMIT),
        name="attention_grad",
    )(
        where_here, *moe_sums, out_grad, residual, gates, misc, dense_full, dense_full, attended,
        moe_in, normed_all, query_rot, key_rot, value_all, totals,
        x_all, dense_full, dense_full, dense_full, bias, cosine, sine,
    )
    return keep, give, tuple(parts[:2]), parts[2], parts[3], residual_grad


def core_halves(keep, got):
    _, rows, cols = keep.shape
    half = rows // 2

    def kernel(keep_ref, got_ref, first_a, first_b, rest_a, rest_b):
        def total(j, lo):
            mine = keep_ref[j, lo : lo + half, :].astype(F32)
            return (mine + got_ref[j, lo : lo + half, :].astype(F32)).astype(B16)

        first_a[0], first_a[1] = total(1, 0), total(3, 0)
        first_b[0], first_b[1] = total(2, half), total(3, half)
        rest_a[0], rest_a[1] = total(0, 0), total(2, 0)
        rest_b[0], rest_b[1] = total(0, half), total(1, half)

    step = cols // 5
    first_a, first_b, rest_a, rest_b = pl.pallas_call(
        kernel,
        grid=(5,),
        in_specs=[pl.BlockSpec((4, rows, step), lambda i: (0, 0, i))] * 2,
        out_specs=[pl.BlockSpec((2, half, step), lambda i: (0, 0, i))] * 4,
        out_shape=[jax.ShapeDtypeStruct((2, half, cols), B16)] * 4,
        compiler_params=pltpu.CompilerParams(vmem_limit_bytes=VMEM_LIMIT),
        name="core_halves",
    )(keep, got)
    return (first_a, first_b), rest_a, rest_b


def join_parts(to_x, to_y):
    count = len(to_x) - 1
    shape = to_x[0].shape[1:]

    def kernel(*refs):
        for i in range(2):
            direct, mine, via = refs[i * (count + 1) : i * (count + 1) + 3]
            out = refs[2 * (count + 1) + i]
            out[0] = direct[0]
            out[1] = plus_low(mine[0], via[0])
            if count == 3:
                out[2] = refs[i * (count + 1) + 3][0]

    steps = 4
    rows = shape[1] // steps
    part = pl.BlockSpec((1, shape[0], rows, shape[2]), lambda i: (0, 0, i, 0))
    return pl.pallas_call(
        kernel,
        grid=(steps,),
        in_specs=[part] * (2 * (count + 1)),
        out_specs=[pl.BlockSpec((count, shape[0], rows, shape[2]), lambda i: (0, 0, i, 0))] * 2,
        out_shape=[jax.ShapeDtypeStruct((count, *shape), B16)] * 2,
        compiler_params=pltpu.CompilerParams(vmem_limit_bytes=VMEM_LIMIT),
        name="join_parts",
    )(*to_x, *to_y)


def dense_outputs(core, mine, other, wide, narrow):
    rows, cols = mine.shape
    at = wide + 2 * narrow
    shapes = [(2 * rows, wide), (2 * rows, narrow), (2 * rows, narrow), (2 * rows, cols - at - EXTRA)]
    shapes += [(2 * rows, EXPERTS), (8, 2 * rows)]

    def kernel(core_ref, mine_ref, other_ref, query, key, value, output, router, gains, extra):
        for c in range(2):
            for ref, side in ((mine_ref, c), (other_ref, 1 - c)):

                @pl.when(core_ref[0] == c)
                def _():
                    lines = slice(side * rows, (side + 1) * rows)
                    query[lines, :] = ref[:, :wide].astype(F32)
                    for i in range(GROUPS):
                        lead = wide + 256 * i
                        lanes = slice(128 * i, 128 * (i + 1))
                        key[lines, lanes] = ref[:, lead : lead + 128].astype(F32)
                        value[lines, lanes] = ref[:, lead + 128 : lead + 256].astype(F32)
                    output[lines, :] = ref[:, at : cols - EXTRA].astype(F32)
                    extra[lines, :] = ref[:, cols - EXTRA :].astype(F32)
        router[...] = extra[:, :EXPERTS]
        gains[...] = jnp.transpose(extra[...])[EXPERTS : EXPERTS + 8, :]

    def fixed(shape):
        return pl.BlockSpec(shape, lambda i, core: (0, 0))

    query, key, value, output, router, gains = pl.pallas_call(
        kernel,
        out_shape=[jax.ShapeDtypeStruct(shape, F32) for shape in shapes],
        grid_spec=pltpu.PrefetchScalarGridSpec(
            num_scalar_prefetch=1,
            grid=(1,),
            in_specs=[fixed(mine.shape)] * 2,
            out_specs=[fixed(shape) for shape in shapes],
            scratch_shapes=[pltpu.VMEM((2 * rows, EXTRA), F32)],
        ),
        compiler_params=pltpu.CompilerParams(vmem_limit_bytes=VMEM_LIMIT),
        name="dense_outputs",
    )(core.astype(jnp.int32)[None], mine, other)
    return query, key, value, output, router, gains[0], gains[1]


def make_body(z_size, small_grid):
    def core_half(shard, core):
        rows = shard.shape[0] // 2
        return lax.dynamic_slice_in_dim(shard, core * rows, rows, 0)

    def dense_assemble(shard, parts, dp_index, core, *hold):
        rows = shard.shape[0] // 2
        moved = after(jnp.concatenate(parts, axis=0), *hold)
        other = swap_core(moved)
        places = [2 * dp_index]
        for which in (core, 1 - core):
            places += [2 * (dp_index ^ (j + 1)) + which for j in range(3)]
        return assemble(jnp.stack(places), shard, moved, other, rows)

    def across_z(mine, z):
        if z_size != 4:
            return lax.psum(mine.astype(F32), "z").astype(B16)
        rows = mine.shape[0] // z_size
        low = mine.astype(B16)
        total = lax.dynamic_slice_in_dim(mine, z * rows, rows, 0)
        for k in range(1, z_size):
            theirs = lax.dynamic_slice_in_dim(low, (z + k) % z_size * rows, rows, 0)
            total = total + cyclic(theirs, z_size, k).astype(F32)
        total = total.astype(B16)
        quarters = [total] + [cyclic(total, z_size, -k) for k in range(1, z_size)]
        places = (jnp.arange(z_size, dtype=jnp.int32) - z) % z_size
        return jnp.take(jnp.stack(quarters), places, axis=0).reshape(mine.shape)

    def dense_sum(grads):
        return lax.psum_scatter(
            lax.psum(grads, ("z", "core")), ("y", "x"), scatter_dimension=0, tiled=True
        )

    def body(
        layer_input,
        attn_gain,
        w_query,
        w_key,
        w_value,
        w_output,
        moe_gain,
        w_router,
        w_gate,
        w_up,
        w_down,
        routes,
        priority,
        prefix_len,
        out_grad,
    ):
        tok_rows, model_width = layer_input.shape
        dp_size = lax.axis_size("y") * lax.axis_size("x")
        dp_index = lax.axis_index("y") * lax.axis_size("x") + lax.axis_index("x")
        z = lax.axis_index("z")
        core = lax.axis_index("core")
        seq_len = tok_rows * dp_size
        top_count = routes.shape[1]
        local = w_gate.shape[0]
        capacity = 5 * tok_rows * top_count // (4 * EXPERTS)
        group_size = H // KVH
        score_scale = HD ** (-0.5)

        gains = jnp.stack([attn_gain, moe_gain], axis=1)
        rows = w_query.shape[0]
        dense_pack = jnp.concatenate(
            [w_output, w_query, w_key, w_value, w_router, gains, jnp.zeros((rows, 94), B16)], axis=1
        )
        wide = H * HD
        narrow = KVH * HD
        expert_ids = jnp.arange(EXPERTS, dtype=jnp.int32)
        hits = routes[:, :, None] == expert_ids[None, None, :]
        routed = jnp.any(hits, axis=1)
        place = jnp.where(
            routed, jnp.sum(jnp.where(hits, priority[:, :, None], 0), axis=1), jnp.int32(1 << 20)
        )
        ranks = jnp.sum((place[:, :, None] < place.T[None, :, :]).astype(F32), axis=0)
        code = pack_code(jnp.where(routed.T, ranks, -1.0).astype(B16))
        lead = ((2 * z + core) * local).astype(jnp.int32)[None]
        grad_pieces = column_pieces(jnp.concatenate([out_grad, code], axis=0), z_size)

        query_pos = dp_index * tok_rows + jnp.arange(tok_rows, dtype=jnp.int32)
        in_float = layer_input.astype(F32)
        steps = jnp.arange(tok_rows, dtype=jnp.int32)
        eff = w_gate.shape[2]
        in_rows, mid_rows = w_gate.shape[1], w_down.shape[1]
        folds = [w_down[:, :, f * eff : (f + 1) * eff] for f in range(model_width // eff)]
        if small_grid:
            relative = dp_index ^ jnp.arange(4, dtype=jnp.int32)
            key_pos = (relative[:, None] * tok_rows + steps[None, :]).reshape(seq_len)
        else:
            relative = jnp.arange(dp_size, dtype=jnp.int32)
            key_pos = jnp.arange(seq_len, dtype=jnp.int32)
        order = jnp.concatenate([relative, lead])
        visible = (key_pos[None, :] <= query_pos[:, None]) | (key_pos[None, :] < prefix_len[0])
        if small_grid:
            side = tok_rows // 2
            x_pack = jnp.concatenate([layer_input[:side], layer_input[side:]], axis=1)
            start_parts = gather_near(jnp.concatenate([x_pack, core_half(dense_pack, core)], axis=1))
            tables = (
                *turn_tables(key_pos.astype(F32)),
                jnp.where(visible.T, 0.0, MASKED_SCORE),
                jnp.pad(routed.astype(F32), ((0, 0), (0, 128 - EXPERTS))),
                [
                    jnp.concatenate([part[e] for part in (w_gate, w_up, *folds)], axis=0)
                    for e in range(local)
                ],
            )
            tables, grad_near = lax.optimization_barrier((tables, grad_pieces[1::2]))
            cosine, sine, bias, routed_wide, packs = tables
            start_parts += gather_far(after(start_parts, tables, *grad_near))
            dense_parts = [part[:, 2 * model_width :] for part in start_parts]
            dense_full = dense_assemble(dense_pack, dense_parts, dp_index, core)
        else:
            dense_full = lax.all_gather(dense_pack, ("y", "x"), axis=0, tiled=True)
            full_output = dense_full[:, :model_width]
            head_full = dense_full[:, model_width:]
            full_query = head_full[:, :wide]
            full_key = head_full[:, wide : wide + narrow]
            full_value = head_full[:, wide + narrow : wide + 2 * narrow]

        if small_grid:
            halves, per = 2, local // 2
            weights = []
            near_0 = gather_near(after(packs[0], *start_parts[2:]))
            far_0 = gather_far(after(near_0, dense_full))
            near_1 = gather_near(after(packs[1], *near_0, dense_full))
        else:
            halves, per = 1, local
            pack = jnp.concatenate([w_gate, w_up, *folds], axis=1)
            every = lax.all_gather(pack, ("y", "x"), axis=0, tiled=False)
            weights = [every[j] for j in range(dp_size)]
        chunks = []
        if small_grid:
            bias = after(bias, *near_0)
            (
                x_all, normed_all, query_rot, key_rot, value_all, attended, totals, misc, residual,
                moe_in, gates,
            ) = attention_forward(
                layer_input,
                start_parts,
                dense_full,
                bias,
                cosine,
                sine,
                routed_wide,
            )
            moe_in = after(moe_in, *near_1, *far_0, *grad_pieces)
            router_rows = misc[:EXPERTS].astype(B16)
            full_attn_gain = misc[EXPERTS]
            full_moe_gain = misc[EXPERTS + 1]
        else:
            places = query_pos.astype(F32)
            router_rows = head_full[:, wide + 2 * narrow : wide + 2 * narrow + EXPERTS].T
            full_attn_gain = head_full[:, wide + 2 * narrow + EXPERTS].astype(F32)
            full_moe_gain = head_full[:, wide + 2 * narrow + EXPERTS + 1].astype(F32)
            normed = rms_norm(in_float, full_attn_gain).astype(B16)
            query_lin = jnp.dot(normed, full_query, preferred_element_type=F32)
            key_lin = jnp.dot(normed, full_key, preferred_element_type=F32)
            value_low = jnp.dot(normed, full_value, preferred_element_type=F32).astype(B16)
            query_rot = (rotate(query_lin.reshape(tok_rows, H, HD), places) * score_scale).astype(B16)
            key_rot = rotate(key_lin.reshape(tok_rows, KVH, HD), places).astype(B16)
            key_rot = key_rot.reshape(tok_rows, narrow)
            both = jnp.concatenate([key_rot, value_low], axis=1)
            both_all = lax.all_gather(both, ("y", "x"), axis=0, tiled=True)
            key_all = both_all[:, :narrow]
            value_all = both_all[:, narrow:]

            def head_scores(head_idx):
                query_head = query_rot[:, head_idx * group_size : (head_idx + 1) * group_size, :]
                key_head = key_all[:, head_idx * HD : (head_idx + 1) * HD]
                scores = jnp.einsum("qgd,kd->gqk", query_head, key_head, preferred_element_type=F32)
                return jnp.where(visible[None, :, :], scores, MASKED_SCORE)

            mixed_heads = []
            log_totals = []
            for head_idx in range(KVH):
                scores = head_scores(head_idx)
                row_max = jnp.max(scores, axis=-1, keepdims=True)
                log_total = row_max + jnp.log(
                    jnp.sum(jnp.exp(scores - row_max), axis=-1, keepdims=True)
                )
                probs_low = jnp.exp(scores - log_total).astype(B16)
                value_head = value_all[:, head_idx * HD : (head_idx + 1) * HD]
                mixed_heads.append(
                    jnp.einsum("gqk,kd->qgd", probs_low, value_head, preferred_element_type=F32)
                )
                log_totals.append(log_total)
            attended = jnp.concatenate(mixed_heads, axis=1).reshape(tok_rows, wide).astype(B16)
            residual = in_float + jnp.dot(attended, full_output, preferred_element_type=F32)
            moe_in = rms_norm(residual, full_moe_gain).astype(B16)

        row_pieces = column_pieces(moe_in, z_size)
        grads_mine = jnp.stack(after(grad_pieces, moe_in))
        grads_other = swap_core(grads_mine)
        stage_1 = stage_2 = last_far = ()
        if small_grid:
            middle = packs[0].shape[0] // 2
            stage_1 = far_and_next(after(near_1, moe_in), packs[2])
        last = z_size // 2
        rows_near = [row_pieces[k] for k in range(z_size) if k != last]
        own_other = swap_core(moe_in)
        if small_grid:
            stage_2 = far_and_next(after(stage_1, *rows_near, grads_other, own_other), packs[3])
        rows_near_other = [own_other] + [
            swap_core(piece) for piece in after(rows_near[1:], *stage_1)
        ]
        (slot_grads_mine,) = dispatch_rows(
            lead, after(grads_mine, *rows_near_other), None, None, local, capacity
        )
        row_last = after(row_pieces[last], slot_grads_mine)
        (slot_grads_other,) = dispatch_rows(
            lead, after(grads_other, row_last), None, None, local, capacity
        )
        if small_grid:
            last_far = gather_far([part[middle:] for part in stage_2])
            chunks = [
                [(part, 0) for part in [packs[0], *near_0, *far_0]],
                [(part, 0) for part in [packs[1], *near_1, *stage_1[::-1]]],
                [(packs[2], 0)]
                + [(part, middle) for part in stage_1]
                + [(part, 0) for part in stage_2[::-1]],
                [(packs[3], 0)]
                + [(part, middle) for part in stage_2]
                + [(part, 0) for part in last_far],
            ]
        rows_mine = after([*rows_near[:last], row_last, *rows_near[last:]], *stage_2)
        rows_other = [*rows_near_other[:last], swap_core(row_last), *rows_near_other[last:]]
        slot_rows_mine, slot_gates_mine = dispatch_rows(
            lead, grads_mine, rows_mine, router_rows, local, capacity
        )
        slot_rows_other, slot_gates_other = dispatch_rows(
            lead, grads_other, after(rows_other, slot_rows_mine), router_rows, local, capacity
        )
        slot_rows_other = after(slot_rows_other, *last_far)
        ys, dxs, weight_grads, sums = [], [], [], []
        for half in range(halves):
            y, dx, grads = experts(
                order,
                half * per,
                per,
                (slot_rows_mine, slot_rows_other),
                (slot_grads_mine, slot_grads_other),
                (slot_gates_mine, slot_gates_other),
                weights,
                chunks[half * per : (half + 1) * per],
                capacity,
                in_rows,
                mid_rows,
            )
            ys.append(y)
            dxs.append(dx)
            weight_grads.append(grads)

        def grid_sum(grads, got):
            totals = []
            for half in range(2):
                own = grads[4 * half][0]
                direct, last = got[half][0], got[1 - half][1]
                totals.append(own.astype(F32) + direct.astype(F32) + last.astype(F32))
            return totals

        def second_step(grads, via, *more):
            _, x_a, y_a, _, _, x_b, y_b, _ = grads
            return cross(*join_parts((x_a, x_b, via[1], *more[:1]), (y_b, y_a, via[0], *more[1:])))

        if small_grid:
            early, late = weight_grads
            via = cross(early[3], early[7])
            dxs = after(dxs, *via)
            early_got = second_step(early, via, late[3], late[7])
        dx_other = combine_rows(lead, z_size, grads_other, dxs, local, capacity)
        y_other = combine_rows(lead, z_size, grads_other, after(ys, dx_other), local, capacity)
        dx_other = after(swap_core(dx_other), y_other)
        dx_low = combine_rows(lead, 0, grads_mine, dxs, local, capacity, dx_other)
        dx_low, y_other = after((dx_low, swap_core(y_other)), dx_low[0])
        dx_pieces = column_send_some(dx_low, z_size) + column_send_last(dx_low, z_size)
        y_low = combine_rows(lead, 0, grads_mine, ys, local, capacity, y_other)
        dx_pieces = after(dx_pieces, *y_low)
        y_pieces = column_send_some(after(y_low, *dx_pieces), z_size)
        if small_grid:
            early_got = after(early_got, *dx_pieces)
            late_got = second_step(late, [got[2:3] for got in early_got])
        if small_grid:
            keep, give, normed_first, normed_a, normed_b, residual_grad = attention_backward(
                jnp.stack([dp_index, core]).astype(jnp.int32),
                (dx_low[0], *dx_pieces),
                out_grad,
                residual,
                gates,
                misc,
                attended,
                moe_in,
                (x_all, normed_all, query_rot, key_rot, value_all, totals),
                dense_full,
                after(bias, *early_got),
                cosine,
                sine,
            )
            late_got, y_pieces = after((late_got, y_pieces), residual_grad)
            normed_first, keep, give = after((normed_first, keep, give), *late_got, *y_pieces)
            y_pieces += column_send_last(y_low, z_size, *y_pieces)
            dense_first, dense_a, dense_b = core_halves(keep, swap_core(give))
            normed_got = grid_scatter_first(*normed_first)
            dense_got = grid_scatter_first(*after(dense_first, *normed_got))
            dense_low = across_z(
                jnp.concatenate(grid_scatter_second(dense_got, dense_a, dense_b), axis=0), z
            )
            (
                query_sum, key_sum, value_sum, output_sum, router_sum, attn_gain_sum, moe_gain_sum,
            ) = dense_outputs(core, dense_low, swap_core(dense_low), wide, narrow)
            y_pieces = after(y_pieces, *dense_got)
            normed_grad = jnp.concatenate(
                grid_scatter_second(normed_got, normed_a, normed_b, *dense_got), axis=0
            )
            first_value, first_pull = jax.vjp(lambda v: rms_norm(v, full_attn_gain), in_float)
            input_grad = residual_grad + first_pull(normed_grad)[0]
        else:
            y_pieces += column_send_last(y_low, z_size)
            moe_sum = column_sum(dx_low[0], dx_pieces)
            moe_in_grad = moe_sum[:, :model_width]
            gate_grad = (
                moe_sum[:, model_width : model_width + EXPERTS]
                + moe_sum[:, model_width + EXPERTS : model_width + 2 * EXPERTS]
            )
            logits = lax.dot_general(moe_in, router_rows, NT, preferred_element_type=F32)
            peak = jnp.max(jnp.where(routed, logits, MASKED_SCORE), axis=-1, keepdims=True)
            lifted = jnp.where(routed, jnp.exp(jnp.minimum(logits - peak, 0.0)), 0.0)
            gate_weights = lifted / jnp.sum(lifted, axis=-1, keepdims=True)
            grad_out = out_grad.astype(F32)
            centre = jnp.sum(gate_weights * gate_grad, axis=-1, keepdims=True)
            logit_low = (gate_weights * (gate_grad - centre)).astype(B16)
            moe_in_grad = moe_in_grad + jnp.dot(logit_low, router_rows, preferred_element_type=F32)
            norm_value, second_pull = jax.vjp(rms_norm, residual, full_moe_gain)
            resid_norm_grad, moe_gain_grad = second_pull(moe_in_grad)
            residual_grad = grad_out + resid_norm_grad
            attn_out_grad = residual_grad.astype(B16)
            router_grad = jnp.einsum("td,te->de", moe_in, logit_low, preferred_element_type=F32)
            wout_grad = jnp.einsum("tc,td->cd", attended, attn_out_grad, preferred_element_type=F32)
            attended_grad = (
                jnp.einsum("td,cd->tc", attn_out_grad, full_output, preferred_element_type=F32)
                .astype(B16)
                .reshape(tok_rows, H, HD)
            )
            query_grads = []
            key_parts = []
            value_parts = []
            for head_idx in range(KVH):
                scores = head_scores(head_idx)
                attention_probs = jnp.exp(scores - log_totals[head_idx])
                probs_low = attention_probs.astype(B16)
                grad_head = attended_grad[:, head_idx * group_size : (head_idx + 1) * group_size, :]
                query_head = query_rot[:, head_idx * group_size : (head_idx + 1) * group_size, :]
                key_head = key_all[:, head_idx * HD : (head_idx + 1) * HD]
                value_head = value_all[:, head_idx * HD : (head_idx + 1) * HD]
                probs_grad = jnp.einsum("qgd,kd->gqk", grad_head, value_head, preferred_element_type=F32)
                row_delta = jnp.sum(attention_probs * probs_grad, axis=-1, keepdims=True)
                score_grad = (attention_probs * (probs_grad - row_delta)).astype(B16)
                query_grads.append(
                    jnp.einsum("gqk,kd->qgd", score_grad, key_head, preferred_element_type=F32)
                )
                key_parts.append(
                    jnp.einsum("gqk,qgd->kd", score_grad, query_head, preferred_element_type=F32)
                )
                value_parts.append(
                    jnp.einsum("gqk,qgd->kd", probs_low, grad_head, preferred_element_type=F32)
                )
            both_part = jnp.concatenate(key_parts + value_parts, axis=1)
            both_sum = lax.psum_scatter(both_part, ("y", "x"), scatter_dimension=0, tiled=True)
            query_rot_grad = jnp.concatenate(query_grads, axis=1) * score_scale
            key_rot_grad = both_sum[:, :narrow].reshape(tok_rows, KVH, HD)
            value_grad = both_sum[:, narrow:].astype(B16)
            query_grad = rotate(query_rot_grad, -places).reshape(tok_rows, wide).astype(B16)
            key_grad = rotate(key_rot_grad, -places).reshape(tok_rows, narrow).astype(B16)
            wq_grad = jnp.einsum("td,tc->dc", normed, query_grad, preferred_element_type=F32)
            wk_grad = jnp.einsum("td,tc->dc", normed, key_grad, preferred_element_type=F32)
            wv_grad = jnp.einsum("td,tc->dc", normed, value_grad, preferred_element_type=F32)
            normed_grad = jnp.einsum("tc,dc->td", query_grad, full_query, preferred_element_type=F32)
            normed_grad = normed_grad + jnp.einsum(
                "tc,dc->td", key_grad, full_key, preferred_element_type=F32
            )
            normed_grad = normed_grad + jnp.einsum(
                "tc,dc->td", value_grad, full_value, preferred_element_type=F32
            )
            first_value, first_pull = jax.vjp(rms_norm, in_float, full_attn_gain)
            input_norm_grad, attn_gain_grad = first_pull(normed_grad)
            input_grad = residual_grad + input_norm_grad
            query_sum = dense_sum(wq_grad)
            key_sum = dense_sum(wk_grad)
            value_sum = dense_sum(wv_grad)
            output_sum = dense_sum(wout_grad)
            extra_sum = dense_sum(
                jnp.concatenate(
                    [
                        router_grad,
                        attn_gain_grad[:, None],
                        moe_gain_grad[:, None],
                        jnp.zeros((model_width, EXTRA - EXPERTS - 2), F32),
                    ],
                    axis=1,
                )
            )
            router_sum = extra_sum[:, :EXPERTS]
            attn_gain_sum = extra_sum[:, EXPERTS]
            moe_gain_sum = extra_sum[:, EXPERTS + 1]
        layer_output = (residual + column_sum(y_low[0], y_pieces)).astype(B16)
        if small_grid:
            parts = grid_sum(early, early_got) + grid_sum(late, late_got)
            pack_grad = jnp.concatenate(parts, axis=0)
        else:
            pack_grad = lax.psum_scatter(
                weight_grads[0][0].astype(F32), ("y", "x"), scatter_dimension=0, tiled=False
            )
        down = 2 * in_rows
        expert_grads = [
            pack_grad[:, :in_rows],
            pack_grad[:, in_rows:down],
            jnp.concatenate(
                [
                    pack_grad[:, down + f * mid_rows : down + (f + 1) * mid_rows]
                    for f in range(model_width // eff)
                ],
                axis=2,
            ),
        ]

        return (
            layer_output,
            input_grad,
            attn_gain_sum,
            query_sum,
            key_sum,
            value_sum,
            output_sum,
            moe_gain_sum,
            router_sum,
            expert_grads[0],
            expert_grads[1],
            expert_grads[2],
        )

    return body


def solution(mesh):
    groups = mesh.shape["expert"]
    members = mesh.shape["dp"]
    z_size = groups // 2
    side = math.isqrt(members)
    grid = Mesh(
        mesh.devices.reshape(z_size, 2, members // side, side), ("z", "core", "y", "x")
    )
    expert = ("z", "core")
    dp = ("y", "x")
    every = expert + dp
    placed = (
        P(every, None),
        P(dp),
        P(dp, None),
        P(dp, None),
        P(dp, None),
        P(dp, None),
        P(dp),
        P(dp, None),
        P(expert, dp, None),
        P(expert, dp, None),
        P(expert, dp, None),
        P(every, None),
        P(every, None),
        P(expert),
        P(every, None),
    )
    return jax.shard_map(
        make_body(z_size, members == 4 and side == 2 and EXPERTS == 4 * groups),
        mesh=grid,
        in_specs=placed,
        out_specs=(
            P(every, None),
            P(every, None),
            P(dp),
            P(dp, None),
            P(dp, None),
            P(dp, None),
            P(dp, None),
            P(dp),
            P(dp, None),
            P(expert, dp, None),
            P(expert, dp, None),
            P(expert, dp, None),
        ),
        check_vma=False,
    )
```

```python
import math

import jax
import jax.numpy as jnp
from jax import lax
from jax.experimental import pallas as pl
from jax.experimental.pallas import tpu as pltpu
from jax.sharding import Mesh
from jax.sharding import PartitionSpec as P

H = 16
KVH = 8
HD = 64
EXPERTS = 32
EPSILON = 1e-06
ROPE_BASE = 10000.0
MASKED_SCORE = -1e30
F32 = jnp.float32
B16 = jnp.bfloat16
SWAP = [(0, 1), (1, 0)]
VMEM_LIMIT = 60 * 1024 * 1024


def rms_norm(values, gain_vec):
    return (
        values * lax.rsqrt(jnp.mean(values * values, axis=-1, keepdims=True) + EPSILON) * gain_vec
    )


def rotate(vectors, places):
    half_dim = vectors.shape[-1] // 2
    frequency = jnp.exp(
        jnp.arange(half_dim, dtype=F32) * (-2.0 * math.log(ROPE_BASE) / vectors.shape[-1])
    )
    angles = places[:, None] * frequency[None, :]
    cosine = jnp.cos(angles)[:, None, :]
    sine_vals = jnp.sin(angles)[:, None, :]
    first_half = vectors[..., :half_dim]
    second = vectors[..., half_dim:]
    return jnp.concatenate(
        [first_half * cosine - second * sine_vals, second * cosine + first_half * sine_vals],
        axis=-1,
    )


def swap_core(rows):
    return lax.ppermute(rows, "core", SWAP)


def cyclic(rows, size, shift):
    return lax.ppermute(rows, "z", [(i, (i + shift) % size) for i in range(size)])


def after(value, *others):
    return lax.optimization_barrier((value, *others))[0]


def gather_near(shard):
    return [lax.ppermute(shard, "x", SWAP), lax.ppermute(shard, "y", SWAP)]


def gather_far(near):
    from_x, from_y = near
    half = from_x.shape[0] // 2
    return [lax.ppermute(from_x[:half], "y", SWAP), lax.ppermute(from_y[half:], "x", SWAP)]


def grid_gather(shard):
    near = gather_near(shard)
    return near + gather_far(near)


def cross(to_x, to_y):
    return lax.ppermute(to_x, "x", SWAP), lax.ppermute(to_y, "y", SWAP)


def far_and_next(near, shard):
    from_x, from_y = near
    half = shard.shape[0] // 2
    return cross(
        jnp.concatenate([from_y[-half:], shard], axis=0),
        jnp.concatenate([from_x[-2 * half : -half], shard], axis=0),
    )


def plus_low(a, b):
    return (a.astype(F32) + b.astype(F32)).astype(B16)


def grid_scatter_first(first_a, first_b):
    return lax.ppermute(first_a, "x", SWAP), lax.ppermute(first_b, "y", SWAP)


def grid_scatter_second(got, rest_a, rest_b, *early):
    got_a, got_b = after(got, *early)
    onward_a = (rest_a[1].astype(F32) + got_a[1].astype(F32)).astype(B16)
    onward_b = (rest_b[1].astype(F32) + got_b[1].astype(F32)).astype(B16)
    last_a = lax.ppermute(onward_a, "y", SWAP)
    last_b = lax.ppermute(onward_b, "x", SWAP)
    return (
        rest_a[0].astype(F32) + got_a[0].astype(F32) + last_a.astype(F32),
        rest_b[0].astype(F32) + got_b[0].astype(F32) + last_b.astype(F32),
    )


def row_halves(parts):
    own, to_x, to_y, diag = [parts[j] for j in range(4)]
    half = own.shape[0] // 2
    first = (
        jnp.stack([to_x[:half], diag[:half]]),
        jnp.stack([to_y[half:], diag[half:]]),
    )
    return first, (own[:half], to_y[:half]), (own[half:], to_x[half:])


def column_pieces(rows, size):
    return [rows] + [cyclic(rows, size, -k) for k in range(1, size)]


def column_send_some(low, size):
    return [cyclic(low[k], size, k) for k in range(1, size) if 2 * k != size]


def column_send_last(low, size, *hold):
    return [cyclic(after(low[size // 2], *hold), size, size // 2)]


def column_sum(own, pieces):
    return own.astype(F32) + sum(piece.astype(F32) for piece in pieces)


def assemble(places, shard, moved, other, rows):
    def kernel(places_ref, shard_ref, moved_ref, other_ref, out_ref):
        def put(i, value):
            start = pl.multiple_of(places_ref[i] * rows, rows)
            out_ref[pl.ds(start, value.shape[0]), :] = value

        put(0, shard_ref[...])
        for j in range(3):
            put(1 + j, moved_ref[j * rows : (j + 1) * rows, :])
            put(4 + j, other_ref[j * rows : (j + 1) * rows, :])

    def whole(array_shape):
        return pl.BlockSpec(array_shape, lambda i, places: (0, 0))

    out_rows, cols = 8 * rows, shard.shape[1]
    return pl.pallas_call(
        kernel,
        out_shape=jax.ShapeDtypeStruct((out_rows, cols), shard.dtype),
        grid_spec=pltpu.PrefetchScalarGridSpec(
            num_scalar_prefetch=1,
            grid=(1,),
            in_specs=[whole(a.shape) for a in (shard, moved, other)],
            out_specs=whole((out_rows, cols)),
        ),
        compiler_params=pltpu.CompilerParams(vmem_limit_bytes=VMEM_LIMIT),
        name="assemble",
    )(places, shard, moved, other)


def one_hot_slots(codes, capacity):
    slots = lax.broadcasted_iota(jnp.int32, (capacity, codes.shape[1]), 0).astype(F32)
    return [(slots == codes[e : e + 1, :]).astype(F32) for e in range(codes.shape[0])]


def row_of(table, index):
    at = lax.broadcasted_iota(jnp.int32, table.shape, 0)
    return jnp.sum(jnp.where(at == index, table, 0.0), axis=0, keepdims=True)


def pack_code(code):
    rows = code.shape[0] // 4
    wide = jnp.concatenate([code[c * rows : (c + 1) * rows] for c in range(4)], axis=1)
    return jnp.concatenate([wide, jnp.full((16 - rows, wide.shape[1]), -1.0, B16)], axis=0)


def unpack_code(block, tokens):
    rows = EXPERTS // 4
    wide = block.astype(F32)
    return jnp.concatenate(
        [wide[:rows, c * tokens : (c + 1) * tokens] for c in range(4)], axis=0
    )


def dispatch_rows(lead, packed, rows, router, local, capacity):
    pieces, packed_rows, width = packed.shape
    tokens = packed_rows - 16
    slots = local * capacity
    with_gates = router is not None

    def kernel(lead_ref, packed_ref, *rest):
        first = lead_ref[0]
        if with_gates:
            router_ref, out_ref, gate_out, rows_ref = rest[pieces:]
            for p in range(pieces):

                @pl.when(pl.program_id(0) == p)
                def _():
                    rows_ref[...] = rest[p][...]

            table = unpack_code(packed_ref[0], tokens)
            source = rows_ref[...]
        else:
            (out_ref,) = rest
            table = unpack_code(packed_ref[0, tokens:, :], tokens)
            source = packed_ref[0, :tokens, :]
        codes = jnp.concatenate([row_of(table, first + e) for e in range(local)], axis=0)
        picks = one_hot_slots(codes, capacity)
        select = jnp.concatenate([p.astype(B16) for p in picks], axis=0)
        out_ref[0] = jnp.dot(select, source, preferred_element_type=F32).astype(B16)
        if with_gates:
            logits = lax.dot_general(
                router_ref[...], source, (((1,), (1,)), ((), ())), preferred_element_type=F32
            )
            routed = table >= 0.0
            peak = jnp.max(jnp.where(routed, logits, MASKED_SCORE), axis=0, keepdims=True)
            lifted = jnp.where(routed, jnp.exp(jnp.minimum(logits - peak, 0.0)), 0.0)
            gates = lifted / jnp.sum(lifted, axis=0, keepdims=True)
            for e in range(local):
                gate_row = row_of(gates, first + e)
                column = jnp.sum(picks[e] * gate_row, axis=1, keepdims=True)
                gate_out[0, e * capacity : (e + 1) * capacity, :] = jnp.broadcast_to(
                    column, (capacity, 128)
                )

    out_specs = [pl.BlockSpec((1, slots, width), lambda p, lead: (p, 0, 0))]
    out_shape = [jax.ShapeDtypeStruct((pieces, slots, width), B16)]
    args = [packed]
    if with_gates:
        in_specs = [
            pl.BlockSpec((1, 16, width), lambda p, lead: (p, tokens // 16, 0)),
            *[pl.BlockSpec((tokens, width), lambda p, lead: (0, 0)) for _ in rows],
            pl.BlockSpec((EXPERTS, width), lambda p, lead: (0, 0)),
        ]
        out_specs.append(pl.BlockSpec((1, slots, 128), lambda p, lead: (p, 0, 0)))
        out_shape.append(jax.ShapeDtypeStruct((pieces, slots, 128), F32))
        args += [*rows, router]
    else:
        in_specs = [pl.BlockSpec((1, packed_rows, width), lambda p, lead: (p, 0, 0))]
    return pl.pallas_call(
        kernel,
        out_shape=out_shape,
        grid_spec=pltpu.PrefetchScalarGridSpec(
            num_scalar_prefetch=1,
            grid=(pieces,),
            in_specs=in_specs,
            out_specs=out_specs,
            scratch_shapes=[pltpu.VMEM((tokens, width), B16)] if with_gates else [],
        ),
        compiler_params=pltpu.CompilerParams(vmem_limit_bytes=VMEM_LIMIT),
        name="dispatch",
    )(lead, *args)


def combine_rows(lead, first, packed, slot_rows, local, capacity, addend=None):
    pieces, packed_rows, code_width = packed.shape
    tokens = packed_rows - 16
    halves = len(slot_rows)
    slots, width = slot_rows[0].shape[1:]
    per = local // halves

    def kernel(lead_ref, code_ref, *rest):
        table = unpack_code(code_ref[0], tokens)
        here = lead_ref[0]
        codes = jnp.concatenate([row_of(table, here + e) for e in range(local)], axis=0)
        picks = one_hot_slots(codes, capacity)
        total = None
        for h in range(halves):
            select = jnp.concatenate(
                [p.astype(B16) for p in picks[h * per : (h + 1) * per]], axis=0
            )
            part = lax.dot_general(
                select, rest[h][0], (((0,), (0,)), ((), ())), preferred_element_type=F32
            )
            total = part if total is None else total + part
        if addend is None:
            rest[halves][0] = total.astype(B16)
        else:
            low = (total + rest[halves][0].astype(F32)).astype(B16)
            for p in range(pieces):

                @pl.when(pl.program_id(0) == p)
                def _():
                    rest[halves + 1 + p][...] = low

    in_specs = [pl.BlockSpec((1, 16, code_width), lambda p, lead: (p, tokens // 16, 0))]
    in_specs += [
        pl.BlockSpec((1, slots, width), lambda p, lead: (p + first, 0, 0)) for _ in range(halves)
    ]
    added = [] if addend is None else [addend]
    in_specs += [pl.BlockSpec((1, tokens, width), lambda p, lead: (p, 0, 0)) for _ in added]
    if addend is None:
        out_shape = jax.ShapeDtypeStruct((pieces, tokens, width), B16)
        out_specs = pl.BlockSpec((1, tokens, width), lambda p, lead: (p, 0, 0))
    else:
        out_shape = [jax.ShapeDtypeStruct((tokens, width), B16)] * pieces
        out_specs = [pl.BlockSpec((tokens, width), lambda p, lead: (0, 0))] * pieces
    return pl.pallas_call(
        kernel,
        out_shape=out_shape,
        grid_spec=pltpu.PrefetchScalarGridSpec(
            num_scalar_prefetch=1,
            grid=(pieces,),
            in_specs=in_specs,
            out_specs=out_specs,
        ),
        compiler_params=pltpu.CompilerParams(vmem_limit_bytes=VMEM_LIMIT),
        name="combine",
    )(lead, packed, *slot_rows, *added)


def experts(order, start, count, rows, grads, gates, weights, chunks, capacity, in_rows, mid_rows):
    half, _, width = rows[0].shape
    pieces = 2 * half
    split = bool(chunks)
    n = 4 if split else len(weights)
    extra = [array for chunk in chunks for array, _ in chunk]
    given = len(weights) + len(extra)
    pack_rows, eff = chunks[0][0][0].shape if split else weights[0].shape[1:]
    folds = width // eff
    total_rows = pieces * capacity
    first_half = count // 2
    large = total_rows > 1000

    def kernel(order_ref, *refs):
        rows_a, rows_b, grads_a, grads_b, gates_a, gates_b = refs[:6]
        pack = refs[6 : 6 + given]
        y_out, dx_out = refs[6 + given : 8 + given]
        outs = refs[8 + given : -6]
        full_g, full_u, full_d, grad_g, grad_u, grad_d = refs[-6:]

        def at_in(j):
            return pl.ds(pl.multiple_of(order_ref[j] * in_rows, in_rows), in_rows)

        def at_mid(j):
            return pl.ds(pl.multiple_of(order_ref[j] * mid_rows, mid_rows), mid_rows)

        def load(j, take):
            full_g[at_in(j), :] = take(0, in_rows)
            full_u[at_in(j), :] = take(in_rows, 2 * in_rows)
            for f in range(folds):
                full_d[at_mid(j), f * eff : (f + 1) * eff] = take(
                    2 * in_rows + f * mid_rows, 2 * in_rows + (f + 1) * mid_rows
                )

        def rows_from(ref, offset):
            return lambda lo, hi: ref[offset + lo : offset + hi, :]

        def two_halves(a, b):
            middle = pack_rows // 2

            def take(lo, hi):
                if hi <= middle:
                    return a(lo, hi)
                if lo >= middle:
                    return b(lo - middle, hi - middle)
                return jnp.concatenate([a(lo, middle), b(0, hi - middle)], axis=0)

            return take

        for j in range(len(weights)):
            load(j, lambda lo, hi, ref=pack[j]: ref[0, lo:hi])
        for c in range(len(chunks)):
            own, from_x, from_y, diag_a, diag_b = [
                rows_from(pack[5 * c + i], chunks[c][i][1]) for i in range(5)
            ]

            @pl.when(pl.program_id(0) == c)
            def _():
                load(0, own)
                load(1, from_x)
                load(2, from_y)
                load(3, two_halves(diag_a, diag_b))

        def joined(a, b, w):
            return jnp.concatenate(
                [
                    a[...].reshape(half * capacity, w),
                    b[...].reshape(half * capacity, w),
                ],
                axis=0,
            )

        x = joined(rows_a, rows_b, width)
        g = joined(grads_a, grads_b, width)
        gate = joined(gates_a, gates_b, 128)[:, 0:1]
        nt = (((1,), (1,)), ((), ()))
        tn = (((0,), (0,)), ((), ()))
        gate_proj = jnp.dot(x, full_g[...], preferred_element_type=F32)
        up_proj = jnp.dot(x, full_u[...], preferred_element_type=F32)
        down_grad = lax.dot_general(g, full_d[...], nt, preferred_element_type=F32)
        sigmoid = 1.0 / (1.0 + jnp.exp(-gate_proj))
        silu = gate_proj * sigmoid
        activated = silu * up_proj
        slot_grad = jnp.sum(activated * down_grad, axis=1, keepdims=True)
        here = order_ref[n] + start + pl.program_id(0)
        lane = lax.broadcasted_iota(jnp.int32, (total_rows, 128), 1)
        high = slot_grad.astype(B16).astype(F32)
        tail = jnp.where(lane == here, high, jnp.where(lane == here + EXPERTS, slot_grad - high, 0.0))
        dx_out[:, :, width:] = tail.astype(B16).reshape(pieces, capacity, 128)
        scaled = (gate * activated).astype(B16)
        act_grad = gate * down_grad
        gate_grad = (act_grad * up_proj * (sigmoid * (1.0 + gate_proj * (1.0 - sigmoid)))).astype(
            B16
        )
        up_grad = (act_grad * silu).astype(B16)
        y = jnp.dot(scaled, full_d[...], preferred_element_type=F32)
        y_out[...] = y.astype(B16).reshape(pieces, capacity, width)
        dx = lax.dot_general(gate_grad, full_g[...], nt, preferred_element_type=F32)
        dx = dx + lax.dot_general(up_grad, full_u[...], nt, preferred_element_type=F32)
        dx_out[:, :, :width] = dx.astype(B16).reshape(pieces, capacity, width)
        grad_g[...] = lax.dot_general(x, gate_grad, tn, preferred_element_type=F32).astype(B16)
        grad_u[...] = lax.dot_general(x, up_grad, tn, preferred_element_type=F32).astype(B16)
        grad_d[...] = lax.dot_general(scaled, g, tn, preferred_element_type=F32).astype(B16)

        def give(ref, slot, j):
            ref[slot, 0, :in_rows] = grad_g[at_in(j), :]
            ref[slot, 0, in_rows : 2 * in_rows] = grad_u[at_in(j), :]
            for f in range(folds):
                ref[slot, 0, 2 * in_rows + f * mid_rows : 2 * in_rows + (f + 1) * mid_rows] = grad_d[
                    at_mid(j), f * eff : (f + 1) * eff
                ]

        if split:

            @pl.when(pl.program_id(0) < first_half)
            def _():
                for j in range(4):
                    give(outs[j], 0, j)

            @pl.when(pl.program_id(0) >= first_half)
            def _():
                for j in range(4):
                    give(outs[4 + j], 0, j)
        else:
            for j in range(n):
                give(outs[0], j, j)

    def single():
        return dict(pipeline_mode=pl.Buffered(1)) if large else {}

    def rows_spec(w):
        return pl.BlockSpec((half, capacity, w), lambda e, o: (0, e + start, 0), **single())

    in_specs = [rows_spec(width)] * 4 + [rows_spec(128)] * 2
    for _ in weights:
        in_specs.append(pl.BlockSpec((1, pack_rows, eff), lambda e, o: (e + start, 0, 0)))
    for part in extra:
        in_specs.append(pl.BlockSpec(part.shape, lambda e, o: (0, 0)))
    slots = count * capacity
    out_specs = [
        pl.BlockSpec((pieces, capacity, w), lambda e, o: (0, e, 0), **single())
        for w in (width, width + 128)
    ]
    out_shape = [
        jax.ShapeDtypeStruct((pieces, slots, width), B16),
        jax.ShapeDtypeStruct((pieces, slots, width + 128), B16),
    ]
    if split:
        for at in (
            lambda e, o: (0, jnp.minimum(e, first_half - 1), 0, 0),
            lambda e, o: (0, jnp.maximum(e - first_half, 0), 0, 0),
        ):
            for _ in range(4):
                out_specs.append(pl.BlockSpec((1, 1, pack_rows, eff), at))
                out_shape.append(jax.ShapeDtypeStruct((1, first_half, pack_rows, eff), B16))
    else:
        out_specs.append(pl.BlockSpec((n, 1, pack_rows, eff), lambda e, o: (0, e, 0, 0)))
        out_shape.append(jax.ShapeDtypeStruct((n, count, pack_rows, eff), B16))
    results = pl.pallas_call(
        kernel,
        out_shape=out_shape,
        grid_spec=pltpu.PrefetchScalarGridSpec(
            num_scalar_prefetch=1,
            grid=(count,),
            in_specs=in_specs,
            out_specs=out_specs,
            scratch_shapes=[
                pltpu.VMEM((n * in_rows, eff), B16),
                pltpu.VMEM((n * in_rows, eff), B16),
                pltpu.VMEM((n * mid_rows, width), B16),
                pltpu.VMEM((n * in_rows, eff), B16),
                pltpu.VMEM((n * in_rows, eff), B16),
                pltpu.VMEM((n * mid_rows, width), B16),
            ],
        ),
        compiler_params=pltpu.CompilerParams(vmem_limit_bytes=VMEM_LIMIT),
        name="experts",
    )(order, *rows, *grads, *gates, *weights, *extra)
    return results[0], results[1], results[2:]


NT = (((1,), (1,)), ((), ()))
TN = (((0,), (0,)), ((), ()))
GROUPS = KVH // 2
EXTRA = 128


def turn(vectors, cosine, sine):
    lane = lax.broadcasted_iota(jnp.int32, vectors.shape, 1)
    ahead = pltpu.roll(vectors, 2 * HD - HD // 2, 1)
    behind = pltpu.roll(vectors, HD // 2, 1)
    return vectors * cosine + jnp.where(lane % HD < HD // 2, ahead, behind) * sine


def turn_tables(places):
    lane = jnp.arange(2 * HD, dtype=jnp.int32)
    frequency = jnp.exp(
        (lane % (HD // 2)).astype(F32) * (-2.0 * math.log(ROPE_BASE) / HD)
    )
    angles = places[:, None] * frequency[None, :]
    sign = jnp.where(lane % HD < HD // 2, -1.0, 1.0)
    return jnp.cos(angles), jnp.sin(angles) * sign[None, :]


def attention_forward(x_own, x_parts, dense_full, bias, cosine, sine, routed):
    tok_rows, width = x_own.shape
    seq_len = 4 * tok_rows
    scale = HD ** (-0.5)
    wide, narrow = H * HD, KVH * HD

    def kernel(
        own_ref, xa_ref, xb_ref, ya_ref, yb_ref, da_ref, db_ref, ea_ref, eb_ref,
        tail_ref, wo_ref, wq_ref, wk_ref, wv_ref, bias_ref, cos_ref, sin_ref, routed_ref,
        x_ref, normed_ref, q_out, k_out, v_out, att_out, total_out, misc_out, residual_out, moe_out,
        gates_out,
    ):
        step = pl.program_id(0)

        @pl.when(step == 0)
        def _():
            rows = jnp.transpose(tail_ref[...].astype(F32))
            misc_out[...] = rows
            at = 0
            for ref in (own_ref, xa_ref, xb_ref, ya_ref, yb_ref, da_ref, ea_ref, db_ref, eb_ref):
                x_ref[at : at + ref.shape[0], :] = ref[...]
                at += ref.shape[0]
            x = x_ref[...].astype(F32)
            scaled = x * lax.rsqrt(jnp.mean(x * x, axis=1, keepdims=True) + EPSILON)
            normed_ref[...] = (scaled * rows[EXPERTS : EXPERTS + 1, :]).astype(B16)
            residual_out[...] = x[:tok_rows]

        normed = normed_ref[...]
        cos, sin = cos_ref[...], sin_ref[...]
        key = turn(jnp.dot(normed, wk_ref[...], preferred_element_type=F32), cos, sin).astype(B16)
        value = jnp.dot(normed, wv_ref[...], preferred_element_type=F32).astype(B16)
        query = jnp.dot(normed[:tok_rows], wq_ref[...], preferred_element_type=F32)
        cos, sin = cos[:tok_rows], sin[:tok_rows]
        query = jnp.concatenate(
            [turn(query[:, 128 * j : 128 * (j + 1)], cos, sin) for j in range(2)], axis=1
        )
        query = (query * scale).astype(B16)
        k_out[...] = key
        v_out[...] = value
        q_out[...] = query
        mixed, totals = [], []
        for j in range(4):
            lanes = slice(HD * (j // 2), HD * (j // 2 + 1))
            scores = lax.dot_general(
                key[:, lanes], query[:, HD * j : HD * (j + 1)], NT, preferred_element_type=F32
            )
            scores = scores + bias_ref[...]
            peak = jnp.max(scores, axis=0, keepdims=True)
            probs = jnp.exp(scores - peak)
            total = jnp.sum(probs, axis=0, keepdims=True)
            out = lax.dot_general(
                value[:, lanes], probs.astype(B16), TN, preferred_element_type=F32
            )
            mixed.append(out / total)
            totals.append(peak + jnp.log(total))
        attended = jnp.transpose(jnp.concatenate(mixed, axis=0)).astype(B16)
        att_out[...] = attended
        total_out[0] = jnp.concatenate(totals + totals, axis=0)
        residual_out[...] += jnp.dot(attended, wo_ref[...], preferred_element_type=F32)

        @pl.when(step == GROUPS - 1)
        def _():
            total = residual_out[...]
            scaled = total * lax.rsqrt(jnp.mean(total * total, axis=1, keepdims=True) + EPSILON)
            moe_in = (scaled * misc_out[EXPERTS + 1 : EXPERTS + 2, :]).astype(B16)
            moe_out[...] = moe_in
            logits = jnp.dot(moe_in, tail_ref[...], preferred_element_type=F32)
            here = routed_ref[...] > 0.0
            peak = jnp.max(jnp.where(here, logits, MASKED_SCORE), axis=1, keepdims=True)
            lifted = jnp.where(here, jnp.exp(jnp.minimum(logits - peak, 0.0)), 0.0)
            gates_out[...] = lifted / jnp.sum(lifted, axis=1, keepdims=True)

    def fixed(*block):
        return pl.BlockSpec(block, lambda i: (0,) * len(block))

    def columns(rows, cols, lead=0):
        return pl.BlockSpec((rows, cols), lambda i: (0, lead + i))

    return pl.pallas_call(
        kernel,
        grid=(GROUPS,),
        in_specs=[
            fixed(tok_rows, width),
            *[
                pl.BlockSpec((part.shape[0], width), lambda i, c=c: (0, c))
                for part in x_parts
                for c in range(2)
            ],
            pl.BlockSpec((width, 128), lambda i: (0, (width + wide + 2 * narrow) // 128)),
            pl.BlockSpec((256, width), lambda i: (i, 0)),
            columns(width, 256, width // 256),
            columns(width, 128, (width + wide) // 128),
            columns(width, 128, (width + wide + narrow) // 128),
            fixed(seq_len, tok_rows),
            fixed(seq_len, 128),
            fixed(seq_len, 128),
            fixed(tok_rows, 128),
        ],
        out_specs=[
            fixed(seq_len, width),
            fixed(seq_len, width),
            columns(tok_rows, 256),
            columns(seq_len, 128),
            columns(seq_len, 128),
            columns(tok_rows, 256),
            pl.BlockSpec((1, 8, tok_rows), lambda i: (i, 0, 0)),
            fixed(128, width),
            fixed(tok_rows, width),
            fixed(tok_rows, width),
            fixed(tok_rows, 128),
        ],
        out_shape=[
            jax.ShapeDtypeStruct((seq_len, width), B16),
            jax.ShapeDtypeStruct((seq_len, width), B16),
            jax.ShapeDtypeStruct((tok_rows, wide), B16),
            jax.ShapeDtypeStruct((seq_len, narrow), B16),
            jax.ShapeDtypeStruct((seq_len, narrow), B16),
            jax.ShapeDtypeStruct((tok_rows, wide), B16),
            jax.ShapeDtypeStruct((GROUPS, 8, tok_rows), F32),
            jax.ShapeDtypeStruct((128, width), F32),
            jax.ShapeDtypeStruct((tok_rows, width), F32),
            jax.ShapeDtypeStruct((tok_rows, width), B16),
            jax.ShapeDtypeStruct((tok_rows, 128), F32),
        ],
        compiler_params=pltpu.CompilerParams(vmem_limit_bytes=VMEM_LIMIT),
        name="attention",
    )(
        x_own, *[part for part in x_parts for _ in range(2)], *[dense_full] * 5,
        bias, cosine, sine, routed,
    )


def attention_backward(
    where_here, moe_sums, out_grad, residual, gates, misc, attended, moe_in, saved,
    dense_full, bias, cosine, sine,
):
    x_all, normed_all, query_rot, key_rot, value_all, totals = saved
    terms = len(moe_sums)
    seq_len, width = x_all.shape
    tok_rows = query_rot.shape[0]
    scale = HD ** (-0.5)
    wide, narrow = H * HD, KVH * HD
    block = width // 8
    output_at = wide + 2 * narrow

    def kernel(here_ref, *refs):
        sums = refs[:terms]
        (
            grad_ref, residual_ref, gates_ref, misc_ref, tail_ref, wo_ref, att_ref, moe_ref,
            normed_ref, q_ref, k_ref, v_ref, total_ref,
            x_ref, wq_ref, wk_ref, wv_ref, bias_ref, cos_ref, sin_ref,
            keep_out, give_out, first_a_out, first_b_out, rest_a_out, rest_b_out, residual_out,
            normed_t, grad_sum, og_ref, logit_ref, gain_ref,
        ) = refs[terms:]
        step = pl.program_id(0)
        dp, core = here_ref[0], here_ref[1]

        @pl.when(step == 0)
        def _():
            normed_t[...] = jnp.transpose(normed_ref[...])
            grad_sum[...] = jnp.zeros((seq_len, width), F32)
            total = sums[0][...].astype(F32)
            for ref in sums[1:]:
                total = total + ref[...].astype(F32)
            behind = total[:, width:]
            gate_grad = behind + pltpu.roll(behind, 128 - EXPERTS, 1)
            gate = gates_ref[...]
            centre = jnp.sum(gate * gate_grad, axis=1, keepdims=True)
            logit_low = (gate * (gate_grad - centre)).astype(B16)
            logit_ref[...] = logit_low
            moe_grad = total[:, :width] + lax.dot_general(
                logit_low, tail_ref[...], NT, preferred_element_type=F32
            )
            residual = residual_ref[...]
            rate = lax.rsqrt(jnp.mean(residual * residual, axis=1, keepdims=True) + EPSILON)
            gain_ref[...] = jnp.sum(moe_grad * residual * rate, axis=0, keepdims=True)
            lifted = moe_grad * misc_ref[EXPERTS + 1 : EXPERTS + 2, :]
            inner = jnp.mean(lifted * residual, axis=1, keepdims=True)
            residual_grad = (
                grad_ref[...].astype(F32) + rate * lifted - residual * (rate * rate * rate * inner)
            )
            residual_out[...] = residual_grad
            og_ref[...] = residual_grad.astype(B16)

        og = og_ref[...]
        att_grad = lax.dot_general(og, wo_ref[...], NT, preferred_element_type=F32).astype(B16)
        query, key, value = q_ref[...], k_ref[...], v_ref[...]
        query_grads, key_grads, value_grads = [], [], []
        for j in range(4):
            lanes = slice(HD * (j // 2), HD * (j // 2 + 1))
            mine = slice(HD * j, HD * (j + 1))
            scores = lax.dot_general(
                key[:, lanes], query[:, mine], NT, preferred_element_type=F32
            )
            probs = jnp.exp(scores + bias_ref[...] - total_ref[0, j : j + 1, :])
            probs_grad = lax.dot_general(
                value[:, lanes], att_grad[:, mine], NT, preferred_element_type=F32
            )
            delta = jnp.sum(probs * probs_grad, axis=0, keepdims=True)
            score_grad = (probs * (probs_grad - delta)).astype(B16)
            query_grads.append(
                lax.dot_general(key[:, lanes], score_grad, TN, preferred_element_type=F32)
            )
            key_part = jnp.dot(score_grad, query[:, mine], preferred_element_type=F32)
            value_part = jnp.dot(probs.astype(B16), att_grad[:, mine], preferred_element_type=F32)
            if j % 2 == 0:
                key_grads.append(key_part)
                value_grads.append(value_part)
            else:
                key_grads[-1] = key_grads[-1] + key_part
                value_grads[-1] = value_grads[-1] + value_part
        cos, sin = cos_ref[...], -sin_ref[...]
        kv_grad = jnp.concatenate(
            [turn(jnp.concatenate(key_grads, axis=1), cos, sin)] + value_grads, axis=1
        ).astype(B16)
        cos, sin = cos[:tok_rows], sin[:tok_rows]
        query_grad = jnp.transpose(jnp.concatenate(query_grads, axis=0)) * scale
        query_grad = jnp.concatenate(
            [turn(query_grad[:, 128 * j : 128 * (j + 1)], cos, sin) for j in range(2)], axis=1
        ).astype(B16)

        def put(at, lanes, rows):
            keep_out[at, :, lanes] = jnp.where(core == 0, rows[0], rows[1]).astype(B16)
            give_out[at, :, lanes] = jnp.where(core == 0, rows[1], rows[0]).astype(B16)

        def give(grad, lanes):
            for m in range(4):
                put(
                    dp ^ m,
                    lanes,
                    [grad[(2 * m + c) * block : (2 * m + c + 1) * block] for c in range(2)],
                )

        give(
            jnp.dot(normed_t[:, :tok_rows], query_grad, preferred_element_type=F32),
            pl.ds(pl.multiple_of(step * 256, 256), 256),
        )
        give(
            jnp.dot(normed_t[...], kv_grad, preferred_element_type=F32),
            pl.ds(pl.multiple_of(wide + step * 256, 256), 256),
        )
        out_part = lax.dot_general(att_ref[...], og, TN, preferred_element_type=F32).astype(B16)
        put(dp ^ step, slice(output_at, output_at + width), [out_part[:block], out_part[block:]])
        kv_weights = jnp.concatenate([wk_ref[...], wv_ref[...]], axis=1)
        grad_sum[...] += lax.dot_general(kv_grad, kv_weights, NT, preferred_element_type=F32)
        grad_sum[:tok_rows, :] += lax.dot_general(
            query_grad, wq_ref[...], NT, preferred_element_type=F32
        )

        @pl.when(step == GROUPS - 1)
        def _():
            total = grad_sum[...]
            low = total.astype(B16)
            half = tok_rows // 2
            first_a_out[0] = low[tok_rows : tok_rows + half]
            first_a_out[1] = low[3 * tok_rows : 3 * tok_rows + half]
            first_b_out[0] = low[2 * tok_rows + half : 3 * tok_rows]
            first_b_out[1] = low[3 * tok_rows + half :]
            rest_a_out[0] = low[:half]
            rest_a_out[1] = low[2 * tok_rows : 2 * tok_rows + half]
            rest_b_out[0] = low[half:tok_rows]
            rest_b_out[1] = low[tok_rows + half : 2 * tok_rows]
            x = x_ref[...].astype(F32)
            lifted = x * lax.rsqrt(jnp.mean(x * x, axis=1, keepdims=True) + EPSILON)
            gain = jnp.sum(total * lifted, axis=0, keepdims=True)
            row = lax.broadcasted_iota(jnp.int32, (EXTRA, width), 0)
            gains = jnp.where(
                row == EXPERTS, gain, jnp.where(row == EXPERTS + 1, gain_ref[...], 0.0)
            )
            extra = lax.dot_general(
                moe_ref[...], logit_ref[...], TN, preferred_element_type=F32
            ) + jnp.transpose(gains)
            give(extra, slice(output_at + width, output_at + width + EXTRA))

    def fixed(*shape):
        return pl.BlockSpec(shape, lambda i, here: (0,) * len(shape))

    def columns(rows, cols, lead=0):
        return pl.BlockSpec((rows, cols), lambda i, here: (0, lead + i))

    shapes = [
        *[jax.ShapeDtypeStruct((4, block, output_at + width + EXTRA), B16)] * 2,
        *[jax.ShapeDtypeStruct((2, tok_rows // 2, width), B16)] * 4,
        jax.ShapeDtypeStruct((tok_rows, width), F32),
    ]
    keep, give, *parts, residual_grad = pl.pallas_call(
        kernel,
        out_shape=shapes,
        grid_spec=pltpu.PrefetchScalarGridSpec(
            num_scalar_prefetch=1,
            grid=(GROUPS,),
            in_specs=[
                *[fixed(tok_rows, width + 128)] * terms,
                fixed(tok_rows, width),
                fixed(tok_rows, width),
                fixed(tok_rows, 128),
                fixed(128, width),
                pl.BlockSpec(
                    (width, 128), lambda i, here: (0, (width + wide + 2 * narrow) // 128)
                ),
                pl.BlockSpec((256, width), lambda i, here: (i, 0)),
                columns(tok_rows, 256),
                fixed(tok_rows, width),
                fixed(seq_len, width),
                columns(tok_rows, 256),
                columns(seq_len, 128),
                columns(seq_len, 128),
                pl.BlockSpec((1, 8, tok_rows), lambda i, here: (i, 0, 0)),
                fixed(seq_len, width),
                columns(width, 256, width // 256),
                columns(width, 128, (width + wide) // 128),
                columns(width, 128, (width + wide + narrow) // 128),
                fixed(seq_len, tok_rows),
                fixed(seq_len, 128),
                fixed(seq_len, 128),
            ],
            out_specs=[fixed(*shape.shape) for shape in shapes],
            scratch_shapes=[
                pltpu.VMEM((width, seq_len), B16),
                pltpu.VMEM((seq_len, width), F32),
                pltpu.VMEM((tok_rows, width), B16),
                pltpu.VMEM((tok_rows, EXTRA), B16),
                pltpu.VMEM((1, width), F32),
            ],
        ),
        compiler_params=pltpu.CompilerParams(vmem_limit_bytes=VMEM_LIMIT),
        name="attention_grad",
    )(
        where_here, *moe_sums, out_grad, residual, gates, misc, dense_full, dense_full, attended,
        moe_in, normed_all, query_rot, key_rot, value_all, totals,
        x_all, dense_full, dense_full, dense_full, bias, cosine, sine,
    )
    return keep, give, tuple(parts[:2]), parts[2], parts[3], residual_grad


def core_halves(keep, got):
    _, rows, cols = keep.shape
    half = rows // 2

    def kernel(keep_ref, got_ref, first_a, first_b, rest_a, rest_b):
        def total(j, lo):
            mine = keep_ref[j, lo : lo + half, :].astype(F32)
            return (mine + got_ref[j, lo : lo + half, :].astype(F32)).astype(B16)

        first_a[0], first_a[1] = total(1, 0), total(3, 0)
        first_b[0], first_b[1] = total(2, half), total(3, half)
        rest_a[0], rest_a[1] = total(0, 0), total(2, 0)
        rest_b[0], rest_b[1] = total(0, half), total(1, half)

    step = cols // 5
    first_a, first_b, rest_a, rest_b = pl.pallas_call(
        kernel,
        grid=(5,),
        in_specs=[pl.BlockSpec((4, rows, step), lambda i: (0, 0, i))] * 2,
        out_specs=[pl.BlockSpec((2, half, step), lambda i: (0, 0, i))] * 4,
        out_shape=[jax.ShapeDtypeStruct((2, half, cols), B16)] * 4,
        compiler_params=pltpu.CompilerParams(vmem_limit_bytes=VMEM_LIMIT),
        name="core_halves",
    )(keep, got)
    return (first_a, first_b), rest_a, rest_b


def join_parts(to_x, to_y, via):
    count = len(to_x)
    shape = to_x[0].shape[1:]

    def kernel(*refs):
        for i in range(2):
            parts = refs[i * count : (i + 1) * count]
            out = refs[2 * (count + 1) + i]
            out[0] = parts[0][0]
            out[1] = plus_low(parts[1][0], refs[2 * count + i][0])
            if count == 3:
                out[2] = parts[2][0]

    steps = 4
    rows = shape[1] // steps
    part = pl.BlockSpec((1, shape[0], rows, shape[2]), lambda i: (0, 0, i, 0))
    end = via[0].shape[0] - 1
    last = pl.BlockSpec((1, shape[0], rows, shape[2]), lambda i: (end, 0, i, 0))
    return pl.pallas_call(
        kernel,
        grid=(steps,),
        in_specs=[part] * (2 * count) + [last] * 2,
        out_specs=[pl.BlockSpec((count, shape[0], rows, shape[2]), lambda i: (0, 0, i, 0))] * 2,
        out_shape=[jax.ShapeDtypeStruct((count, *shape), B16)] * 2,
        compiler_params=pltpu.CompilerParams(vmem_limit_bytes=VMEM_LIMIT),
        name="join_parts",
    )(*to_x, *to_y, *via)


def dense_outputs(core, mine, other, wide, narrow):
    rows, cols = mine.shape
    at = wide + 2 * narrow
    shapes = [(2 * rows, wide), (2 * rows, narrow), (2 * rows, narrow), (2 * rows, cols - at - EXTRA)]
    shapes += [(2 * rows, EXPERTS), (8, 2 * rows)]

    def kernel(core_ref, mine_ref, other_ref, query, key, value, output, router, gains, extra):
        for c in range(2):
            for ref, side in ((mine_ref, c), (other_ref, 1 - c)):

                @pl.when(core_ref[0] == c)
                def _():
                    lines = slice(side * rows, (side + 1) * rows)
                    query[lines, :] = ref[:, :wide].astype(F32)
                    for i in range(GROUPS):
                        lead = wide + 256 * i
                        lanes = slice(128 * i, 128 * (i + 1))
                        key[lines, lanes] = ref[:, lead : lead + 128].astype(F32)
                        value[lines, lanes] = ref[:, lead + 128 : lead + 256].astype(F32)
                    output[lines, :] = ref[:, at : cols - EXTRA].astype(F32)
                    extra[lines, :] = ref[:, cols - EXTRA :].astype(F32)
        router[...] = extra[:, :EXPERTS]
        gains[...] = jnp.transpose(extra[...])[EXPERTS : EXPERTS + 8, :]

    def fixed(shape):
        return pl.BlockSpec(shape, lambda i, core: (0, 0))

    query, key, value, output, router, gains = pl.pallas_call(
        kernel,
        out_shape=[jax.ShapeDtypeStruct(shape, F32) for shape in shapes],
        grid_spec=pltpu.PrefetchScalarGridSpec(
            num_scalar_prefetch=1,
            grid=(1,),
            in_specs=[fixed(mine.shape)] * 2,
            out_specs=[fixed(shape) for shape in shapes],
            scratch_shapes=[pltpu.VMEM((2 * rows, EXTRA), F32)],
        ),
        compiler_params=pltpu.CompilerParams(vmem_limit_bytes=VMEM_LIMIT),
        name="dense_outputs",
    )(core.astype(jnp.int32)[None], mine, other)
    return query, key, value, output, router, gains[0], gains[1]


def make_body(z_size, small_grid):
    def core_half(shard, core):
        rows = shard.shape[0] // 2
        return lax.dynamic_slice_in_dim(shard, core * rows, rows, 0)

    def dense_assemble(shard, parts, dp_index, core, *hold):
        rows = shard.shape[0] // 2
        moved = after(jnp.concatenate(parts, axis=0), *hold)
        other = swap_core(moved)
        places = [2 * dp_index]
        for which in (core, 1 - core):
            places += [2 * (dp_index ^ (j + 1)) + which for j in range(3)]
        return assemble(jnp.stack(places), shard, moved, other, rows)

    def across_z(mine, z):
        if z_size != 4:
            return lax.psum(mine.astype(F32), "z").astype(B16)
        rows = mine.shape[0] // z_size
        low = mine.astype(B16)
        steps = [2, 1, 3]
        got = []
        for k in steps:
            theirs = lax.dynamic_slice_in_dim(low, (z + k) % z_size * rows, rows, 0)
            got.append(cyclic(theirs, z_size, k))
        total = column_sum(lax.dynamic_slice_in_dim(mine, z * rows, rows, 0), got).astype(B16)
        sent = {k: cyclic(total, z_size, -k) for k in steps}
        quarters = [total] + [sent[k] for k in range(1, z_size)]
        places = (jnp.arange(z_size, dtype=jnp.int32) - z) % z_size
        return jnp.take(jnp.stack(quarters), places, axis=0).reshape(mine.shape)

    def dense_sum(grads):
        return lax.psum_scatter(
            lax.psum(grads, ("z", "core")), ("y", "x"), scatter_dimension=0, tiled=True
        )

    def body(
        layer_input,
        attn_gain,
        w_query,
        w_key,
        w_value,
        w_output,
        moe_gain,
        w_router,
        w_gate,
        w_up,
        w_down,
        routes,
        priority,
        prefix_len,
        out_grad,
    ):
        tok_rows, model_width = layer_input.shape
        dp_size = lax.axis_size("y") * lax.axis_size("x")
        dp_index = lax.axis_index("y") * lax.axis_size("x") + lax.axis_index("x")
        z = lax.axis_index("z")
        core = lax.axis_index("core")
        seq_len = tok_rows * dp_size
        top_count = routes.shape[1]
        local = w_gate.shape[0]
        capacity = 5 * tok_rows * top_count // (4 * EXPERTS)
        group_size = H // KVH
        score_scale = HD ** (-0.5)

        gains = jnp.stack([attn_gain, moe_gain], axis=1)
        rows = w_query.shape[0]
        dense_pack = jnp.concatenate(
            [w_output, w_query, w_key, w_value, w_router, gains, jnp.zeros((rows, 94), B16)], axis=1
        )
        wide = H * HD
        narrow = KVH * HD
        expert_ids = jnp.arange(EXPERTS, dtype=jnp.int32)
        hits = routes[:, :, None] == expert_ids[None, None, :]
        routed = jnp.any(hits, axis=1)
        place = jnp.where(
            routed, jnp.sum(jnp.where(hits, priority[:, :, None], 0), axis=1), jnp.int32(1 << 20)
        )
        ranks = jnp.sum((place[:, :, None] < place.T[None, :, :]).astype(F32), axis=0)
        code = pack_code(jnp.where(routed.T, ranks, -1.0).astype(B16))
        lead = ((2 * z + core) * local).astype(jnp.int32)[None]
        if small_grid:
            side = tok_rows // 2
            x_pack = jnp.concatenate([layer_input[:side], layer_input[side:]], axis=1)
            start_pack = jnp.concatenate([x_pack, core_half(dense_pack, core)], axis=1)
        else:
            grad_pieces = column_pieces(jnp.concatenate([out_grad, code], axis=0), z_size)

        query_pos = dp_index * tok_rows + jnp.arange(tok_rows, dtype=jnp.int32)
        in_float = layer_input.astype(F32)
        steps = jnp.arange(tok_rows, dtype=jnp.int32)
        eff = w_gate.shape[2]
        in_rows, mid_rows = w_gate.shape[1], w_down.shape[1]
        folds = [w_down[:, :, f * eff : (f + 1) * eff] for f in range(model_width // eff)]
        if small_grid:
            relative = dp_index ^ jnp.arange(4, dtype=jnp.int32)
            key_pos = (relative[:, None] * tok_rows + steps[None, :]).reshape(seq_len)
        else:
            relative = jnp.arange(dp_size, dtype=jnp.int32)
            key_pos = jnp.arange(seq_len, dtype=jnp.int32)
        order = jnp.concatenate([relative, lead])
        visible = (key_pos[None, :] <= query_pos[:, None]) | (key_pos[None, :] < prefix_len[0])
        if small_grid:
            start_parts = gather_near(start_pack)
            tables = (
                *turn_tables(key_pos.astype(F32)),
                jnp.where(visible.T, 0.0, MASKED_SCORE),
                jnp.pad(routed.astype(F32), ((0, 0), (0, 128 - EXPERTS))),
                [
                    jnp.concatenate([part[e] for part in (w_gate, w_up, *folds)], axis=0)
                    for e in range(local)
                ],
            )
            tables, code = lax.optimization_barrier((tables, code))
            grad_pieces = column_pieces(jnp.concatenate([out_grad, code], axis=0), z_size)
            grad_near = grad_pieces[1::2]
            cosine, sine, bias, routed_wide, packs = tables
            start_parts += gather_far(after(start_parts, tables, *grad_near))
            dense_parts = [part[:, 2 * model_width :] for part in start_parts]
            dense_full = dense_assemble(dense_pack, dense_parts, dp_index, core)
        else:
            dense_full = lax.all_gather(dense_pack, ("y", "x"), axis=0, tiled=True)
            full_output = dense_full[:, :model_width]
            head_full = dense_full[:, model_width:]
            full_query = head_full[:, :wide]
            full_key = head_full[:, wide : wide + narrow]
            full_value = head_full[:, wide + narrow : wide + 2 * narrow]

        if small_grid:
            halves, per = 2, local // 2
            weights = []
            near_0 = gather_near(after(packs[0], *start_parts[2:]))
            far_0 = gather_far(after(near_0, dense_full))
            near_1 = gather_near(after(packs[1], *near_0, dense_full))
        else:
            halves, per = 1, local
            pack = jnp.concatenate([w_gate, w_up, *folds], axis=1)
            every = lax.all_gather(pack, ("y", "x"), axis=0, tiled=False)
            weights = [every[j] for j in range(dp_size)]
        chunks = []
        if small_grid:
            bias = after(bias, *near_0)
            (
                x_all, normed_all, query_rot, key_rot, value_all, attended, totals, misc, residual,
                moe_in, gates,
            ) = attention_forward(
                layer_input,
                start_parts,
                dense_full,
                bias,
                cosine,
                sine,
                routed_wide,
            )
            moe_in = after(moe_in, *near_1, *far_0, *grad_pieces)
            router_rows = misc[:EXPERTS].astype(B16)
            full_attn_gain = misc[EXPERTS]
            full_moe_gain = misc[EXPERTS + 1]
        else:
            places = query_pos.astype(F32)
            router_rows = head_full[:, wide + 2 * narrow : wide + 2 * narrow + EXPERTS].T
            full_attn_gain = head_full[:, wide + 2 * narrow + EXPERTS].astype(F32)
            full_moe_gain = head_full[:, wide + 2 * narrow + EXPERTS + 1].astype(F32)
            normed = rms_norm(in_float, full_attn_gain).astype(B16)
            query_lin = jnp.dot(normed, full_query, preferred_element_type=F32)
            key_lin = jnp.dot(normed, full_key, preferred_element_type=F32)
            value_low = jnp.dot(normed, full_value, preferred_element_type=F32).astype(B16)
            query_rot = (rotate(query_lin.reshape(tok_rows, H, HD), places) * score_scale).astype(B16)
            key_rot = rotate(key_lin.reshape(tok_rows, KVH, HD), places).astype(B16)
            key_rot = key_rot.reshape(tok_rows, narrow)
            both = jnp.concatenate([key_rot, value_low], axis=1)
            both_all = lax.all_gather(both, ("y", "x"), axis=0, tiled=True)
            key_all = both_all[:, :narrow]
            value_all = both_all[:, narrow:]

            def head_scores(head_idx):
                query_head = query_rot[:, head_idx * group_size : (head_idx + 1) * group_size, :]
                key_head = key_all[:, head_idx * HD : (head_idx + 1) * HD]
                scores = jnp.einsum("qgd,kd->gqk", query_head, key_head, preferred_element_type=F32)
                return jnp.where(visible[None, :, :], scores, MASKED_SCORE)

            mixed_heads = []
            log_totals = []
            for head_idx in range(KVH):
                scores = head_scores(head_idx)
                row_max = jnp.max(scores, axis=-1, keepdims=True)
                log_total = row_max + jnp.log(
                    jnp.sum(jnp.exp(scores - row_max), axis=-1, keepdims=True)
                )
                probs_low = jnp.exp(scores - log_total).astype(B16)
                value_head = value_all[:, head_idx * HD : (head_idx + 1) * HD]
                mixed_heads.append(
                    jnp.einsum("gqk,kd->qgd", probs_low, value_head, preferred_element_type=F32)
                )
                log_totals.append(log_total)
            attended = jnp.concatenate(mixed_heads, axis=1).reshape(tok_rows, wide).astype(B16)
            residual = in_float + jnp.dot(attended, full_output, preferred_element_type=F32)
            moe_in = rms_norm(residual, full_moe_gain).astype(B16)

        row_pieces = column_pieces(moe_in, z_size)
        grads_mine = jnp.stack(after(grad_pieces, moe_in))
        grads_other = swap_core(grads_mine)
        stage_1 = stage_2 = last_far = ()
        if small_grid:
            middle = packs[0].shape[0] // 2
            stage_1 = far_and_next(after(near_1, moe_in), packs[2])
        last = z_size // 2
        rows_near = [row_pieces[k] for k in range(z_size) if k != last]
        own_other = swap_core(after(moe_in, grads_other))
        if small_grid:
            stage_2 = far_and_next(after(stage_1, *rows_near, grads_other, own_other), packs[3])
        rows_near_other = [own_other] + [
            swap_core(piece) for piece in after(rows_near[1:], *stage_1)
        ]
        (slot_grads_mine,) = dispatch_rows(
            lead, after(grads_mine, *rows_near_other), None, None, local, capacity
        )
        (slot_grads_other,) = dispatch_rows(
            lead, after(grads_other, slot_grads_mine), None, None, local, capacity
        )
        row_last = after(row_pieces[last], slot_grads_other)
        if small_grid:
            last_far = gather_far([part[middle:] for part in stage_2])
            chunks = [
                [(part, 0) for part in [packs[0], *near_0, *far_0]],
                [(part, 0) for part in [packs[1], *near_1, *stage_1[::-1]]],
                [(packs[2], 0)]
                + [(part, middle) for part in stage_1]
                + [(part, 0) for part in stage_2[::-1]],
                [(packs[3], 0)]
                + [(part, middle) for part in stage_2]
                + [(part, 0) for part in last_far],
            ]
        rows_mine = after([*rows_near[:last], row_last, *rows_near[last:]], *stage_2)
        rows_other = [*rows_near_other[:last], swap_core(row_last), *rows_near_other[last:]]
        slot_rows_mine, slot_gates_mine = dispatch_rows(
            lead, grads_mine, rows_mine, router_rows, local, capacity
        )
        slot_rows_other, slot_gates_other = dispatch_rows(
            lead, grads_other, after(rows_other, slot_rows_mine), router_rows, local, capacity
        )
        slot_rows_other = after(slot_rows_other, *last_far)
        ys, dxs, weight_grads, sums = [], [], [], []
        for half in range(halves):
            y, dx, grads = experts(
                order,
                half * per,
                per,
                (slot_rows_mine, slot_rows_other),
                (slot_grads_mine, slot_grads_other),
                (slot_gates_mine, slot_gates_other),
                weights,
                chunks[half * per : (half + 1) * per],
                capacity,
                in_rows,
                mid_rows,
            )
            ys.append(y)
            dxs.append(dx)
            weight_grads.append(grads)

        def grid_sum(grads, got):
            totals = []
            for half in range(2):
                own = grads[4 * half][0]
                direct, last = got[half][0], got[1 - half][1]
                totals.append(own.astype(F32) + direct.astype(F32) + last.astype(F32))
            return totals

        def second_step(grads, via, *more):
            _, x_a, y_a, _, _, x_b, y_b, _ = grads
            return cross(*join_parts((x_a, x_b, *more[:1]), (y_b, y_a, *more[1:]), via[::-1]))

        if small_grid:
            early, late = weight_grads
            via = cross(early[3], early[7])
            dxs = after(dxs, *via)
            early_got = second_step(early, via, late[3], late[7])
        dx_other = combine_rows(lead, z_size, grads_other, dxs, local, capacity)
        y_other = combine_rows(lead, z_size, grads_other, after(ys, dx_other), local, capacity)
        dx_other = after(swap_core(dx_other), y_other)
        dx_low = combine_rows(lead, 0, grads_mine, dxs, local, capacity, dx_other)
        dx_low, y_other = after((dx_low, swap_core(y_other)), dx_low[0])
        dx_pieces = column_send_last(dx_low, z_size) + column_send_some(dx_low, z_size)
        y_low = combine_rows(lead, 0, grads_mine, ys, local, capacity, y_other)
        dx_pieces = after(dx_pieces, *y_low)
        y_pieces = column_send_some(after(y_low, *dx_pieces), z_size)
        if small_grid:
            early_got = after(early_got, *dx_pieces)
            late_got = second_step(late, early_got)
        if small_grid:
            keep, give, normed_first, normed_a, normed_b, residual_grad = attention_backward(
                jnp.stack([dp_index, core]).astype(jnp.int32),
                (dx_low[0], *dx_pieces),
                out_grad,
                residual,
                gates,
                misc,
                attended,
                moe_in,
                (x_all, normed_all, query_rot, key_rot, value_all, totals),
                dense_full,
                after(bias, *early_got),
                cosine,
                sine,
            )
            late_got, y_pieces = after((late_got, y_pieces), residual_grad)
            normed_first, keep, give = after((normed_first, keep, give), *late_got, *y_pieces)
            y_pieces += column_send_last(y_low, z_size, *y_pieces)
            dense_first, dense_a, dense_b = core_halves(keep, swap_core(give))
            normed_got = grid_scatter_first(*normed_first)
            dense_got = grid_scatter_first(*after(dense_first, *normed_got))
            dense_low = across_z(
                jnp.concatenate(grid_scatter_second(dense_got, dense_a, dense_b), axis=0), z
            )
            (
                query_sum, key_sum, value_sum, output_sum, router_sum, attn_gain_sum, moe_gain_sum,
            ) = dense_outputs(core, dense_low, swap_core(dense_low), wide, narrow)
            y_pieces = after(y_pieces, *dense_got)
            normed_grad = jnp.concatenate(
                grid_scatter_second(normed_got, normed_a, normed_b, *dense_got), axis=0
            )
            first_value, first_pull = jax.vjp(lambda v: rms_norm(v, full_attn_gain), in_float)
            input_grad = residual_grad + first_pull(normed_grad)[0]
        else:
            y_pieces += column_send_last(y_low, z_size)
            moe_sum = column_sum(dx_low[0], dx_pieces)
            moe_in_grad = moe_sum[:, :model_width]
            gate_grad = (
                moe_sum[:, model_width : model_width + EXPERTS]
                + moe_sum[:, model_width + EXPERTS : model_width + 2 * EXPERTS]
            )
            logits = lax.dot_general(moe_in, router_rows, NT, preferred_element_type=F32)
            peak = jnp.max(jnp.where(routed, logits, MASKED_SCORE), axis=-1, keepdims=True)
            lifted = jnp.where(routed, jnp.exp(jnp.minimum(logits - peak, 0.0)), 0.0)
            gate_weights = lifted / jnp.sum(lifted, axis=-1, keepdims=True)
            grad_out = out_grad.astype(F32)
            centre = jnp.sum(gate_weights * gate_grad, axis=-1, keepdims=True)
            logit_low = (gate_weights * (gate_grad - centre)).astype(B16)
            moe_in_grad = moe_in_grad + jnp.dot(logit_low, router_rows, preferred_element_type=F32)
            norm_value, second_pull = jax.vjp(rms_norm, residual, full_moe_gain)
            resid_norm_grad, moe_gain_grad = second_pull(moe_in_grad)
            residual_grad = grad_out + resid_norm_grad
            attn_out_grad = residual_grad.astype(B16)
            router_grad = jnp.einsum("td,te->de", moe_in, logit_low, preferred_element_type=F32)
            wout_grad = jnp.einsum("tc,td->cd", attended, attn_out_grad, preferred_element_type=F32)
            attended_grad = (
                jnp.einsum("td,cd->tc", attn_out_grad, full_output, preferred_element_type=F32)
                .astype(B16)
                .reshape(tok_rows, H, HD)
            )
            query_grads = []
            key_parts = []
            value_parts = []
            for head_idx in range(KVH):
                scores = head_scores(head_idx)
                attention_probs = jnp.exp(scores - log_totals[head_idx])
                probs_low = attention_probs.astype(B16)
                grad_head = attended_grad[:, head_idx * group_size : (head_idx + 1) * group_size, :]
                query_head = query_rot[:, head_idx * group_size : (head_idx + 1) * group_size, :]
                key_head = key_all[:, head_idx * HD : (head_idx + 1) * HD]
                value_head = value_all[:, head_idx * HD : (head_idx + 1) * HD]
                probs_grad = jnp.einsum("qgd,kd->gqk", grad_head, value_head, preferred_element_type=F32)
                row_delta = jnp.sum(attention_probs * probs_grad, axis=-1, keepdims=True)
                score_grad = (attention_probs * (probs_grad - row_delta)).astype(B16)
                query_grads.append(
                    jnp.einsum("gqk,kd->qgd", score_grad, key_head, preferred_element_type=F32)
                )
                key_parts.append(
                    jnp.einsum("gqk,qgd->kd", score_grad, query_head, preferred_element_type=F32)
                )
                value_parts.append(
                    jnp.einsum("gqk,qgd->kd", probs_low, grad_head, preferred_element_type=F32)
                )
            both_part = jnp.concatenate(key_parts + value_parts, axis=1)
            both_sum = lax.psum_scatter(both_part, ("y", "x"), scatter_dimension=0, tiled=True)
            query_rot_grad = jnp.concatenate(query_grads, axis=1) * score_scale
            key_rot_grad = both_sum[:, :narrow].reshape(tok_rows, KVH, HD)
            value_grad = both_sum[:, narrow:].astype(B16)
            query_grad = rotate(query_rot_grad, -places).reshape(tok_rows, wide).astype(B16)
            key_grad = rotate(key_rot_grad, -places).reshape(tok_rows, narrow).astype(B16)
            wq_grad = jnp.einsum("td,tc->dc", normed, query_grad, preferred_element_type=F32)
            wk_grad = jnp.einsum("td,tc->dc", normed, key_grad, preferred_element_type=F32)
            wv_grad = jnp.einsum("td,tc->dc", normed, value_grad, preferred_element_type=F32)
            normed_grad = jnp.einsum("tc,dc->td", query_grad, full_query, preferred_element_type=F32)
            normed_grad = normed_grad + jnp.einsum(
                "tc,dc->td", key_grad, full_key, preferred_element_type=F32
            )
            normed_grad = normed_grad + jnp.einsum(
                "tc,dc->td", value_grad, full_value, preferred_element_type=F32
            )
            first_value, first_pull = jax.vjp(rms_norm, in_float, full_attn_gain)
            input_norm_grad, attn_gain_grad = first_pull(normed_grad)
            input_grad = residual_grad + input_norm_grad
            query_sum = dense_sum(wq_grad)
            key_sum = dense_sum(wk_grad)
            value_sum = dense_sum(wv_grad)
            output_sum = dense_sum(wout_grad)
            extra_sum = dense_sum(
                jnp.concatenate(
                    [
                        router_grad,
                        attn_gain_grad[:, None],
                        moe_gain_grad[:, None],
                        jnp.zeros((model_width, EXTRA - EXPERTS - 2), F32),
                    ],
                    axis=1,
                )
            )
            router_sum = extra_sum[:, :EXPERTS]
            attn_gain_sum = extra_sum[:, EXPERTS]
            moe_gain_sum = extra_sum[:, EXPERTS + 1]
        layer_output = (residual + column_sum(y_low[0], y_pieces)).astype(B16)
        if small_grid:
            parts = grid_sum(early, early_got) + grid_sum(late, late_got)
            pack_grad = jnp.concatenate(parts, axis=0)
        else:
            pack_grad = lax.psum_scatter(
                weight_grads[0][0].astype(F32), ("y", "x"), scatter_dimension=0, tiled=False
            )
        down = 2 * in_rows
        expert_grads = [
            pack_grad[:, :in_rows],
            pack_grad[:, in_rows:down],
            jnp.concatenate(
                [
                    pack_grad[:, down + f * mid_rows : down + (f + 1) * mid_rows]
                    for f in range(model_width // eff)
                ],
                axis=2,
            ),
        ]

        return (
            layer_output,
            input_grad,
            attn_gain_sum,
            query_sum,
            key_sum,
            value_sum,
            output_sum,
            moe_gain_sum,
            router_sum,
            expert_grads[0],
            expert_grads[1],
            expert_grads[2],
        )

    return body


def solution(mesh):
    groups = mesh.shape["expert"]
    members = mesh.shape["dp"]
    z_size = groups // 2
    side = math.isqrt(members)
    grid = Mesh(
        mesh.devices.reshape(z_size, 2, members // side, side), ("z", "core", "y", "x")
    )
    expert = ("z", "core")
    dp = ("y", "x")
    every = expert + dp
    placed = (
        P(every, None),
        P(dp),
        P(dp, None),
        P(dp, None),
        P(dp, None),
        P(dp, None),
        P(dp),
        P(dp, None),
        P(expert, dp, None),
        P(expert, dp, None),
        P(expert, dp, None),
        P(every, None),
        P(every, None),
        P(expert),
        P(every, None),
    )
    return jax.shard_map(
        make_body(z_size, members == 4 and side == 2 and EXPERTS == 4 * groups),
        mesh=grid,
        in_specs=placed,
        out_specs=(
            P(every, None),
            P(every, None),
            P(dp),
            P(dp, None),
            P(dp, None),
            P(dp, None),
            P(dp, None),
            P(dp),
            P(dp, None),
            P(expert, dp, None),
            P(expert, dp, None),
            P(expert, dp, None),
        ),
        check_vma=False,
    )
```

```python
import math

import jax
import jax.numpy as jnp
from jax import lax
from jax.experimental import pallas as pl
from jax.experimental.pallas import tpu as pltpu
from jax.sharding import Mesh
from jax.sharding import PartitionSpec as P

H = 16
KVH = 8
HD = 64
EXPERTS = 32
EPSILON = 1e-06
ROPE_BASE = 10000.0
MASKED_SCORE = -1e30
F32 = jnp.float32
B16 = jnp.bfloat16
SWAP = [(0, 1), (1, 0)]
VMEM_LIMIT = 60 * 1024 * 1024


def rms_norm(values, gain_vec):
    return (
        values * lax.rsqrt(jnp.mean(values * values, axis=-1, keepdims=True) + EPSILON) * gain_vec
    )


def rotate(vectors, places):
    half_dim = vectors.shape[-1] // 2
    frequency = jnp.exp(
        jnp.arange(half_dim, dtype=F32) * (-2.0 * math.log(ROPE_BASE) / vectors.shape[-1])
    )
    angles = places[:, None] * frequency[None, :]
    cosine = jnp.cos(angles)[:, None, :]
    sine_vals = jnp.sin(angles)[:, None, :]
    first_half = vectors[..., :half_dim]
    second = vectors[..., half_dim:]
    return jnp.concatenate(
        [first_half * cosine - second * sine_vals, second * cosine + first_half * sine_vals],
        axis=-1,
    )


def swap_core(rows):
    return lax.ppermute(rows, "core", SWAP)


def cyclic(rows, size, shift):
    return lax.ppermute(rows, "z", [(i, (i + shift) % size) for i in range(size)])


def after(value, *others):
    return lax.optimization_barrier((value, *others))[0]


def gather_near(shard):
    return [lax.ppermute(shard, "x", SWAP), lax.ppermute(shard, "y", SWAP)]


def gather_far(near):
    from_x, from_y = near
    half = from_x.shape[0] // 2
    return [lax.ppermute(from_x[:half], "y", SWAP), lax.ppermute(from_y[half:], "x", SWAP)]


def grid_gather(shard):
    near = gather_near(shard)
    return near + gather_far(near)


def cross(to_x, to_y):
    return lax.ppermute(to_x, "x", SWAP), lax.ppermute(to_y, "y", SWAP)


def far_and_next(nears, shard):
    rows = shard.shape[0]
    half = rows // 2
    return cross(
        jnp.concatenate([from_y[-half:] for _, from_y in nears] + [shard], axis=0),
        jnp.concatenate([from_x[-rows:-half] for from_x, _ in nears] + [shard], axis=0),
    )


def plus_low(a, b):
    return (a.astype(F32) + b.astype(F32)).astype(B16)


def grid_scatter_first(first_a, first_b):
    return lax.ppermute(first_a, "x", SWAP), lax.ppermute(first_b, "y", SWAP)


def grid_scatter_second(got, rest_a, rest_b, *early):
    got_a, got_b = after(got, *early)
    onward_a = (rest_a[1].astype(F32) + got_a[1].astype(F32)).astype(B16)
    onward_b = (rest_b[1].astype(F32) + got_b[1].astype(F32)).astype(B16)
    last_a = lax.ppermute(onward_a, "y", SWAP)
    last_b = lax.ppermute(onward_b, "x", SWAP)
    return (
        rest_a[0].astype(F32) + got_a[0].astype(F32) + last_a.astype(F32),
        rest_b[0].astype(F32) + got_b[0].astype(F32) + last_b.astype(F32),
    )


def row_halves(parts):
    own, to_x, to_y, diag = [parts[j] for j in range(4)]
    half = own.shape[0] // 2
    first = (
        jnp.stack([to_x[:half], diag[:half]]),
        jnp.stack([to_y[half:], diag[half:]]),
    )
    return first, (own[:half], to_y[:half]), (own[half:], to_x[half:])


def column_pieces(rows, size):
    return [rows] + [cyclic(rows, size, -k) for k in range(1, size)]


def column_send_some(low, size):
    return [cyclic(low[k], size, k) for k in range(1, size) if 2 * k != size]


def column_send_last(low, size, *hold):
    return [cyclic(after(low[size // 2], *hold), size, size // 2)]


def column_sum(own, pieces):
    return own.astype(F32) + sum(piece.astype(F32) for piece in pieces)


def assemble(places, shard, moved, other, rows):
    def kernel(places_ref, shard_ref, moved_ref, other_ref, out_ref):
        def put(i, value):
            start = pl.multiple_of(places_ref[i] * rows, rows)
            out_ref[pl.ds(start, value.shape[0]), :] = value

        put(0, shard_ref[...])
        for j in range(3):
            put(1 + j, moved_ref[j * rows : (j + 1) * rows, :])
            put(4 + j, other_ref[j * rows : (j + 1) * rows, :])

    def whole(array_shape):
        return pl.BlockSpec(array_shape, lambda i, places: (0, 0))

    out_rows, cols = 8 * rows, shard.shape[1]
    return pl.pallas_call(
        kernel,
        out_shape=jax.ShapeDtypeStruct((out_rows, cols), shard.dtype),
        grid_spec=pltpu.PrefetchScalarGridSpec(
            num_scalar_prefetch=1,
            grid=(1,),
            in_specs=[whole(a.shape) for a in (shard, moved, other)],
            out_specs=whole((out_rows, cols)),
        ),
        compiler_params=pltpu.CompilerParams(vmem_limit_bytes=VMEM_LIMIT),
        name="assemble",
    )(places, shard, moved, other)


def one_hot_slots(codes, capacity):
    slots = lax.broadcasted_iota(jnp.int32, (capacity, codes.shape[1]), 0).astype(F32)
    return [(slots == codes[e : e + 1, :]).astype(F32) for e in range(codes.shape[0])]


def row_of(table, index):
    at = lax.broadcasted_iota(jnp.int32, table.shape, 0)
    return jnp.sum(jnp.where(at == index, table, 0.0), axis=0, keepdims=True)


def pack_code(code):
    rows = code.shape[0] // 4
    wide = jnp.concatenate([code[c * rows : (c + 1) * rows] for c in range(4)], axis=1)
    return jnp.concatenate([wide, jnp.full((16 - rows, wide.shape[1]), -1.0, B16)], axis=0)


def unpack_code(block, tokens):
    rows = EXPERTS // 4
    wide = block.astype(F32)
    return jnp.concatenate(
        [wide[:rows, c * tokens : (c + 1) * tokens] for c in range(4)], axis=0
    )


def dispatch_rows(lead, packed, rows, router, local, capacity):
    pieces, packed_rows, width = packed.shape
    tokens = packed_rows - 16
    slots = local * capacity
    with_gates = router is not None

    def kernel(lead_ref, packed_ref, *rest):
        first = lead_ref[0]
        if with_gates:
            router_ref, out_ref, gate_out, rows_ref = rest[pieces:]
            for p in range(pieces):

                @pl.when(pl.program_id(0) == p)
                def _():
                    rows_ref[...] = rest[p][...]

            table = unpack_code(packed_ref[0], tokens)
            source = rows_ref[...]
        else:
            (out_ref,) = rest
            table = unpack_code(packed_ref[0, tokens:, :], tokens)
            source = packed_ref[0, :tokens, :]
        codes = jnp.concatenate([row_of(table, first + e) for e in range(local)], axis=0)
        picks = one_hot_slots(codes, capacity)
        select = jnp.concatenate([p.astype(B16) for p in picks], axis=0)
        out_ref[0] = jnp.dot(select, source, preferred_element_type=F32).astype(B16)
        if with_gates:
            logits = lax.dot_general(
                router_ref[...], source, (((1,), (1,)), ((), ())), preferred_element_type=F32
            )
            routed = table >= 0.0
            peak = jnp.max(jnp.where(routed, logits, MASKED_SCORE), axis=0, keepdims=True)
            lifted = jnp.where(routed, jnp.exp(jnp.minimum(logits - peak, 0.0)), 0.0)
            gates = lifted / jnp.sum(lifted, axis=0, keepdims=True)
            for e in range(local):
                gate_row = row_of(gates, first + e)
                column = jnp.sum(picks[e] * gate_row, axis=1, keepdims=True)
                gate_out[0, e * capacity : (e + 1) * capacity, :] = jnp.broadcast_to(
                    column, (capacity, 128)
                )

    out_specs = [pl.BlockSpec((1, slots, width), lambda p, lead: (p, 0, 0))]
    out_shape = [jax.ShapeDtypeStruct((pieces, slots, width), B16)]
    args = [packed]
    if with_gates:
        in_specs = [
            pl.BlockSpec((1, 16, width), lambda p, lead: (p, tokens // 16, 0)),
            *[pl.BlockSpec((tokens, width), lambda p, lead: (0, 0)) for _ in rows],
            pl.BlockSpec((EXPERTS, width), lambda p, lead: (0, 0)),
        ]
        out_specs.append(pl.BlockSpec((1, slots, 128), lambda p, lead: (p, 0, 0)))
        out_shape.append(jax.ShapeDtypeStruct((pieces, slots, 128), F32))
        args += [*rows, router]
    else:
        in_specs = [pl.BlockSpec((1, packed_rows, width), lambda p, lead: (p, 0, 0))]
    return pl.pallas_call(
        kernel,
        out_shape=out_shape,
        grid_spec=pltpu.PrefetchScalarGridSpec(
            num_scalar_prefetch=1,
            grid=(pieces,),
            in_specs=in_specs,
            out_specs=out_specs,
            scratch_shapes=[pltpu.VMEM((tokens, width), B16)] if with_gates else [],
        ),
        compiler_params=pltpu.CompilerParams(vmem_limit_bytes=VMEM_LIMIT),
        name="dispatch",
    )(lead, *args)


def combine_rows(lead, first, packed, slot_rows, local, capacity, addend=None):
    pieces, packed_rows, code_width = packed.shape
    tokens = packed_rows - 16
    halves = len(slot_rows)
    slots, width = slot_rows[0].shape[1:]
    per = local // halves

    def kernel(lead_ref, code_ref, *rest):
        table = unpack_code(code_ref[0], tokens)
        here = lead_ref[0]
        codes = jnp.concatenate([row_of(table, here + e) for e in range(local)], axis=0)
        picks = one_hot_slots(codes, capacity)
        total = None
        for h in range(halves):
            select = jnp.concatenate(
                [p.astype(B16) for p in picks[h * per : (h + 1) * per]], axis=0
            )
            part = lax.dot_general(
                select, rest[h][0], (((0,), (0,)), ((), ())), preferred_element_type=F32
            )
            total = part if total is None else total + part
        if addend is None:
            rest[halves][0] = total.astype(B16)
        else:
            low = (total + rest[halves][0].astype(F32)).astype(B16)
            for p in range(pieces):

                @pl.when(pl.program_id(0) == p)
                def _():
                    rest[halves + 1 + p][...] = low

    in_specs = [pl.BlockSpec((1, 16, code_width), lambda p, lead: (p, tokens // 16, 0))]
    in_specs += [
        pl.BlockSpec((1, slots, width), lambda p, lead: (p + first, 0, 0)) for _ in range(halves)
    ]
    added = [] if addend is None else [addend]
    in_specs += [pl.BlockSpec((1, tokens, width), lambda p, lead: (p, 0, 0)) for _ in added]
    if addend is None:
        out_shape = jax.ShapeDtypeStruct((pieces, tokens, width), B16)
        out_specs = pl.BlockSpec((1, tokens, width), lambda p, lead: (p, 0, 0))
    else:
        out_shape = [jax.ShapeDtypeStruct((tokens, width), B16)] * pieces
        out_specs = [pl.BlockSpec((tokens, width), lambda p, lead: (0, 0))] * pieces
    return pl.pallas_call(
        kernel,
        out_shape=out_shape,
        grid_spec=pltpu.PrefetchScalarGridSpec(
            num_scalar_prefetch=1,
            grid=(pieces,),
            in_specs=in_specs,
            out_specs=out_specs,
        ),
        compiler_params=pltpu.CompilerParams(vmem_limit_bytes=VMEM_LIMIT),
        name="combine",
    )(lead, packed, *slot_rows, *added)


def experts(order, start, count, rows, grads, gates, weights, chunks, capacity, in_rows, mid_rows):
    half, _, width = rows[0].shape
    pieces = 2 * half
    split = bool(chunks)
    n = 4 if split else len(weights)
    extra = [array for chunk in chunks for array, _ in chunk]
    given = len(weights) + len(extra)
    pack_rows, eff = chunks[0][0][0].shape if split else weights[0].shape[1:]
    folds = width // eff
    total_rows = pieces * capacity
    first_half = count // 2
    large = total_rows > 1000

    def kernel(order_ref, *refs):
        rows_a, rows_b, grads_a, grads_b, gates_a, gates_b = refs[:6]
        pack = refs[6 : 6 + given]
        y_out, dx_out = refs[6 + given : 8 + given]
        outs = refs[8 + given : -6]
        full_g, full_u, full_d, grad_g, grad_u, grad_d = refs[-6:]

        def at_in(j):
            return pl.ds(pl.multiple_of(order_ref[j] * in_rows, in_rows), in_rows)

        def at_mid(j):
            return pl.ds(pl.multiple_of(order_ref[j] * mid_rows, mid_rows), mid_rows)

        def load(j, take):
            full_g[at_in(j), :] = take(0, in_rows)
            full_u[at_in(j), :] = take(in_rows, 2 * in_rows)
            for f in range(folds):
                full_d[at_mid(j), f * eff : (f + 1) * eff] = take(
                    2 * in_rows + f * mid_rows, 2 * in_rows + (f + 1) * mid_rows
                )

        def rows_from(ref, offset):
            return lambda lo, hi: ref[offset + lo : offset + hi, :]

        def two_halves(a, b):
            middle = pack_rows // 2

            def take(lo, hi):
                if hi <= middle:
                    return a(lo, hi)
                if lo >= middle:
                    return b(lo - middle, hi - middle)
                return jnp.concatenate([a(lo, middle), b(0, hi - middle)], axis=0)

            return take

        for j in range(len(weights)):
            load(j, lambda lo, hi, ref=pack[j]: ref[0, lo:hi])
        for c in range(len(chunks)):
            own, from_x, from_y, diag_a, diag_b = [
                rows_from(pack[5 * c + i], chunks[c][i][1]) for i in range(5)
            ]

            @pl.when(pl.program_id(0) == c)
            def _():
                load(0, own)
                load(1, from_x)
                load(2, from_y)
                load(3, two_halves(diag_a, diag_b))

        def joined(a, b, w):
            return jnp.concatenate(
                [
                    a[...].reshape(half * capacity, w),
                    b[...].reshape(half * capacity, w),
                ],
                axis=0,
            )

        x = joined(rows_a, rows_b, width)
        g = joined(grads_a, grads_b, width)
        gate = joined(gates_a, gates_b, 128)[:, 0:1]
        nt = (((1,), (1,)), ((), ()))
        tn = (((0,), (0,)), ((), ()))
        gate_proj = jnp.dot(x, full_g[...], preferred_element_type=F32)
        up_proj = jnp.dot(x, full_u[...], preferred_element_type=F32)
        down_grad = lax.dot_general(g, full_d[...], nt, preferred_element_type=F32)
        sigmoid = 1.0 / (1.0 + jnp.exp(-gate_proj))
        silu = gate_proj * sigmoid
        activated = silu * up_proj
        slot_grad = jnp.sum(activated * down_grad, axis=1, keepdims=True)
        here = order_ref[n] + start + pl.program_id(0)
        lane = lax.broadcasted_iota(jnp.int32, (total_rows, 128), 1)
        high = slot_grad.astype(B16).astype(F32)
        tail = jnp.where(lane == here, high, jnp.where(lane == here + EXPERTS, slot_grad - high, 0.0))
        dx_out[:, :, width:] = tail.astype(B16).reshape(pieces, capacity, 128)
        scaled = (gate * activated).astype(B16)
        act_grad = gate * down_grad
        gate_grad = (act_grad * up_proj * (sigmoid * (1.0 + gate_proj * (1.0 - sigmoid)))).astype(
            B16
        )
        up_grad = (act_grad * silu).astype(B16)
        y = jnp.dot(scaled, full_d[...], preferred_element_type=F32)
        y_out[...] = y.astype(B16).reshape(pieces, capacity, width)
        dx = lax.dot_general(gate_grad, full_g[...], nt, preferred_element_type=F32)
        dx = dx + lax.dot_general(up_grad, full_u[...], nt, preferred_element_type=F32)
        dx_out[:, :, :width] = dx.astype(B16).reshape(pieces, capacity, width)
        grad_g[...] = lax.dot_general(x, gate_grad, tn, preferred_element_type=F32).astype(B16)
        grad_u[...] = lax.dot_general(x, up_grad, tn, preferred_element_type=F32).astype(B16)
        grad_d[...] = lax.dot_general(scaled, g, tn, preferred_element_type=F32).astype(B16)

        def give(ref, slot, j):
            ref[slot, 0, :in_rows] = grad_g[at_in(j), :]
            ref[slot, 0, in_rows : 2 * in_rows] = grad_u[at_in(j), :]
            for f in range(folds):
                ref[slot, 0, 2 * in_rows + f * mid_rows : 2 * in_rows + (f + 1) * mid_rows] = grad_d[
                    at_mid(j), f * eff : (f + 1) * eff
                ]

        if split:

            @pl.when(pl.program_id(0) < first_half)
            def _():
                for j in range(4):
                    give(outs[j], 0, j)

            @pl.when(pl.program_id(0) >= first_half)
            def _():
                for j in range(4):
                    give(outs[4 + j], 0, j)
        else:
            for j in range(n):
                give(outs[0], j, j)

    def single():
        return dict(pipeline_mode=pl.Buffered(1)) if large else {}

    def rows_spec(w):
        return pl.BlockSpec((half, capacity, w), lambda e, o: (0, e + start, 0), **single())

    in_specs = [rows_spec(width)] * 4 + [rows_spec(128)] * 2
    for _ in weights:
        in_specs.append(pl.BlockSpec((1, pack_rows, eff), lambda e, o: (e + start, 0, 0)))
    for part in extra:
        in_specs.append(pl.BlockSpec(part.shape, lambda e, o: (0, 0)))
    slots = count * capacity
    out_specs = [
        pl.BlockSpec((pieces, capacity, w), lambda e, o: (0, e, 0), **single())
        for w in (width, width + 128)
    ]
    out_shape = [
        jax.ShapeDtypeStruct((pieces, slots, width), B16),
        jax.ShapeDtypeStruct((pieces, slots, width + 128), B16),
    ]
    if split:
        for at in (
            lambda e, o: (0, jnp.minimum(e, first_half - 1), 0, 0),
            lambda e, o: (0, jnp.maximum(e - first_half, 0), 0, 0),
        ):
            for _ in range(4):
                out_specs.append(pl.BlockSpec((1, 1, pack_rows, eff), at))
                out_shape.append(jax.ShapeDtypeStruct((1, first_half, pack_rows, eff), B16))
    else:
        out_specs.append(pl.BlockSpec((n, 1, pack_rows, eff), lambda e, o: (0, e, 0, 0)))
        out_shape.append(jax.ShapeDtypeStruct((n, count, pack_rows, eff), B16))
    results = pl.pallas_call(
        kernel,
        out_shape=out_shape,
        grid_spec=pltpu.PrefetchScalarGridSpec(
            num_scalar_prefetch=1,
            grid=(count,),
            in_specs=in_specs,
            out_specs=out_specs,
            scratch_shapes=[
                pltpu.VMEM((n * in_rows, eff), B16),
                pltpu.VMEM((n * in_rows, eff), B16),
                pltpu.VMEM((n * mid_rows, width), B16),
                pltpu.VMEM((n * in_rows, eff), B16),
                pltpu.VMEM((n * in_rows, eff), B16),
                pltpu.VMEM((n * mid_rows, width), B16),
            ],
        ),
        compiler_params=pltpu.CompilerParams(vmem_limit_bytes=VMEM_LIMIT),
        name="experts",
    )(order, *rows, *grads, *gates, *weights, *extra)
    return results[0], results[1], results[2:]


NT = (((1,), (1,)), ((), ()))
TN = (((0,), (0,)), ((), ()))
GROUPS = KVH // 2
EXTRA = 128


def turn(vectors, cosine, sine):
    lane = lax.broadcasted_iota(jnp.int32, vectors.shape, 1)
    ahead = pltpu.roll(vectors, 2 * HD - HD // 2, 1)
    behind = pltpu.roll(vectors, HD // 2, 1)
    return vectors * cosine + jnp.where(lane % HD < HD // 2, ahead, behind) * sine


def turn_tables(places):
    lane = jnp.arange(2 * HD, dtype=jnp.int32)
    frequency = jnp.exp(
        (lane % (HD // 2)).astype(F32) * (-2.0 * math.log(ROPE_BASE) / HD)
    )
    angles = places[:, None] * frequency[None, :]
    sign = jnp.where(lane % HD < HD // 2, -1.0, 1.0)
    return jnp.cos(angles), jnp.sin(angles) * sign[None, :]


def attention_forward(x_own, x_parts, dense_full, bias, cosine, sine, routed):
    tok_rows, width = x_own.shape
    seq_len = 4 * tok_rows
    scale = HD ** (-0.5)
    wide, narrow = H * HD, KVH * HD

    def kernel(
        own_ref, xa_ref, xb_ref, ya_ref, yb_ref, da_ref, db_ref, ea_ref, eb_ref,
        tail_ref, wo_ref, wq_ref, wk_ref, wv_ref, bias_ref, cos_ref, sin_ref, routed_ref,
        x_ref, normed_ref, q_out, k_out, v_out, att_out, total_out, misc_out, residual_out, moe_out,
        gates_out,
    ):
        step = pl.program_id(0)

        @pl.when(step == 0)
        def _():
            rows = jnp.transpose(tail_ref[...].astype(F32))
            misc_out[...] = rows
            at = 0
            for ref in (own_ref, xa_ref, xb_ref, ya_ref, yb_ref, da_ref, ea_ref, db_ref, eb_ref):
                x_ref[at : at + ref.shape[0], :] = ref[...]
                at += ref.shape[0]
            x = x_ref[...].astype(F32)
            scaled = x * lax.rsqrt(jnp.mean(x * x, axis=1, keepdims=True) + EPSILON)
            normed_ref[...] = (scaled * rows[EXPERTS : EXPERTS + 1, :]).astype(B16)
            residual_out[...] = x[:tok_rows]

        normed = normed_ref[...]
        cos, sin = cos_ref[...], sin_ref[...]
        key = turn(jnp.dot(normed, wk_ref[...], preferred_element_type=F32), cos, sin).astype(B16)
        value = jnp.dot(normed, wv_ref[...], preferred_element_type=F32).astype(B16)
        query = jnp.dot(normed[:tok_rows], wq_ref[...], preferred_element_type=F32)
        cos, sin = cos[:tok_rows], sin[:tok_rows]
        query = jnp.concatenate(
            [turn(query[:, 128 * j : 128 * (j + 1)], cos, sin) for j in range(2)], axis=1
        )
        query = (query * scale).astype(B16)
        k_out[...] = key
        v_out[...] = value
        q_out[...] = query
        mixed, totals = [], []
        for j in range(4):
            lanes = slice(HD * (j // 2), HD * (j // 2 + 1))
            scores = lax.dot_general(
                key[:, lanes], query[:, HD * j : HD * (j + 1)], NT, preferred_element_type=F32
            )
            scores = scores + bias_ref[...]
            peak = jnp.max(scores, axis=0, keepdims=True)
            probs = jnp.exp(scores - peak)
            total = jnp.sum(probs, axis=0, keepdims=True)
            out = lax.dot_general(
                value[:, lanes], probs.astype(B16), TN, preferred_element_type=F32
            )
            mixed.append(out / total)
            totals.append(peak + jnp.log(total))
        attended = jnp.transpose(jnp.concatenate(mixed, axis=0)).astype(B16)
        att_out[...] = attended
        total_out[0] = jnp.concatenate(totals + totals, axis=0)
        residual_out[...] += jnp.dot(attended, wo_ref[...], preferred_element_type=F32)

        @pl.when(step == GROUPS - 1)
        def _():
            total = residual_out[...]
            scaled = total * lax.rsqrt(jnp.mean(total * total, axis=1, keepdims=True) + EPSILON)
            moe_in = (scaled * misc_out[EXPERTS + 1 : EXPERTS + 2, :]).astype(B16)
            moe_out[...] = moe_in
            logits = jnp.dot(moe_in, tail_ref[...], preferred_element_type=F32)
            here = routed_ref[...] > 0.0
            peak = jnp.max(jnp.where(here, logits, MASKED_SCORE), axis=1, keepdims=True)
            lifted = jnp.where(here, jnp.exp(jnp.minimum(logits - peak, 0.0)), 0.0)
            gates_out[...] = lifted / jnp.sum(lifted, axis=1, keepdims=True)

    def fixed(*block):
        return pl.BlockSpec(block, lambda i: (0,) * len(block))

    def columns(rows, cols, lead=0):
        return pl.BlockSpec((rows, cols), lambda i: (0, lead + i))

    return pl.pallas_call(
        kernel,
        grid=(GROUPS,),
        in_specs=[
            fixed(tok_rows, width),
            *[
                pl.BlockSpec((part.shape[0], width), lambda i, c=c: (0, c))
                for part in x_parts
                for c in range(2)
            ],
            pl.BlockSpec((width, 128), lambda i: (0, (width + wide + 2 * narrow) // 128)),
            pl.BlockSpec((256, width), lambda i: (i, 0)),
            columns(width, 256, width // 256),
            columns(width, 128, (width + wide) // 128),
            columns(width, 128, (width + wide + narrow) // 128),
            fixed(seq_len, tok_rows),
            fixed(seq_len, 128),
            fixed(seq_len, 128),
            fixed(tok_rows, 128),
        ],
        out_specs=[
            fixed(seq_len, width),
            fixed(seq_len, width),
            columns(tok_rows, 256),
            columns(seq_len, 128),
            columns(seq_len, 128),
            columns(tok_rows, 256),
            pl.BlockSpec((1, 8, tok_rows), lambda i: (i, 0, 0)),
            fixed(128, width),
            fixed(tok_rows, width),
            fixed(tok_rows, width),
            fixed(tok_rows, 128),
        ],
        out_shape=[
            jax.ShapeDtypeStruct((seq_len, width), B16),
            jax.ShapeDtypeStruct((seq_len, width), B16),
            jax.ShapeDtypeStruct((tok_rows, wide), B16),
            jax.ShapeDtypeStruct((seq_len, narrow), B16),
            jax.ShapeDtypeStruct((seq_len, narrow), B16),
            jax.ShapeDtypeStruct((tok_rows, wide), B16),
            jax.ShapeDtypeStruct((GROUPS, 8, tok_rows), F32),
            jax.ShapeDtypeStruct((128, width), F32),
            jax.ShapeDtypeStruct((tok_rows, width), F32),
            jax.ShapeDtypeStruct((tok_rows, width), B16),
            jax.ShapeDtypeStruct((tok_rows, 128), F32),
        ],
        compiler_params=pltpu.CompilerParams(vmem_limit_bytes=VMEM_LIMIT),
        name="attention",
    )(
        x_own, *[part for part in x_parts for _ in range(2)], *[dense_full] * 5,
        bias, cosine, sine, routed,
    )


def attention_backward(
    where_here, moe_sums, out_grad, residual, gates, misc, attended, moe_in, saved,
    dense_full, bias, cosine, sine,
):
    x_all, normed_all, query_rot, key_rot, value_all, totals = saved
    terms = len(moe_sums)
    seq_len, width = x_all.shape
    tok_rows = query_rot.shape[0]
    scale = HD ** (-0.5)
    wide, narrow = H * HD, KVH * HD
    block = width // 8
    output_at = wide + 2 * narrow

    def kernel(here_ref, *refs):
        sums = refs[:terms]
        (
            grad_ref, residual_ref, gates_ref, misc_ref, tail_ref, wo_ref, att_ref, moe_ref,
            normed_ref, q_ref, k_ref, v_ref, total_ref,
            x_ref, wq_ref, wk_ref, wv_ref, bias_ref, cos_ref, sin_ref,
            keep_out, give_out, first_a_out, first_b_out, rest_a_out, rest_b_out, residual_out,
            normed_t, grad_sum, og_ref, logit_ref, gain_ref,
        ) = refs[terms:]
        step = pl.program_id(0)
        dp, core = here_ref[0], here_ref[1]

        @pl.when(step == 0)
        def _():
            normed_t[...] = jnp.transpose(normed_ref[...])
            grad_sum[...] = jnp.zeros((seq_len, width), F32)
            total = sums[0][...].astype(F32)
            for ref in sums[1:]:
                total = total + ref[...].astype(F32)
            behind = total[:, width:]
            gate_grad = behind + pltpu.roll(behind, 128 - EXPERTS, 1)
            gate = gates_ref[...]
            centre = jnp.sum(gate * gate_grad, axis=1, keepdims=True)
            logit_low = (gate * (gate_grad - centre)).astype(B16)
            logit_ref[...] = logit_low
            moe_grad = total[:, :width] + lax.dot_general(
                logit_low, tail_ref[...], NT, preferred_element_type=F32
            )
            residual = residual_ref[...]
            rate = lax.rsqrt(jnp.mean(residual * residual, axis=1, keepdims=True) + EPSILON)
            gain_ref[...] = jnp.sum(moe_grad * residual * rate, axis=0, keepdims=True)
            lifted = moe_grad * misc_ref[EXPERTS + 1 : EXPERTS + 2, :]
            inner = jnp.mean(lifted * residual, axis=1, keepdims=True)
            residual_grad = (
                grad_ref[...].astype(F32) + rate * lifted - residual * (rate * rate * rate * inner)
            )
            residual_out[...] = residual_grad
            og_ref[...] = residual_grad.astype(B16)

        og = og_ref[...]
        att_grad = lax.dot_general(og, wo_ref[...], NT, preferred_element_type=F32).astype(B16)
        query, key, value = q_ref[...], k_ref[...], v_ref[...]
        query_grads, key_grads, value_grads = [], [], []
        for j in range(4):
            lanes = slice(HD * (j // 2), HD * (j // 2 + 1))
            mine = slice(HD * j, HD * (j + 1))
            scores = lax.dot_general(
                key[:, lanes], query[:, mine], NT, preferred_element_type=F32
            )
            probs = jnp.exp(scores + bias_ref[...] - total_ref[0, j : j + 1, :])
            probs_grad = lax.dot_general(
                value[:, lanes], att_grad[:, mine], NT, preferred_element_type=F32
            )
            delta = jnp.sum(probs * probs_grad, axis=0, keepdims=True)
            score_grad = (probs * (probs_grad - delta)).astype(B16)
            query_grads.append(
                lax.dot_general(key[:, lanes], score_grad, TN, preferred_element_type=F32)
            )
            key_part = jnp.dot(score_grad, query[:, mine], preferred_element_type=F32)
            value_part = jnp.dot(probs.astype(B16), att_grad[:, mine], preferred_element_type=F32)
            if j % 2 == 0:
                key_grads.append(key_part)
                value_grads.append(value_part)
            else:
                key_grads[-1] = key_grads[-1] + key_part
                value_grads[-1] = value_grads[-1] + value_part
        cos, sin = cos_ref[...], -sin_ref[...]
        kv_grad = jnp.concatenate(
            [turn(jnp.concatenate(key_grads, axis=1), cos, sin)] + value_grads, axis=1
        ).astype(B16)
        cos, sin = cos[:tok_rows], sin[:tok_rows]
        query_grad = jnp.transpose(jnp.concatenate(query_grads, axis=0)) * scale
        query_grad = jnp.concatenate(
            [turn(query_grad[:, 128 * j : 128 * (j + 1)], cos, sin) for j in range(2)], axis=1
        ).astype(B16)

        def put(at, lanes, rows):
            keep_out[at, :, lanes] = jnp.where(core == 0, rows[0], rows[1]).astype(B16)
            give_out[at, :, lanes] = jnp.where(core == 0, rows[1], rows[0]).astype(B16)

        def give(grad, lanes):
            for m in range(4):
                put(
                    dp ^ m,
                    lanes,
                    [grad[(2 * m + c) * block : (2 * m + c + 1) * block] for c in range(2)],
                )

        give(
            jnp.dot(normed_t[:, :tok_rows], query_grad, preferred_element_type=F32),
            pl.ds(pl.multiple_of(step * 256, 256), 256),
        )
        give(
            jnp.dot(normed_t[...], kv_grad, preferred_element_type=F32),
            pl.ds(pl.multiple_of(wide + step * 256, 256), 256),
        )
        out_part = lax.dot_general(att_ref[...], og, TN, preferred_element_type=F32).astype(B16)
        put(dp ^ step, slice(output_at, output_at + width), [out_part[:block], out_part[block:]])
        kv_weights = jnp.concatenate([wk_ref[...], wv_ref[...]], axis=1)
        grad_sum[...] += lax.dot_general(kv_grad, kv_weights, NT, preferred_element_type=F32)
        grad_sum[:tok_rows, :] += lax.dot_general(
            query_grad, wq_ref[...], NT, preferred_element_type=F32
        )

        @pl.when(step == GROUPS - 1)
        def _():
            total = grad_sum[...]
            low = total.astype(B16)
            half = tok_rows // 2
            first_a_out[0] = low[tok_rows : tok_rows + half]
            first_a_out[1] = low[3 * tok_rows : 3 * tok_rows + half]
            first_b_out[0] = low[2 * tok_rows + half : 3 * tok_rows]
            first_b_out[1] = low[3 * tok_rows + half :]
            rest_a_out[0] = low[:half]
            rest_a_out[1] = low[2 * tok_rows : 2 * tok_rows + half]
            rest_b_out[0] = low[half:tok_rows]
            rest_b_out[1] = low[tok_rows + half : 2 * tok_rows]
            x = x_ref[...].astype(F32)
            lifted = x * lax.rsqrt(jnp.mean(x * x, axis=1, keepdims=True) + EPSILON)
            gain = jnp.sum(total * lifted, axis=0, keepdims=True)
            row = lax.broadcasted_iota(jnp.int32, (EXTRA, width), 0)
            gains = jnp.where(
                row == EXPERTS, gain, jnp.where(row == EXPERTS + 1, gain_ref[...], 0.0)
            )
            extra = lax.dot_general(
                moe_ref[...], logit_ref[...], TN, preferred_element_type=F32
            ) + jnp.transpose(gains)
            give(extra, slice(output_at + width, output_at + width + EXTRA))

    def fixed(*shape):
        return pl.BlockSpec(shape, lambda i, here: (0,) * len(shape))

    def columns(rows, cols, lead=0):
        return pl.BlockSpec((rows, cols), lambda i, here: (0, lead + i))

    shapes = [
        *[jax.ShapeDtypeStruct((4, block, output_at + width + EXTRA), B16)] * 2,
        *[jax.ShapeDtypeStruct((2, tok_rows // 2, width), B16)] * 4,
        jax.ShapeDtypeStruct((tok_rows, width), F32),
    ]
    keep, give, *parts, residual_grad = pl.pallas_call(
        kernel,
        out_shape=shapes,
        grid_spec=pltpu.PrefetchScalarGridSpec(
            num_scalar_prefetch=1,
            grid=(GROUPS,),
            in_specs=[
                *[fixed(tok_rows, width + 128)] * terms,
                fixed(tok_rows, width),
                fixed(tok_rows, width),
                fixed(tok_rows, 128),
                fixed(128, width),
                pl.BlockSpec(
                    (width, 128), lambda i, here: (0, (width + wide + 2 * narrow) // 128)
                ),
                pl.BlockSpec((256, width), lambda i, here: (i, 0)),
                columns(tok_rows, 256),
                fixed(tok_rows, width),
                fixed(seq_len, width),
                columns(tok_rows, 256),
                columns(seq_len, 128),
                columns(seq_len, 128),
                pl.BlockSpec((1, 8, tok_rows), lambda i, here: (i, 0, 0)),
                fixed(seq_len, width),
                columns(width, 256, width // 256),
                columns(width, 128, (width + wide) // 128),
                columns(width, 128, (width + wide + narrow) // 128),
                fixed(seq_len, tok_rows),
                fixed(seq_len, 128),
                fixed(seq_len, 128),
            ],
            out_specs=[fixed(*shape.shape) for shape in shapes],
            scratch_shapes=[
                pltpu.VMEM((width, seq_len), B16),
                pltpu.VMEM((seq_len, width), F32),
                pltpu.VMEM((tok_rows, width), B16),
                pltpu.VMEM((tok_rows, EXTRA), B16),
                pltpu.VMEM((1, width), F32),
            ],
        ),
        compiler_params=pltpu.CompilerParams(vmem_limit_bytes=VMEM_LIMIT),
        name="attention_grad",
    )(
        where_here, *moe_sums, out_grad, residual, gates, misc, dense_full, dense_full, attended,
        moe_in, normed_all, query_rot, key_rot, value_all, totals,
        x_all, dense_full, dense_full, dense_full, bias, cosine, sine,
    )
    return keep, give, tuple(parts[:2]), parts[2], parts[3], residual_grad


def core_halves(keep, got):
    _, rows, cols = keep.shape
    half = rows // 2

    def kernel(keep_ref, got_ref, first_a, first_b, rest_a, rest_b):
        def total(j, lo):
            mine = keep_ref[j, lo : lo + half, :].astype(F32)
            return (mine + got_ref[j, lo : lo + half, :].astype(F32)).astype(B16)

        first_a[0], first_a[1] = total(1, 0), total(3, 0)
        first_b[0], first_b[1] = total(2, half), total(3, half)
        rest_a[0], rest_a[1] = total(0, 0), total(2, 0)
        rest_b[0], rest_b[1] = total(0, half), total(1, half)

    step = cols // 5
    first_a, first_b, rest_a, rest_b = pl.pallas_call(
        kernel,
        grid=(5,),
        in_specs=[pl.BlockSpec((4, rows, step), lambda i: (0, 0, i))] * 2,
        out_specs=[pl.BlockSpec((2, half, step), lambda i: (0, 0, i))] * 4,
        out_shape=[jax.ShapeDtypeStruct((2, half, cols), B16)] * 4,
        compiler_params=pltpu.CompilerParams(vmem_limit_bytes=VMEM_LIMIT),
        name="core_halves",
    )(keep, got)
    return (first_a, first_b), rest_a, rest_b


def join_parts(to_x, to_y, via):
    count = len(to_x)
    shape = to_x[0].shape[1:]

    def kernel(*refs):
        for i in range(2):
            parts = refs[i * count : (i + 1) * count]
            out = refs[2 * (count + 1) + i]
            out[0] = parts[0][0]
            out[1] = plus_low(parts[1][0], refs[2 * count + i][0])
            if count == 3:
                out[2] = parts[2][0]

    steps = 4
    rows = shape[1] // steps
    part = pl.BlockSpec((1, shape[0], rows, shape[2]), lambda i: (0, 0, i, 0))
    end = via[0].shape[0] - 1
    last = pl.BlockSpec((1, shape[0], rows, shape[2]), lambda i: (end, 0, i, 0))
    return pl.pallas_call(
        kernel,
        grid=(steps,),
        in_specs=[part] * (2 * count) + [last] * 2,
        out_specs=[pl.BlockSpec((count, shape[0], rows, shape[2]), lambda i: (0, 0, i, 0))] * 2,
        out_shape=[jax.ShapeDtypeStruct((count, *shape), B16)] * 2,
        compiler_params=pltpu.CompilerParams(vmem_limit_bytes=VMEM_LIMIT),
        name="join_parts",
    )(*to_x, *to_y, *via)


def dense_outputs(core, mine, other, wide, narrow):
    rows, cols = mine.shape
    at = wide + 2 * narrow
    shapes = [(2 * rows, wide), (2 * rows, narrow), (2 * rows, narrow), (2 * rows, cols - at - EXTRA)]
    shapes += [(2 * rows, EXPERTS), (8, 2 * rows)]

    def kernel(core_ref, mine_ref, other_ref, query, key, value, output, router, gains, extra):
        for c in range(2):
            for ref, side in ((mine_ref, c), (other_ref, 1 - c)):

                @pl.when(core_ref[0] == c)
                def _():
                    lines = slice(side * rows, (side + 1) * rows)
                    query[lines, :] = ref[:, :wide].astype(F32)
                    for i in range(GROUPS):
                        lead = wide + 256 * i
                        lanes = slice(128 * i, 128 * (i + 1))
                        key[lines, lanes] = ref[:, lead : lead + 128].astype(F32)
                        value[lines, lanes] = ref[:, lead + 128 : lead + 256].astype(F32)
                    output[lines, :] = ref[:, at : cols - EXTRA].astype(F32)
                    extra[lines, :] = ref[:, cols - EXTRA :].astype(F32)
        router[...] = extra[:, :EXPERTS]
        gains[...] = jnp.transpose(extra[...])[EXPERTS : EXPERTS + 8, :]

    def fixed(shape):
        return pl.BlockSpec(shape, lambda i, core: (0, 0))

    query, key, value, output, router, gains = pl.pallas_call(
        kernel,
        out_shape=[jax.ShapeDtypeStruct(shape, F32) for shape in shapes],
        grid_spec=pltpu.PrefetchScalarGridSpec(
            num_scalar_prefetch=1,
            grid=(1,),
            in_specs=[fixed(mine.shape)] * 2,
            out_specs=[fixed(shape) for shape in shapes],
            scratch_shapes=[pltpu.VMEM((2 * rows, EXTRA), F32)],
        ),
        compiler_params=pltpu.CompilerParams(vmem_limit_bytes=VMEM_LIMIT),
        name="dense_outputs",
    )(core.astype(jnp.int32)[None], mine, other)
    return query, key, value, output, router, gains[0], gains[1]


def make_body(z_size, small_grid):
    def core_half(shard, core):
        rows = shard.shape[0] // 2
        return lax.dynamic_slice_in_dim(shard, core * rows, rows, 0)

    def dense_assemble(shard, parts, dp_index, core, *hold):
        rows = shard.shape[0] // 2
        moved = after(jnp.concatenate(parts, axis=0), *hold)
        other = swap_core(moved)
        places = [2 * dp_index]
        for which in (core, 1 - core):
            places += [2 * (dp_index ^ (j + 1)) + which for j in range(3)]
        return assemble(jnp.stack(places), shard, moved, other, rows)

    def across_z(mine, z):
        if z_size != 4:
            return lax.psum(mine.astype(F32), "z").astype(B16)
        rows = mine.shape[0] // z_size
        low = mine.astype(B16)
        steps = [2, 1, 3]
        got = []
        for k in steps:
            theirs = lax.dynamic_slice_in_dim(low, (z + k) % z_size * rows, rows, 0)
            got.append(cyclic(theirs, z_size, k))
        total = column_sum(lax.dynamic_slice_in_dim(mine, z * rows, rows, 0), got).astype(B16)
        sent = {k: cyclic(total, z_size, -k) for k in steps}
        quarters = [total] + [sent[k] for k in steps]
        places = (jnp.arange(z_size, dtype=jnp.int32) - z) % z_size
        places = jnp.where((places == 1) | (places == 2), 3 - places, places)
        return jnp.take(jnp.stack(quarters), places, axis=0).reshape(mine.shape)

    def dense_sum(grads):
        return lax.psum_scatter(
            lax.psum(grads, ("z", "core")), ("y", "x"), scatter_dimension=0, tiled=True
        )

    def body(
        layer_input,
        attn_gain,
        w_query,
        w_key,
        w_value,
        w_output,
        moe_gain,
        w_router,
        w_gate,
        w_up,
        w_down,
        routes,
        priority,
        prefix_len,
        out_grad,
    ):
        tok_rows, model_width = layer_input.shape
        dp_size = lax.axis_size("y") * lax.axis_size("x")
        dp_index = lax.axis_index("y") * lax.axis_size("x") + lax.axis_index("x")
        z = lax.axis_index("z")
        core = lax.axis_index("core")
        seq_len = tok_rows * dp_size
        top_count = routes.shape[1]
        local = w_gate.shape[0]
        capacity = 5 * tok_rows * top_count // (4 * EXPERTS)
        group_size = H // KVH
        score_scale = HD ** (-0.5)

        gains = jnp.stack([attn_gain, moe_gain], axis=1)
        rows = w_query.shape[0]
        dense_pack = jnp.concatenate(
            [w_output, w_query, w_key, w_value, w_router, gains, jnp.zeros((rows, 94), B16)], axis=1
        )
        wide = H * HD
        narrow = KVH * HD
        expert_ids = jnp.arange(EXPERTS, dtype=jnp.int32)
        hits = routes[:, :, None] == expert_ids[None, None, :]
        routed = jnp.any(hits, axis=1)
        place = jnp.where(
            routed, jnp.sum(jnp.where(hits, priority[:, :, None], 0), axis=1), jnp.int32(1 << 20)
        )
        ranks = jnp.sum((place[:, :, None] < place.T[None, :, :]).astype(F32), axis=0)
        code = pack_code(jnp.where(routed.T, ranks, -1.0).astype(B16))
        lead = ((2 * z + core) * local).astype(jnp.int32)[None]
        if small_grid:
            side = tok_rows // 2
            x_pack = jnp.concatenate([layer_input[:side], layer_input[side:]], axis=1)
            start_pack = jnp.concatenate([x_pack, core_half(dense_pack, core)], axis=1)
        else:
            grad_pieces = column_pieces(jnp.concatenate([out_grad, code], axis=0), z_size)

        query_pos = dp_index * tok_rows + jnp.arange(tok_rows, dtype=jnp.int32)
        in_float = layer_input.astype(F32)
        steps = jnp.arange(tok_rows, dtype=jnp.int32)
        eff = w_gate.shape[2]
        in_rows, mid_rows = w_gate.shape[1], w_down.shape[1]
        folds = [w_down[:, :, f * eff : (f + 1) * eff] for f in range(model_width // eff)]
        if small_grid:
            relative = dp_index ^ jnp.arange(4, dtype=jnp.int32)
            key_pos = (relative[:, None] * tok_rows + steps[None, :]).reshape(seq_len)
        else:
            relative = jnp.arange(dp_size, dtype=jnp.int32)
            key_pos = jnp.arange(seq_len, dtype=jnp.int32)
        order = jnp.concatenate([relative, lead])
        visible = (key_pos[None, :] <= query_pos[:, None]) | (key_pos[None, :] < prefix_len[0])
        if small_grid:
            start_parts = gather_near(start_pack)
            tables = (
                *turn_tables(key_pos.astype(F32)),
                jnp.where(visible.T, 0.0, MASKED_SCORE),
                jnp.pad(routed.astype(F32), ((0, 0), (0, 128 - EXPERTS))),
                [
                    jnp.concatenate([part[e] for part in (w_gate, w_up, *folds)], axis=0)
                    for e in range(local)
                ],
            )
            code = after(code, *tables[:3])
            grad_pieces = column_pieces(jnp.concatenate([out_grad, code], axis=0), z_size)
            grad_near = grad_pieces[1::2]
            start_parts, tables = after((start_parts, tables), *grad_near)
            cosine, sine, bias, routed_wide, packs = tables
            start_parts += gather_far(after(start_parts, tables))
            dense_parts = [part[:, 2 * model_width :] for part in start_parts]
            dense_full = dense_assemble(dense_pack, dense_parts, dp_index, core)
        else:
            dense_full = lax.all_gather(dense_pack, ("y", "x"), axis=0, tiled=True)
            full_output = dense_full[:, :model_width]
            head_full = dense_full[:, model_width:]
            full_query = head_full[:, :wide]
            full_key = head_full[:, wide : wide + narrow]
            full_value = head_full[:, wide + narrow : wide + 2 * narrow]

        if small_grid:
            halves, per = 2, local // 2
            weights = []
            near_0 = gather_near(after(packs[0], *start_parts[2:]))
            near_1 = gather_near(after(packs[1], dense_full))
        else:
            halves, per = 1, local
            pack = jnp.concatenate([w_gate, w_up, *folds], axis=1)
            every = lax.all_gather(pack, ("y", "x"), axis=0, tiled=False)
            weights = [every[j] for j in range(dp_size)]
        chunks = []
        if small_grid:
            (
                x_all, normed_all, query_rot, key_rot, value_all, attended, totals, misc, residual,
                moe_in, gates,
            ) = attention_forward(
                layer_input,
                start_parts,
                dense_full,
                bias,
                cosine,
                sine,
                routed_wide,
            )
            moe_in = after(moe_in, *near_0, *near_1, *grad_pieces)
            router_rows = misc[:EXPERTS].astype(B16)
            full_attn_gain = misc[EXPERTS]
            full_moe_gain = misc[EXPERTS + 1]
        else:
            places = query_pos.astype(F32)
            router_rows = head_full[:, wide + 2 * narrow : wide + 2 * narrow + EXPERTS].T
            full_attn_gain = head_full[:, wide + 2 * narrow + EXPERTS].astype(F32)
            full_moe_gain = head_full[:, wide + 2 * narrow + EXPERTS + 1].astype(F32)
            normed = rms_norm(in_float, full_attn_gain).astype(B16)
            query_lin = jnp.dot(normed, full_query, preferred_element_type=F32)
            key_lin = jnp.dot(normed, full_key, preferred_element_type=F32)
            value_low = jnp.dot(normed, full_value, preferred_element_type=F32).astype(B16)
            query_rot = (rotate(query_lin.reshape(tok_rows, H, HD), places) * score_scale).astype(B16)
            key_rot = rotate(key_lin.reshape(tok_rows, KVH, HD), places).astype(B16)
            key_rot = key_rot.reshape(tok_rows, narrow)
            both = jnp.concatenate([key_rot, value_low], axis=1)
            both_all = lax.all_gather(both, ("y", "x"), axis=0, tiled=True)
            key_all = both_all[:, :narrow]
            value_all = both_all[:, narrow:]

            def head_scores(head_idx):
                query_head = query_rot[:, head_idx * group_size : (head_idx + 1) * group_size, :]
                key_head = key_all[:, head_idx * HD : (head_idx + 1) * HD]
                scores = jnp.einsum("qgd,kd->gqk", query_head, key_head, preferred_element_type=F32)
                return jnp.where(visible[None, :, :], scores, MASKED_SCORE)

            mixed_heads = []
            log_totals = []
            for head_idx in range(KVH):
                scores = head_scores(head_idx)
                row_max = jnp.max(scores, axis=-1, keepdims=True)
                log_total = row_max + jnp.log(
                    jnp.sum(jnp.exp(scores - row_max), axis=-1, keepdims=True)
                )
                probs_low = jnp.exp(scores - log_total).astype(B16)
                value_head = value_all[:, head_idx * HD : (head_idx + 1) * HD]
                mixed_heads.append(
                    jnp.einsum("gqk,kd->qgd", probs_low, value_head, preferred_element_type=F32)
                )
                log_totals.append(log_total)
            attended = jnp.concatenate(mixed_heads, axis=1).reshape(tok_rows, wide).astype(B16)
            residual = in_float + jnp.dot(attended, full_output, preferred_element_type=F32)
            moe_in = rms_norm(residual, full_moe_gain).astype(B16)

        row_pieces = column_pieces(moe_in, z_size)
        grads_mine = jnp.stack(after(grad_pieces, moe_in))
        grads_other = swap_core(grads_mine)
        stage_1 = stage_2 = last_far = ()
        if small_grid:
            middle = packs[0].shape[0] // 2
            stage_1 = far_and_next(after((near_0, near_1), moe_in), packs[2])
        last = z_size // 2
        rows_near = [row_pieces[k] for k in range(z_size) if k != last]
        own_other = swap_core(after(moe_in, grads_other))
        if small_grid:
            stage_2 = far_and_next(
                [after(stage_1, *rows_near, grads_other, own_other)], packs[3]
            )
        rows_near_other = [own_other] + [
            swap_core(piece) for piece in after(rows_near[1:], *stage_1)
        ]
        (slot_grads_mine,) = dispatch_rows(
            lead, after(grads_mine, *rows_near_other), None, None, local, capacity
        )
        (slot_grads_other,) = dispatch_rows(
            lead, after(grads_other, slot_grads_mine), None, None, local, capacity
        )
        row_last = after(row_pieces[last], slot_grads_other)
        if small_grid:
            last_far = gather_far([part[middle:] for part in stage_2])
            chunks = [
                [(part, 0) for part in [packs[0], *near_0, *stage_1[::-1]]],
                [(part, 0) for part in [packs[1], *near_1]]
                + [(part, middle) for part in stage_1[::-1]],
                [(packs[2], 0)]
                + [(part, 2 * middle) for part in stage_1]
                + [(part, 0) for part in stage_2[::-1]],
                [(packs[3], 0)]
                + [(part, middle) for part in stage_2]
                + [(part, 0) for part in last_far],
            ]
        rows_mine = after([*rows_near[:last], row_last, *rows_near[last:]], *stage_2)
        rows_other = [*rows_near_other[:last], swap_core(row_last), *rows_near_other[last:]]
        slot_rows_mine, slot_gates_mine = dispatch_rows(
            lead, grads_mine, rows_mine, router_rows, local, capacity
        )
        slot_rows_other, slot_gates_other = dispatch_rows(
            lead, grads_other, after(rows_other, slot_rows_mine), router_rows, local, capacity
        )
        slot_rows_other = after(slot_rows_other, *last_far)
        ys, dxs, weight_grads, sums = [], [], [], []
        for half in range(halves):
            y, dx, grads = experts(
                order,
                half * per,
                per,
                (slot_rows_mine, slot_rows_other),
                (slot_grads_mine, slot_grads_other),
                (slot_gates_mine, slot_gates_other),
                weights,
                chunks[half * per : (half + 1) * per],
                capacity,
                in_rows,
                mid_rows,
            )
            ys.append(y)
            dxs.append(dx)
            weight_grads.append(grads)

        def grid_sum(grads, got):
            totals = []
            for half in range(2):
                own = grads[4 * half][0]
                direct, last = got[half][0], got[1 - half][1]
                totals.append(own.astype(F32) + direct.astype(F32) + last.astype(F32))
            return totals

        def second_step(grads, via, *more):
            _, x_a, y_a, _, _, x_b, y_b, _ = grads
            return cross(*join_parts((x_a, x_b, *more[:1]), (y_b, y_a, *more[1:]), via[::-1]))

        if small_grid:
            early, late = weight_grads
            via = cross(early[3], early[7])
            dxs = after(dxs, *via)
            early_got = second_step(early, via, late[3], late[7])
        dx_other = combine_rows(lead, z_size, grads_other, dxs, local, capacity)
        y_other = combine_rows(lead, z_size, grads_other, after(ys, dx_other), local, capacity)
        dx_other = after(swap_core(dx_other), y_other)
        dx_low = combine_rows(lead, 0, grads_mine, dxs, local, capacity, dx_other)
        dx_low, y_other = after((dx_low, swap_core(y_other)), dx_low[0])
        dx_pieces = column_send_last(dx_low, z_size) + column_send_some(dx_low, z_size)
        y_low = combine_rows(lead, 0, grads_mine, ys, local, capacity, y_other)
        dx_pieces = after(dx_pieces, *y_low)
        y_pieces = column_send_some(after(y_low, *dx_pieces), z_size)
        if small_grid:
            early_got = after(early_got, *dx_pieces)
            late_got = second_step(late, early_got)
        if small_grid:
            keep, give, normed_first, normed_a, normed_b, residual_grad = attention_backward(
                jnp.stack([dp_index, core]).astype(jnp.int32),
                (dx_low[0], *dx_pieces),
                out_grad,
                residual,
                gates,
                misc,
                attended,
                moe_in,
                (x_all, normed_all, query_rot, key_rot, value_all, totals),
                dense_full,
                after(bias, *early_got),
                cosine,
                sine,
            )
            late_got, y_pieces = after((late_got, y_pieces), residual_grad)
            normed_first, keep, give = after((normed_first, keep, give), *late_got, *y_pieces)
            y_pieces += column_send_last(y_low, z_size, *y_pieces)
            dense_first, dense_a, dense_b = core_halves(keep, swap_core(give))
            normed_got = grid_scatter_first(*normed_first)
            dense_got = grid_scatter_first(*after(dense_first, *normed_got))
            early_got, late_got = after((early_got, late_got), *dense_got)
            dense_low = across_z(
                jnp.concatenate(grid_scatter_second(dense_got, dense_a, dense_b), axis=0), z
            )
            (
                query_sum, key_sum, value_sum, output_sum, router_sum, attn_gain_sum, moe_gain_sum,
            ) = dense_outputs(core, dense_low, swap_core(dense_low), wide, narrow)
            y_pieces = after(y_pieces, *dense_got)
            normed_grad = jnp.concatenate(
                grid_scatter_second(normed_got, normed_a, normed_b, *dense_got), axis=0
            )
            first_value, first_pull = jax.vjp(lambda v: rms_norm(v, full_attn_gain), in_float)
            input_grad = residual_grad + first_pull(normed_grad)[0]
        else:
            y_pieces += column_send_last(y_low, z_size)
            moe_sum = column_sum(dx_low[0], dx_pieces)
            moe_in_grad = moe_sum[:, :model_width]
            gate_grad = (
                moe_sum[:, model_width : model_width + EXPERTS]
                + moe_sum[:, model_width + EXPERTS : model_width + 2 * EXPERTS]
            )
            logits = lax.dot_general(moe_in, router_rows, NT, preferred_element_type=F32)
            peak = jnp.max(jnp.where(routed, logits, MASKED_SCORE), axis=-1, keepdims=True)
            lifted = jnp.where(routed, jnp.exp(jnp.minimum(logits - peak, 0.0)), 0.0)
            gate_weights = lifted / jnp.sum(lifted, axis=-1, keepdims=True)
            grad_out = out_grad.astype(F32)
            centre = jnp.sum(gate_weights * gate_grad, axis=-1, keepdims=True)
            logit_low = (gate_weights * (gate_grad - centre)).astype(B16)
            moe_in_grad = moe_in_grad + jnp.dot(logit_low, router_rows, preferred_element_type=F32)
            norm_value, second_pull = jax.vjp(rms_norm, residual, full_moe_gain)
            resid_norm_grad, moe_gain_grad = second_pull(moe_in_grad)
            residual_grad = grad_out + resid_norm_grad
            attn_out_grad = residual_grad.astype(B16)
            router_grad = jnp.einsum("td,te->de", moe_in, logit_low, preferred_element_type=F32)
            wout_grad = jnp.einsum("tc,td->cd", attended, attn_out_grad, preferred_element_type=F32)
            attended_grad = (
                jnp.einsum("td,cd->tc", attn_out_grad, full_output, preferred_element_type=F32)
                .astype(B16)
                .reshape(tok_rows, H, HD)
            )
            query_grads = []
            key_parts = []
            value_parts = []
            for head_idx in range(KVH):
                scores = head_scores(head_idx)
                attention_probs = jnp.exp(scores - log_totals[head_idx])
                probs_low = attention_probs.astype(B16)
                grad_head = attended_grad[:, head_idx * group_size : (head_idx + 1) * group_size, :]
                query_head = query_rot[:, head_idx * group_size : (head_idx + 1) * group_size, :]
                key_head = key_all[:, head_idx * HD : (head_idx + 1) * HD]
                value_head = value_all[:, head_idx * HD : (head_idx + 1) * HD]
                probs_grad = jnp.einsum("qgd,kd->gqk", grad_head, value_head, preferred_element_type=F32)
                row_delta = jnp.sum(attention_probs * probs_grad, axis=-1, keepdims=True)
                score_grad = (attention_probs * (probs_grad - row_delta)).astype(B16)
                query_grads.append(
                    jnp.einsum("gqk,kd->qgd", score_grad, key_head, preferred_element_type=F32)
                )
                key_parts.append(
                    jnp.einsum("gqk,qgd->kd", score_grad, query_head, preferred_element_type=F32)
                )
                value_parts.append(
                    jnp.einsum("gqk,qgd->kd", probs_low, grad_head, preferred_element_type=F32)
                )
            both_part = jnp.concatenate(key_parts + value_parts, axis=1)
            both_sum = lax.psum_scatter(both_part, ("y", "x"), scatter_dimension=0, tiled=True)
            query_rot_grad = jnp.concatenate(query_grads, axis=1) * score_scale
            key_rot_grad = both_sum[:, :narrow].reshape(tok_rows, KVH, HD)
            value_grad = both_sum[:, narrow:].astype(B16)
            query_grad = rotate(query_rot_grad, -places).reshape(tok_rows, wide).astype(B16)
            key_grad = rotate(key_rot_grad, -places).reshape(tok_rows, narrow).astype(B16)
            wq_grad = jnp.einsum("td,tc->dc", normed, query_grad, preferred_element_type=F32)
            wk_grad = jnp.einsum("td,tc->dc", normed, key_grad, preferred_element_type=F32)
            wv_grad = jnp.einsum("td,tc->dc", normed, value_grad, preferred_element_type=F32)
            normed_grad = jnp.einsum("tc,dc->td", query_grad, full_query, preferred_element_type=F32)
            normed_grad = normed_grad + jnp.einsum(
                "tc,dc->td", key_grad, full_key, preferred_element_type=F32
            )
            normed_grad = normed_grad + jnp.einsum(
                "tc,dc->td", value_grad, full_value, preferred_element_type=F32
            )
            first_value, first_pull = jax.vjp(rms_norm, in_float, full_attn_gain)
            input_norm_grad, attn_gain_grad = first_pull(normed_grad)
            input_grad = residual_grad + input_norm_grad
            query_sum = dense_sum(wq_grad)
            key_sum = dense_sum(wk_grad)
            value_sum = dense_sum(wv_grad)
            output_sum = dense_sum(wout_grad)
            extra_sum = dense_sum(
                jnp.concatenate(
                    [
                        router_grad,
                        attn_gain_grad[:, None],
                        moe_gain_grad[:, None],
                        jnp.zeros((model_width, EXTRA - EXPERTS - 2), F32),
                    ],
                    axis=1,
                )
            )
            router_sum = extra_sum[:, :EXPERTS]
            attn_gain_sum = extra_sum[:, EXPERTS]
            moe_gain_sum = extra_sum[:, EXPERTS + 1]
        layer_output = (residual + column_sum(y_low[0], y_pieces)).astype(B16)
        if small_grid:
            parts = grid_sum(early, early_got) + grid_sum(late, late_got)
            pack_grad = jnp.concatenate(parts, axis=0)
        else:
            pack_grad = lax.psum_scatter(
                weight_grads[0][0].astype(F32), ("y", "x"), scatter_dimension=0, tiled=False
            )
        down = 2 * in_rows
        expert_grads = [
            pack_grad[:, :in_rows],
            pack_grad[:, in_rows:down],
            jnp.concatenate(
                [
                    pack_grad[:, down + f * mid_rows : down + (f + 1) * mid_rows]
                    for f in range(model_width // eff)
                ],
                axis=2,
            ),
        ]

        return (
            layer_output,
            input_grad,
            attn_gain_sum,
            query_sum,
            key_sum,
            value_sum,
            output_sum,
            moe_gain_sum,
            router_sum,
            expert_grads[0],
            expert_grads[1],
            expert_grads[2],
        )

    return body


def solution(mesh):
    groups = mesh.shape["expert"]
    members = mesh.shape["dp"]
    z_size = groups // 2
    side = math.isqrt(members)
    grid = Mesh(
        mesh.devices.reshape(z_size, 2, members // side, side), ("z", "core", "y", "x")
    )
    expert = ("z", "core")
    dp = ("y", "x")
    every = expert + dp
    placed = (
        P(every, None),
        P(dp),
        P(dp, None),
        P(dp, None),
        P(dp, None),
        P(dp, None),
        P(dp),
        P(dp, None),
        P(expert, dp, None),
        P(expert, dp, None),
        P(expert, dp, None),
        P(every, None),
        P(every, None),
        P(expert),
        P(every, None),
    )
    return jax.shard_map(
        make_body(z_size, members == 4 and side == 2 and EXPERTS == 4 * groups),
        mesh=grid,
        in_specs=placed,
        out_specs=(
            P(every, None),
            P(every, None),
            P(dp),
            P(dp, None),
            P(dp, None),
            P(dp, None),
            P(dp, None),
            P(dp),
            P(dp, None),
            P(expert, dp, None),
            P(expert, dp, None),
            P(expert, dp, None),
        ),
        check_vma=False,
    )
```

```python
import math

import jax
import jax.numpy as jnp
from jax import lax
from jax.experimental import pallas as pl
from jax.experimental.pallas import tpu as pltpu
from jax.sharding import Mesh
from jax.sharding import PartitionSpec as P

H = 16
KVH = 8
HD = 64
EXPERTS = 32
EPSILON = 1e-06
ROPE_BASE = 10000.0
MASKED_SCORE = -1e30
F32 = jnp.float32
B16 = jnp.bfloat16
SWAP = [(0, 1), (1, 0)]
VMEM_LIMIT = 60 * 1024 * 1024


def rms_norm(values, gain_vec):
    return (
        values * lax.rsqrt(jnp.mean(values * values, axis=-1, keepdims=True) + EPSILON) * gain_vec
    )


def rotate(vectors, places):
    half_dim = vectors.shape[-1] // 2
    frequency = jnp.exp(
        jnp.arange(half_dim, dtype=F32) * (-2.0 * math.log(ROPE_BASE) / vectors.shape[-1])
    )
    angles = places[:, None] * frequency[None, :]
    cosine = jnp.cos(angles)[:, None, :]
    sine_vals = jnp.sin(angles)[:, None, :]
    first_half = vectors[..., :half_dim]
    second = vectors[..., half_dim:]
    return jnp.concatenate(
        [first_half * cosine - second * sine_vals, second * cosine + first_half * sine_vals],
        axis=-1,
    )


def swap_core(rows):
    return lax.ppermute(rows, "core", SWAP)


def cyclic(rows, size, shift):
    return lax.ppermute(rows, "z", [(i, (i + shift) % size) for i in range(size)])


def after(value, *others):
    return lax.optimization_barrier((value, *others))[0]


def gather_near(shard):
    return [lax.ppermute(shard, "x", SWAP), lax.ppermute(shard, "y", SWAP)]


def gather_far(near):
    from_x, from_y = near
    half = from_x.shape[0] // 2
    return [lax.ppermute(from_x[:half], "y", SWAP), lax.ppermute(from_y[half:], "x", SWAP)]


def grid_gather(shard):
    near = gather_near(shard)
    return near + gather_far(near)


def cross(to_x, to_y):
    return lax.ppermute(to_x, "x", SWAP), lax.ppermute(to_y, "y", SWAP)


def far_and_next(nears, shard):
    rows = shard.shape[0]
    half = rows // 2
    return cross(
        jnp.concatenate([from_y[-half:] for _, from_y in nears] + [shard], axis=0),
        jnp.concatenate([from_x[-rows:-half] for from_x, _ in nears] + [shard], axis=0),
    )


def plus_low(a, b):
    return (a.astype(F32) + b.astype(F32)).astype(B16)


def grid_scatter_first(first_a, first_b):
    return lax.ppermute(first_a, "x", SWAP), lax.ppermute(first_b, "y", SWAP)


def grid_scatter_second(got, rest_a, rest_b, *early):
    got_a, got_b = after(got, *early)
    onward_a = (rest_a[1].astype(F32) + got_a[1].astype(F32)).astype(B16)
    onward_b = (rest_b[1].astype(F32) + got_b[1].astype(F32)).astype(B16)
    last_a = lax.ppermute(onward_a, "y", SWAP)
    last_b = lax.ppermute(onward_b, "x", SWAP)
    return (
        rest_a[0].astype(F32) + got_a[0].astype(F32) + last_a.astype(F32),
        rest_b[0].astype(F32) + got_b[0].astype(F32) + last_b.astype(F32),
    )


def row_halves(parts):
    own, to_x, to_y, diag = [parts[j] for j in range(4)]
    half = own.shape[0] // 2
    first = (
        jnp.stack([to_x[:half], diag[:half]]),
        jnp.stack([to_y[half:], diag[half:]]),
    )
    return first, (own[:half], to_y[:half]), (own[half:], to_x[half:])


def column_pieces(rows, size):
    return [rows] + [cyclic(rows, size, -k) for k in range(1, size)]


def column_send_some(low, size):
    return [cyclic(low[k], size, k) for k in range(1, size) if 2 * k != size]


def column_send_last(low, size, *hold):
    return [cyclic(after(low[size // 2], *hold), size, size // 2)]


def column_sum(own, pieces):
    return own.astype(F32) + sum(piece.astype(F32) for piece in pieces)


def assemble(places, shard, moved, other, rows):
    def kernel(places_ref, shard_ref, moved_ref, other_ref, out_ref):
        def put(i, value):
            start = pl.multiple_of(places_ref[i] * rows, rows)
            out_ref[pl.ds(start, value.shape[0]), :] = value

        put(0, shard_ref[...])
        for j in range(3):
            put(1 + j, moved_ref[j * rows : (j + 1) * rows, :])
            put(4 + j, other_ref[j * rows : (j + 1) * rows, :])

    def whole(array_shape):
        return pl.BlockSpec(array_shape, lambda i, places: (0, 0))

    out_rows, cols = 8 * rows, shard.shape[1]
    return pl.pallas_call(
        kernel,
        out_shape=jax.ShapeDtypeStruct((out_rows, cols), shard.dtype),
        grid_spec=pltpu.PrefetchScalarGridSpec(
            num_scalar_prefetch=1,
            grid=(1,),
            in_specs=[whole(a.shape) for a in (shard, moved, other)],
            out_specs=whole((out_rows, cols)),
        ),
        compiler_params=pltpu.CompilerParams(vmem_limit_bytes=VMEM_LIMIT),
        name="assemble",
    )(places, shard, moved, other)


def one_hot_slots(codes, capacity):
    slots = lax.broadcasted_iota(jnp.int32, (capacity, codes.shape[1]), 0).astype(F32)
    return [(slots == codes[e : e + 1, :]).astype(F32) for e in range(codes.shape[0])]


def row_of(table, index):
    at = lax.broadcasted_iota(jnp.int32, table.shape, 0)
    return jnp.sum(jnp.where(at == index, table, 0.0), axis=0, keepdims=True)


def pack_code(code):
    rows = code.shape[0] // 4
    wide = jnp.concatenate([code[c * rows : (c + 1) * rows] for c in range(4)], axis=1)
    return jnp.concatenate([wide, jnp.full((16 - rows, wide.shape[1]), -1.0, B16)], axis=0)


def unpack_code(block, tokens):
    rows = EXPERTS // 4
    wide = block.astype(F32)
    return jnp.concatenate(
        [wide[:rows, c * tokens : (c + 1) * tokens] for c in range(4)], axis=0
    )


def dispatch_rows(lead, packed, rows, router, local, capacity):
    pieces, packed_rows, width = packed.shape
    tokens = packed_rows - 16
    slots = local * capacity
    with_gates = router is not None

    def kernel(lead_ref, packed_ref, *rest):
        first = lead_ref[0]
        if with_gates:
            router_ref, out_ref, gate_out, rows_ref = rest[pieces:]
            for p in range(pieces):

                @pl.when(pl.program_id(0) == p)
                def _():
                    rows_ref[...] = rest[p][...]

            table = unpack_code(packed_ref[0], tokens)
            source = rows_ref[...]
        else:
            (out_ref,) = rest
            table = unpack_code(packed_ref[0, tokens:, :], tokens)
            source = packed_ref[0, :tokens, :]
        codes = jnp.concatenate([row_of(table, first + e) for e in range(local)], axis=0)
        picks = one_hot_slots(codes, capacity)
        select = jnp.concatenate([p.astype(B16) for p in picks], axis=0)
        out_ref[0] = jnp.dot(select, source, preferred_element_type=F32).astype(B16)
        if with_gates:
            logits = lax.dot_general(
                router_ref[...], source, (((1,), (1,)), ((), ())), preferred_element_type=F32
            )
            routed = table >= 0.0
            peak = jnp.max(jnp.where(routed, logits, MASKED_SCORE), axis=0, keepdims=True)
            lifted = jnp.where(routed, jnp.exp(jnp.minimum(logits - peak, 0.0)), 0.0)
            gates = lifted / jnp.sum(lifted, axis=0, keepdims=True)
            for e in range(local):
                gate_row = row_of(gates, first + e)
                column = jnp.sum(picks[e] * gate_row, axis=1, keepdims=True)
                gate_out[0, e * capacity : (e + 1) * capacity, :] = jnp.broadcast_to(
                    column, (capacity, 128)
                )

    out_specs = [pl.BlockSpec((1, slots, width), lambda p, lead: (p, 0, 0))]
    out_shape = [jax.ShapeDtypeStruct((pieces, slots, width), B16)]
    args = [packed]
    if with_gates:
        in_specs = [
            pl.BlockSpec((1, 16, width), lambda p, lead: (p, tokens // 16, 0)),
            *[pl.BlockSpec((tokens, width), lambda p, lead: (0, 0)) for _ in rows],
            pl.BlockSpec((EXPERTS, width), lambda p, lead: (0, 0)),
        ]
        out_specs.append(pl.BlockSpec((1, slots, 128), lambda p, lead: (p, 0, 0)))
        out_shape.append(jax.ShapeDtypeStruct((pieces, slots, 128), F32))
        args += [*rows, router]
    else:
        in_specs = [pl.BlockSpec((1, packed_rows, width), lambda p, lead: (p, 0, 0))]
    return pl.pallas_call(
        kernel,
        out_shape=out_shape,
        grid_spec=pltpu.PrefetchScalarGridSpec(
            num_scalar_prefetch=1,
            grid=(pieces,),
            in_specs=in_specs,
            out_specs=out_specs,
            scratch_shapes=[pltpu.VMEM((tokens, width), B16)] if with_gates else [],
        ),
        compiler_params=pltpu.CompilerParams(vmem_limit_bytes=VMEM_LIMIT),
        name="dispatch",
    )(lead, *args)


def combine_rows(lead, first, packed, slot_rows, local, capacity, addend=None):
    pieces, packed_rows, code_width = packed.shape
    tokens = packed_rows - 16
    halves = len(slot_rows)
    slots, width = slot_rows[0].shape[1:]
    per = local // halves

    def kernel(lead_ref, code_ref, *rest):
        table = unpack_code(code_ref[0], tokens)
        here = lead_ref[0]
        codes = jnp.concatenate([row_of(table, here + e) for e in range(local)], axis=0)
        picks = one_hot_slots(codes, capacity)
        total = None
        for h in range(halves):
            select = jnp.concatenate(
                [p.astype(B16) for p in picks[h * per : (h + 1) * per]], axis=0
            )
            part = lax.dot_general(
                select, rest[h][0], (((0,), (0,)), ((), ())), preferred_element_type=F32
            )
            total = part if total is None else total + part
        if addend is None:
            rest[halves][0] = total.astype(B16)
        else:
            low = (total + rest[halves][0].astype(F32)).astype(B16)
            for p in range(pieces):

                @pl.when(pl.program_id(0) == p)
                def _():
                    rest[halves + 1 + p][...] = low

    in_specs = [pl.BlockSpec((1, 16, code_width), lambda p, lead: (p, tokens // 16, 0))]
    in_specs += [
        pl.BlockSpec((1, slots, width), lambda p, lead: (p + first, 0, 0)) for _ in range(halves)
    ]
    added = [] if addend is None else [addend]
    in_specs += [pl.BlockSpec((1, tokens, width), lambda p, lead: (p, 0, 0)) for _ in added]
    if addend is None:
        out_shape = jax.ShapeDtypeStruct((pieces, tokens, width), B16)
        out_specs = pl.BlockSpec((1, tokens, width), lambda p, lead: (p, 0, 0))
    else:
        out_shape = [jax.ShapeDtypeStruct((tokens, width), B16)] * pieces
        out_specs = [pl.BlockSpec((tokens, width), lambda p, lead: (0, 0))] * pieces
    return pl.pallas_call(
        kernel,
        out_shape=out_shape,
        grid_spec=pltpu.PrefetchScalarGridSpec(
            num_scalar_prefetch=1,
            grid=(pieces,),
            in_specs=in_specs,
            out_specs=out_specs,
        ),
        compiler_params=pltpu.CompilerParams(vmem_limit_bytes=VMEM_LIMIT),
        name="combine",
    )(lead, packed, *slot_rows, *added)


def experts(order, start, count, rows, grads, gates, weights, chunks, capacity, in_rows, mid_rows):
    half, _, width = rows[0].shape
    pieces = 2 * half
    split = bool(chunks)
    n = 4 if split else len(weights)
    extra = [array for chunk in chunks for array, _ in chunk]
    given = len(weights) + len(extra)
    pack_rows, eff = chunks[0][0][0].shape if split else weights[0].shape[1:]
    folds = width // eff
    total_rows = pieces * capacity
    first_half = count // 2
    large = total_rows > 1000

    def kernel(order_ref, *refs):
        rows_a, rows_b, grads_a, grads_b, gates_a, gates_b = refs[:6]
        pack = refs[6 : 6 + given]
        y_out, dx_out = refs[6 + given : 8 + given]
        outs = refs[8 + given : -6]
        full_g, full_u, full_d, grad_g, grad_u, grad_d = refs[-6:]

        def at_in(j):
            return pl.ds(pl.multiple_of(order_ref[j] * in_rows, in_rows), in_rows)

        def at_mid(j):
            return pl.ds(pl.multiple_of(order_ref[j] * mid_rows, mid_rows), mid_rows)

        def load(j, take):
            full_g[at_in(j), :] = take(0, in_rows)
            full_u[at_in(j), :] = take(in_rows, 2 * in_rows)
            for f in range(folds):
                full_d[at_mid(j), f * eff : (f + 1) * eff] = take(
                    2 * in_rows + f * mid_rows, 2 * in_rows + (f + 1) * mid_rows
                )

        def rows_from(ref, offset):
            return lambda lo, hi: ref[offset + lo : offset + hi, :]

        def two_halves(a, b):
            middle = pack_rows // 2

            def take(lo, hi):
                if hi <= middle:
                    return a(lo, hi)
                if lo >= middle:
                    return b(lo - middle, hi - middle)
                return jnp.concatenate([a(lo, middle), b(0, hi - middle)], axis=0)

            return take

        for j in range(len(weights)):
            load(j, lambda lo, hi, ref=pack[j]: ref[0, lo:hi])
        for c in range(len(chunks)):
            own, from_x, from_y, diag_a, diag_b = [
                rows_from(pack[5 * c + i], chunks[c][i][1]) for i in range(5)
            ]

            @pl.when(pl.program_id(0) == c)
            def _():
                load(0, own)
                load(1, from_x)
                load(2, from_y)
                load(3, two_halves(diag_a, diag_b))

        def joined(a, b, w):
            return jnp.concatenate(
                [
                    a[...].reshape(half * capacity, w),
                    b[...].reshape(half * capacity, w),
                ],
                axis=0,
            )

        x = joined(rows_a, rows_b, width)
        g = joined(grads_a, grads_b, width)
        gate = joined(gates_a, gates_b, 128)[:, 0:1]
        nt = (((1,), (1,)), ((), ()))
        tn = (((0,), (0,)), ((), ()))
        gate_proj = jnp.dot(x, full_g[...], preferred_element_type=F32)
        up_proj = jnp.dot(x, full_u[...], preferred_element_type=F32)
        down_grad = lax.dot_general(g, full_d[...], nt, preferred_element_type=F32)
        sigmoid = 1.0 / (1.0 + jnp.exp(-gate_proj))
        silu = gate_proj * sigmoid
        activated = silu * up_proj
        slot_grad = jnp.sum(activated * down_grad, axis=1, keepdims=True)
        here = order_ref[n] + start + pl.program_id(0)
        lane = lax.broadcasted_iota(jnp.int32, (total_rows, 128), 1)
        high = slot_grad.astype(B16).astype(F32)
        tail = jnp.where(lane == here, high, jnp.where(lane == here + EXPERTS, slot_grad - high, 0.0))
        dx_out[:, :, width:] = tail.astype(B16).reshape(pieces, capacity, 128)
        scaled = (gate * activated).astype(B16)
        act_grad = gate * down_grad
        gate_grad = (act_grad * up_proj * (sigmoid * (1.0 + gate_proj * (1.0 - sigmoid)))).astype(
            B16
        )
        up_grad = (act_grad * silu).astype(B16)
        y = jnp.dot(scaled, full_d[...], preferred_element_type=F32)
        y_out[...] = y.astype(B16).reshape(pieces, capacity, width)
        dx = lax.dot_general(gate_grad, full_g[...], nt, preferred_element_type=F32)
        dx = dx + lax.dot_general(up_grad, full_u[...], nt, preferred_element_type=F32)
        dx_out[:, :, :width] = dx.astype(B16).reshape(pieces, capacity, width)
        grad_g[...] = lax.dot_general(x, gate_grad, tn, preferred_element_type=F32).astype(B16)
        grad_u[...] = lax.dot_general(x, up_grad, tn, preferred_element_type=F32).astype(B16)
        grad_d[...] = lax.dot_general(scaled, g, tn, preferred_element_type=F32).astype(B16)

        def give(ref, slot, j):
            ref[slot, 0, :in_rows] = grad_g[at_in(j), :]
            ref[slot, 0, in_rows : 2 * in_rows] = grad_u[at_in(j), :]
            for f in range(folds):
                ref[slot, 0, 2 * in_rows + f * mid_rows : 2 * in_rows + (f + 1) * mid_rows] = grad_d[
                    at_mid(j), f * eff : (f + 1) * eff
                ]

        if split:

            @pl.when(pl.program_id(0) < first_half)
            def _():
                for j in range(4):
                    give(outs[j], 0, j)

            @pl.when(pl.program_id(0) >= first_half)
            def _():
                for j in range(4):
                    give(outs[4 + j], 0, j)
        else:
            for j in range(n):
                give(outs[0], j, j)

    def single():
        return dict(pipeline_mode=pl.Buffered(1)) if large else {}

    def rows_spec(w):
        return pl.BlockSpec((half, capacity, w), lambda e, o: (0, e + start, 0), **single())

    in_specs = [rows_spec(width)] * 4 + [rows_spec(128)] * 2
    for _ in weights:
        in_specs.append(pl.BlockSpec((1, pack_rows, eff), lambda e, o: (e + start, 0, 0)))
    for part in extra:
        in_specs.append(pl.BlockSpec(part.shape, lambda e, o: (0, 0)))
    slots = count * capacity
    out_specs = [
        pl.BlockSpec((pieces, capacity, w), lambda e, o: (0, e, 0), **single())
        for w in (width, width + 128)
    ]
    out_shape = [
        jax.ShapeDtypeStruct((pieces, slots, width), B16),
        jax.ShapeDtypeStruct((pieces, slots, width + 128), B16),
    ]
    if split:
        for at in (
            lambda e, o: (0, jnp.minimum(e, first_half - 1), 0, 0),
            lambda e, o: (0, jnp.maximum(e - first_half, 0), 0, 0),
        ):
            for _ in range(4):
                out_specs.append(pl.BlockSpec((1, 1, pack_rows, eff), at))
                out_shape.append(jax.ShapeDtypeStruct((1, first_half, pack_rows, eff), B16))
    else:
        out_specs.append(pl.BlockSpec((n, 1, pack_rows, eff), lambda e, o: (0, e, 0, 0)))
        out_shape.append(jax.ShapeDtypeStruct((n, count, pack_rows, eff), B16))
    results = pl.pallas_call(
        kernel,
        out_shape=out_shape,
        grid_spec=pltpu.PrefetchScalarGridSpec(
            num_scalar_prefetch=1,
            grid=(count,),
            in_specs=in_specs,
            out_specs=out_specs,
            scratch_shapes=[
                pltpu.VMEM((n * in_rows, eff), B16),
                pltpu.VMEM((n * in_rows, eff), B16),
                pltpu.VMEM((n * mid_rows, width), B16),
                pltpu.VMEM((n * in_rows, eff), B16),
                pltpu.VMEM((n * in_rows, eff), B16),
                pltpu.VMEM((n * mid_rows, width), B16),
            ],
        ),
        compiler_params=pltpu.CompilerParams(vmem_limit_bytes=VMEM_LIMIT),
        name="experts",
    )(order, *rows, *grads, *gates, *weights, *extra)
    return results[0], results[1], results[2:]


NT = (((1,), (1,)), ((), ()))
TN = (((0,), (0,)), ((), ()))
GROUPS = KVH // 2
EXTRA = 128


def turn(vectors, cosine, sine):
    lane = lax.broadcasted_iota(jnp.int32, vectors.shape, 1)
    ahead = pltpu.roll(vectors, 2 * HD - HD // 2, 1)
    behind = pltpu.roll(vectors, HD // 2, 1)
    return vectors * cosine + jnp.where(lane % HD < HD // 2, ahead, behind) * sine


def turn_tables(places):
    lane = jnp.arange(2 * HD, dtype=jnp.int32)
    frequency = jnp.exp(
        (lane % (HD // 2)).astype(F32) * (-2.0 * math.log(ROPE_BASE) / HD)
    )
    angles = places[:, None] * frequency[None, :]
    sign = jnp.where(lane % HD < HD // 2, -1.0, 1.0)
    return jnp.cos(angles), jnp.sin(angles) * sign[None, :]


def attention_forward(x_own, x_parts, dense_full, bias, cosine, sine, routed):
    tok_rows, width = x_own.shape
    seq_len = 4 * tok_rows
    scale = HD ** (-0.5)
    wide, narrow = H * HD, KVH * HD

    def kernel(
        own_ref, xa_ref, xb_ref, ya_ref, yb_ref, da_ref, db_ref, ea_ref, eb_ref,
        tail_ref, wo_ref, wq_ref, wk_ref, wv_ref, bias_ref, cos_ref, sin_ref, routed_ref,
        x_ref, normed_ref, q_out, k_out, v_out, att_out, total_out, misc_out, residual_out, moe_out,
        gates_out,
    ):
        step = pl.program_id(0)

        @pl.when(step == 0)
        def _():
            rows = jnp.transpose(tail_ref[...].astype(F32))
            misc_out[...] = rows
            at = 0
            for ref in (own_ref, xa_ref, xb_ref, ya_ref, yb_ref, da_ref, ea_ref, db_ref, eb_ref):
                x_ref[at : at + ref.shape[0], :] = ref[...]
                at += ref.shape[0]
            x = x_ref[...].astype(F32)
            scaled = x * lax.rsqrt(jnp.mean(x * x, axis=1, keepdims=True) + EPSILON)
            normed_ref[...] = (scaled * rows[EXPERTS : EXPERTS + 1, :]).astype(B16)
            residual_out[...] = x[:tok_rows]

        normed = normed_ref[...]
        cos, sin = cos_ref[...], sin_ref[...]
        key = turn(jnp.dot(normed, wk_ref[...], preferred_element_type=F32), cos, sin).astype(B16)
        value = jnp.dot(normed, wv_ref[...], preferred_element_type=F32).astype(B16)
        query = jnp.dot(normed[:tok_rows], wq_ref[...], preferred_element_type=F32)
        cos, sin = cos[:tok_rows], sin[:tok_rows]
        query = jnp.concatenate(
            [turn(query[:, 128 * j : 128 * (j + 1)], cos, sin) for j in range(2)], axis=1
        )
        query = (query * scale).astype(B16)
        k_out[...] = key
        v_out[...] = value
        q_out[...] = query
        mixed, totals = [], []
        for j in range(4):
            lanes = slice(HD * (j // 2), HD * (j // 2 + 1))
            scores = lax.dot_general(
                key[:, lanes], query[:, HD * j : HD * (j + 1)], NT, preferred_element_type=F32
            )
            scores = scores + bias_ref[...]
            peak = jnp.max(scores, axis=0, keepdims=True)
            probs = jnp.exp(scores - peak)
            total = jnp.sum(probs, axis=0, keepdims=True)
            out = lax.dot_general(
                value[:, lanes], probs.astype(B16), TN, preferred_element_type=F32
            )
            mixed.append(out / total)
            totals.append(peak + jnp.log(total))
        attended = jnp.transpose(jnp.concatenate(mixed, axis=0)).astype(B16)
        att_out[...] = attended
        total_out[0] = jnp.concatenate(totals + totals, axis=0)
        residual_out[...] += jnp.dot(attended, wo_ref[...], preferred_element_type=F32)

        @pl.when(step == GROUPS - 1)
        def _():
            total = residual_out[...]
            scaled = total * lax.rsqrt(jnp.mean(total * total, axis=1, keepdims=True) + EPSILON)
            moe_in = (scaled * misc_out[EXPERTS + 1 : EXPERTS + 2, :]).astype(B16)
            moe_out[...] = moe_in
            logits = jnp.dot(moe_in, tail_ref[...], preferred_element_type=F32)
            here = routed_ref[...] > 0.0
            peak = jnp.max(jnp.where(here, logits, MASKED_SCORE), axis=1, keepdims=True)
            lifted = jnp.where(here, jnp.exp(jnp.minimum(logits - peak, 0.0)), 0.0)
            gates_out[...] = lifted / jnp.sum(lifted, axis=1, keepdims=True)

    def fixed(*block):
        return pl.BlockSpec(block, lambda i: (0,) * len(block))

    def columns(rows, cols, lead=0):
        return pl.BlockSpec((rows, cols), lambda i: (0, lead + i))

    return pl.pallas_call(
        kernel,
        grid=(GROUPS,),
        in_specs=[
            fixed(tok_rows, width),
            *[
                pl.BlockSpec((part.shape[0], width), lambda i, c=c: (0, c))
                for part in x_parts
                for c in range(2)
            ],
            pl.BlockSpec((width, 128), lambda i: (0, (width + wide + 2 * narrow) // 128)),
            pl.BlockSpec((256, width), lambda i: (i, 0)),
            columns(width, 256, width // 256),
            columns(width, 128, (width + wide) // 128),
            columns(width, 128, (width + wide + narrow) // 128),
            fixed(seq_len, tok_rows),
            fixed(seq_len, 128),
            fixed(seq_len, 128),
            fixed(tok_rows, 128),
        ],
        out_specs=[
            fixed(seq_len, width),
            fixed(seq_len, width),
            columns(tok_rows, 256),
            columns(seq_len, 128),
            columns(seq_len, 128),
            columns(tok_rows, 256),
            pl.BlockSpec((1, 8, tok_rows), lambda i: (i, 0, 0)),
            fixed(128, width),
            fixed(tok_rows, width),
            fixed(tok_rows, width),
            fixed(tok_rows, 128),
        ],
        out_shape=[
            jax.ShapeDtypeStruct((seq_len, width), B16),
            jax.ShapeDtypeStruct((seq_len, width), B16),
            jax.ShapeDtypeStruct((tok_rows, wide), B16),
            jax.ShapeDtypeStruct((seq_len, narrow), B16),
            jax.ShapeDtypeStruct((seq_len, narrow), B16),
            jax.ShapeDtypeStruct((tok_rows, wide), B16),
            jax.ShapeDtypeStruct((GROUPS, 8, tok_rows), F32),
            jax.ShapeDtypeStruct((128, width), F32),
            jax.ShapeDtypeStruct((tok_rows, width), F32),
            jax.ShapeDtypeStruct((tok_rows, width), B16),
            jax.ShapeDtypeStruct((tok_rows, 128), F32),
        ],
        compiler_params=pltpu.CompilerParams(vmem_limit_bytes=VMEM_LIMIT),
        name="attention",
    )(
        x_own, *[part for part in x_parts for _ in range(2)], *[dense_full] * 5,
        bias, cosine, sine, routed,
    )


def attention_backward(
    where_here, moe_sums, out_grad, residual, gates, misc, attended, moe_in, saved,
    dense_full, bias, cosine, sine,
):
    x_all, normed_all, query_rot, key_rot, value_all, totals = saved
    terms = len(moe_sums)
    seq_len, width = x_all.shape
    tok_rows = query_rot.shape[0]
    scale = HD ** (-0.5)
    wide, narrow = H * HD, KVH * HD
    block = width // 8
    output_at = wide + 2 * narrow

    def kernel(here_ref, *refs):
        sums = refs[:terms]
        (
            grad_ref, residual_ref, gates_ref, misc_ref, tail_ref, wo_ref, att_ref, moe_ref,
            normed_ref, q_ref, k_ref, v_ref, total_ref,
            x_ref, wq_ref, wk_ref, wv_ref, bias_ref, cos_ref, sin_ref,
            keep_out, give_out, first_a_out, first_b_out, rest_a_out, rest_b_out, residual_out,
            normed_t, grad_sum, og_ref, logit_ref, gain_ref,
        ) = refs[terms:]
        step = pl.program_id(0)
        dp, core = here_ref[0], here_ref[1]

        @pl.when(step == 0)
        def _():
            normed_t[...] = jnp.transpose(normed_ref[...])
            grad_sum[...] = jnp.zeros((seq_len, width), F32)
            total = sums[0][...].astype(F32)
            for ref in sums[1:]:
                total = total + ref[...].astype(F32)
            behind = total[:, width:]
            gate_grad = behind + pltpu.roll(behind, 128 - EXPERTS, 1)
            gate = gates_ref[...]
            centre = jnp.sum(gate * gate_grad, axis=1, keepdims=True)
            logit_low = (gate * (gate_grad - centre)).astype(B16)
            logit_ref[...] = logit_low
            moe_grad = total[:, :width] + lax.dot_general(
                logit_low, tail_ref[...], NT, preferred_element_type=F32
            )
            residual = residual_ref[...]
            rate = lax.rsqrt(jnp.mean(residual * residual, axis=1, keepdims=True) + EPSILON)
            gain_ref[...] = jnp.sum(moe_grad * residual * rate, axis=0, keepdims=True)
            lifted = moe_grad * misc_ref[EXPERTS + 1 : EXPERTS + 2, :]
            inner = jnp.mean(lifted * residual, axis=1, keepdims=True)
            residual_grad = (
                grad_ref[...].astype(F32) + rate * lifted - residual * (rate * rate * rate * inner)
            )
            residual_out[...] = residual_grad
            og_ref[...] = residual_grad.astype(B16)

        og = og_ref[...]
        att_grad = lax.dot_general(og, wo_ref[...], NT, preferred_element_type=F32).astype(B16)
        query, key, value = q_ref[...], k_ref[...], v_ref[...]
        query_grads, key_grads, value_grads = [], [], []
        for j in range(4):
            lanes = slice(HD * (j // 2), HD * (j // 2 + 1))
            mine = slice(HD * j, HD * (j + 1))
            scores = lax.dot_general(
                key[:, lanes], query[:, mine], NT, preferred_element_type=F32
            )
            probs = jnp.exp(scores + bias_ref[...] - total_ref[0, j : j + 1, :])
            probs_grad = lax.dot_general(
                value[:, lanes], att_grad[:, mine], NT, preferred_element_type=F32
            )
            delta = jnp.sum(probs * probs_grad, axis=0, keepdims=True)
            score_grad = (probs * (probs_grad - delta)).astype(B16)
            query_grads.append(
                lax.dot_general(key[:, lanes], score_grad, TN, preferred_element_type=F32)
            )
            key_part = jnp.dot(score_grad, query[:, mine], preferred_element_type=F32)
            value_part = jnp.dot(probs.astype(B16), att_grad[:, mine], preferred_element_type=F32)
            if j % 2 == 0:
                key_grads.append(key_part)
                value_grads.append(value_part)
            else:
                key_grads[-1] = key_grads[-1] + key_part
                value_grads[-1] = value_grads[-1] + value_part
        cos, sin = cos_ref[...], -sin_ref[...]
        kv_grad = jnp.concatenate(
            [turn(jnp.concatenate(key_grads, axis=1), cos, sin)] + value_grads, axis=1
        ).astype(B16)
        cos, sin = cos[:tok_rows], sin[:tok_rows]
        query_grad = jnp.transpose(jnp.concatenate(query_grads, axis=0)) * scale
        query_grad = jnp.concatenate(
            [turn(query_grad[:, 128 * j : 128 * (j + 1)], cos, sin) for j in range(2)], axis=1
        ).astype(B16)

        def put(at, lanes, rows):
            keep_out[at, :, lanes] = jnp.where(core == 0, rows[0], rows[1]).astype(B16)
            give_out[at, :, lanes] = jnp.where(core == 0, rows[1], rows[0]).astype(B16)

        def give(grad, lanes):
            for m in range(4):
                put(
                    dp ^ m,
                    lanes,
                    [grad[(2 * m + c) * block : (2 * m + c + 1) * block] for c in range(2)],
                )

        give(
            jnp.dot(normed_t[:, :tok_rows], query_grad, preferred_element_type=F32),
            pl.ds(pl.multiple_of(step * 256, 256), 256),
        )
        give(
            jnp.dot(normed_t[...], kv_grad, preferred_element_type=F32),
            pl.ds(pl.multiple_of(wide + step * 256, 256), 256),
        )
        out_part = lax.dot_general(att_ref[...], og, TN, preferred_element_type=F32).astype(B16)
        put(dp ^ step, slice(output_at, output_at + width), [out_part[:block], out_part[block:]])
        kv_weights = jnp.concatenate([wk_ref[...], wv_ref[...]], axis=1)
        grad_sum[...] += lax.dot_general(kv_grad, kv_weights, NT, preferred_element_type=F32)
        grad_sum[:tok_rows, :] += lax.dot_general(
            query_grad, wq_ref[...], NT, preferred_element_type=F32
        )

        @pl.when(step == GROUPS - 1)
        def _():
            total = grad_sum[...]
            low = total.astype(B16)
            half = tok_rows // 2
            first_a_out[0] = low[tok_rows : tok_rows + half]
            first_a_out[1] = low[3 * tok_rows : 3 * tok_rows + half]
            first_b_out[0] = low[2 * tok_rows + half : 3 * tok_rows]
            first_b_out[1] = low[3 * tok_rows + half :]
            rest_a_out[0] = low[:half]
            rest_a_out[1] = low[2 * tok_rows : 2 * tok_rows + half]
            rest_b_out[0] = low[half:tok_rows]
            rest_b_out[1] = low[tok_rows + half : 2 * tok_rows]
            x = x_ref[...].astype(F32)
            lifted = x * lax.rsqrt(jnp.mean(x * x, axis=1, keepdims=True) + EPSILON)
            gain = jnp.sum(total * lifted, axis=0, keepdims=True)
            row = lax.broadcasted_iota(jnp.int32, (EXTRA, width), 0)
            gains = jnp.where(
                row == EXPERTS, gain, jnp.where(row == EXPERTS + 1, gain_ref[...], 0.0)
            )
            extra = lax.dot_general(
                moe_ref[...], logit_ref[...], TN, preferred_element_type=F32
            ) + jnp.transpose(gains)
            give(extra, slice(output_at + width, output_at + width + EXTRA))

    def fixed(*shape):
        return pl.BlockSpec(shape, lambda i, here: (0,) * len(shape))

    def columns(rows, cols, lead=0):
        return pl.BlockSpec((rows, cols), lambda i, here: (0, lead + i))

    shapes = [
        *[jax.ShapeDtypeStruct((4, block, output_at + width + EXTRA), B16)] * 2,
        *[jax.ShapeDtypeStruct((2, tok_rows // 2, width), B16)] * 4,
        jax.ShapeDtypeStruct((tok_rows, width), F32),
    ]
    keep, give, *parts, residual_grad = pl.pallas_call(
        kernel,
        out_shape=shapes,
        grid_spec=pltpu.PrefetchScalarGridSpec(
            num_scalar_prefetch=1,
            grid=(GROUPS,),
            in_specs=[
                *[fixed(tok_rows, width + 128)] * terms,
                fixed(tok_rows, width),
                fixed(tok_rows, width),
                fixed(tok_rows, 128),
                fixed(128, width),
                pl.BlockSpec(
                    (width, 128), lambda i, here: (0, (width + wide + 2 * narrow) // 128)
                ),
                pl.BlockSpec((256, width), lambda i, here: (i, 0)),
                columns(tok_rows, 256),
                fixed(tok_rows, width),
                fixed(seq_len, width),
                columns(tok_rows, 256),
                columns(seq_len, 128),
                columns(seq_len, 128),
                pl.BlockSpec((1, 8, tok_rows), lambda i, here: (i, 0, 0)),
                fixed(seq_len, width),
                columns(width, 256, width // 256),
                columns(width, 128, (width + wide) // 128),
                columns(width, 128, (width + wide + narrow) // 128),
                fixed(seq_len, tok_rows),
                fixed(seq_len, 128),
                fixed(seq_len, 128),
            ],
            out_specs=[fixed(*shape.shape) for shape in shapes],
            scratch_shapes=[
                pltpu.VMEM((width, seq_len), B16),
                pltpu.VMEM((seq_len, width), F32),
                pltpu.VMEM((tok_rows, width), B16),
                pltpu.VMEM((tok_rows, EXTRA), B16),
                pltpu.VMEM((1, width), F32),
            ],
        ),
        compiler_params=pltpu.CompilerParams(vmem_limit_bytes=VMEM_LIMIT),
        name="attention_grad",
    )(
        where_here, *moe_sums, out_grad, residual, gates, misc, dense_full, dense_full, attended,
        moe_in, normed_all, query_rot, key_rot, value_all, totals,
        x_all, dense_full, dense_full, dense_full, bias, cosine, sine,
    )
    return keep, give, tuple(parts[:2]), parts[2], parts[3], residual_grad


def core_halves(keep, got):
    _, rows, cols = keep.shape
    half = rows // 2

    def kernel(keep_ref, got_ref, first_a, first_b, rest_a, rest_b):
        def total(j, lo):
            mine = keep_ref[j, lo : lo + half, :].astype(F32)
            return (mine + got_ref[j, lo : lo + half, :].astype(F32)).astype(B16)

        first_a[0], first_a[1] = total(1, 0), total(3, 0)
        first_b[0], first_b[1] = total(2, half), total(3, half)
        rest_a[0], rest_a[1] = total(0, 0), total(2, 0)
        rest_b[0], rest_b[1] = total(0, half), total(1, half)

    step = cols // 5
    first_a, first_b, rest_a, rest_b = pl.pallas_call(
        kernel,
        grid=(5,),
        in_specs=[pl.BlockSpec((4, rows, step), lambda i: (0, 0, i))] * 2,
        out_specs=[pl.BlockSpec((2, half, step), lambda i: (0, 0, i))] * 4,
        out_shape=[jax.ShapeDtypeStruct((2, half, cols), B16)] * 4,
        compiler_params=pltpu.CompilerParams(vmem_limit_bytes=VMEM_LIMIT),
        name="core_halves",
    )(keep, got)
    return (first_a, first_b), rest_a, rest_b


def join_parts(to_x, to_y, via):
    count = len(to_x)
    shape = to_x[0].shape[1:]

    def kernel(*refs):
        for i in range(2):
            parts = refs[i * count : (i + 1) * count]
            out = refs[2 * (count + 1) + i]
            out[0] = parts[0][0]
            out[1] = plus_low(parts[1][0], refs[2 * count + i][0])
            if count == 3:
                out[2] = parts[2][0]

    steps = 4
    rows = shape[1] // steps
    part = pl.BlockSpec((1, shape[0], rows, shape[2]), lambda i: (0, 0, i, 0))
    end = via[0].shape[0] - 1
    last = pl.BlockSpec((1, shape[0], rows, shape[2]), lambda i: (end, 0, i, 0))
    return pl.pallas_call(
        kernel,
        grid=(steps,),
        in_specs=[part] * (2 * count) + [last] * 2,
        out_specs=[pl.BlockSpec((count, shape[0], rows, shape[2]), lambda i: (0, 0, i, 0))] * 2,
        out_shape=[jax.ShapeDtypeStruct((count, *shape), B16)] * 2,
        compiler_params=pltpu.CompilerParams(vmem_limit_bytes=VMEM_LIMIT),
        name="join_parts",
    )(*to_x, *to_y, *via)


def dense_outputs(core, mine, other, wide, narrow):
    rows, cols = mine.shape
    at = wide + 2 * narrow
    shapes = [(2 * rows, wide), (2 * rows, narrow), (2 * rows, narrow), (2 * rows, cols - at - EXTRA)]
    shapes += [(2 * rows, EXPERTS), (8, 2 * rows)]

    def kernel(core_ref, mine_ref, other_ref, query, key, value, output, router, gains, extra):
        for c in range(2):
            for ref, side in ((mine_ref, c), (other_ref, 1 - c)):

                @pl.when(core_ref[0] == c)
                def _():
                    lines = slice(side * rows, (side + 1) * rows)
                    query[lines, :] = ref[:, :wide].astype(F32)
                    for i in range(GROUPS):
                        lead = wide + 256 * i
                        lanes = slice(128 * i, 128 * (i + 1))
                        key[lines, lanes] = ref[:, lead : lead + 128].astype(F32)
                        value[lines, lanes] = ref[:, lead + 128 : lead + 256].astype(F32)
                    output[lines, :] = ref[:, at : cols - EXTRA].astype(F32)
                    extra[lines, :] = ref[:, cols - EXTRA :].astype(F32)
        router[...] = extra[:, :EXPERTS]
        gains[...] = jnp.transpose(extra[...])[EXPERTS : EXPERTS + 8, :]

    def fixed(shape):
        return pl.BlockSpec(shape, lambda i, core: (0, 0))

    query, key, value, output, router, gains = pl.pallas_call(
        kernel,
        out_shape=[jax.ShapeDtypeStruct(shape, F32) for shape in shapes],
        grid_spec=pltpu.PrefetchScalarGridSpec(
            num_scalar_prefetch=1,
            grid=(1,),
            in_specs=[fixed(mine.shape)] * 2,
            out_specs=[fixed(shape) for shape in shapes],
            scratch_shapes=[pltpu.VMEM((2 * rows, EXTRA), F32)],
        ),
        compiler_params=pltpu.CompilerParams(vmem_limit_bytes=VMEM_LIMIT),
        name="dense_outputs",
    )(core.astype(jnp.int32)[None], mine, other)
    return query, key, value, output, router, gains[0], gains[1]


def make_body(z_size, small_grid):
    def core_half(shard, core):
        rows = shard.shape[0] // 2
        return lax.dynamic_slice_in_dim(shard, core * rows, rows, 0)

    def dense_assemble(shard, parts, dp_index, core, *hold):
        rows = shard.shape[0] // 2
        moved = after(jnp.concatenate(parts, axis=0), *hold)
        other = swap_core(moved)
        places = [2 * dp_index]
        for which in (core, 1 - core):
            places += [2 * (dp_index ^ (j + 1)) + which for j in range(3)]
        return assemble(jnp.stack(places), shard, moved, other, rows)

    def across_z(mine, z):
        if z_size != 4:
            return lax.psum(mine.astype(F32), "z").astype(B16)
        rows = mine.shape[0] // z_size
        low = mine.astype(B16)
        steps = [2, 1, 3]
        got = []
        for k in steps:
            theirs = lax.dynamic_slice_in_dim(low, (z + k) % z_size * rows, rows, 0)
            got.append(cyclic(theirs, z_size, k))
        total = column_sum(lax.dynamic_slice_in_dim(mine, z * rows, rows, 0), got).astype(B16)
        sent = {k: cyclic(total, z_size, -k) for k in steps}
        quarters = [total] + [sent[k] for k in steps]
        places = (jnp.arange(z_size, dtype=jnp.int32) - z) % z_size
        places = jnp.where((places == 1) | (places == 2), 3 - places, places)
        return jnp.take(jnp.stack(quarters), places, axis=0).reshape(mine.shape)

    def dense_sum(grads):
        return lax.psum_scatter(
            lax.psum(grads, ("z", "core")), ("y", "x"), scatter_dimension=0, tiled=True
        )

    def body(
        layer_input,
        attn_gain,
        w_query,
        w_key,
        w_value,
        w_output,
        moe_gain,
        w_router,
        w_gate,
        w_up,
        w_down,
        routes,
        priority,
        prefix_len,
        out_grad,
    ):
        tok_rows, model_width = layer_input.shape
        dp_size = lax.axis_size("y") * lax.axis_size("x")
        dp_index = lax.axis_index("y") * lax.axis_size("x") + lax.axis_index("x")
        z = lax.axis_index("z")
        core = lax.axis_index("core")
        seq_len = tok_rows * dp_size
        top_count = routes.shape[1]
        local = w_gate.shape[0]
        capacity = 5 * tok_rows * top_count // (4 * EXPERTS)
        group_size = H // KVH
        score_scale = HD ** (-0.5)

        gains = jnp.stack([attn_gain, moe_gain], axis=1)
        rows = w_query.shape[0]
        dense_pack = jnp.concatenate(
            [w_output, w_query, w_key, w_value, w_router, gains, jnp.zeros((rows, 94), B16)], axis=1
        )
        wide = H * HD
        narrow = KVH * HD
        expert_ids = jnp.arange(EXPERTS, dtype=jnp.int32)
        hits = routes[:, :, None] == expert_ids[None, None, :]
        routed = jnp.any(hits, axis=1)
        place = jnp.where(
            routed, jnp.sum(jnp.where(hits, priority[:, :, None], 0), axis=1), jnp.int32(1 << 20)
        )
        ranks = jnp.sum((place[:, :, None] < place.T[None, :, :]).astype(F32), axis=0)
        code = pack_code(jnp.where(routed.T, ranks, -1.0).astype(B16))
        lead = ((2 * z + core) * local).astype(jnp.int32)[None]
        if small_grid:
            side = tok_rows // 2
            x_pack = jnp.concatenate([layer_input[:side], layer_input[side:]], axis=1)
            start_pack = jnp.concatenate([x_pack, core_half(dense_pack, core)], axis=1)
        else:
            grad_pieces = column_pieces(jnp.concatenate([out_grad, code], axis=0), z_size)

        query_pos = dp_index * tok_rows + jnp.arange(tok_rows, dtype=jnp.int32)
        in_float = layer_input.astype(F32)
        steps = jnp.arange(tok_rows, dtype=jnp.int32)
        eff = w_gate.shape[2]
        in_rows, mid_rows = w_gate.shape[1], w_down.shape[1]
        folds = [w_down[:, :, f * eff : (f + 1) * eff] for f in range(model_width // eff)]
        if small_grid:
            relative = dp_index ^ jnp.arange(4, dtype=jnp.int32)
            key_pos = (relative[:, None] * tok_rows + steps[None, :]).reshape(seq_len)
        else:
            relative = jnp.arange(dp_size, dtype=jnp.int32)
            key_pos = jnp.arange(seq_len, dtype=jnp.int32)
        order = jnp.concatenate([relative, lead])
        visible = (key_pos[None, :] <= query_pos[:, None]) | (key_pos[None, :] < prefix_len[0])
        if small_grid:
            start_parts = gather_near(start_pack)
            tables = (
                *turn_tables(key_pos.astype(F32)),
                jnp.where(visible.T, 0.0, MASKED_SCORE),
                jnp.pad(routed.astype(F32), ((0, 0), (0, 128 - EXPERTS))),
                [
                    jnp.concatenate([part[e] for part in (w_gate, w_up, *folds)], axis=0)
                    for e in range(local)
                ],
            )
            code = after(code, *tables[:3])
            grad_pieces = column_pieces(jnp.concatenate([out_grad, code], axis=0), z_size)
            grad_near = grad_pieces[1::2]
            start_parts, tables = after((start_parts, tables), grad_near[0])
            cosine, sine, bias, routed_wide, packs = tables
            start_parts += gather_far(after(start_parts, tables))
            dense_parts = [part[:, 2 * model_width :] for part in start_parts]
            dense_full = dense_assemble(dense_pack, dense_parts, dp_index, core, *grad_near[1:])
        else:
            dense_full = lax.all_gather(dense_pack, ("y", "x"), axis=0, tiled=True)
            full_output = dense_full[:, :model_width]
            head_full = dense_full[:, model_width:]
            full_query = head_full[:, :wide]
            full_key = head_full[:, wide : wide + narrow]
            full_value = head_full[:, wide + narrow : wide + 2 * narrow]

        if small_grid:
            halves, per = 2, local // 2
            weights = []
            near_0 = gather_near(after(packs[0], *start_parts[2:]))
            near_1 = gather_near(after(packs[1], dense_full))
        else:
            halves, per = 1, local
            pack = jnp.concatenate([w_gate, w_up, *folds], axis=1)
            every = lax.all_gather(pack, ("y", "x"), axis=0, tiled=False)
            weights = [every[j] for j in range(dp_size)]
        chunks = []
        if small_grid:
            (
                x_all, normed_all, query_rot, key_rot, value_all, attended, totals, misc, residual,
                moe_in, gates,
            ) = attention_forward(
                layer_input,
                start_parts,
                dense_full,
                bias,
                cosine,
                sine,
                routed_wide,
            )
            moe_in = after(moe_in, *near_0, *near_1, *grad_pieces)
            router_rows = misc[:EXPERTS].astype(B16)
            full_attn_gain = misc[EXPERTS]
            full_moe_gain = misc[EXPERTS + 1]
        else:
            places = query_pos.astype(F32)
            router_rows = head_full[:, wide + 2 * narrow : wide + 2 * narrow + EXPERTS].T
            full_attn_gain = head_full[:, wide + 2 * narrow + EXPERTS].astype(F32)
            full_moe_gain = head_full[:, wide + 2 * narrow + EXPERTS + 1].astype(F32)
            normed = rms_norm(in_float, full_attn_gain).astype(B16)
            query_lin = jnp.dot(normed, full_query, preferred_element_type=F32)
            key_lin = jnp.dot(normed, full_key, preferred_element_type=F32)
            value_low = jnp.dot(normed, full_value, preferred_element_type=F32).astype(B16)
            query_rot = (rotate(query_lin.reshape(tok_rows, H, HD), places) * score_scale).astype(B16)
            key_rot = rotate(key_lin.reshape(tok_rows, KVH, HD), places).astype(B16)
            key_rot = key_rot.reshape(tok_rows, narrow)
            both = jnp.concatenate([key_rot, value_low], axis=1)
            both_all = lax.all_gather(both, ("y", "x"), axis=0, tiled=True)
            key_all = both_all[:, :narrow]
            value_all = both_all[:, narrow:]

            def head_scores(head_idx):
                query_head = query_rot[:, head_idx * group_size : (head_idx + 1) * group_size, :]
                key_head = key_all[:, head_idx * HD : (head_idx + 1) * HD]
                scores = jnp.einsum("qgd,kd->gqk", query_head, key_head, preferred_element_type=F32)
                return jnp.where(visible[None, :, :], scores, MASKED_SCORE)

            mixed_heads = []
            log_totals = []
            for head_idx in range(KVH):
                scores = head_scores(head_idx)
                row_max = jnp.max(scores, axis=-1, keepdims=True)
                log_total = row_max + jnp.log(
                    jnp.sum(jnp.exp(scores - row_max), axis=-1, keepdims=True)
                )
                probs_low = jnp.exp(scores - log_total).astype(B16)
                value_head = value_all[:, head_idx * HD : (head_idx + 1) * HD]
                mixed_heads.append(
                    jnp.einsum("gqk,kd->qgd", probs_low, value_head, preferred_element_type=F32)
                )
                log_totals.append(log_total)
            attended = jnp.concatenate(mixed_heads, axis=1).reshape(tok_rows, wide).astype(B16)
            residual = in_float + jnp.dot(attended, full_output, preferred_element_type=F32)
            moe_in = rms_norm(residual, full_moe_gain).astype(B16)

        row_pieces = column_pieces(moe_in, z_size)
        grads_mine = jnp.stack(after(grad_pieces, moe_in))
        grads_other = swap_core(grads_mine)
        stage_1 = stage_2 = last_far = ()
        if small_grid:
            middle = packs[0].shape[0] // 2
            stage_1 = far_and_next(after((near_0, near_1), moe_in), packs[2])
        last = z_size // 2
        rows_near = [row_pieces[k] for k in range(z_size) if k != last]
        own_other = swap_core(after(moe_in, grads_other))
        if small_grid:
            stage_2 = far_and_next(
                [after(stage_1, *rows_near, grads_other, own_other)], packs[3]
            )
        rows_near_other = [own_other] + [
            swap_core(piece) for piece in after(rows_near[1:], *stage_1)
        ]
        (slot_grads_mine,) = dispatch_rows(
            lead, after(grads_mine, *rows_near_other), None, None, local, capacity
        )
        (slot_grads_other,) = dispatch_rows(
            lead, after(grads_other, slot_grads_mine), None, None, local, capacity
        )
        row_last = after(row_pieces[last], slot_grads_other)
        if small_grid:
            last_far = gather_far([part[middle:] for part in stage_2])
            chunks = [
                [(part, 0) for part in [packs[0], *near_0, *stage_1[::-1]]],
                [(part, 0) for part in [packs[1], *near_1]]
                + [(part, middle) for part in stage_1[::-1]],
                [(packs[2], 0)]
                + [(part, 2 * middle) for part in stage_1]
                + [(part, 0) for part in stage_2[::-1]],
                [(packs[3], 0)]
                + [(part, middle) for part in stage_2]
                + [(part, 0) for part in last_far],
            ]
        rows_mine = after([*rows_near[:last], row_last, *rows_near[last:]], *stage_2)
        rows_other = [*rows_near_other[:last], swap_core(row_last), *rows_near_other[last:]]
        slot_rows_mine, slot_gates_mine = dispatch_rows(
            lead, grads_mine, rows_mine, router_rows, local, capacity
        )
        slot_rows_other, slot_gates_other = dispatch_rows(
            lead, grads_other, after(rows_other, slot_rows_mine), router_rows, local, capacity
        )
        slot_rows_other = after(slot_rows_other, *last_far)
        ys, dxs, weight_grads, sums = [], [], [], []
        for half in range(halves):
            y, dx, grads = experts(
                order,
                half * per,
                per,
                (slot_rows_mine, slot_rows_other),
                (slot_grads_mine, slot_grads_other),
                (slot_gates_mine, slot_gates_other),
                weights,
                chunks[half * per : (half + 1) * per],
                capacity,
                in_rows,
                mid_rows,
            )
            ys.append(y)
            dxs.append(dx)
            weight_grads.append(grads)

        def grid_sum(grads, got):
            totals = []
            for half in range(2):
                own = grads[4 * half][0]
                direct, last = got[half][0], got[1 - half][1]
                totals.append(own.astype(F32) + direct.astype(F32) + last.astype(F32))
            return totals

        def second_step(grads, via, *more):
            _, x_a, y_a, _, _, x_b, y_b, _ = grads
            return cross(*join_parts((x_a, x_b, *more[:1]), (y_b, y_a, *more[1:]), via[::-1]))

        if small_grid:
            early, late = weight_grads
            via = cross(early[3], early[7])
            dxs = after(dxs, *via)
            early_got = second_step(early, via, late[3], late[7])
        dx_other = combine_rows(lead, z_size, grads_other, dxs, local, capacity)
        y_other = combine_rows(lead, z_size, grads_other, after(ys, dx_other), local, capacity)
        dx_other = after(swap_core(dx_other), y_other)
        dx_low = combine_rows(lead, 0, grads_mine, dxs, local, capacity, dx_other)
        dx_low, y_other = after((dx_low, swap_core(y_other)), dx_low[0])
        dx_pieces = column_send_last(dx_low, z_size) + column_send_some(dx_low, z_size)
        y_low = combine_rows(lead, 0, grads_mine, ys, local, capacity, y_other)
        dx_pieces = after(dx_pieces, *y_low)
        y_pieces = column_send_some(after(y_low, *dx_pieces), z_size)
        if small_grid:
            early_got = after(early_got, *dx_pieces)
            late_got = second_step(late, early_got)
        if small_grid:
            keep, give, normed_first, normed_a, normed_b, residual_grad = attention_backward(
                jnp.stack([dp_index, core]).astype(jnp.int32),
                (dx_low[0], *dx_pieces),
                out_grad,
                residual,
                gates,
                misc,
                attended,
                moe_in,
                (x_all, normed_all, query_rot, key_rot, value_all, totals),
                dense_full,
                after(bias, *early_got),
                cosine,
                sine,
            )
            late_got, y_pieces = after((late_got, y_pieces), residual_grad)
            normed_first, keep, give = after((normed_first, keep, give), *late_got, *y_pieces)
            y_pieces += column_send_last(y_low, z_size, *y_pieces)
            dense_first, dense_a, dense_b = core_halves(keep, swap_core(give))
            normed_got = grid_scatter_first(*normed_first)
            dense_got = grid_scatter_first(*after(dense_first, *normed_got))
            early_got, late_got = after((early_got, late_got), *dense_got)
            dense_low = across_z(
                jnp.concatenate(grid_scatter_second(dense_got, dense_a, dense_b), axis=0), z
            )
            (
                query_sum, key_sum, value_sum, output_sum, router_sum, attn_gain_sum, moe_gain_sum,
            ) = dense_outputs(core, dense_low, swap_core(dense_low), wide, narrow)
            y_pieces = after(y_pieces, *dense_got)
            normed_grad = jnp.concatenate(
                grid_scatter_second(normed_got, normed_a, normed_b, *dense_got), axis=0
            )
            first_value, first_pull = jax.vjp(lambda v: rms_norm(v, full_attn_gain), in_float)
            input_grad = residual_grad + first_pull(normed_grad)[0]
        else:
            y_pieces += column_send_last(y_low, z_size)
            moe_sum = column_sum(dx_low[0], dx_pieces)
            moe_in_grad = moe_sum[:, :model_width]
            gate_grad = (
                moe_sum[:, model_width : model_width + EXPERTS]
                + moe_sum[:, model_width + EXPERTS : model_width + 2 * EXPERTS]
            )
            logits = lax.dot_general(moe_in, router_rows, NT, preferred_element_type=F32)
            peak = jnp.max(jnp.where(routed, logits, MASKED_SCORE), axis=-1, keepdims=True)
            lifted = jnp.where(routed, jnp.exp(jnp.minimum(logits - peak, 0.0)), 0.0)
            gate_weights = lifted / jnp.sum(lifted, axis=-1, keepdims=True)
            grad_out = out_grad.astype(F32)
            centre = jnp.sum(gate_weights * gate_grad, axis=-1, keepdims=True)
            logit_low = (gate_weights * (gate_grad - centre)).astype(B16)
            moe_in_grad = moe_in_grad + jnp.dot(logit_low, router_rows, preferred_element_type=F32)
            norm_value, second_pull = jax.vjp(rms_norm, residual, full_moe_gain)
            resid_norm_grad, moe_gain_grad = second_pull(moe_in_grad)
            residual_grad = grad_out + resid_norm_grad
            attn_out_grad = residual_grad.astype(B16)
            router_grad = jnp.einsum("td,te->de", moe_in, logit_low, preferred_element_type=F32)
            wout_grad = jnp.einsum("tc,td->cd", attended, attn_out_grad, preferred_element_type=F32)
            attended_grad = (
                jnp.einsum("td,cd->tc", attn_out_grad, full_output, preferred_element_type=F32)
                .astype(B16)
                .reshape(tok_rows, H, HD)
            )
            query_grads = []
            key_parts = []
            value_parts = []
            for head_idx in range(KVH):
                scores = head_scores(head_idx)
                attention_probs = jnp.exp(scores - log_totals[head_idx])
                probs_low = attention_probs.astype(B16)
                grad_head = attended_grad[:, head_idx * group_size : (head_idx + 1) * group_size, :]
                query_head = query_rot[:, head_idx * group_size : (head_idx + 1) * group_size, :]
                key_head = key_all[:, head_idx * HD : (head_idx + 1) * HD]
                value_head = value_all[:, head_idx * HD : (head_idx + 1) * HD]
                probs_grad = jnp.einsum("qgd,kd->gqk", grad_head, value_head, preferred_element_type=F32)
                row_delta = jnp.sum(attention_probs * probs_grad, axis=-1, keepdims=True)
                score_grad = (attention_probs * (probs_grad - row_delta)).astype(B16)
                query_grads.append(
                    jnp.einsum("gqk,kd->qgd", score_grad, key_head, preferred_element_type=F32)
                )
                key_parts.append(
                    jnp.einsum("gqk,qgd->kd", score_grad, query_head, preferred_element_type=F32)
                )
                value_parts.append(
                    jnp.einsum("gqk,qgd->kd", probs_low, grad_head, preferred_element_type=F32)
                )
            both_part = jnp.concatenate(key_parts + value_parts, axis=1)
            both_sum = lax.psum_scatter(both_part, ("y", "x"), scatter_dimension=0, tiled=True)
            query_rot_grad = jnp.concatenate(query_grads, axis=1) * score_scale
            key_rot_grad = both_sum[:, :narrow].reshape(tok_rows, KVH, HD)
            value_grad = both_sum[:, narrow:].astype(B16)
            query_grad = rotate(query_rot_grad, -places).reshape(tok_rows, wide).astype(B16)
            key_grad = rotate(key_rot_grad, -places).reshape(tok_rows, narrow).astype(B16)
            wq_grad = jnp.einsum("td,tc->dc", normed, query_grad, preferred_element_type=F32)
            wk_grad = jnp.einsum("td,tc->dc", normed, key_grad, preferred_element_type=F32)
            wv_grad = jnp.einsum("td,tc->dc", normed, value_grad, preferred_element_type=F32)
            normed_grad = jnp.einsum("tc,dc->td", query_grad, full_query, preferred_element_type=F32)
            normed_grad = normed_grad + jnp.einsum(
                "tc,dc->td", key_grad, full_key, preferred_element_type=F32
            )
            normed_grad = normed_grad + jnp.einsum(
                "tc,dc->td", value_grad, full_value, preferred_element_type=F32
            )
            first_value, first_pull = jax.vjp(rms_norm, in_float, full_attn_gain)
            input_norm_grad, attn_gain_grad = first_pull(normed_grad)
            input_grad = residual_grad + input_norm_grad
            query_sum = dense_sum(wq_grad)
            key_sum = dense_sum(wk_grad)
            value_sum = dense_sum(wv_grad)
            output_sum = dense_sum(wout_grad)
            extra_sum = dense_sum(
                jnp.concatenate(
                    [
                        router_grad,
                        attn_gain_grad[:, None],
                        moe_gain_grad[:, None],
                        jnp.zeros((model_width, EXTRA - EXPERTS - 2), F32),
                    ],
                    axis=1,
                )
            )
            router_sum = extra_sum[:, :EXPERTS]
            attn_gain_sum = extra_sum[:, EXPERTS]
            moe_gain_sum = extra_sum[:, EXPERTS + 1]
        layer_output = (residual + column_sum(y_low[0], y_pieces)).astype(B16)
        if small_grid:
            parts = grid_sum(early, early_got) + grid_sum(late, late_got)
            pack_grad = jnp.concatenate(parts, axis=0)
        else:
            pack_grad = lax.psum_scatter(
                weight_grads[0][0].astype(F32), ("y", "x"), scatter_dimension=0, tiled=False
            )
        down = 2 * in_rows
        expert_grads = [
            pack_grad[:, :in_rows],
            pack_grad[:, in_rows:down],
            jnp.concatenate(
                [
                    pack_grad[:, down + f * mid_rows : down + (f + 1) * mid_rows]
                    for f in range(model_width // eff)
                ],
                axis=2,
            ),
        ]

        return (
            layer_output,
            input_grad,
            attn_gain_sum,
            query_sum,
            key_sum,
            value_sum,
            output_sum,
            moe_gain_sum,
            router_sum,
            expert_grads[0],
            expert_grads[1],
            expert_grads[2],
        )

    return body


def solution(mesh):
    groups = mesh.shape["expert"]
    members = mesh.shape["dp"]
    z_size = groups // 2
    side = math.isqrt(members)
    grid = Mesh(
        mesh.devices.reshape(z_size, 2, members // side, side), ("z", "core", "y", "x")
    )
    expert = ("z", "core")
    dp = ("y", "x")
    every = expert + dp
    placed = (
        P(every, None),
        P(dp),
        P(dp, None),
        P(dp, None),
        P(dp, None),
        P(dp, None),
        P(dp),
        P(dp, None),
        P(expert, dp, None),
        P(expert, dp, None),
        P(expert, dp, None),
        P(every, None),
        P(every, None),
        P(expert),
        P(every, None),
    )
    return jax.shard_map(
        make_body(z_size, members == 4 and side == 2 and EXPERTS == 4 * groups),
        mesh=grid,
        in_specs=placed,
        out_specs=(
            P(every, None),
            P(every, None),
            P(dp),
            P(dp, None),
            P(dp, None),
            P(dp, None),
            P(dp, None),
            P(dp),
            P(dp, None),
            P(expert, dp, None),
            P(expert, dp, None),
            P(expert, dp, None),
        ),
        check_vma=False,
    )
```

```python
import math

import jax
import jax.numpy as jnp
from jax import lax
from jax.experimental import pallas as pl
from jax.experimental.pallas import tpu as pltpu
from jax.sharding import Mesh
from jax.sharding import PartitionSpec as P

H = 16
KVH = 8
HD = 64
EXPERTS = 32
EPSILON = 1e-06
ROPE_BASE = 10000.0
MASKED_SCORE = -1e30
F32 = jnp.float32
B16 = jnp.bfloat16
SWAP = [(0, 1), (1, 0)]
VMEM_LIMIT = 60 * 1024 * 1024


def rms_norm(values, gain_vec):
    return (
        values * lax.rsqrt(jnp.mean(values * values, axis=-1, keepdims=True) + EPSILON) * gain_vec
    )


def rotate(vectors, places):
    half_dim = vectors.shape[-1] // 2
    frequency = jnp.exp(
        jnp.arange(half_dim, dtype=F32) * (-2.0 * math.log(ROPE_BASE) / vectors.shape[-1])
    )
    angles = places[:, None] * frequency[None, :]
    cosine = jnp.cos(angles)[:, None, :]
    sine_vals = jnp.sin(angles)[:, None, :]
    first_half = vectors[..., :half_dim]
    second = vectors[..., half_dim:]
    return jnp.concatenate(
        [first_half * cosine - second * sine_vals, second * cosine + first_half * sine_vals],
        axis=-1,
    )


def swap_core(rows):
    return lax.ppermute(rows, "core", SWAP)


def cyclic(rows, size, shift):
    return lax.ppermute(rows, "z", [(i, (i + shift) % size) for i in range(size)])


def after(value, *others):
    return lax.optimization_barrier((value, *others))[0]


def gather_near(shard):
    return [lax.ppermute(shard, "x", SWAP), lax.ppermute(shard, "y", SWAP)]


def gather_far(near):
    from_x, from_y = near
    half = from_x.shape[0] // 2
    return [lax.ppermute(from_x[:half], "y", SWAP), lax.ppermute(from_y[half:], "x", SWAP)]


def grid_gather(shard):
    near = gather_near(shard)
    return near + gather_far(near)


def cross(to_x, to_y):
    return lax.ppermute(to_x, "x", SWAP), lax.ppermute(to_y, "y", SWAP)


def far_and_next(nears, shard):
    rows = shard.shape[0]
    half = rows // 2
    return cross(
        jnp.concatenate([from_y[-half:] for _, from_y in nears] + [shard], axis=0),
        jnp.concatenate([from_x[-rows:-half] for from_x, _ in nears] + [shard], axis=0),
    )


def plus_low(a, b):
    return (a.astype(F32) + b.astype(F32)).astype(B16)


def grid_scatter_first(first_a, first_b):
    return lax.ppermute(first_a, "x", SWAP), lax.ppermute(first_b, "y", SWAP)


def grid_scatter_second(got, rest_a, rest_b, *early):
    got_a, got_b = after(got, *early)
    onward_a = (rest_a[1].astype(F32) + got_a[1].astype(F32)).astype(B16)
    onward_b = (rest_b[1].astype(F32) + got_b[1].astype(F32)).astype(B16)
    last_a = lax.ppermute(onward_a, "y", SWAP)
    last_b = lax.ppermute(onward_b, "x", SWAP)
    return (
        rest_a[0].astype(F32) + got_a[0].astype(F32) + last_a.astype(F32),
        rest_b[0].astype(F32) + got_b[0].astype(F32) + last_b.astype(F32),
    )


def row_halves(parts):
    own, to_x, to_y, diag = [parts[j] for j in range(4)]
    half = own.shape[0] // 2
    first = (
        jnp.stack([to_x[:half], diag[:half]]),
        jnp.stack([to_y[half:], diag[half:]]),
    )
    return first, (own[:half], to_y[:half]), (own[half:], to_x[half:])


def column_pieces(rows, size):
    return [rows] + [cyclic(rows, size, -k) for k in range(1, size)]


def column_send_some(low, size):
    return [cyclic(low[k], size, k) for k in range(1, size) if 2 * k != size]


def column_send_last(low, size, *hold):
    return [cyclic(after(low[size // 2], *hold), size, size // 2)]


def column_sum(own, pieces):
    return own.astype(F32) + sum(piece.astype(F32) for piece in pieces)


def assemble(places, shard, moved, other, rows):
    def kernel(places_ref, shard_ref, moved_ref, other_ref, out_ref):
        def put(i, value):
            start = pl.multiple_of(places_ref[i] * rows, rows)
            out_ref[pl.ds(start, value.shape[0]), :] = value

        put(0, shard_ref[...])
        for j in range(3):
            put(1 + j, moved_ref[j * rows : (j + 1) * rows, :])
            put(4 + j, other_ref[j * rows : (j + 1) * rows, :])

    def whole(array_shape):
        return pl.BlockSpec(array_shape, lambda i, places: (0, 0))

    out_rows, cols = 8 * rows, shard.shape[1]
    return pl.pallas_call(
        kernel,
        out_shape=jax.ShapeDtypeStruct((out_rows, cols), shard.dtype),
        grid_spec=pltpu.PrefetchScalarGridSpec(
            num_scalar_prefetch=1,
            grid=(1,),
            in_specs=[whole(a.shape) for a in (shard, moved, other)],
            out_specs=whole((out_rows, cols)),
        ),
        compiler_params=pltpu.CompilerParams(vmem_limit_bytes=VMEM_LIMIT),
        name="assemble",
    )(places, shard, moved, other)


def one_hot_slots(codes, capacity):
    slots = lax.broadcasted_iota(jnp.int32, (capacity, codes.shape[1]), 0).astype(F32)
    return [(slots == codes[e : e + 1, :]).astype(F32) for e in range(codes.shape[0])]


def row_of(table, index):
    at = lax.broadcasted_iota(jnp.int32, table.shape, 0)
    return jnp.sum(jnp.where(at == index, table, 0.0), axis=0, keepdims=True)


def pack_code(code):
    rows = code.shape[0] // 4
    wide = jnp.concatenate([code[c * rows : (c + 1) * rows] for c in range(4)], axis=1)
    return jnp.concatenate([wide, jnp.full((16 - rows, wide.shape[1]), -1.0, B16)], axis=0)


def unpack_code(block, tokens):
    rows = EXPERTS // 4
    wide = block.astype(F32)
    return jnp.concatenate(
        [wide[:rows, c * tokens : (c + 1) * tokens] for c in range(4)], axis=0
    )


def dispatch_rows(lead, packed, rows, router, local, capacity):
    pieces, packed_rows, width = packed.shape
    tokens = packed_rows - 16
    slots = local * capacity
    with_gates = router is not None

    def kernel(lead_ref, packed_ref, *rest):
        first = lead_ref[0]
        if with_gates:
            router_ref, out_ref, gate_out, rows_ref = rest[pieces:]
            for p in range(pieces):

                @pl.when(pl.program_id(0) == p)
                def _():
                    rows_ref[...] = rest[p][...]

            table = unpack_code(packed_ref[0], tokens)
            source = rows_ref[...]
        else:
            (out_ref,) = rest
            table = unpack_code(packed_ref[0, tokens:, :], tokens)
            source = packed_ref[0, :tokens, :]
        codes = jnp.concatenate([row_of(table, first + e) for e in range(local)], axis=0)
        picks = one_hot_slots(codes, capacity)
        select = jnp.concatenate([p.astype(B16) for p in picks], axis=0)
        out_ref[0] = jnp.dot(select, source, preferred_element_type=F32).astype(B16)
        if with_gates:
            logits = lax.dot_general(
                router_ref[...], source, (((1,), (1,)), ((), ())), preferred_element_type=F32
            )
            routed = table >= 0.0
            peak = jnp.max(jnp.where(routed, logits, MASKED_SCORE), axis=0, keepdims=True)
            lifted = jnp.where(routed, jnp.exp(jnp.minimum(logits - peak, 0.0)), 0.0)
            gates = lifted / jnp.sum(lifted, axis=0, keepdims=True)
            for e in range(local):
                gate_row = row_of(gates, first + e)
                column = jnp.sum(picks[e] * gate_row, axis=1, keepdims=True)
                gate_out[0, e * capacity : (e + 1) * capacity, :] = jnp.broadcast_to(
                    column, (capacity, 128)
                )

    out_specs = [pl.BlockSpec((1, slots, width), lambda p, lead: (p, 0, 0))]
    out_shape = [jax.ShapeDtypeStruct((pieces, slots, width), B16)]
    args = [packed]
    if with_gates:
        in_specs = [
            pl.BlockSpec((1, 16, width), lambda p, lead: (p, tokens // 16, 0)),
            *[pl.BlockSpec((tokens, width), lambda p, lead: (0, 0)) for _ in rows],
            pl.BlockSpec((EXPERTS, width), lambda p, lead: (0, 0)),
        ]
        out_specs.append(pl.BlockSpec((1, slots, 128), lambda p, lead: (p, 0, 0)))
        out_shape.append(jax.ShapeDtypeStruct((pieces, slots, 128), F32))
        args += [*rows, router]
    else:
        in_specs = [pl.BlockSpec((1, packed_rows, width), lambda p, lead: (p, 0, 0))]
    return pl.pallas_call(
        kernel,
        out_shape=out_shape,
        grid_spec=pltpu.PrefetchScalarGridSpec(
            num_scalar_prefetch=1,
            grid=(pieces,),
            in_specs=in_specs,
            out_specs=out_specs,
            scratch_shapes=[pltpu.VMEM((tokens, width), B16)] if with_gates else [],
        ),
        compiler_params=pltpu.CompilerParams(vmem_limit_bytes=VMEM_LIMIT),
        name="dispatch",
    )(lead, *args)


def combine_rows(lead, first, packed, slot_rows, local, capacity, addend=None):
    pieces, packed_rows, code_width = packed.shape
    tokens = packed_rows - 16
    halves = len(slot_rows)
    slots, width = slot_rows[0].shape[1:]
    per = local // halves

    def kernel(lead_ref, code_ref, *rest):
        table = unpack_code(code_ref[0], tokens)
        here = lead_ref[0]
        codes = jnp.concatenate([row_of(table, here + e) for e in range(local)], axis=0)
        picks = one_hot_slots(codes, capacity)
        total = None
        for h in range(halves):
            select = jnp.concatenate(
                [p.astype(B16) for p in picks[h * per : (h + 1) * per]], axis=0
            )
            part = lax.dot_general(
                select, rest[h][0], (((0,), (0,)), ((), ())), preferred_element_type=F32
            )
            total = part if total is None else total + part
        if addend is None:
            rest[halves][0] = total.astype(B16)
        else:
            low = (total + rest[halves][0].astype(F32)).astype(B16)
            for p in range(pieces):

                @pl.when(pl.program_id(0) == p)
                def _():
                    rest[halves + 1 + p][...] = low

    in_specs = [pl.BlockSpec((1, 16, code_width), lambda p, lead: (p, tokens // 16, 0))]
    in_specs += [
        pl.BlockSpec((1, slots, width), lambda p, lead: (p + first, 0, 0)) for _ in range(halves)
    ]
    added = [] if addend is None else [addend]
    in_specs += [pl.BlockSpec((1, tokens, width), lambda p, lead: (p, 0, 0)) for _ in added]
    if addend is None:
        out_shape = jax.ShapeDtypeStruct((pieces, tokens, width), B16)
        out_specs = pl.BlockSpec((1, tokens, width), lambda p, lead: (p, 0, 0))
    else:
        out_shape = [jax.ShapeDtypeStruct((tokens, width), B16)] * pieces
        out_specs = [pl.BlockSpec((tokens, width), lambda p, lead: (0, 0))] * pieces
    return pl.pallas_call(
        kernel,
        out_shape=out_shape,
        grid_spec=pltpu.PrefetchScalarGridSpec(
            num_scalar_prefetch=1,
            grid=(pieces,),
            in_specs=in_specs,
            out_specs=out_specs,
        ),
        compiler_params=pltpu.CompilerParams(vmem_limit_bytes=VMEM_LIMIT),
        name="combine",
    )(lead, packed, *slot_rows, *added)


def experts(order, start, count, rows, grads, gates, weights, chunks, capacity, in_rows, mid_rows):
    half, _, width = rows[0].shape
    pieces = 2 * half
    split = bool(chunks)
    n = 4 if split else len(weights)
    extra = [array for chunk in chunks for array, _ in chunk]
    given = len(weights) + len(extra)
    pack_rows, eff = chunks[0][0][0].shape if split else weights[0].shape[1:]
    folds = width // eff
    total_rows = pieces * capacity
    first_half = count // 2
    large = total_rows > 1000

    def kernel(order_ref, *refs):
        rows_a, rows_b, grads_a, grads_b, gates_a, gates_b = refs[:6]
        pack = refs[6 : 6 + given]
        y_out, dx_out = refs[6 + given : 8 + given]
        outs = refs[8 + given : -6]
        full_g, full_u, full_d, grad_g, grad_u, grad_d = refs[-6:]

        def at_in(j):
            return pl.ds(pl.multiple_of(order_ref[j] * in_rows, in_rows), in_rows)

        def at_mid(j):
            return pl.ds(pl.multiple_of(order_ref[j] * mid_rows, mid_rows), mid_rows)

        def load(j, take):
            full_g[at_in(j), :] = take(0, in_rows)
            full_u[at_in(j), :] = take(in_rows, 2 * in_rows)
            for f in range(folds):
                full_d[at_mid(j), f * eff : (f + 1) * eff] = take(
                    2 * in_rows + f * mid_rows, 2 * in_rows + (f + 1) * mid_rows
                )

        def rows_from(ref, offset):
            return lambda lo, hi: ref[offset + lo : offset + hi, :]

        def two_halves(a, b):
            middle = pack_rows // 2

            def take(lo, hi):
                if hi <= middle:
                    return a(lo, hi)
                if lo >= middle:
                    return b(lo - middle, hi - middle)
                return jnp.concatenate([a(lo, middle), b(0, hi - middle)], axis=0)

            return take

        for j in range(len(weights)):
            load(j, lambda lo, hi, ref=pack[j]: ref[0, lo:hi])
        for c in range(len(chunks)):
            own, from_x, from_y, diag_a, diag_b = [
                rows_from(pack[5 * c + i], chunks[c][i][1]) for i in range(5)
            ]

            @pl.when(pl.program_id(0) == c)
            def _():
                load(0, own)
                load(1, from_x)
                load(2, from_y)
                load(3, two_halves(diag_a, diag_b))

        def joined(a, b, w):
            return jnp.concatenate(
                [
                    a[...].reshape(half * capacity, w),
                    b[...].reshape(half * capacity, w),
                ],
                axis=0,
            )

        x = joined(rows_a, rows_b, width)
        g = joined(grads_a, grads_b, width)
        gate = joined(gates_a, gates_b, 128)[:, 0:1]
        nt = (((1,), (1,)), ((), ()))
        tn = (((0,), (0,)), ((), ()))
        gate_proj = jnp.dot(x, full_g[...], preferred_element_type=F32)
        up_proj = jnp.dot(x, full_u[...], preferred_element_type=F32)
        down_grad = lax.dot_general(g, full_d[...], nt, preferred_element_type=F32)
        sigmoid = 1.0 / (1.0 + jnp.exp(-gate_proj))
        silu = gate_proj * sigmoid
        activated = silu * up_proj
        slot_grad = jnp.sum(activated * down_grad, axis=1, keepdims=True)
        here = order_ref[n] + start + pl.program_id(0)
        lane = lax.broadcasted_iota(jnp.int32, (total_rows, 128), 1)
        high = slot_grad.astype(B16).astype(F32)
        tail = jnp.where(lane == here, high, jnp.where(lane == here + EXPERTS, slot_grad - high, 0.0))
        dx_out[:, :, width:] = tail.astype(B16).reshape(pieces, capacity, 128)
        scaled = (gate * activated).astype(B16)
        act_grad = gate * down_grad
        gate_grad = (act_grad * up_proj * (sigmoid * (1.0 + gate_proj * (1.0 - sigmoid)))).astype(
            B16
        )
        up_grad = (act_grad * silu).astype(B16)
        y = jnp.dot(scaled, full_d[...], preferred_element_type=F32)
        y_out[...] = y.astype(B16).reshape(pieces, capacity, width)
        dx = lax.dot_general(gate_grad, full_g[...], nt, preferred_element_type=F32)
        dx = dx + lax.dot_general(up_grad, full_u[...], nt, preferred_element_type=F32)
        dx_out[:, :, :width] = dx.astype(B16).reshape(pieces, capacity, width)
        grad_g[...] = lax.dot_general(x, gate_grad, tn, preferred_element_type=F32).astype(B16)
        grad_u[...] = lax.dot_general(x, up_grad, tn, preferred_element_type=F32).astype(B16)
        grad_d[...] = lax.dot_general(scaled, g, tn, preferred_element_type=F32).astype(B16)

        def give(ref, slot, j):
            ref[slot, 0, :in_rows] = grad_g[at_in(j), :]
            ref[slot, 0, in_rows : 2 * in_rows] = grad_u[at_in(j), :]
            for f in range(folds):
                ref[slot, 0, 2 * in_rows + f * mid_rows : 2 * in_rows + (f + 1) * mid_rows] = grad_d[
                    at_mid(j), f * eff : (f + 1) * eff
                ]

        if split:

            @pl.when(pl.program_id(0) < first_half)
            def _():
                for j in range(4):
                    give(outs[j], 0, j)

            @pl.when(pl.program_id(0) >= first_half)
            def _():
                for j in range(4):
                    give(outs[4 + j], 0, j)
        else:
            for j in range(n):
                give(outs[0], j, j)

    def single():
        return dict(pipeline_mode=pl.Buffered(1)) if large else {}

    def rows_spec(w):
        return pl.BlockSpec((half, capacity, w), lambda e, o: (0, e + start, 0), **single())

    in_specs = [rows_spec(width)] * 4 + [rows_spec(128)] * 2
    for _ in weights:
        in_specs.append(pl.BlockSpec((1, pack_rows, eff), lambda e, o: (e + start, 0, 0)))
    for part in extra:
        in_specs.append(pl.BlockSpec(part.shape, lambda e, o: (0, 0)))
    slots = count * capacity
    out_specs = [
        pl.BlockSpec((pieces, capacity, w), lambda e, o: (0, e, 0), **single())
        for w in (width, width + 128)
    ]
    out_shape = [
        jax.ShapeDtypeStruct((pieces, slots, width), B16),
        jax.ShapeDtypeStruct((pieces, slots, width + 128), B16),
    ]
    if split:
        for at in (
            lambda e, o: (0, jnp.minimum(e, first_half - 1), 0, 0),
            lambda e, o: (0, jnp.maximum(e - first_half, 0), 0, 0),
        ):
            for _ in range(4):
                out_specs.append(pl.BlockSpec((1, 1, pack_rows, eff), at))
                out_shape.append(jax.ShapeDtypeStruct((1, first_half, pack_rows, eff), B16))
    else:
        out_specs.append(pl.BlockSpec((n, 1, pack_rows, eff), lambda e, o: (0, e, 0, 0)))
        out_shape.append(jax.ShapeDtypeStruct((n, count, pack_rows, eff), B16))
    results = pl.pallas_call(
        kernel,
        out_shape=out_shape,
        grid_spec=pltpu.PrefetchScalarGridSpec(
            num_scalar_prefetch=1,
            grid=(count,),
            in_specs=in_specs,
            out_specs=out_specs,
            scratch_shapes=[
                pltpu.VMEM((n * in_rows, eff), B16),
                pltpu.VMEM((n * in_rows, eff), B16),
                pltpu.VMEM((n * mid_rows, width), B16),
                pltpu.VMEM((n * in_rows, eff), B16),
                pltpu.VMEM((n * in_rows, eff), B16),
                pltpu.VMEM((n * mid_rows, width), B16),
            ],
        ),
        compiler_params=pltpu.CompilerParams(vmem_limit_bytes=VMEM_LIMIT),
        name="experts",
    )(order, *rows, *grads, *gates, *weights, *extra)
    return results[0], results[1], results[2:]


NT = (((1,), (1,)), ((), ()))
TN = (((0,), (0,)), ((), ()))
GROUPS = KVH // 2
EXTRA = 128


def turn(vectors, cosine, sine):
    lane = lax.broadcasted_iota(jnp.int32, vectors.shape, 1)
    ahead = pltpu.roll(vectors, 2 * HD - HD // 2, 1)
    behind = pltpu.roll(vectors, HD // 2, 1)
    return vectors * cosine + jnp.where(lane % HD < HD // 2, ahead, behind) * sine


def turn_tables(places):
    lane = jnp.arange(2 * HD, dtype=jnp.int32)
    frequency = jnp.exp(
        (lane % (HD // 2)).astype(F32) * (-2.0 * math.log(ROPE_BASE) / HD)
    )
    angles = places[:, None] * frequency[None, :]
    sign = jnp.where(lane % HD < HD // 2, -1.0, 1.0)
    return jnp.cos(angles), jnp.sin(angles) * sign[None, :]


def attention_forward(x_own, x_parts, dense_full, bias, cosine, sine, routed):
    tok_rows, width = x_own.shape
    seq_len = 4 * tok_rows
    scale = HD ** (-0.5)
    wide, narrow = H * HD, KVH * HD

    def kernel(
        own_ref, xa_ref, xb_ref, ya_ref, yb_ref, da_ref, db_ref, ea_ref, eb_ref,
        tail_ref, wo_ref, wq_ref, wk_ref, wv_ref, bias_ref, cos_ref, sin_ref, routed_ref,
        x_ref, normed_ref, q_out, k_out, v_out, att_out, total_out, misc_out, residual_out, moe_out,
        gates_out,
    ):
        step = pl.program_id(0)

        @pl.when(step == 0)
        def _():
            rows = jnp.transpose(tail_ref[...].astype(F32))
            misc_out[...] = rows
            at = 0
            for ref in (own_ref, xa_ref, xb_ref, ya_ref, yb_ref, da_ref, ea_ref, db_ref, eb_ref):
                x_ref[at : at + ref.shape[0], :] = ref[...]
                at += ref.shape[0]
            x = x_ref[...].astype(F32)
            scaled = x * lax.rsqrt(jnp.mean(x * x, axis=1, keepdims=True) + EPSILON)
            normed_ref[...] = (scaled * rows[EXPERTS : EXPERTS + 1, :]).astype(B16)
            residual_out[...] = x[:tok_rows]

        normed = normed_ref[...]
        cos, sin = cos_ref[...], sin_ref[...]
        key = turn(jnp.dot(normed, wk_ref[...], preferred_element_type=F32), cos, sin).astype(B16)
        value = jnp.dot(normed, wv_ref[...], preferred_element_type=F32).astype(B16)
        query = jnp.dot(normed[:tok_rows], wq_ref[...], preferred_element_type=F32)
        cos, sin = cos[:tok_rows], sin[:tok_rows]
        query = jnp.concatenate(
            [turn(query[:, 128 * j : 128 * (j + 1)], cos, sin) for j in range(2)], axis=1
        )
        query = (query * scale).astype(B16)
        k_out[...] = key
        v_out[...] = value
        q_out[...] = query
        mixed, totals = [], []
        for j in range(4):
            lanes = slice(HD * (j // 2), HD * (j // 2 + 1))
            scores = lax.dot_general(
                key[:, lanes], query[:, HD * j : HD * (j + 1)], NT, preferred_element_type=F32
            )
            scores = scores + bias_ref[...]
            peak = jnp.max(scores, axis=0, keepdims=True)
            probs = jnp.exp(scores - peak)
            total = jnp.sum(probs, axis=0, keepdims=True)
            out = lax.dot_general(
                value[:, lanes], probs.astype(B16), TN, preferred_element_type=F32
            )
            mixed.append(out / total)
            totals.append(peak + jnp.log(total))
        attended = jnp.transpose(jnp.concatenate(mixed, axis=0)).astype(B16)
        att_out[...] = attended
        total_out[0] = jnp.concatenate(totals + totals, axis=0)
        residual_out[...] += jnp.dot(attended, wo_ref[...], preferred_element_type=F32)

        @pl.when(step == GROUPS - 1)
        def _():
            total = residual_out[...]
            scaled = total * lax.rsqrt(jnp.mean(total * total, axis=1, keepdims=True) + EPSILON)
            moe_in = (scaled * misc_out[EXPERTS + 1 : EXPERTS + 2, :]).astype(B16)
            moe_out[...] = moe_in
            logits = jnp.dot(moe_in, tail_ref[...], preferred_element_type=F32)
            here = routed_ref[...] > 0.0
            peak = jnp.max(jnp.where(here, logits, MASKED_SCORE), axis=1, keepdims=True)
            lifted = jnp.where(here, jnp.exp(jnp.minimum(logits - peak, 0.0)), 0.0)
            gates_out[...] = lifted / jnp.sum(lifted, axis=1, keepdims=True)

    def fixed(*block):
        return pl.BlockSpec(block, lambda i: (0,) * len(block))

    def columns(rows, cols, lead=0):
        return pl.BlockSpec((rows, cols), lambda i: (0, lead + i))

    return pl.pallas_call(
        kernel,
        grid=(GROUPS,),
        in_specs=[
            fixed(tok_rows, width),
            *[
                pl.BlockSpec((part.shape[0], width), lambda i, c=c: (0, c))
                for part in x_parts
                for c in range(2)
            ],
            pl.BlockSpec((width, 128), lambda i: (0, (width + wide + 2 * narrow) // 128)),
            pl.BlockSpec((256, width), lambda i: (i, 0)),
            columns(width, 256, width // 256),
            columns(width, 128, (width + wide) // 128),
            columns(width, 128, (width + wide + narrow) // 128),
            fixed(seq_len, tok_rows),
            fixed(seq_len, 128),
            fixed(seq_len, 128),
            fixed(tok_rows, 128),
        ],
        out_specs=[
            fixed(seq_len, width),
            fixed(seq_len, width),
            columns(tok_rows, 256),
            columns(seq_len, 128),
            columns(seq_len, 128),
            columns(tok_rows, 256),
            pl.BlockSpec((1, 8, tok_rows), lambda i: (i, 0, 0)),
            fixed(128, width),
            fixed(tok_rows, width),
            fixed(tok_rows, width),
            fixed(tok_rows, 128),
        ],
        out_shape=[
            jax.ShapeDtypeStruct((seq_len, width), B16),
            jax.ShapeDtypeStruct((seq_len, width), B16),
            jax.ShapeDtypeStruct((tok_rows, wide), B16),
            jax.ShapeDtypeStruct((seq_len, narrow), B16),
            jax.ShapeDtypeStruct((seq_len, narrow), B16),
            jax.ShapeDtypeStruct((tok_rows, wide), B16),
            jax.ShapeDtypeStruct((GROUPS, 8, tok_rows), F32),
            jax.ShapeDtypeStruct((128, width), F32),
            jax.ShapeDtypeStruct((tok_rows, width), F32),
            jax.ShapeDtypeStruct((tok_rows, width), B16),
            jax.ShapeDtypeStruct((tok_rows, 128), F32),
        ],
        compiler_params=pltpu.CompilerParams(vmem_limit_bytes=VMEM_LIMIT),
        name="attention",
    )(
        x_own, *[part for part in x_parts for _ in range(2)], *[dense_full] * 5,
        bias, cosine, sine, routed,
    )


def attention_backward(
    where_here, moe_sums, out_grad, residual, gates, misc, attended, moe_in, saved,
    dense_full, bias, cosine, sine,
):
    x_all, normed_all, query_rot, key_rot, value_all, totals = saved
    terms = len(moe_sums)
    seq_len, width = x_all.shape
    tok_rows = query_rot.shape[0]
    scale = HD ** (-0.5)
    wide, narrow = H * HD, KVH * HD
    block = width // 8
    output_at = wide + 2 * narrow

    def kernel(here_ref, *refs):
        sums = refs[:terms]
        (
            grad_ref, residual_ref, gates_ref, misc_ref, tail_ref, wo_ref, att_ref, moe_ref,
            normed_ref, q_ref, k_ref, v_ref, total_ref,
            x_ref, wq_ref, wk_ref, wv_ref, bias_ref, cos_ref, sin_ref,
            keep_out, give_out, first_a_out, first_b_out, rest_a_out, rest_b_out, residual_out,
            normed_t, grad_sum, og_ref, logit_ref, gain_ref,
        ) = refs[terms:]
        step = pl.program_id(0)
        dp, core = here_ref[0], here_ref[1]

        @pl.when(step == 0)
        def _():
            normed_t[...] = jnp.transpose(normed_ref[...])
            grad_sum[...] = jnp.zeros((seq_len, width), F32)
            total = sums[0][...].astype(F32)
            for ref in sums[1:]:
                total = total + ref[...].astype(F32)
            behind = total[:, width:]
            gate_grad = behind + pltpu.roll(behind, 128 - EXPERTS, 1)
            gate = gates_ref[...]
            centre = jnp.sum(gate * gate_grad, axis=1, keepdims=True)
            logit_low = (gate * (gate_grad - centre)).astype(B16)
            logit_ref[...] = logit_low
            moe_grad = total[:, :width] + lax.dot_general(
                logit_low, tail_ref[...], NT, preferred_element_type=F32
            )
            residual = residual_ref[...]
            rate = lax.rsqrt(jnp.mean(residual * residual, axis=1, keepdims=True) + EPSILON)
            gain_ref[...] = jnp.sum(moe_grad * residual * rate, axis=0, keepdims=True)
            lifted = moe_grad * misc_ref[EXPERTS + 1 : EXPERTS + 2, :]
            inner = jnp.mean(lifted * residual, axis=1, keepdims=True)
            residual_grad = (
                grad_ref[...].astype(F32) + rate * lifted - residual * (rate * rate * rate * inner)
            )
            residual_out[...] = residual_grad
            og_ref[...] = residual_grad.astype(B16)

        og = og_ref[...]
        att_grad = lax.dot_general(og, wo_ref[...], NT, preferred_element_type=F32).astype(B16)
        query, key, value = q_ref[...], k_ref[...], v_ref[...]
        query_grads, key_grads, value_grads = [], [], []
        for j in range(4):
            lanes = slice(HD * (j // 2), HD * (j // 2 + 1))
            mine = slice(HD * j, HD * (j + 1))
            scores = lax.dot_general(
                key[:, lanes], query[:, mine], NT, preferred_element_type=F32
            )
            probs = jnp.exp(scores + bias_ref[...] - total_ref[0, j : j + 1, :])
            probs_grad = lax.dot_general(
                value[:, lanes], att_grad[:, mine], NT, preferred_element_type=F32
            )
            delta = jnp.sum(probs * probs_grad, axis=0, keepdims=True)
            score_grad = (probs * (probs_grad - delta)).astype(B16)
            query_grads.append(
                lax.dot_general(key[:, lanes], score_grad, TN, preferred_element_type=F32)
            )
            key_part = jnp.dot(score_grad, query[:, mine], preferred_element_type=F32)
            value_part = jnp.dot(probs.astype(B16), att_grad[:, mine], preferred_element_type=F32)
            if j % 2 == 0:
                key_grads.append(key_part)
                value_grads.append(value_part)
            else:
                key_grads[-1] = key_grads[-1] + key_part
                value_grads[-1] = value_grads[-1] + value_part
        cos, sin = cos_ref[...], -sin_ref[...]
        kv_grad = jnp.concatenate(
            [turn(jnp.concatenate(key_grads, axis=1), cos, sin)] + value_grads, axis=1
        ).astype(B16)
        cos, sin = cos[:tok_rows], sin[:tok_rows]
        query_grad = jnp.transpose(jnp.concatenate(query_grads, axis=0)) * scale
        query_grad = jnp.concatenate(
            [turn(query_grad[:, 128 * j : 128 * (j + 1)], cos, sin) for j in range(2)], axis=1
        ).astype(B16)

        def put(at, lanes, rows):
            keep_out[at, :, lanes] = jnp.where(core == 0, rows[0], rows[1]).astype(B16)
            give_out[at, :, lanes] = jnp.where(core == 0, rows[1], rows[0]).astype(B16)

        def give(grad, lanes):
            for m in range(4):
                put(
                    dp ^ m,
                    lanes,
                    [grad[(2 * m + c) * block : (2 * m + c + 1) * block] for c in range(2)],
                )

        give(
            jnp.dot(normed_t[:, :tok_rows], query_grad, preferred_element_type=F32),
            pl.ds(pl.multiple_of(step * 256, 256), 256),
        )
        give(
            jnp.dot(normed_t[...], kv_grad, preferred_element_type=F32),
            pl.ds(pl.multiple_of(wide + step * 256, 256), 256),
        )
        out_part = lax.dot_general(att_ref[...], og, TN, preferred_element_type=F32).astype(B16)
        put(dp ^ step, slice(output_at, output_at + width), [out_part[:block], out_part[block:]])
        kv_weights = jnp.concatenate([wk_ref[...], wv_ref[...]], axis=1)
        grad_sum[...] += lax.dot_general(kv_grad, kv_weights, NT, preferred_element_type=F32)
        grad_sum[:tok_rows, :] += lax.dot_general(
            query_grad, wq_ref[...], NT, preferred_element_type=F32
        )

        @pl.when(step == GROUPS - 1)
        def _():
            total = grad_sum[...]
            low = total.astype(B16)
            half = tok_rows // 2
            first_a_out[0] = low[tok_rows : tok_rows + half]
            first_a_out[1] = low[3 * tok_rows : 3 * tok_rows + half]
            first_b_out[0] = low[2 * tok_rows + half : 3 * tok_rows]
            first_b_out[1] = low[3 * tok_rows + half :]
            rest_a_out[0] = low[:half]
            rest_a_out[1] = low[2 * tok_rows : 2 * tok_rows + half]
            rest_b_out[0] = low[half:tok_rows]
            rest_b_out[1] = low[tok_rows + half : 2 * tok_rows]
            x = x_ref[...].astype(F32)
            lifted = x * lax.rsqrt(jnp.mean(x * x, axis=1, keepdims=True) + EPSILON)
            gain = jnp.sum(total * lifted, axis=0, keepdims=True)
            row = lax.broadcasted_iota(jnp.int32, (EXTRA, width), 0)
            gains = jnp.where(
                row == EXPERTS, gain, jnp.where(row == EXPERTS + 1, gain_ref[...], 0.0)
            )
            extra = lax.dot_general(
                moe_ref[...], logit_ref[...], TN, preferred_element_type=F32
            ) + jnp.transpose(gains)
            give(extra, slice(output_at + width, output_at + width + EXTRA))

    def fixed(*shape):
        return pl.BlockSpec(shape, lambda i, here: (0,) * len(shape))

    def columns(rows, cols, lead=0):
        return pl.BlockSpec((rows, cols), lambda i, here: (0, lead + i))

    shapes = [
        *[jax.ShapeDtypeStruct((4, block, output_at + width + EXTRA), B16)] * 2,
        *[jax.ShapeDtypeStruct((2, tok_rows // 2, width), B16)] * 4,
        jax.ShapeDtypeStruct((tok_rows, width), F32),
    ]
    keep, give, *parts, residual_grad = pl.pallas_call(
        kernel,
        out_shape=shapes,
        grid_spec=pltpu.PrefetchScalarGridSpec(
            num_scalar_prefetch=1,
            grid=(GROUPS,),
            in_specs=[
                *[fixed(tok_rows, width + 128)] * terms,
                fixed(tok_rows, width),
                fixed(tok_rows, width),
                fixed(tok_rows, 128),
                fixed(128, width),
                pl.BlockSpec(
                    (width, 128), lambda i, here: (0, (width + wide + 2 * narrow) // 128)
                ),
                pl.BlockSpec((256, width), lambda i, here: (i, 0)),
                columns(tok_rows, 256),
                fixed(tok_rows, width),
                fixed(seq_len, width),
                columns(tok_rows, 256),
                columns(seq_len, 128),
                columns(seq_len, 128),
                pl.BlockSpec((1, 8, tok_rows), lambda i, here: (i, 0, 0)),
                fixed(seq_len, width),
                columns(width, 256, width // 256),
                columns(width, 128, (width + wide) // 128),
                columns(width, 128, (width + wide + narrow) // 128),
                fixed(seq_len, tok_rows),
                fixed(seq_len, 128),
                fixed(seq_len, 128),
            ],
            out_specs=[fixed(*shape.shape) for shape in shapes],
            scratch_shapes=[
                pltpu.VMEM((width, seq_len), B16),
                pltpu.VMEM((seq_len, width), F32),
                pltpu.VMEM((tok_rows, width), B16),
                pltpu.VMEM((tok_rows, EXTRA), B16),
                pltpu.VMEM((1, width), F32),
            ],
        ),
        compiler_params=pltpu.CompilerParams(vmem_limit_bytes=VMEM_LIMIT),
        name="attention_grad",
    )(
        where_here, *moe_sums, out_grad, residual, gates, misc, dense_full, dense_full, attended,
        moe_in, normed_all, query_rot, key_rot, value_all, totals,
        x_all, dense_full, dense_full, dense_full, bias, cosine, sine,
    )
    return keep, give, tuple(parts[:2]), parts[2], parts[3], residual_grad


def core_halves(keep, got):
    _, rows, cols = keep.shape
    half = rows // 2

    def kernel(keep_ref, got_ref, first_a, first_b, rest_a, rest_b):
        def total(j, lo):
            mine = keep_ref[j, lo : lo + half, :].astype(F32)
            return (mine + got_ref[j, lo : lo + half, :].astype(F32)).astype(B16)

        first_a[0], first_a[1] = total(1, 0), total(3, 0)
        first_b[0], first_b[1] = total(2, half), total(3, half)
        rest_a[0], rest_a[1] = total(0, 0), total(2, 0)
        rest_b[0], rest_b[1] = total(0, half), total(1, half)

    step = cols // 5
    first_a, first_b, rest_a, rest_b = pl.pallas_call(
        kernel,
        grid=(5,),
        in_specs=[pl.BlockSpec((4, rows, step), lambda i: (0, 0, i))] * 2,
        out_specs=[pl.BlockSpec((2, half, step), lambda i: (0, 0, i))] * 4,
        out_shape=[jax.ShapeDtypeStruct((2, half, cols), B16)] * 4,
        compiler_params=pltpu.CompilerParams(vmem_limit_bytes=VMEM_LIMIT),
        name="core_halves",
    )(keep, got)
    return (first_a, first_b), rest_a, rest_b


def join_parts(to_x, to_y, via):
    count = len(to_x)
    shape = to_x[0].shape[1:]

    def kernel(*refs):
        for i in range(2):
            parts = refs[i * count : (i + 1) * count]
            out = refs[2 * (count + 1) + i]
            out[0] = parts[0][0]
            out[1] = plus_low(parts[1][0], refs[2 * count + i][0])
            if count == 3:
                out[2] = parts[2][0]

    steps = 4
    rows = shape[1] // steps
    part = pl.BlockSpec((1, shape[0], rows, shape[2]), lambda i: (0, 0, i, 0))
    end = via[0].shape[0] - 1
    last = pl.BlockSpec((1, shape[0], rows, shape[2]), lambda i: (end, 0, i, 0))
    return pl.pallas_call(
        kernel,
        grid=(steps,),
        in_specs=[part] * (2 * count) + [last] * 2,
        out_specs=[pl.BlockSpec((count, shape[0], rows, shape[2]), lambda i: (0, 0, i, 0))] * 2,
        out_shape=[jax.ShapeDtypeStruct((count, *shape), B16)] * 2,
        compiler_params=pltpu.CompilerParams(vmem_limit_bytes=VMEM_LIMIT),
        name="join_parts",
    )(*to_x, *to_y, *via)


def dense_outputs(core, mine, other, wide, narrow):
    rows, cols = mine.shape
    at = wide + 2 * narrow
    shapes = [(2 * rows, wide), (2 * rows, narrow), (2 * rows, narrow), (2 * rows, cols - at - EXTRA)]
    shapes += [(2 * rows, EXPERTS), (8, 2 * rows)]

    def kernel(core_ref, mine_ref, other_ref, query, key, value, output, router, gains, extra):
        for c in range(2):
            for ref, side in ((mine_ref, c), (other_ref, 1 - c)):

                @pl.when(core_ref[0] == c)
                def _():
                    lines = slice(side * rows, (side + 1) * rows)
                    query[lines, :] = ref[:, :wide].astype(F32)
                    for i in range(GROUPS):
                        lead = wide + 256 * i
                        lanes = slice(128 * i, 128 * (i + 1))
                        key[lines, lanes] = ref[:, lead : lead + 128].astype(F32)
                        value[lines, lanes] = ref[:, lead + 128 : lead + 256].astype(F32)
                    output[lines, :] = ref[:, at : cols - EXTRA].astype(F32)
                    extra[lines, :] = ref[:, cols - EXTRA :].astype(F32)
        router[...] = extra[:, :EXPERTS]
        gains[...] = jnp.transpose(extra[...])[EXPERTS : EXPERTS + 8, :]

    def fixed(shape):
        return pl.BlockSpec(shape, lambda i, core: (0, 0))

    query, key, value, output, router, gains = pl.pallas_call(
        kernel,
        out_shape=[jax.ShapeDtypeStruct(shape, F32) for shape in shapes],
        grid_spec=pltpu.PrefetchScalarGridSpec(
            num_scalar_prefetch=1,
            grid=(1,),
            in_specs=[fixed(mine.shape)] * 2,
            out_specs=[fixed(shape) for shape in shapes],
            scratch_shapes=[pltpu.VMEM((2 * rows, EXTRA), F32)],
        ),
        compiler_params=pltpu.CompilerParams(vmem_limit_bytes=VMEM_LIMIT),
        name="dense_outputs",
    )(core.astype(jnp.int32)[None], mine, other)
    return query, key, value, output, router, gains[0], gains[1]


def make_body(z_size, small_grid):
    def core_half(shard, core):
        rows = shard.shape[0] // 2
        return lax.dynamic_slice_in_dim(shard, core * rows, rows, 0)

    def dense_assemble(shard, parts, dp_index, core, *hold):
        rows = shard.shape[0] // 2
        moved = after(jnp.concatenate(parts, axis=0), *hold)
        other = swap_core(moved)
        places = [2 * dp_index]
        for which in (core, 1 - core):
            places += [2 * (dp_index ^ (j + 1)) + which for j in range(3)]
        return assemble(jnp.stack(places), shard, moved, other, rows)

    def across_z(mine, z):
        if z_size != 4:
            return lax.psum(mine.astype(F32), "z").astype(B16)
        rows = mine.shape[0] // z_size
        low = mine.astype(B16)
        steps = [2, 1, 3]
        got = []
        for k in steps:
            theirs = lax.dynamic_slice_in_dim(low, (z + k) % z_size * rows, rows, 0)
            got.append(cyclic(theirs, z_size, k))
        total = column_sum(lax.dynamic_slice_in_dim(mine, z * rows, rows, 0), got).astype(B16)
        sent = {k: cyclic(total, z_size, -k) for k in steps}
        quarters = [total] + [sent[k] for k in steps]
        places = (jnp.arange(z_size, dtype=jnp.int32) - z) % z_size
        places = jnp.where((places == 1) | (places == 2), 3 - places, places)
        return jnp.take(jnp.stack(quarters), places, axis=0).reshape(mine.shape)

    def dense_sum(grads):
        return lax.psum_scatter(
            lax.psum(grads, ("z", "core")), ("y", "x"), scatter_dimension=0, tiled=True
        )

    def body(
        layer_input,
        attn_gain,
        w_query,
        w_key,
        w_value,
        w_output,
        moe_gain,
        w_router,
        w_gate,
        w_up,
        w_down,
        routes,
        priority,
        prefix_len,
        out_grad,
    ):
        tok_rows, model_width = layer_input.shape
        dp_size = lax.axis_size("y") * lax.axis_size("x")
        dp_index = lax.axis_index("y") * lax.axis_size("x") + lax.axis_index("x")
        z = lax.axis_index("z")
        core = lax.axis_index("core")
        seq_len = tok_rows * dp_size
        top_count = routes.shape[1]
        local = w_gate.shape[0]
        capacity = 5 * tok_rows * top_count // (4 * EXPERTS)
        group_size = H // KVH
        score_scale = HD ** (-0.5)

        gains = jnp.stack([attn_gain, moe_gain], axis=1)
        rows = w_query.shape[0]
        dense_pack = jnp.concatenate(
            [w_output, w_query, w_key, w_value, w_router, gains, jnp.zeros((rows, 94), B16)], axis=1
        )
        wide = H * HD
        narrow = KVH * HD
        expert_ids = jnp.arange(EXPERTS, dtype=jnp.int32)
        hits = routes[:, :, None] == expert_ids[None, None, :]
        routed = jnp.any(hits, axis=1)
        place = jnp.where(
            routed, jnp.sum(jnp.where(hits, priority[:, :, None], 0), axis=1), jnp.int32(1 << 20)
        )
        ranks = jnp.sum((place[:, :, None] < place.T[None, :, :]).astype(F32), axis=0)
        code = pack_code(jnp.where(routed.T, ranks, -1.0).astype(B16))
        lead = ((2 * z + core) * local).astype(jnp.int32)[None]
        if small_grid:
            side = tok_rows // 2
            x_pack = jnp.concatenate([layer_input[:side], layer_input[side:]], axis=1)
            start_pack = jnp.concatenate([x_pack, core_half(dense_pack, core)], axis=1)
        else:
            grad_pieces = column_pieces(jnp.concatenate([out_grad, code], axis=0), z_size)

        query_pos = dp_index * tok_rows + jnp.arange(tok_rows, dtype=jnp.int32)
        in_float = layer_input.astype(F32)
        steps = jnp.arange(tok_rows, dtype=jnp.int32)
        eff = w_gate.shape[2]
        in_rows, mid_rows = w_gate.shape[1], w_down.shape[1]
        folds = [w_down[:, :, f * eff : (f + 1) * eff] for f in range(model_width // eff)]
        if small_grid:
            relative = dp_index ^ jnp.arange(4, dtype=jnp.int32)
            key_pos = (relative[:, None] * tok_rows + steps[None, :]).reshape(seq_len)
        else:
            relative = jnp.arange(dp_size, dtype=jnp.int32)
            key_pos = jnp.arange(seq_len, dtype=jnp.int32)
        order = jnp.concatenate([relative, lead])
        visible = (key_pos[None, :] <= query_pos[:, None]) | (key_pos[None, :] < prefix_len[0])
        if small_grid:
            start_parts = gather_near(start_pack)
            tables = (
                *turn_tables(key_pos.astype(F32)),
                jnp.where(visible.T, 0.0, MASKED_SCORE),
                jnp.pad(routed.astype(F32), ((0, 0), (0, 128 - EXPERTS))),
                [
                    jnp.concatenate([part[e] for part in (w_gate, w_up, *folds)], axis=0)
                    for e in range(local)
                ],
            )
            code = after(code, *tables[:3])
            grad_pieces = column_pieces(jnp.concatenate([out_grad, code], axis=0), z_size)
            grad_near = grad_pieces[1::2]
            start_parts, tables = after((start_parts, tables), grad_near[0])
            cosine, sine, bias, routed_wide, packs = tables
            start_parts += gather_far(after(start_parts, tables))
            dense_parts = [part[:, 2 * model_width :] for part in start_parts]
            dense_full = dense_assemble(dense_pack, dense_parts, dp_index, core, *grad_near[1:])
        else:
            dense_full = lax.all_gather(dense_pack, ("y", "x"), axis=0, tiled=True)
            full_output = dense_full[:, :model_width]
            head_full = dense_full[:, model_width:]
            full_query = head_full[:, :wide]
            full_key = head_full[:, wide : wide + narrow]
            full_value = head_full[:, wide + narrow : wide + 2 * narrow]

        if small_grid:
            halves, per = 2, local // 2
            weights = []
            near_0 = gather_near(after(packs[0], *start_parts[2:]))
            near_1 = gather_near(after(packs[1], dense_full))
        else:
            halves, per = 1, local
            pack = jnp.concatenate([w_gate, w_up, *folds], axis=1)
            every = lax.all_gather(pack, ("y", "x"), axis=0, tiled=False)
            weights = [every[j] for j in range(dp_size)]
        chunks = []
        if small_grid:
            (
                x_all, normed_all, query_rot, key_rot, value_all, attended, totals, misc, residual,
                moe_in, gates,
            ) = attention_forward(
                layer_input,
                start_parts,
                dense_full,
                bias,
                cosine,
                sine,
                routed_wide,
            )
            moe_in = after(moe_in, *near_0, *near_1, *grad_pieces)
            router_rows = misc[:EXPERTS].astype(B16)
            full_attn_gain = misc[EXPERTS]
            full_moe_gain = misc[EXPERTS + 1]
        else:
            places = query_pos.astype(F32)
            router_rows = head_full[:, wide + 2 * narrow : wide + 2 * narrow + EXPERTS].T
            full_attn_gain = head_full[:, wide + 2 * narrow + EXPERTS].astype(F32)
            full_moe_gain = head_full[:, wide + 2 * narrow + EXPERTS + 1].astype(F32)
            normed = rms_norm(in_float, full_attn_gain).astype(B16)
            query_lin = jnp.dot(normed, full_query, preferred_element_type=F32)
            key_lin = jnp.dot(normed, full_key, preferred_element_type=F32)
            value_low = jnp.dot(normed, full_value, preferred_element_type=F32).astype(B16)
            query_rot = (rotate(query_lin.reshape(tok_rows, H, HD), places) * score_scale).astype(B16)
            key_rot = rotate(key_lin.reshape(tok_rows, KVH, HD), places).astype(B16)
            key_rot = key_rot.reshape(tok_rows, narrow)
            both = jnp.concatenate([key_rot, value_low], axis=1)
            both_all = lax.all_gather(both, ("y", "x"), axis=0, tiled=True)
            key_all = both_all[:, :narrow]
            value_all = both_all[:, narrow:]

            def head_scores(head_idx):
                query_head = query_rot[:, head_idx * group_size : (head_idx + 1) * group_size, :]
                key_head = key_all[:, head_idx * HD : (head_idx + 1) * HD]
                scores = jnp.einsum("qgd,kd->gqk", query_head, key_head, preferred_element_type=F32)
                return jnp.where(visible[None, :, :], scores, MASKED_SCORE)

            mixed_heads = []
            log_totals = []
            for head_idx in range(KVH):
                scores = head_scores(head_idx)
                row_max = jnp.max(scores, axis=-1, keepdims=True)
                log_total = row_max + jnp.log(
                    jnp.sum(jnp.exp(scores - row_max), axis=-1, keepdims=True)
                )
                probs_low = jnp.exp(scores - log_total).astype(B16)
                value_head = value_all[:, head_idx * HD : (head_idx + 1) * HD]
                mixed_heads.append(
                    jnp.einsum("gqk,kd->qgd", probs_low, value_head, preferred_element_type=F32)
                )
                log_totals.append(log_total)
            attended = jnp.concatenate(mixed_heads, axis=1).reshape(tok_rows, wide).astype(B16)
            residual = in_float + jnp.dot(attended, full_output, preferred_element_type=F32)
            moe_in = rms_norm(residual, full_moe_gain).astype(B16)

        row_pieces = column_pieces(moe_in, z_size)
        grads_mine = jnp.stack(after(grad_pieces, moe_in))
        grads_other = swap_core(grads_mine)
        stage_1 = stage_2 = last_far = ()
        if small_grid:
            middle = packs[0].shape[0] // 2
            stage_1 = far_and_next(after((near_0, near_1), moe_in), packs[2])
        last = z_size // 2
        rows_near = [row_pieces[k] for k in range(z_size) if k != last]
        own_other = swap_core(after(moe_in, grads_other))
        if small_grid:
            stage_2 = far_and_next(
                [after(stage_1, *rows_near, grads_other, own_other)], packs[3]
            )
        rows_near_other = [own_other] + [
            swap_core(piece) for piece in after(rows_near[1:], *stage_1)
        ]
        (slot_grads_mine,) = dispatch_rows(
            lead, after(grads_mine, *rows_near_other), None, None, local, capacity
        )
        (slot_grads_other,) = dispatch_rows(
            lead, after(grads_other, slot_grads_mine), None, None, local, capacity
        )
        row_last = after(row_pieces[last], slot_grads_other)
        if small_grid:
            last_far = gather_far([part[middle:] for part in stage_2])
            chunks = [
                [(part, 0) for part in [packs[0], *near_0, *stage_1[::-1]]],
                [(part, 0) for part in [packs[1], *near_1]]
                + [(part, middle) for part in stage_1[::-1]],
                [(packs[2], 0)]
                + [(part, 2 * middle) for part in stage_1]
                + [(part, 0) for part in stage_2[::-1]],
                [(packs[3], 0)]
                + [(part, middle) for part in stage_2]
                + [(part, 0) for part in last_far],
            ]
        rows_mine = after([*rows_near[:last], row_last, *rows_near[last:]], *stage_2)
        rows_other = [*rows_near_other[:last], swap_core(row_last), *rows_near_other[last:]]
        slot_rows_mine, slot_gates_mine = dispatch_rows(
            lead, grads_mine, rows_mine, router_rows, local, capacity
        )
        slot_rows_other, slot_gates_other = dispatch_rows(
            lead, grads_other, after(rows_other, slot_rows_mine), router_rows, local, capacity
        )
        slot_rows_other = after(slot_rows_other, *last_far)
        ys, dxs, weight_grads, sums = [], [], [], []
        for half in range(halves):
            y, dx, grads = experts(
                order,
                half * per,
                per,
                (slot_rows_mine, slot_rows_other),
                (slot_grads_mine, slot_grads_other),
                (slot_gates_mine, slot_gates_other),
                weights,
                chunks[half * per : (half + 1) * per],
                capacity,
                in_rows,
                mid_rows,
            )
            ys.append(y)
            dxs.append(dx)
            weight_grads.append(grads)

        def grid_sum(grads, got):
            totals = []
            for half in range(2):
                own = grads[4 * half][0]
                direct, last = got[half][0], got[1 - half][1]
                totals.append(own.astype(F32) + direct.astype(F32) + last.astype(F32))
            return totals

        def second_step(grads, via, *more):
            _, x_a, y_a, _, _, x_b, y_b, _ = grads
            return cross(*join_parts((x_a, x_b, *more[:1]), (y_b, y_a, *more[1:]), via[::-1]))

        if small_grid:
            early, late = weight_grads
            via = cross(early[3], early[7])
            dxs = after(dxs, *via)
            early_got = second_step(early, via, late[3], late[7])
        dx_other = combine_rows(lead, z_size, grads_other, dxs, local, capacity)
        y_other = combine_rows(lead, z_size, grads_other, after(ys, dx_other), local, capacity)
        dx_other = after(swap_core(dx_other), y_other)
        dx_low = combine_rows(lead, 0, grads_mine, dxs, local, capacity, dx_other)
        dx_low, y_other = after((dx_low, swap_core(y_other)), dx_low[0])
        dx_pieces = column_send_last(dx_low, z_size) + column_send_some(dx_low, z_size)
        y_low = combine_rows(lead, 0, grads_mine, ys, local, capacity, y_other)
        dx_pieces = after(dx_pieces, *y_low)
        y_pieces = column_send_some(after(y_low, *dx_pieces), z_size)
        if small_grid:
            early_got = after(early_got, *dx_pieces)
            late_got = second_step(late, early_got)
        if small_grid:
            keep, give, normed_first, normed_a, normed_b, residual_grad = attention_backward(
                jnp.stack([dp_index, core]).astype(jnp.int32),
                (dx_low[0], *dx_pieces),
                out_grad,
                residual,
                gates,
                misc,
                attended,
                moe_in,
                (x_all, normed_all, query_rot, key_rot, value_all, totals),
                dense_full,
                after(bias, *early_got),
                cosine,
                sine,
            )
            late_got, y_pieces = after((late_got, y_pieces), residual_grad)
            normed_first, keep, give = after((normed_first, keep, give), *late_got, *y_pieces)
            y_pieces += column_send_last(y_low, z_size, *y_pieces)
            dense_first, dense_a, dense_b = core_halves(keep, swap_core(give))
            normed_got = grid_scatter_first(*normed_first)
            dense_got = grid_scatter_first(*after(dense_first, *normed_got))
            early_got, late_got = after((early_got, late_got), *dense_got)
            dense_halves = grid_scatter_second(dense_got, dense_a, dense_b)
            dense_low = across_z(
                jnp.concatenate(dense_halves, axis=0), z
            )
            (
                query_sum, key_sum, value_sum, output_sum, router_sum, attn_gain_sum, moe_gain_sum,
            ) = dense_outputs(core, dense_low, swap_core(dense_low), wide, narrow)
            y_pieces = after(y_pieces, *dense_halves)
            normed_grad = jnp.concatenate(
                grid_scatter_second(normed_got, normed_a, normed_b, *dense_halves), axis=0
            )
            first_value, first_pull = jax.vjp(lambda v: rms_norm(v, full_attn_gain), in_float)
            input_grad = residual_grad + first_pull(normed_grad)[0]
        else:
            y_pieces += column_send_last(y_low, z_size)
            moe_sum = column_sum(dx_low[0], dx_pieces)
            moe_in_grad = moe_sum[:, :model_width]
            gate_grad = (
                moe_sum[:, model_width : model_width + EXPERTS]
                + moe_sum[:, model_width + EXPERTS : model_width + 2 * EXPERTS]
            )
            logits = lax.dot_general(moe_in, router_rows, NT, preferred_element_type=F32)
            peak = jnp.max(jnp.where(routed, logits, MASKED_SCORE), axis=-1, keepdims=True)
            lifted = jnp.where(routed, jnp.exp(jnp.minimum(logits - peak, 0.0)), 0.0)
            gate_weights = lifted / jnp.sum(lifted, axis=-1, keepdims=True)
            grad_out = out_grad.astype(F32)
            centre = jnp.sum(gate_weights * gate_grad, axis=-1, keepdims=True)
            logit_low = (gate_weights * (gate_grad - centre)).astype(B16)
            moe_in_grad = moe_in_grad + jnp.dot(logit_low, router_rows, preferred_element_type=F32)
            norm_value, second_pull = jax.vjp(rms_norm, residual, full_moe_gain)
            resid_norm_grad, moe_gain_grad = second_pull(moe_in_grad)
            residual_grad = grad_out + resid_norm_grad
            attn_out_grad = residual_grad.astype(B16)
            router_grad = jnp.einsum("td,te->de", moe_in, logit_low, preferred_element_type=F32)
            wout_grad = jnp.einsum("tc,td->cd", attended, attn_out_grad, preferred_element_type=F32)
            attended_grad = (
                jnp.einsum("td,cd->tc", attn_out_grad, full_output, preferred_element_type=F32)
                .astype(B16)
                .reshape(tok_rows, H, HD)
            )
            query_grads = []
            key_parts = []
            value_parts = []
            for head_idx in range(KVH):
                scores = head_scores(head_idx)
                attention_probs = jnp.exp(scores - log_totals[head_idx])
                probs_low = attention_probs.astype(B16)
                grad_head = attended_grad[:, head_idx * group_size : (head_idx + 1) * group_size, :]
                query_head = query_rot[:, head_idx * group_size : (head_idx + 1) * group_size, :]
                key_head = key_all[:, head_idx * HD : (head_idx + 1) * HD]
                value_head = value_all[:, head_idx * HD : (head_idx + 1) * HD]
                probs_grad = jnp.einsum("qgd,kd->gqk", grad_head, value_head, preferred_element_type=F32)
                row_delta = jnp.sum(attention_probs * probs_grad, axis=-1, keepdims=True)
                score_grad = (attention_probs * (probs_grad - row_delta)).astype(B16)
                query_grads.append(
                    jnp.einsum("gqk,kd->qgd", score_grad, key_head, preferred_element_type=F32)
                )
                key_parts.append(
                    jnp.einsum("gqk,qgd->kd", score_grad, query_head, preferred_element_type=F32)
                )
                value_parts.append(
                    jnp.einsum("gqk,qgd->kd", probs_low, grad_head, preferred_element_type=F32)
                )
            both_part = jnp.concatenate(key_parts + value_parts, axis=1)
            both_sum = lax.psum_scatter(both_part, ("y", "x"), scatter_dimension=0, tiled=True)
            query_rot_grad = jnp.concatenate(query_grads, axis=1) * score_scale
            key_rot_grad = both_sum[:, :narrow].reshape(tok_rows, KVH, HD)
            value_grad = both_sum[:, narrow:].astype(B16)
            query_grad = rotate(query_rot_grad, -places).reshape(tok_rows, wide).astype(B16)
            key_grad = rotate(key_rot_grad, -places).reshape(tok_rows, narrow).astype(B16)
            wq_grad = jnp.einsum("td,tc->dc", normed, query_grad, preferred_element_type=F32)
            wk_grad = jnp.einsum("td,tc->dc", normed, key_grad, preferred_element_type=F32)
            wv_grad = jnp.einsum("td,tc->dc", normed, value_grad, preferred_element_type=F32)
            normed_grad = jnp.einsum("tc,dc->td", query_grad, full_query, preferred_element_type=F32)
            normed_grad = normed_grad + jnp.einsum(
                "tc,dc->td", key_grad, full_key, preferred_element_type=F32
            )
            normed_grad = normed_grad + jnp.einsum(
                "tc,dc->td", value_grad, full_value, preferred_element_type=F32
            )
            first_value, first_pull = jax.vjp(rms_norm, in_float, full_attn_gain)
            input_norm_grad, attn_gain_grad = first_pull(normed_grad)
            input_grad = residual_grad + input_norm_grad
            query_sum = dense_sum(wq_grad)
            key_sum = dense_sum(wk_grad)
            value_sum = dense_sum(wv_grad)
            output_sum = dense_sum(wout_grad)
            extra_sum = dense_sum(
                jnp.concatenate(
                    [
                        router_grad,
                        attn_gain_grad[:, None],
                        moe_gain_grad[:, None],
                        jnp.zeros((model_width, EXTRA - EXPERTS - 2), F32),
                    ],
                    axis=1,
                )
            )
            router_sum = extra_sum[:, :EXPERTS]
            attn_gain_sum = extra_sum[:, EXPERTS]
            moe_gain_sum = extra_sum[:, EXPERTS + 1]
        layer_output = (residual + column_sum(y_low[0], y_pieces)).astype(B16)
        if small_grid:
            parts = grid_sum(early, early_got) + grid_sum(late, late_got)
            pack_grad = jnp.concatenate(parts, axis=0)
        else:
            pack_grad = lax.psum_scatter(
                weight_grads[0][0].astype(F32), ("y", "x"), scatter_dimension=0, tiled=False
            )
        down = 2 * in_rows
        expert_grads = [
            pack_grad[:, :in_rows],
            pack_grad[:, in_rows:down],
            jnp.concatenate(
                [
                    pack_grad[:, down + f * mid_rows : down + (f + 1) * mid_rows]
                    for f in range(model_width // eff)
                ],
                axis=2,
            ),
        ]

        return (
            layer_output,
            input_grad,
            attn_gain_sum,
            query_sum,
            key_sum,
            value_sum,
            output_sum,
            moe_gain_sum,
            router_sum,
            expert_grads[0],
            expert_grads[1],
            expert_grads[2],
        )

    return body


def solution(mesh):
    groups = mesh.shape["expert"]
    members = mesh.shape["dp"]
    z_size = groups // 2
    side = math.isqrt(members)
    grid = Mesh(
        mesh.devices.reshape(z_size, 2, members // side, side), ("z", "core", "y", "x")
    )
    expert = ("z", "core")
    dp = ("y", "x")
    every = expert + dp
    placed = (
        P(every, None),
        P(dp),
        P(dp, None),
        P(dp, None),
        P(dp, None),
        P(dp, None),
        P(dp),
        P(dp, None),
        P(expert, dp, None),
        P(expert, dp, None),
        P(expert, dp, None),
        P(every, None),
        P(every, None),
        P(expert),
        P(every, None),
    )
    return jax.shard_map(
        make_body(z_size, members == 4 and side == 2 and EXPERTS == 4 * groups),
        mesh=grid,
        in_specs=placed,
        out_specs=(
            P(every, None),
            P(every, None),
            P(dp),
            P(dp, None),
            P(dp, None),
            P(dp, None),
            P(dp, None),
            P(dp),
            P(dp, None),
            P(expert, dp, None),
            P(expert, dp, None),
            P(expert, dp, None),
        ),
        check_vma=False,
    )
```
